32 devices in a mesh: dp: 16 (over z, y, x), seq: 2 (over core).
Axes of the slice: x: 2, y: 2, z: 4, core: 2. Of those that a mesh axis runs over, the one named last changes fastest.
Arguments:
- images: bfloat16 [16, 1024, 1024], P('dp', 'seq'), may hold values from -6 to 6
- encoder_states: bfloat16 [16, 128, 1024], P('dp'), may hold values from -6 to 6
- image_row: int32 [16], P('dp'), may hold values from 0 to 15
- image_seg: int32 [16], P('dp'), may hold values from 0 to 3
- caption_seg: int32 [16, 128], replicated, may hold values from 0 to 3, never falling along the last dimension, each value on 1 to 64 neighbouring positions
- ln1_gain: bfloat16 [1024], P(('dp', 'seq')), may hold values from 0.5 to 1.5
- ln1_bias: bfloat16 [1024], P(('dp', 'seq')), may hold values from -1 to 1
- w_query: bfloat16 [1024, 1024], P(('dp', 'seq')), may hold values from -0.1875 to 0.1875
- w_key: bfloat16 [1024, 1024], P(('dp', 'seq')), may hold values from -0.1875 to 0.1875
- w_value: bfloat16 [1024, 1024], P(('dp', 'seq')), may hold values from -0.1875 to 0.1875
- w_out: bfloat16 [1024, 1024], P(('dp', 'seq')), may hold values from -1.5 to 1.5
- ln2_gain: bfloat16 [1024], P(('dp', 'seq')), may hold values from 0.5 to 1.5
- ln2_bias: bfloat16 [1024], P(('dp', 'seq')), may hold values from -1 to 1
- c_query: bfloat16 [1024, 1024], P(('dp', 'seq')), may hold values from -0.1875 to 0.1875
- c_key: bfloat16 [1024, 1024], P(('dp', 'seq')), may hold values from -0.1875 to 0.1875
- c_value: bfloat16 [1024, 1024], P(('dp', 'seq')), may hold values from -0.1875 to 0.1875
- c_out: bfloat16 [1024, 1024], P(('dp', 'seq')), may hold values from -0.75 to 0.75
- ln3_gain: bfloat16 [1024], P(('dp', 'seq')), may hold values from 0.5 to 1.5
- ln3_bias: bfloat16 [1024], P(('dp', 'seq')), may hold values from -1 to 1
- w_in: bfloat16 [1024, 4096], P(('dp', 'seq')), may hold values from -0.1875 to 0.1875
- b_in: bfloat16 [4096], P(('dp', 'seq')), may hold values from -1 to 1
- w_outer: bfloat16 [4096, 1024], P(('dp', 'seq')), may hold values from -0.09375 to 0.09375
- b_outer: bfloat16 [1024], P(('dp', 'seq')), may hold values from -2 to 2
- cotangent: bfloat16 [16, 1024, 1024], P('dp', 'seq'), may hold values from -6 to 6
Outputs:
- block_out: bfloat16 [16, 1024, 1024], P('dp', 'seq')
- image_grad: float32 [16, 1024, 1024], P('dp', 'seq')
- caption_grad: float32 [16, 128, 1024], P('dp', 'seq')
- grad_ln1_gain: float32 [1024], P(('dp', 'seq'))
- grad_ln1_bias: float32 [1024], P(('dp', 'seq'))
- grad_w_query: float32 [1024, 1024], P(('dp', 'seq'))
- grad_w_key: float32 [1024, 1024], P(('dp', 'seq'))
- grad_w_value: float32 [1024, 1024], P(('dp', 'seq'))
- grad_w_out: float32 [1024, 1024], P(('dp', 'seq'))
- grad_ln2_gain: float32 [1024], P(('dp', 'seq'))
- grad_ln2_bias: float32 [1024], P(('dp', 'seq'))
- grad_c_query: float32 [1024, 1024], P(('dp', 'seq'))
- grad_c_key: float32 [1024, 1024], P(('dp', 'seq'))
- grad_c_value: float32 [1024, 1024], P(('dp', 'seq'))
- grad_c_out: float32 [1024, 1024], P(('dp', 'seq'))
- grad_ln3_gain: float32 [1024], P(('dp', 'seq'))
- grad_ln3_bias: float32 [1024], P(('dp', 'seq'))
- grad_w_in: float32 [1024, 4096], P(('dp', 'seq'))
- grad_b_in: float32 [4096], P(('dp', 'seq'))
- grad_w_outer: float32 [4096, 1024], P(('dp', 'seq'))
- grad_b_outer: float32 [1024], P(('dp', 'seq'))
The draws below stay inside these ranges and needn't reach their ends.
Inputs may be any that keep to these rules, and one draw needn't show every extreme that they name: `image_row`: each image names the row that holds its caption. `image_seg`: the caption's segment within its row. `caption_seg`: along a row segment ids never fall; each of the 4 segments holds at least one token.
All inputs are finite; a program needn't handle non-finite values.
Results may differ from the reference program's by a relative error of at most 0.025.
Values may be sent and summed in bfloat16 or wider, within the bound.
A program may use at most 320 MiB of HBM per device.

```python
import math
import jax
import jax.numpy as jnp
import numpy as np
from jax import lax

D = 1024
HEADS = 16
HEAD_DIM = 64
FF = 4096
LEN = 1024
ENC_LEN = 128
SEGS = 4
IMG_DEV = 1
IMAGES = 16
ENC_ROWS = 16


def with_ends(entries, own_key, smallest, high):
    longest = entries.shape.index(max(entries.shape))
    spots = []
    for shift in (0, 1):
        where = [jax.random.randint(jax.random.fold_in(own_key, axis), (), 0, length) for axis, length in enumerate(entries.shape)]
        where[longest] = (where[longest] + shift) % entries.shape[longest]
        spots.append(tuple(where))
    return entries.at[spots[0]].set(smallest).at[spots[1]].set(high)


def block_levels(stream_key, dims, cuts, smallest, top_value):
    level, own = 1.0, jax.random.fold_in(stream_key, 6)
    for dim, blocks in cuts:
        heights = jnp.exp(jax.random.uniform(jax.random.fold_in(own, dim), (blocks,), jnp.float32, smallest / len(cuts), top_value / len(cuts)))
        level = level * jnp.repeat(heights, dims[dim] // blocks).reshape([-1 if axis == dim else 1 for axis in range(len(dims))])
    return level


def profile(amount, total, bound, skew):
    loads = [(1 << 20) // math.isqrt(standing ** skew) + 1 for standing in range(2, amount + 1)]
    rest, given = total - bound - (amount - 1), [1] * (amount - 1)
    while rest > 0:
        free = [i for i in range(amount - 1) if given[i] < bound]
        mass, left = sum([loads[i] for i in free]), rest
        for i in free:
            more = min(bound - given[i], max(1, left * loads[i] // mass), rest)
            given[i] = given[i] + more
            rest = rest - more
    return np.array([bound] + given)


def ragged(rng, amount, total, most, slope):
    if amount == 2:
        one = jax.random.randint(rng, (), max(1, total - most), min(most, total - 1) + 1)
        return jnp.stack([one, total - one])
    tallies = jnp.asarray(profile(amount, total, most, slope), jnp.int32)
    pairs = (amount - 1) // 2
    giver, taker = tallies[1:1 + 2 * pairs:2], tallies[2:2 + 2 * pairs:2]
    margin = jnp.minimum(giver - 1, most - taker)
    shifted = jax.random.randint(jax.random.fold_in(rng, 1), (pairs,), 0, 1 << 20) % (margin + 1)
    tallies = tallies.at[1:1 + 2 * pairs:2].set(giver - shifted).at[2:2 + 2 * pairs:2].set(taker + shifted)
    return tallies[jax.random.permutation(jax.random.fold_in(rng, 2), amount)]


def bell_draw(own_key, extent, deviation, most, cuts=(), dtype=jnp.bfloat16):
    values = deviation * jax.random.normal(own_key, extent, jnp.float32)
    if cuts:
        values = values * block_levels(own_key, extent, cuts, -0.22, 0.18)
    return jnp.clip(values, -most, most).astype(dtype)


def setup_inputs(seed: int = 0) -> dict:
    arg_keys = jax.random.split(jax.random.key(seed), 25)
    images = bell_draw(arg_keys[0], (IMAGES, LEN, D), 1.0, 6.0, ((0, 16), (1, 2)))
    encoder_states = bell_draw(arg_keys[1], (ENC_ROWS, ENC_LEN, D), 1.0, 6.0, ((0, 16),))
    image_row = with_ends(jax.random.randint(arg_keys[2], (IMAGES,), 0, ENC_ROWS), jax.random.fold_in(arg_keys[2], 1), 0, ENC_ROWS - 1).astype(jnp.int32)
    image_seg = with_ends(jax.random.randint(arg_keys[3], (IMAGES,), 0, SEGS), jax.random.fold_in(arg_keys[3], 1), 0, SEGS - 1).astype(jnp.int32)
    caption_seg = jax.vmap(lambda own: jnp.searchsorted(jnp.cumsum(ragged(own, SEGS, ENC_LEN, ENC_LEN // 2, 1)), jnp.arange(ENC_LEN), side="right"))(jax.random.split(arg_keys[4], ENC_ROWS)).reshape((ENC_ROWS, ENC_LEN)).astype(jnp.int32)
    ln1_gain = jnp.clip(1.0 + 0.1 * jax.random.normal(arg_keys[5], (D,), jnp.float32), 0.5, 1.5).astype(jnp.bfloat16)
    ln1_bias = bell_draw(arg_keys[6], (D,), 0.2, 1.0, ((0, 32),))
    w_query = bell_draw(arg_keys[7], (D, D), D ** -0.5, 0.1875, ((0, 32),))
    w_key = bell_draw(arg_keys[8], (D, D), D ** -0.5, 0.1875, ((0, 32),))
    w_value = bell_draw(arg_keys[9], (D, D), D ** -0.5, 0.1875, ((0, 32),))
    w_out = bell_draw(arg_keys[10], (D, D), (D // 64) ** -0.5, 1.5, ((0, 32),))
    ln2_gain = jnp.clip(1.0 + 0.1 * jax.random.normal(arg_keys[11], (D,), jnp.float32), 0.5, 1.5).astype(jnp.bfloat16)
    ln2_bias = bell_draw(arg_keys[12], (D,), 0.2, 1.0, ((0, 32),))
    c_query = bell_draw(arg_keys[13], (D, D), D ** -0.5, 0.1875, ((0, 32),))
    c_key = bell_draw(arg_keys[14], (D, D), D ** -0.5, 0.1875, ((0, 32),))
    c_value = bell_draw(arg_keys[15], (D, D), D ** -0.5, 0.1875, ((0, 32),))
    c_out = bell_draw(arg_keys[16], (D, D), (D // 16) ** -0.5, 0.75, ((0, 32),))
    ln3_gain = jnp.clip(1.0 + 0.1 * jax.random.normal(arg_keys[17], (D,), jnp.float32), 0.5, 1.5).astype(jnp.bfloat16)
    ln3_bias = bell_draw(arg_keys[18], (D,), 0.2, 1.0, ((0, 32),))
    w_in = bell_draw(arg_keys[19], (D, FF), D ** -0.5, 0.1875, ((0, 32),))
    b_in = bell_draw(arg_keys[20], (FF,), 0.2, 1.0, ((0, 32),))
    w_outer = bell_draw(arg_keys[21], (FF, D), FF ** -0.5, 0.09375, ((0, 32),))
    b_outer = bell_draw(arg_keys[22], (D,), 0.4, 2.0, ((0, 32),))
    cotangent = bell_draw(arg_keys[23], (IMAGES, LEN, D), 1.0, 6.0, ((0, 16), (1, 2)))
    return dict(images=images, encoder_states=encoder_states, image_row=image_row, image_seg=image_seg, caption_seg=caption_seg, ln1_gain=ln1_gain, ln1_bias=ln1_bias, w_query=w_query, w_key=w_key, w_value=w_value, w_out=w_out, ln2_gain=ln2_gain, ln2_bias=ln2_bias, c_query=c_query, c_key=c_key, c_value=c_value, c_out=c_out, ln3_gain=ln3_gain, ln3_bias=ln3_bias, w_in=w_in, b_in=b_in, w_outer=w_outer, b_outer=b_outer, cotangent=cotangent)


@jax.custom_vjp
def low(v):
    return lax.optimization_barrier(v.astype(jnp.bfloat16)).astype(jnp.float32)

@jax.custom_vjp
def low_back(v):
    return v

def low_keep(v):
    return (low(v), None)

def low_pass(kept, grad):
    return (grad,)

def back_keep(v):
    return (v, None)

def back_low(kept, grad):
    return (low(grad),)
low.defvjp(low_keep, low_pass)
low_back.defvjp(back_keep, back_low)
EPSILON = 1e-05
NEG_BIG = -1e+30
HIGHEST_PREC = lax.Precision.HIGHEST

def rounded_both(value):
    return low_back(low(value))

def norm_rows(value, gain, shift):
    center = value - lax.optimization_barrier(jnp.mean(value, axis=-1, keepdims=True))
    spread = lax.optimization_barrier(jnp.mean(center * center, axis=-1, keepdims=True))
    return center * lax.rsqrt(spread + EPSILON) * gain + shift

def project(rows, weight):
    return jnp.einsum('gld,de->gle', rows, weight, precision=HIGHEST_PREC)

def split_heads(value):
    return value.reshape(value.shape[0], value.shape[1], HEADS, HEAD_DIM)

def join_heads(value):
    return value.reshape(value.shape[0], value.shape[1], HEADS * HEAD_DIM)

def attention(queries, keys_in, values_in, allowed):
    scores = low_back(jnp.einsum('gqhd,gkhd->ghqk', split_heads(queries), split_heads(keys_in), precision=HIGHEST_PREC) * 0.125)
    scores = jnp.where(allowed, scores, NEG_BIG)
    row_max = lax.optimization_barrier(jnp.max(scores, axis=-1, keepdims=True))
    exponent = jnp.exp(scores - row_max)
    attn_weights = exponent / lax.optimization_barrier(jnp.sum(exponent, axis=-1, keepdims=True))
    mixed_rows = jnp.einsum('ghqk,gkhd->gqhd', low(attn_weights), split_heads(values_in), precision=HIGHEST_PREC)
    return rounded_both(join_heads(mixed_rows))

def block_group(images_group, rows_group, segs_group, encoder, caption_ids, params):
    gain_a, bias_a, query_w, key_w, value_w, out_w, gain_b, bias_b, cross_qw, cross_kw, cross_vw, cross_ow, gain_c, bias_c, inner_w, inner_b, outer_w, outer_b = params
    normed_a = low(norm_rows(images_group, gain_a, bias_a))
    queries = rounded_both(project(normed_a, query_w))
    keys_self = rounded_both(project(normed_a, key_w))
    values_self = rounded_both(project(normed_a, value_w))
    position = jnp.arange(LEN)
    causal = (position[None, :] <= position[:, None])[None, None]
    self_out = attention(queries, keys_self, values_self, causal)
    after_self = images_group + low_back(project(self_out, out_w))
    normed_b = low(norm_rows(after_self, gain_b, bias_b))
    cross_queries = rounded_both(project(normed_b, cross_qw))
    caption = jnp.take(encoder, rows_group, axis=0)
    cross_keys = rounded_both(project(caption, cross_kw))
    cross_values = rounded_both(project(caption, cross_vw))
    caption_mask = (jnp.take(caption_ids, rows_group, axis=0) == segs_group[:, None])[:, None, None, :]
    cross_out = attention(cross_queries, cross_keys, cross_values, caption_mask)
    after_cross = after_self + low_back(project(cross_out, cross_ow))
    normed_c = low(norm_rows(after_cross, gain_c, bias_c))
    hidden_pre = low_back(project(normed_c, inner_w) + inner_b)
    activated = low(jax.nn.gelu(hidden_pre))
    return after_cross + low_back(project(activated, outer_w) + outer_b)

def reference(images, encoder_states, image_row, image_seg, caption_seg, ln1_gain, ln1_bias, w_query, w_key, w_value, w_out, ln2_gain, ln2_bias, c_query, c_key, c_value, c_out, ln3_gain, ln3_bias, w_in, b_in, w_outer, b_outer, cotangent):
    params = tuple((weight_arr.astype(jnp.float32) for weight_arr in (ln1_gain, ln1_bias, w_query, w_key, w_value, w_out, ln2_gain, ln2_bias, c_query, c_key, c_value, c_out, ln3_gain, ln3_bias, w_in, b_in, w_outer, b_outer)))
    groups = IMAGES // IMG_DEV
    row_groups = image_row.reshape(groups, IMG_DEV)
    seg_groups = image_seg.reshape(groups, IMG_DEV)

    def forward(image_values, encoder_values, weights):

        def scan_step(carry, inputs):
            images_group, rows_group, segs_group = inputs
            result = jax.checkpoint(block_group)(images_group, rows_group, segs_group, encoder_values, caption_seg, weights)
            return (carry, result)
        _, outputs = lax.scan(scan_step, jnp.zeros((), jnp.float32), (image_values.reshape(groups, IMG_DEV, LEN, D), row_groups, seg_groups))
        return outputs.reshape(IMAGES, LEN, D)
    block_out, pull_back = jax.vjp(forward, images.astype(jnp.float32), encoder_states.astype(jnp.float32), params)
    image_grad, caption_grad, wgrads = pull_back(cotangent.astype(jnp.float32))
    return (block_out.astype(jnp.bfloat16), image_grad, caption_grad, wgrads[0], wgrads[1], wgrads[2], wgrads[3], wgrads[4], wgrads[5], wgrads[6], wgrads[7], wgrads[8], wgrads[9], wgrads[10], wgrads[11], wgrads[12], wgrads[13], wgrads[14], wgrads[15], wgrads[16], wgrads[17])
```

```python
import functools

import jax
import jax.numpy as jnp
from jax import lax
from jax.experimental import pallas as pl
from jax.experimental.pallas import tpu as pltpu
from jax.sharding import PartitionSpec as P

MESH = pl.DeviceIdType.MESH
ANY = pl.BlockSpec(memory_space=pl.ANY)


def place():
    dp, c = lax.axis_index("dp"), lax.axis_index("seq")
    x, y, z = dp % 2, (dp // 2) % 2, dp // 4
    return z, y, x, c


def flip(bit, on):
    return bit + on * (1 - 2 * bit)


def zxor(z, k):
    if k == 0:
        return z
    if k == 1:
        return z + 1 - 2 * (z % 2)
    if k == 2:
        return z + 2 - 4 * (z // 2)
    return 3 - z


def chip(z, y, x):
    return z * 4 + y * 2 + x


def greet(partners):
    barrier = pltpu.get_barrier_semaphore()
    for partner in partners:
        pl.semaphore_signal(barrier, inc=1, device_id=partner, device_id_type=MESH)
    pl.semaphore_wait(barrier, len(partners))


class Gather:
    def __init__(self, own, full, send_sem, recv_sem, local_sem):
        self.own, self.full = own, full
        self.send_sem, self.recv_sem, self.local_sem = send_sem, recv_sem, local_sem
        z, y, x, c = place()
        self.z, self.y, self.x, self.c = z, y, x, c
        self.yx = {
            (0, 0): (y, x),
            (1, 0): (flip(y, 1 - c), flip(x, c)),
            (0, 1): (flip(y, c), flip(x, 1 - c)),
            (1, 1): (1 - y, 1 - x),
        }

    def partners(self):
        z, c = self.z, self.c
        return [(chip(zxor(z, k), self.y, self.x), c) for k in (1, 2, 3)] + [
            (chip(z, *self.yx[1, 0]), c),
            (chip(z, *self.yx[0, 1]), c),
            (chip(z, self.y, self.x), 1 - c),
        ]

    def block(self, g, k, way, core):
        rows = self.own[g].shape[0]
        r = 2 * chip(zxor(self.z, k), *self.yx[way]) + core
        return self.full[g].at[pl.ds(pl.multiple_of(r * rows, rows), rows)]

    def copy(self, g, src, k, way, core, to, idx):
        return pltpu.make_async_remote_copy(
            src_ref=src,
            dst_ref=self.block(g, k, way, core),
            send_sem=self.send_sem.at[g, idx],
            recv_sem=self.recv_sem.at[g, idx],
            device_id=to,
            device_id_type=MESH,
        )

    def forward(self, g, k, way, src=None):
        z, c = self.z, self.c
        src = self.block(g, k, way, c) if src is None else src
        i1, i2 = way
        sends = []
        if i1 == 0 and i2 == 0:
            sends.append(((chip(z, *self.yx[1, 0]), c), 3 + k))
        if i2 == 0:
            sends.append(((chip(z, *self.yx[0, 1]), c), 7 + i1 * 4 + k))
        sends.append(((chip(z, self.y, self.x), 1 - c), 15 + i2 * 8 + i1 * 4 + k))
        for to, idx in sends:
            self.copy(g, src, k, way, c, to, idx).start()

    def start(self, g):
        c = self.c
        pltpu.make_async_copy(
            self.own[g], self.block(g, 0, (0, 0), c), self.local_sem.at[g]
        ).start()
        for k in (1, 2, 3):
            to = (chip(zxor(self.z, k), self.y, self.x), c)
            self.copy(g, self.own[g], 0, (0, 0), c, to, k - 1).start()
        self.forward(g, 0, (0, 0), self.own[g])

    def arrive(self, g, k, way, core, idx):
        me = (chip(self.z, self.y, self.x), 1 - self.c)
        self.copy(g, self.own[g], k, way, core, me, idx).wait_recv()

    def along_z(self, g):
        for k in (1, 2, 3):
            self.arrive(g, k, (0, 0), self.c, k - 1)
            self.forward(g, k, (0, 0))

    def first(self, g):
        for k in range(4):
            self.arrive(g, k, (1, 0), self.c, 3 + k)
            self.forward(g, k, (1, 0))

    def second(self, g):
        for i1 in range(2):
            for k in range(4):
                self.arrive(g, k, (i1, 1), self.c, 7 + i1 * 4 + k)
                self.forward(g, k, (i1, 1))

    def finish(self, g):
        for i2 in range(2):
            for i1 in range(2):
                for k in range(4):
                    self.arrive(g, k, (i2, i1), 1 - self.c, 15 + i2 * 8 + i1 * 4 + k)
        pltpu.make_async_copy(
            self.own[g], self.block(g, 0, (0, 0), self.c), self.local_sem.at[g]
        ).wait()
        me = (chip(self.z, self.y, self.x), 1 - self.c)
        for idx in range(31):
            self.copy(g, self.own[g], 0, (0, 0), self.c, me, idx).wait_send()


def gather_body(n, *refs):
    own, full = refs[:n], refs[n : 2 * n]
    ring = Gather(own, full, *refs[2 * n :])
    greet(ring.partners())
    for g in range(n):
        ring.start(g)
    for t in range(n + 2):
        if t < n:
            ring.along_z(t)
        if 0 <= t - 1 < n:
            ring.first(t - 1)
        if 0 <= t - 2 < n:
            ring.second(t - 2)
    for g in range(n):
        ring.finish(g)


def gather_all(blocks, count, collective_id):
    n = len(blocks)
    return pl.pallas_call(
        functools.partial(gather_body, n),
        out_shape=[
            jax.ShapeDtypeStruct((count * b.shape[0], b.shape[1]), b.dtype) for b in blocks
        ],
        in_specs=[ANY] * n,
        out_specs=[ANY] * n,
        scratch_shapes=[
            pltpu.SemaphoreType.DMA((n, 31)),
            pltpu.SemaphoreType.DMA((n, 31)),
            pltpu.SemaphoreType.DMA((n,)),
        ],
        compiler_params=pltpu.CompilerParams(
            collective_id=collective_id, has_side_effects=True
        ),
        name="gather_all",
    )(*blocks)


class Scatter:
    def __init__(self, view, own, from_core, from_first, from_second, from_z, out, sems):
        self.view, self.own, self.out = view, own, out
        self.from_core, self.from_first = from_core, from_first
        self.from_second, self.from_z = from_second, from_z
        self.send_sem, self.recv_sem, self.local_sem = sems
        z, y, x, c = place()
        self.z, self.y, self.x, self.c = z, y, x, c

    def ways(self, core):
        y, x = self.y, self.x
        return [
            flip(y, core * i1 + (1 - core) * i2) * 2 + flip(x, (1 - core) * i1 + core * i2)
            for i1 in range(2)
            for i2 in range(2)
        ]

    def partners(self):
        z, c = self.z, self.c
        way = self.ways(c)
        return [(zxor(z, k) * 4 + way[0], c) for k in (1, 2, 3)] + [
            (z * 4 + way[2], c),
            (z * 4 + way[1], c),
            (z * 4 + way[0], 1 - c),
        ]

    def remote(self, src, dst, u, idx, to):
        return pltpu.make_async_remote_copy(
            src_ref=src,
            dst_ref=dst,
            send_sem=self.send_sem.at[u, idx],
            recv_sem=self.recv_sem.at[u, idx],
            device_id=to,
            device_id_type=MESH,
        )

    def to_core(self, u, j):
        c = self.c
        return self.remote(
            self.view(u, self.ways(1 - c)[j], 1 - c),
            self.from_core(u).at[j],
            u,
            j,
            (self.z * 4 + self.ways(c)[0], 1 - c),
        )

    def to_own(self, u, j):
        c = self.c
        return pltpu.make_async_copy(
            self.view(u, self.ways(c)[j], c), self.own(u).at[j], self.local_sem.at[u, j]
        )

    def to_first(self, u):
        to = (self.z * 4 + self.ways(self.c)[2], self.c)
        return self.remote(self.own(u).at[pl.ds(2, 2)], self.from_first(u), u, 4, to)

    def to_second(self, u):
        to = (self.z * 4 + self.ways(self.c)[1], self.c)
        return self.remote(self.own(u).at[1], self.from_second(u), u, 5, to)

    def to_z(self, u, k):
        zk = zxor(self.z, k)
        to = (zk * 4 + self.ways(self.c)[0], self.c)
        return self.remote(self.own(u).at[0, zk], self.from_z(u).at[k - 1], u, 5 + k, to)

    def step0(self, u):
        for j in (2, 3, 0, 1):
            self.to_core(u, j).start()
            self.to_own(u, j).start()

    def step1(self, u):
        own, got = self.own(u), self.from_core(u)
        for j in (2, 3, 0, 1):
            self.to_core(u, j).wait_recv()
            self.to_own(u, j).wait()

            @pl.loop(0, 4)
            def _(i, j=j):
                own[j, i] = own[j, i] + got[j, i]

            if j == 3:
                self.to_first(u).start()

    def step2(self, u):
        own, got = self.own(u), self.from_first(u)
        self.to_first(u).wait_recv()
        for j in (1, 0):

            @pl.loop(0, 4)
            def _(i, j=j):
                own[j, i] = own[j, i] + got[j, i]

            if j == 1:
                self.to_second(u).start()

    def step3(self, u):
        own, got = self.own(u), self.from_second(u)
        self.to_second(u).wait_recv()

        @pl.loop(0, 4)
        def _(i):
            own[0, i] = own[0, i] + got[i]

        for k in (2, 3, 1):
            self.to_z(u, k).start()

    def step4(self, u):
        own, got = self.own(u), self.from_z(u)
        for k in (1, 2, 3):
            self.to_z(u, k).wait_recv()
        total = own[0, self.z].astype(jnp.float32) + got[0].astype(jnp.float32)
        total = total + (got[1].astype(jnp.float32) + got[2].astype(jnp.float32))
        self.out(u, total)

    def finish(self, u):
        for j in range(4):
            self.to_core(u, j).wait_send()
        self.to_first(u).wait_send()
        self.to_second(u).wait_send()
        for k in (1, 2, 3):
            self.to_z(u, k).wait_send()


LAG = 1


def run_scatter(units, ring):
    greet(ring.partners())
    for t in range(units + 4 * LAG + 2):
        for lag, step in (
            (0, ring.step0),
            (2, ring.step1),
            (2 + LAG, ring.step2),
            (2 + 2 * LAG, ring.step3),
            (2 + 3 * LAG, ring.step4),
        ):
            if 0 <= t - lag < units:
                step(t - lag)
    for u in range(units):
        ring.finish(u)


def scatter_body(pieces, n, *refs):
    grads, outs = refs[:n], refs[n : 2 * n]
    own, core, first, second, along = refs[2 * n : 2 * n + 5]
    small = refs[2 * n + 5 : 2 * n + 10]
    sems = refs[2 * n + 10 :]

    def pick(big, little, u):
        return little if pieces[u] is None else big.at[u]

    def view(u, yx, c):
        if pieces[u] is None:
            return grads[n - 1].at[:, yx, c]
        a, row, col = pieces[u]
        return grads[a].at[:, yx, c, pl.ds(row, 32), pl.ds(col, 1024)]

    def out(u, total):
        if pieces[u] is None:
            outs[n - 1][...] = total
        else:
            a, row, col = pieces[u]
            outs[a][pl.ds(row, 32), pl.ds(col, 1024)] = total

    ring = Scatter(
        view,
        lambda u: pick(own, small[0], u),
        lambda u: pick(core, small[1], u),
        lambda u: pick(first, small[2], u),
        lambda u: pick(second, small[3], u),
        lambda u: pick(along, small[4], u),
        out,
        sems,
    )
    run_scatter(len(pieces), ring)


def scatter_all(grads, collective_id):
    n = len(grads)
    views, pieces, outs = [], [], []
    for a, g in enumerate(grads):
        rows = g.shape[0] // 32
        views.append(g.reshape(4, 4, 2, rows, g.shape[1]))
        outs.append(jax.ShapeDtypeStruct((rows, g.shape[1]), jnp.float32))
        if a == n - 1:
            pieces.append(None)
        else:
            pieces += [
                (a, row, col) for row in range(0, rows, 32) for col in range(0, g.shape[1], 1024)
            ]
    u = len(pieces)

    def buffers(count, dtype, *tail):
        lead = () if count is None else (count,)
        return [
            pltpu.VMEM(lead + (4, 4) + tail, dtype),
            pltpu.VMEM(lead + (4, 4) + tail, dtype),
            pltpu.VMEM(lead + (2, 4) + tail, dtype),
            pltpu.VMEM(lead + (4,) + tail, dtype),
            pltpu.VMEM(lead + (3,) + tail, dtype),
        ]

    return pl.pallas_call(
        functools.partial(scatter_body, tuple(pieces), n),
        out_shape=outs,
        in_specs=[ANY] * n,
        out_specs=[pl.BlockSpec(memory_space=pltpu.VMEM)] * n,
        scratch_shapes=buffers(u - 1, jnp.bfloat16, 32, 1024)
        + buffers(None, jnp.float32, 8, 128)
        + [
            pltpu.SemaphoreType.DMA((u, 9)),
            pltpu.SemaphoreType.DMA((u, 9)),
            pltpu.SemaphoreType.DMA((u, 4)),
        ],
        compiler_params=pltpu.CompilerParams(
            collective_id=collective_id,
            has_side_effects=True,
            vmem_limit_bytes=58 * 1024 * 1024,
        ),
        name="scatter_all",
    )(*views)

HEADS = 16
HEAD_DIM = 64


EPSILON = 1e-05
NEG_BIG = -1e30


def norm_rows(value, gain, shift):
    center = value - jnp.mean(value, axis=-1, keepdims=True)
    spread = jnp.mean(center * center, axis=-1, keepdims=True)
    return center * lax.rsqrt(spread + EPSILON) * gain + shift


def project(rows, weight):
    return jnp.einsum("bsd,de->bse", rows, weight, preferred_element_type=jnp.float32)


def project_back(grads, weight):
    return jnp.einsum("bse,de->bsd", grads, weight, preferred_element_type=jnp.float32)


def weight_grad(rows, grads):
    return jnp.einsum("bsd,bse->de", rows, grads, preferred_element_type=jnp.float32)


def row_total(grads):
    return jnp.sum(grads.astype(jnp.float32), axis=(0, 1))


def split_heads(value):
    return value.reshape(value.shape[0], value.shape[1], HEADS, HEAD_DIM)


def join_heads(value):
    return value.reshape(value.shape[0], value.shape[1], HEADS * HEAD_DIM)


def scores_of(queries, keys_in, allowed):
    raw_scores = (
        jnp.einsum(
            "bqhd,bkhd->bhqk",
            split_heads(queries),
            split_heads(keys_in),
            preferred_element_type=jnp.float32,
        )
        * 0.125
    )
    return jnp.where(allowed, raw_scores, NEG_BIG)


def attend(queries, keys_in, values_in, allowed):
    scores = scores_of(queries, keys_in, allowed)
    row_max = jnp.max(scores, axis=-1, keepdims=True)
    exponent = jnp.exp(scores - row_max)
    total = jnp.sum(exponent, axis=-1, keepdims=True)
    attn_weights = exponent / total
    mixed_rows = jnp.einsum(
        "bhqk,bkhd->bqhd",
        attn_weights.astype(jnp.bfloat16),
        split_heads(values_in),
        preferred_element_type=jnp.float32,
    )
    return (join_heads(mixed_rows).astype(jnp.bfloat16), row_max + jnp.log(total))


def attend_back(queries, keys_in, values_in, allowed, log_total, grad_mixed):
    attn_weights = jnp.exp(scores_of(queries, keys_in, allowed) - log_total)
    grad_heads = split_heads(grad_mixed)
    grad_weights = jnp.einsum(
        "bqhd,bkhd->bhqk", grad_heads, split_heads(values_in), preferred_element_type=jnp.float32
    )
    grad_values = jnp.einsum(
        "bhqk,bqhd->bkhd",
        attn_weights.astype(jnp.bfloat16),
        grad_heads,
        preferred_element_type=jnp.float32,
    )
    inner_sum = jnp.sum(grad_weights * attn_weights, axis=-1, keepdims=True)
    grad_scores = (attn_weights * (grad_weights - inner_sum)).astype(jnp.bfloat16)
    grad_queries = (
        jnp.einsum(
            "bhqk,bkhd->bqhd", grad_scores, split_heads(keys_in), preferred_element_type=jnp.float32
        )
        * 0.125
    )
    grad_keys = (
        jnp.einsum(
            "bhqk,bqhd->bkhd", grad_scores, split_heads(queries), preferred_element_type=jnp.float32
        )
        * 0.125
    )
    return (join_heads(grad_queries), join_heads(grad_keys), join_heads(grad_values))


def on_block():
    return lax.axis_size("dp") == 16 and lax.axis_size("seq") == 2


def gather_params(vectors, weights, encoder_states):
    axes = ("dp", "seq")
    if not on_block():
        return (
            [lax.all_gather(v, axes, axis=0, tiled=True) for v in vectors],
            [lax.all_gather(w, axes, axis=0, tiled=True) for w in weights],
            lax.all_gather(encoder_states, "dp", axis=0, tiled=True),
        )
    packed = jnp.concatenate([v.astype(jnp.float32) for v in vectors])
    packed = jnp.pad(packed, (0, 1024 - packed.shape[0])).reshape(8, 128)
    half = encoder_states.shape[1] // 2
    tokens = lax.dynamic_slice_in_dim(encoder_states[0], lax.axis_index("seq") * half, half, 0)
    full = gather_all([packed, *weights, tokens], 32, 1)
    table = full[0].reshape(32, 1024)
    wide, at = [], 0
    for v in vectors:
        wide.append(table[:, at : at + v.shape[0]].reshape(-1))
        at += v.shape[0]
    return wide, full[1:-1], full[-1].reshape(16, 2 * half, -1)


def scatter_grads(vectors, weights):
    if not on_block():
        axes = ("dp", "seq")
        add = lambda g: lax.psum_scatter(g, axes, scatter_dimension=0, tiled=True)
        return [add(v) for v in vectors], [add(w) for w in weights]
    table = jnp.concatenate([v.reshape(32, -1) for v in vectors], axis=1)
    table = jnp.pad(table, ((0, 0), (0, 1024 - table.shape[1]))).reshape(256, 128)
    sums = scatter_all([*[w.astype(jnp.bfloat16) for w in weights], table], 2)
    flat, small, at = sums[-1].reshape(-1), [], 0
    for v in vectors:
        size = v.shape[0] // 32
        small.append(flat[at : at + size])
        at += size
    return small, sums[:-1]


def per_device(
    images,
    encoder_states,
    image_row,
    image_seg,
    caption_seg,
    ln1_gain,
    ln1_bias,
    w_query,
    w_key,
    w_value,
    w_out,
    ln2_gain,
    ln2_bias,
    c_query,
    c_key,
    c_value,
    c_out,
    ln3_gain,
    ln3_bias,
    w_in,
    b_in,
    w_outer,
    b_outer,
    cotangent,
):
    gathered = gather_params(
        (ln1_gain, ln1_bias, ln2_gain, ln2_bias, ln3_gain, ln3_bias, b_outer, b_in),
        (w_query, w_key, w_value, w_out, c_query, c_key, c_value, c_out, w_in, w_outer),
        encoder_states,
    )
    (gain_a, bias_a, gain_b, bias_b, gain_c, bias_c, outer_b, inner_b) = gathered[0]
    (query_w, key_w, value_w, out_w, cross_qw, cross_kw, cross_vw, cross_ow, inner_w, outer_w) = (
        gathered[1]
    )
    encoder_all = gathered[2]
    shard = images.shape[1]
    seq_index = lax.axis_index("seq")
    full_len = shard * lax.axis_size("seq")
    inputs_f = images.astype(jnp.float32)
    gain_a32, bias_a32 = (gain_a.astype(jnp.float32), bias_a.astype(jnp.float32))
    normed_a = norm_rows(inputs_f, gain_a32, bias_a32).astype(jnp.bfloat16)
    queries = project(normed_a, query_w).astype(jnp.bfloat16)
    keys_local = project(normed_a, key_w).astype(jnp.bfloat16)
    values_local = project(normed_a, value_w).astype(jnp.bfloat16)
    keys_all, values_all = (
        lax.all_gather(keys_local, "seq", axis=1, tiled=True),
        lax.all_gather(values_local, "seq", axis=1, tiled=True),
    )
    query_pos = seq_index * shard + jnp.arange(shard, dtype=jnp.int32)
    key_pos = jnp.arange(full_len, dtype=jnp.int32)
    causal = (key_pos[None, :] <= query_pos[:, None])[None, None]
    self_out, self_lse = attend(queries, keys_all, values_all, causal)
    after_self = inputs_f + project(self_out, out_w)
    gain_b32, bias_b32 = (gain_b.astype(jnp.float32), bias_b.astype(jnp.float32))
    normed_b = norm_rows(after_self, gain_b32, bias_b32).astype(jnp.bfloat16)
    cross_queries = project(normed_b, cross_qw).astype(jnp.bfloat16)
    caption = jnp.take(encoder_all, image_row, axis=0)
    cross_keys = project(caption, cross_kw).astype(jnp.bfloat16)
    cross_values = project(caption, cross_vw).astype(jnp.bfloat16)
    caption_mask = (jnp.take(caption_seg, image_row, axis=0) == image_seg[:, None])[
        :, None, None, :
    ]
    cross_out, cross_lse = attend(cross_queries, cross_keys, cross_values, caption_mask)
    after_cross = after_self + project(cross_out, cross_ow)
    gain_c32, bias_c32 = (gain_c.astype(jnp.float32), bias_c.astype(jnp.float32))
    normed_c = norm_rows(after_cross, gain_c32, bias_c32).astype(jnp.bfloat16)
    hidden_pre = project(normed_c, inner_w) + inner_b.astype(jnp.float32)
    activated = jax.nn.gelu(hidden_pre).astype(jnp.bfloat16)
    result = after_cross + project(activated, outer_w) + outer_b.astype(jnp.float32)
    block_out = result.astype(jnp.bfloat16)
    inner_wb, outer_wb = (inner_w, outer_w)
    grad_result = cotangent.astype(jnp.float32)
    grad_outer_w = weight_grad(activated, cotangent)
    grad_outer_b = row_total(cotangent)
    grad_act = project_back(cotangent, outer_wb)
    _, gelu_back = jax.vjp(jax.nn.gelu, hidden_pre)
    grad_hidden = gelu_back(grad_act)[0].astype(jnp.bfloat16)
    grad_inner_w = weight_grad(normed_c, grad_hidden)
    grad_inner_b = row_total(grad_hidden)
    grad_normed_c = project_back(grad_hidden, inner_wb)
    _, norm_c_back = jax.vjp(norm_rows, after_cross, gain_c32, bias_c32)
    grad_cross_part, grad_gain_c, grad_bias_c = norm_c_back(grad_normed_c)
    grad_after_cross = grad_result + grad_cross_part
    query_wb, key_wb, value_wb, out_wb = (query_w, key_w, value_w, out_w)
    cross_qwb, cross_kwb, cross_vwb, cross_owb = (cross_qw, cross_kw, cross_vw, cross_ow)
    grad_branch_b = grad_after_cross.astype(jnp.bfloat16)
    grad_cross_ow = weight_grad(cross_out, grad_branch_b)
    grad_cross_out = project_back(grad_branch_b, cross_owb).astype(jnp.bfloat16)
    grad_cq_raw, grad_ck_raw, grad_cv_raw = attend_back(
        cross_queries, cross_keys, cross_values, caption_mask, cross_lse, grad_cross_out
    )
    grad_cross_q = grad_cq_raw.astype(jnp.bfloat16)
    grad_ck_sum, grad_cv_sum = (
        lax.psum_scatter(
            grad_ck_raw.astype(jnp.bfloat16), "seq", scatter_dimension=1, tiled=True
        ).astype(jnp.float32),
        lax.psum_scatter(
            grad_cv_raw.astype(jnp.bfloat16), "seq", scatter_dimension=1, tiled=True
        ).astype(jnp.float32),
    )
    grad_ck_low = grad_ck_sum.astype(jnp.bfloat16)
    grad_cv_low = grad_cv_sum.astype(jnp.bfloat16)
    piece_len = grad_ck_sum.shape[1]
    caption_piece = lax.dynamic_slice_in_dim(caption, seq_index * piece_len, piece_len, 1)
    grad_cross_kw = weight_grad(caption_piece, grad_ck_low)
    grad_cross_vw = weight_grad(caption_piece, grad_cv_low)
    grad_caption = project_back(grad_ck_low, cross_kwb) + project_back(grad_cv_low, cross_vwb)
    row_count = encoder_all.shape[0]
    row_onehot = (image_row[:, None] == jnp.arange(row_count, dtype=jnp.int32)[None, :]).astype(
        jnp.float32
    )
    grad_rows = jnp.einsum("br,bsd->rsd", row_onehot, grad_caption, precision=lax.Precision.HIGHEST)
    caption_grad = lax.psum_scatter(
        grad_rows.astype(jnp.bfloat16), "dp", scatter_dimension=0, tiled=True
    ).astype(jnp.float32)
    grad_cross_qw = weight_grad(normed_b, grad_cross_q)
    grad_normed_b = project_back(grad_cross_q, cross_qwb)
    _, norm_b_back = jax.vjp(norm_rows, after_self, gain_b32, bias_b32)
    grad_self_part, grad_gain_b, grad_bias_b = norm_b_back(grad_normed_b)
    grad_after_self = grad_after_cross + grad_self_part
    grad_branch_a = grad_after_self.astype(jnp.bfloat16)
    grad_out_w = weight_grad(self_out, grad_branch_a)
    grad_self_out = project_back(grad_branch_a, out_wb).astype(jnp.bfloat16)
    keys_back, values_back = (keys_all, values_all)
    grad_q_raw, grad_k_raw, grad_v_raw = attend_back(
        queries, keys_back, values_back, causal, self_lse, grad_self_out
    )
    grad_k_sum, grad_v_sum = (
        lax.psum_scatter(
            grad_k_raw.astype(jnp.bfloat16), "seq", scatter_dimension=1, tiled=True
        ).astype(jnp.float32),
        lax.psum_scatter(
            grad_v_raw.astype(jnp.bfloat16), "seq", scatter_dimension=1, tiled=True
        ).astype(jnp.float32),
    )
    grad_q_low = grad_q_raw.astype(jnp.bfloat16)
    grad_k_low = grad_k_sum.astype(jnp.bfloat16)
    grad_v_low = grad_v_sum.astype(jnp.bfloat16)
    grad_query_w = weight_grad(normed_a, grad_q_low)
    grad_key_w = weight_grad(normed_a, grad_k_low)
    grad_value_w = weight_grad(normed_a, grad_v_low)
    grad_normed_a = (
        project_back(grad_q_low, query_wb)
        + project_back(grad_k_low, key_wb)
        + project_back(grad_v_low, value_wb)
    )
    _, norm_a_back = jax.vjp(norm_rows, inputs_f, gain_a32, bias_a32)
    grad_input_part, grad_gain_a, grad_bias_a = norm_a_back(grad_normed_a)
    image_grad = grad_after_self + grad_input_part
    small, big = scatter_grads(
        (
            grad_gain_a,
            grad_bias_a,
            grad_gain_b,
            grad_bias_b,
            grad_gain_c,
            grad_bias_c,
            grad_outer_b,
            grad_inner_b,
        ),
        (
            grad_query_w,
            grad_key_w,
            grad_value_w,
            grad_out_w,
            grad_cross_qw,
            grad_cross_kw,
            grad_cross_vw,
            grad_cross_ow,
            grad_inner_w,
            grad_outer_w,
        ),
    )
    return (
        block_out,
        image_grad,
        caption_grad,
        small[0],
        small[1],
        big[0],
        big[1],
        big[2],
        big[3],
        small[2],
        small[3],
        big[4],
        big[5],
        big[6],
        big[7],
        small[4],
        small[5],
        big[8],
        small[7],
        big[9],
        small[6],
    )


def solution(mesh):
    in_specs = (
        P("dp", "seq", None),
        P("dp", None, None),
        P("dp"),
        P("dp"),
        P(),
        P(("dp", "seq")),
        P(("dp", "seq")),
        P(("dp", "seq"), None),
        P(("dp", "seq"), None),
        P(("dp", "seq"), None),
        P(("dp", "seq"), None),
        P(("dp", "seq")),
        P(("dp", "seq")),
        P(("dp", "seq"), None),
        P(("dp", "seq"), None),
        P(("dp", "seq"), None),
        P(("dp", "seq"), None),
        P(("dp", "seq")),
        P(("dp", "seq")),
        P(("dp", "seq"), None),
        P(("dp", "seq")),
        P(("dp", "seq"), None),
        P(("dp", "seq")),
        P("dp", "seq", None),
    )
    out_specs = (
        P("dp", "seq", None),
        P("dp", "seq", None),
        P("dp", "seq", None),
        P(("dp", "seq")),
        P(("dp", "seq")),
        P(("dp", "seq"), None),
        P(("dp", "seq"), None),
        P(("dp", "seq"), None),
        P(("dp", "seq"), None),
        P(("dp", "seq")),
        P(("dp", "seq")),
        P(("dp", "seq"), None),
        P(("dp", "seq"), None),
        P(("dp", "seq"), None),
        P(("dp", "seq"), None),
        P(("dp", "seq")),
        P(("dp", "seq")),
        P(("dp", "seq"), None),
        P(("dp", "seq")),
        P(("dp", "seq"), None),
        P(("dp", "seq")),
    )
    return jax.shard_map(
        per_device, mesh=mesh, in_specs=in_specs, out_specs=out_specs, check_vma=False
    )
```

```python
import functools

import jax
import jax.numpy as jnp
from jax import lax
from jax.experimental import pallas as pl
from jax.experimental.pallas import tpu as pltpu
from jax.sharding import PartitionSpec as P

MESH = pl.DeviceIdType.MESH
ANY = pl.BlockSpec(memory_space=pl.ANY)


def place():
    dp, c = lax.axis_index("dp"), lax.axis_index("seq")
    x, y, z = dp % 2, (dp // 2) % 2, dp // 4
    return z, y, x, c


def flip(bit, on):
    return bit + on * (1 - 2 * bit)


def zxor(z, k):
    if k == 0:
        return z
    if k == 1:
        return z + 1 - 2 * (z % 2)
    if k == 2:
        return z + 2 - 4 * (z // 2)
    return 3 - z


def chip(z, y, x):
    return z * 4 + y * 2 + x


def greet(partners):
    barrier = pltpu.get_barrier_semaphore()
    for partner in partners:
        pl.semaphore_signal(barrier, inc=1, device_id=partner, device_id_type=MESH)
    pl.semaphore_wait(barrier, len(partners))


class Gather:
    def __init__(self, split, own, full, send_sem, recv_sem, local_sem):
        self.split, self.own, self.full = split, own, full
        self.send_sem, self.recv_sem, self.local_sem = send_sem, recv_sem, local_sem
        z, y, x, c = place()
        self.z, self.y, self.x, self.c = z, y, x, c
        self.yx = {
            (0, 0): (y, x),
            (1, 0): (flip(y, 1 - c), flip(x, c)),
            (0, 1): (flip(y, c), flip(x, 1 - c)),
            (1, 1): (1 - y, 1 - x),
        }
        self.other = (chip(z, y, x), 1 - c)

    def partners(self):
        z, c = self.z, self.c
        return [(chip(zxor(z, k), self.y, self.x), c) for k in (1, 2, 3)] + [
            (chip(z, *self.yx[1, 0]), c),
            (chip(z, *self.yx[0, 1]), c),
            self.other,
        ]

    def block(self, g, k, way, core):
        rows = self.own[g].shape[0]
        r = chip(zxor(self.z, k), *self.yx[way])
        if g < self.split:
            return self.full[g].at[pl.ds(pl.multiple_of(2 * r * rows, rows), 2 * rows)]
        return self.full[g].at[pl.ds(pl.multiple_of((2 * r + core) * rows, rows), rows)]

    def remote(self, g, src, dst, to, idx):
        return pltpu.make_async_remote_copy(
            src_ref=src,
            dst_ref=dst,
            send_sem=self.send_sem.at[g, idx],
            recv_sem=self.recv_sem.at[g, idx],
            device_id=to,
            device_id_type=MESH,
        )

    def copy(self, g, src, k, way, core, to, idx):
        return self.remote(g, src, self.block(g, k, way, core), to, idx)

    def forward(self, g, k, way, src=None):
        z, c = self.z, self.c
        src = self.block(g, k, way, c) if src is None else src
        i1, i2 = way
        sends = []
        if i1 == 0 and i2 == 0:
            sends.append(((chip(z, *self.yx[1, 0]), c), 3 + k))
        if i2 == 0:
            sends.append(((chip(z, *self.yx[0, 1]), c), 7 + i1 * 4 + k))
        if g >= self.split:
            sends.append((self.other, 15 + i2 * 8 + i1 * 4 + k))
        for to, idx in sends:
            self.copy(g, src, k, way, c, to, idx).start()

    def half(self, g, core):
        rows, columns = self.own[g].shape
        columns //= 2
        at = pl.multiple_of((2 * chip(self.z, self.y, self.x) + self.c) * rows, rows)
        return (
            self.own[g].at[:, pl.ds(pl.multiple_of(core * columns, columns), columns)],
            self.full[g].at[pl.ds(at, rows)],
        )

    def keep(self, g):
        if g < self.split:
            src, dst = self.half(g, self.c)
        else:
            src, dst = self.own[g], self.block(g, 0, (0, 0), self.c)
        return pltpu.make_async_copy(src, dst, self.local_sem.at[g])

    def swap(self, g):
        src, dst = self.half(g, 1 - self.c)
        return self.remote(g, src, dst, self.other, 15)

    def start(self, g):
        self.keep(g).start()
        if g < self.split:
            self.swap(g).start()
        else:
            self.begin(g, self.own[g])

    def swapped(self, g):
        self.swap(g).wait_recv()
        self.keep(g).wait()
        self.begin(g, self.block(g, 0, (0, 0), self.c))

    def begin(self, g, src):
        for k in (1, 2, 3):
            to = (chip(zxor(self.z, k), self.y, self.x), self.c)
            self.copy(g, src, 0, (0, 0), self.c, to, k - 1).start()
        self.forward(g, 0, (0, 0), src)

    def arrive(self, g, k, way, core, idx):
        block = self.block(g, k, way, core)
        self.remote(g, block, block, self.other, idx).wait_recv()

    def along_z(self, g):
        for k in (1, 2, 3):
            self.arrive(g, k, (0, 0), self.c, k - 1)
            self.forward(g, k, (0, 0))

    def first(self, g):
        for k in range(4):
            self.arrive(g, k, (1, 0), self.c, 3 + k)
            self.forward(g, k, (1, 0))

    def second(self, g):
        for i1 in range(2):
            for k in range(4):
                self.arrive(g, k, (i1, 1), self.c, 7 + i1 * 4 + k)
                self.forward(g, k, (i1, 1))

    def finish(self, g):
        if g >= self.split:
            for i2 in range(2):
                for i1 in range(2):
                    for k in range(4):
                        self.arrive(g, k, (i2, i1), 1 - self.c, 15 + i2 * 8 + i1 * 4 + k)
            self.keep(g).wait()
        else:
            self.swap(g).wait_send()
        block = self.block(g, 0, (0, 0), self.c)
        for idx in range(15 if g < self.split else 31):
            self.remote(g, block, block, self.other, idx).wait_send()


AHEAD = 3


def gather_body(n, split, *refs):
    own, pair = refs[:n], refs[n]
    full, both = refs[n + 1 : 2 * n + 1], refs[2 * n + 1]
    pair_sem = refs[-1]
    ring = Gather(split, own, full, *refs[2 * n + 2 : -1])
    greet(ring.partners())
    for g in range(split):
        ring.start(g)
    rows = pair.shape[0]
    mine = both.at[pl.ds(pl.multiple_of(ring.c * rows, rows), rows)]
    keep = pltpu.make_async_copy(pair, mine, pair_sem.at[0])
    give = pltpu.make_async_remote_copy(
        src_ref=pair,
        dst_ref=mine,
        send_sem=pair_sem.at[1],
        recv_sem=pair_sem.at[2],
        device_id=ring.other,
        device_id_type=MESH,
    )
    keep.start()
    give.start()
    for g in range(split):
        ring.swapped(g)
    for t in range(n + 2):
        if t < n:
            ring.along_z(t)
        if max(split, AHEAD) <= t + AHEAD < n:
            ring.start(t + AHEAD)
        if 0 <= t - 1 < n:
            ring.first(t - 1)
        if 0 <= t - 2 < n:
            ring.second(t - 2)
    for g in range(n):
        ring.finish(g)
    keep.wait()
    give.wait()


def gather_all(blocks, split, pair, collective_id):
    n = len(blocks)
    shapes = [
        (32 * b.shape[0], b.shape[1] // 2 if g < split else b.shape[1])
        for g, b in enumerate(blocks)
    ]
    return pl.pallas_call(
        functools.partial(gather_body, n, split),
        out_shape=[jax.ShapeDtypeStruct(s, b.dtype) for s, b in zip(shapes, blocks)]
        + [jax.ShapeDtypeStruct((2 * pair.shape[0], pair.shape[1]), pair.dtype)],
        in_specs=[ANY] * (n + 1),
        out_specs=[ANY] * (n + 1),
        scratch_shapes=[
            pltpu.SemaphoreType.DMA((n, 31)),
            pltpu.SemaphoreType.DMA((n, 31)),
            pltpu.SemaphoreType.DMA((n,)),
            pltpu.SemaphoreType.DMA((3,)),
        ],
        compiler_params=pltpu.CompilerParams(
            collective_id=collective_id, has_side_effects=True
        ),
        name="gather_all",
    )(*blocks, pair)


class Scatter:
    def __init__(self, late, view, own, from_core, from_first, from_second, from_z, part, from_late, out, sems):
        self.late, self.part, self.from_late = late, part, from_late
        self.view, self.own, self.out = view, own, out
        self.from_core, self.from_first = from_core, from_first
        self.from_second, self.from_z = from_second, from_z
        self.send_sem, self.recv_sem, self.local_sem = sems
        z, y, x, c = place()
        self.z, self.y, self.x, self.c = z, y, x, c

    def ways(self, core):
        y, x = self.y, self.x
        return [
            flip(y, core * i1 + (1 - core) * i2) * 2 + flip(x, (1 - core) * i1 + core * i2)
            for i1 in range(2)
            for i2 in range(2)
        ]

    def partners(self):
        z, c = self.z, self.c
        way = self.ways(c)
        return [(zxor(z, k) * 4 + way[0], c) for k in (1, 2, 3)] + [
            (z * 4 + way[2], c),
            (z * 4 + way[1], c),
            (z * 4 + way[0], 1 - c),
        ]

    def remote(self, src, dst, u, idx, to):
        return pltpu.make_async_remote_copy(
            src_ref=src,
            dst_ref=dst,
            send_sem=self.send_sem.at[u, idx],
            recv_sem=self.recv_sem.at[u, idx],
            device_id=to,
            device_id_type=MESH,
        )

    def to_core(self, u, j):
        c = self.c
        return self.remote(
            self.view(u, self.ways(1 - c)[j], 1 - c),
            self.from_core(u).at[j],
            u,
            j,
            (self.z * 4 + self.ways(c)[0], 1 - c),
        )

    def to_own(self, u, j):
        c = self.c
        return pltpu.make_async_copy(
            self.view(u, self.ways(c)[j], c), self.own(u).at[j], self.local_sem.at[u, j]
        )

    def to_first(self, u):
        to = (self.z * 4 + self.ways(self.c)[2], self.c)
        return self.remote(self.own(u).at[pl.ds(2, 2)], self.from_first(u), u, 4, to)

    def to_second(self, u):
        to = (self.z * 4 + self.ways(self.c)[1], self.c)
        return self.remote(self.own(u).at[1], self.from_second(u), u, 5, to)

    def to_z(self, u, k):
        zk = zxor(self.z, k)
        to = (zk * 4 + self.ways(self.c)[0], self.c)
        return self.remote(self.own(u).at[0, zk], self.from_z(u).at[k - 1], u, 5 + k, to)

    def step0(self, u):
        for j in (2, 3, 0, 1):
            if not self.late(u):
                self.to_core(u, j).start()
            self.to_own(u, j).start()

    def step1(self, u):
        own = self.own(u)
        if self.late(u):
            for j in range(4):
                self.to_own(u, j).wait()
            self.to_first(u).start()
            return
        got = self.from_core(u)
        for j in (2, 3, 0, 1):
            self.to_core(u, j).wait_recv()
            self.to_own(u, j).wait()

            @pl.loop(0, 4)
            def _(i, j=j):
                own[j, i] = own[j, i] + got[j, i]

            if j == 3:
                self.to_first(u).start()

    def step2(self, u):
        own, got = self.own(u), self.from_first(u)
        self.to_first(u).wait_recv()
        for j in (1, 0):

            @pl.loop(0, 4)
            def _(i, j=j):
                own[j, i] = own[j, i] + got[j, i]

            if j == 1:
                self.to_second(u).start()

    def step3(self, u):
        own, got = self.own(u), self.from_second(u)
        self.to_second(u).wait_recv()

        @pl.loop(0, 4)
        def _(i):
            own[0, i] = own[0, i] + got[i]

        for k in (2, 3, 1):
            self.to_z(u, k).start()

    def step4(self, u):
        own, got = self.own(u), self.from_z(u)
        for k in (1, 2, 3):
            self.to_z(u, k).wait_recv()
        total = own[0, self.z].astype(jnp.float32) + got[0].astype(jnp.float32)
        total = total + (got[1].astype(jnp.float32) + got[2].astype(jnp.float32))
        if self.late(u):
            self.part(u)[...] = total
            self.to_late(u).start()
        else:
            self.out(u, total)

    def to_late(self, u):
        rows = self.part(u).shape[0] // 2
        theirs = pl.ds(pl.multiple_of((1 - self.c) * rows, rows), rows)
        to = (self.z * 4 + self.ways(self.c)[0], 1 - self.c)
        return self.remote(self.part(u).at[theirs], self.from_late(u), u, 0, to)

    def step5(self, u):
        if self.late(u):
            rows = self.part(u).shape[0] // 2
            self.to_late(u).wait_recv()
            mine = self.part(u)[pl.ds(pl.multiple_of(self.c * rows, rows), rows)]
            self.out(u, mine, self.from_late(u)[...])

    def finish(self, u):
        if self.late(u):
            self.to_late(u).wait_send()
        else:
            for j in range(4):
                self.to_core(u, j).wait_send()
        self.to_first(u).wait_send()
        self.to_second(u).wait_send()
        for k in (1, 2, 3):
            self.to_z(u, k).wait_send()


LAG = 1


def run_scatter(units, ring):
    greet(ring.partners())
    for t in range(units + 3 * LAG + 4):
        for lag, step in (
            (0, ring.step0),
            (2, ring.step1),
            (2 + LAG, ring.step2),
            (2 + 2 * LAG, ring.step3),
            (2 + 3 * LAG, ring.step4),
            (3 + 3 * LAG, ring.step5),
        ):
            if 0 <= t - lag < units:
                step(t - lag)
    for u in range(units):
        ring.finish(u)


def scatter_body(pieces, split, n, *refs):
    grads, outs = refs[:n], refs[n : 2 * n]
    bufs = refs[2 * n : 2 * n + 16]
    late, big, small = bufs[:6], bufs[6:11], bufs[11:]
    sems = refs[2 * n + 16 :]
    core = lax.axis_index("seq")

    def pick(i):
        def ref(u):
            if u < split:
                return late[i if i == 0 else i - 1].at[u]
            return small[i] if pieces[u] is None else big[i].at[u - split]

        return ref

    def view(u, yx, c):
        if pieces[u] is None:
            return grads[n - 1].at[:, yx, c]
        a, row, col = pieces[u]
        if u < split:
            return grads[a].at[:, yx]
        return grads[a].at[:, yx, c, pl.ds(row, 32), pl.ds(col, 1024)]

    def out(u, total, other=None):
        if pieces[u] is None:
            outs[n - 1][...] = total
            return
        a, row, col = pieces[u]
        if u < split:
            width = total.shape[1]
            outs[a][:, pl.ds(pl.multiple_of(core * width, width), width)] = total
            outs[a][:, pl.ds(pl.multiple_of((1 - core) * width, width), width)] = other
        else:
            outs[a][pl.ds(row, 32), pl.ds(col, 1024)] = total

    ring = Scatter(
        lambda u: u < split,
        view,
        pick(0),
        pick(1),
        pick(2),
        pick(3),
        pick(4),
        lambda u: late[4].at[u],
        lambda u: late[5].at[u],
        out,
        sems,
    )
    run_scatter(len(pieces), ring)


def scatter_all(grads, split, collective_id):
    n = len(grads)
    views, pieces, outs = [], [], []
    for a, g in enumerate(grads):
        rows, columns = g.shape[0] // 32, g.shape[1]
        if a < split:
            views.append(g.reshape(4, 4, 2 * rows, columns))
            outs.append(jax.ShapeDtypeStruct((rows, 2 * columns), jnp.float32))
            pieces.append((a, 0, 0))
            continue
        views.append(g.reshape(4, 4, 2, rows, columns))
        outs.append(jax.ShapeDtypeStruct((rows, columns), jnp.float32))
        if a == n - 1:
            pieces.append(None)
        else:
            pieces += [
                (a, row, col) for row in range(0, rows, 32) for col in range(0, columns, 1024)
            ]
    u = len(pieces)

    def buffers(count, dtype, *tail):
        lead = () if count is None else (count,)
        return [
            pltpu.VMEM(lead + (4, 4) + tail, dtype),
            pltpu.VMEM(lead + (4, 4) + tail, dtype),
            pltpu.VMEM(lead + (2, 4) + tail, dtype),
            pltpu.VMEM(lead + (4,) + tail, dtype),
            pltpu.VMEM(lead + (3,) + tail, dtype),
        ]

    head = buffers(split, jnp.bfloat16, 64, 512)
    return pl.pallas_call(
        functools.partial(scatter_body, tuple(pieces), split, n),
        out_shape=outs,
        in_specs=[ANY] * n,
        out_specs=[pl.BlockSpec(memory_space=pltpu.VMEM)] * n,
        scratch_shapes=head[:1]
        + head[2:]
        + [pltpu.VMEM((split, 64, 512), jnp.float32), pltpu.VMEM((split, 32, 512), jnp.float32)]
        + buffers(u - split - 1, jnp.bfloat16, 32, 1024)
        + buffers(None, jnp.float32, 8, 128)
        + [
            pltpu.SemaphoreType.DMA((u, 9)),
            pltpu.SemaphoreType.DMA((u, 9)),
            pltpu.SemaphoreType.DMA((u, 4)),
        ],
        compiler_params=pltpu.CompilerParams(
            collective_id=collective_id,
            has_side_effects=True,
            vmem_limit_bytes=58 * 1024 * 1024,
        ),
        name="scatter_all",
    )(*views)


NT = (((1,), (1,)), ((), ()))
TN = (((0,), (0,)), ((), ()))
NN = (((1,), (0,)), ((), ()))


def mul(a, b, dims=NN):
    return lax.dot_general(a, b, dims, preferred_element_type=jnp.float32)


def low_lanes(rows):
    return lax.broadcasted_iota(jnp.int32, (rows, 128), 1) < 64


def self_fwd_pair(q_ref, k_ref, v_ref, lse_ref, put):
    length, b = q_ref.shape[0], 256
    low = low_lanes(b)
    row = lax.broadcasted_iota(jnp.int32, (b, b), 0)
    col = lax.broadcasted_iota(jnp.int32, (b, b), 1)
    for n in range(b, length + 1, b):
        q = q_ref[n - b : n, :] * jnp.asarray(0.125, jnp.bfloat16)
        mixed, lses = [], []
        for mine in (low, ~low):
            s = mul(jnp.where(mine, q, jnp.zeros_like(q)), k_ref[0:n, :], NT)
            last = jnp.where(col <= row, s[:, n - b :], NEG_BIG)
            s = jnp.concatenate([s[:, : n - b], last], axis=1) if n > b else last
            top = jnp.max(s, axis=1, keepdims=True)
            e = jnp.exp(s - top)
            total = jnp.sum(e, axis=1, keepdims=True)
            mixed.append(mul(e.astype(jnp.bfloat16), v_ref[0:n, :]) / total)
            lses.append(jnp.broadcast_to(top + jnp.log(total), (b, 128)))
        put(n - b, jnp.where(low, mixed[0], mixed[1]).astype(jnp.bfloat16))
        turned = jnp.where(low, lses[0], lses[1]).T
        lse_ref[0, :, n - b : n] = jnp.concatenate([turned[0:1], turned[64:65]], axis=0)


def self_fwd_body(q_ref, k_ref, v_ref, o_ref, lse_ref, joined, obuf, send_sem, recv_sem, keep_sem):
    p = pl.program_id(0)
    dp, c = lax.axis_index("dp"), lax.axis_index("seq")
    rows = joined.shape[0]
    width = pl.num_programs(0) * 128

    def keep(i):
        at = pl.multiple_of(c * width + i * 128, 128)
        mine = pl.ds(pl.multiple_of(c * rows, rows), rows)
        return pltpu.make_async_copy(
            obuf.at[i, mine], joined.at[:, pl.ds(at, 128)], keep_sem.at[i]
        )

    def give(i):
        at = pl.multiple_of(c * width + i * 128, 128)
        theirs = pl.ds(pl.multiple_of((1 - c) * rows, rows), rows)
        return pltpu.make_async_remote_copy(
            src_ref=obuf.at[i, theirs],
            dst_ref=joined.at[:, pl.ds(at, 128)],
            send_sem=send_sem.at[i],
            recv_sem=recv_sem.at[i],
            device_id=(dp, 1 - c),
            device_id_type=MESH,
        )

    @pl.when(p == 0)
    def _():
        greet([(dp, 1 - c)])

    def put(at, value):
        o_ref[at : at + value.shape[0], :] = value
        obuf[p, pl.ds(at, value.shape[0]), :] = value

    self_fwd_pair(q_ref, k_ref, v_ref, lse_ref, put)
    keep(p).start()
    give(p).start()

    @pl.when(p == pl.num_programs(0) - 1)
    def _():
        for i in range(obuf.shape[0]):
            keep(i).wait()
            give(i).wait()


def self_fwd(q, k, v, collective_id):
    length, width = q.shape
    pairs = width // 128
    spec = pl.BlockSpec((length, 128), lambda i: (0, i))
    return pl.pallas_call(
        self_fwd_body,
        grid=(pairs,),
        in_specs=[spec] * 3,
        out_specs=[spec, pl.BlockSpec((1, 2, length), lambda i: (i, 0, 0)), ANY],
        out_shape=[
            jax.ShapeDtypeStruct((length, width), jnp.bfloat16),
            jax.ShapeDtypeStruct((pairs, 2, length), jnp.float32),
            jax.ShapeDtypeStruct((length // 2, 2 * width), jnp.bfloat16),
        ],
        scratch_shapes=[
            pltpu.VMEM((pairs, length, 128), jnp.bfloat16),
            pltpu.SemaphoreType.DMA((pairs,)),
            pltpu.SemaphoreType.DMA((pairs,)),
            pltpu.SemaphoreType.DMA((pairs,)),
        ],
        compiler_params=pltpu.CompilerParams(
            collective_id=collective_id,
            has_side_effects=True,
            vmem_limit_bytes=40 * 1024 * 1024,
        ),
        name="self_fwd",
    )(q, k, v)


def self_bwd_pair(q_ref, k_ref, v_ref, o_ref, do_ref, lse_ref, dq_ref, dk_ref, dv_ref, acc):
    length, b = q_ref.shape[0], 256
    low = low_lanes(b)
    row = lax.broadcasted_iota(jnp.int32, (b, b), 0)
    col = lax.broadcasted_iota(jnp.int32, (b, b), 1)
    prod = do_ref[...].astype(jnp.float32) * o_ref[...].astype(jnp.float32)
    lane = lax.broadcasted_iota(jnp.int32, (8, 128), 1)
    head = lax.broadcasted_iota(jnp.int32, (8, 128), 0)
    pick = jnp.where(lane // 64 == head, 1.0, 0.0)
    inner = lax.dot_general(
        pick, prod, NT, precision=lax.Precision.HIGHEST, preferred_element_type=jnp.float32
    )
    acc[...] = jnp.zeros_like(acc)
    for at in range(0, length, b):
        k, v = k_ref[at : at + b, :], v_ref[at : at + b, :]
        qs, dos = q_ref[at:length, :], do_ref[at:length, :]
        dks, dvs = [], []
        for h, mine in enumerate((low, ~low)):
            km = jnp.where(mine, k, jnp.zeros_like(k))
            vm = jnp.where(mine, v, jnp.zeros_like(v))
            s = mul(km * jnp.asarray(0.125, jnp.bfloat16), qs, NT)
            w = jnp.exp(s - lse_ref[0, h : h + 1, at:length])
            first = jnp.where(row <= col, w[:, :b], 0.0)
            w = jnp.concatenate([first, w[:, b:]], axis=1) if length - at > b else first
            ds = (w * (mul(vm, dos, NT) - inner[h : h + 1, at:length])).astype(jnp.bfloat16)
            dvs.append(mul(w.astype(jnp.bfloat16), dos))
            dks.append(mul(ds, qs))
            acc[at:length, :] += mul(ds, km, TN)
        dk_ref[at : at + b, :] = (jnp.where(low, dks[0], dks[1]) * 0.125).astype(jnp.bfloat16)
        dv_ref[at : at + b, :] = jnp.where(low, dvs[0], dvs[1]).astype(jnp.bfloat16)
    dq_ref[...] = (acc[...] * 0.125).astype(jnp.bfloat16)


def self_bwd_body(q_ref, k_ref, v_ref, o_ref, lse_ref, grad, dq_ref, dk_ref, dv_ref, dobuf, acc, send_sem, recv_sem, keep_sem):
    p = pl.program_id(0)
    dp, c = lax.axis_index("dp"), lax.axis_index("seq")
    pairs, length, _ = dobuf.shape
    rows = length // 2
    mine = pl.ds(pl.multiple_of(c * rows, rows), rows)

    def keep(i):
        at = pl.multiple_of(c * pairs * 128 + i * 128, 128)
        return pltpu.make_async_copy(
            grad.at[:, pl.ds(at, 128)], dobuf.at[i, mine], keep_sem.at[i]
        )

    def give(i):
        at = pl.multiple_of((1 - c) * pairs * 128 + i * 128, 128)
        return pltpu.make_async_remote_copy(
            src_ref=grad.at[:, pl.ds(at, 128)],
            dst_ref=dobuf.at[i, mine],
            send_sem=send_sem.at[i],
            recv_sem=recv_sem.at[i],
            device_id=(dp, 1 - c),
            device_id_type=MESH,
        )

    @pl.when(p == 0)
    def _():
        greet([(dp, 1 - c)])
        for i in range(pairs):
            give(i).start()
            keep(i).start()

    keep(p).wait()
    give(p).wait()
    self_bwd_pair(
        q_ref, k_ref, v_ref, o_ref, dobuf.at[p], lse_ref, dq_ref, dk_ref, dv_ref, acc
    )


def self_bwd(q, k, v, o, lse, grad, collective_id):
    length, width = q.shape
    pairs = width // 128
    spec = pl.BlockSpec((length, 128), lambda i: (0, i))
    return pl.pallas_call(
        self_bwd_body,
        grid=(pairs,),
        in_specs=[spec] * 4 + [pl.BlockSpec((1, 2, length), lambda i: (i, 0, 0)), ANY],
        out_specs=[spec] * 3,
        out_shape=[jax.ShapeDtypeStruct((length, width), jnp.bfloat16)] * 3,
        scratch_shapes=[
            pltpu.VMEM((pairs, length, 128), jnp.bfloat16),
            pltpu.VMEM((length, 128), jnp.float32),
            pltpu.SemaphoreType.DMA((pairs,)),
            pltpu.SemaphoreType.DMA((pairs,)),
            pltpu.SemaphoreType.DMA((pairs,)),
        ],
        compiler_params=pltpu.CompilerParams(
            collective_id=collective_id,
            has_side_effects=True,
            vmem_limit_bytes=48 * 1024 * 1024,
        ),
        name="self_bwd",
    )(q, k, v, o, lse, grad)


def cross_fwd_body(q_ref, k_ref, v_ref, ok_ref, o_ref):
    low = low_lanes(q_ref.shape[0])
    q = q_ref[...] * jnp.asarray(0.125, jnp.bfloat16)
    mixed = []
    for mine in (low, ~low):
        s = mul(jnp.where(mine, q, jnp.zeros_like(q)), k_ref[...], NT)
        s = jnp.where(ok_ref[0:1, :] > 0, s, NEG_BIG)
        e = jnp.exp(s - jnp.max(s, axis=1, keepdims=True))
        total = jnp.sum(e, axis=1, keepdims=True)
        mixed.append(mul(e.astype(jnp.bfloat16), v_ref[...]) / total)
    o_ref[...] = jnp.where(low, mixed[0], mixed[1]).astype(jnp.bfloat16)


def cross_specs(rows, keys):
    return (
        pl.BlockSpec((rows, 128), lambda i: (0, i)),
        pl.BlockSpec((keys, 128), lambda i: (0, i)),
    )


def cross_fwd(q, k, v, ok):
    (rows, width), keys = q.shape, k.shape[0]
    queries, table = cross_specs(rows, keys)
    return pl.pallas_call(
        cross_fwd_body,
        grid=(width // 128,),
        in_specs=[queries, table, table, pl.BlockSpec((8, keys), lambda i: (0, 0))],
        out_specs=queries,
        out_shape=jax.ShapeDtypeStruct((rows, width), jnp.bfloat16),
        name="cross_fwd",
    )(q, k, v, ok)


def cross_bwd_body(q_ref, k_ref, v_ref, ok_ref, do_ref, dq_ref, dk_ref, dv_ref):
    keys = k_ref.shape[0]
    low = low_lanes(keys)
    wide = low_lanes(q_ref.shape[0])
    q, do, k, v = q_ref[...], do_ref[...], k_ref[...], v_ref[...]
    dqs, dks, dvs = [], [], []
    for mine in (low, ~low):
        km = jnp.where(mine, k, jnp.zeros_like(k))
        vm = jnp.where(mine, v, jnp.zeros_like(v))
        s = mul(km * jnp.asarray(0.125, jnp.bfloat16), q, NT)
        s = jnp.where(ok_ref[:, 0:1] > 0, s, NEG_BIG)
        e = jnp.exp(s - jnp.max(s, axis=0, keepdims=True))
        w = e / jnp.sum(e, axis=0, keepdims=True)
        dw = mul(vm, do, NT)
        inner = jnp.sum(dw * w, axis=0, keepdims=True)
        ds = (w * (dw - inner)).astype(jnp.bfloat16)
        dvs.append(mul(w.astype(jnp.bfloat16), do))
        dks.append(mul(ds, q))
        dqs.append(mul(ds, km, TN))
    dq_ref[...] = (jnp.where(wide, dqs[0], dqs[1]) * 0.125).astype(jnp.bfloat16)
    dk_ref[...] = (jnp.where(low, dks[0], dks[1]) * 0.125).astype(jnp.bfloat16)
    dv_ref[...] = jnp.where(low, dvs[0], dvs[1]).astype(jnp.bfloat16)


def cross_bwd(q, k, v, ok, do):
    (rows, width), keys = q.shape, k.shape[0]
    queries, table = cross_specs(rows, keys)
    return pl.pallas_call(
        cross_bwd_body,
        grid=(width // 128,),
        in_specs=[queries, table, table, pl.BlockSpec((keys, 128), lambda i: (0, 0)), queries],
        out_specs=[queries, table, table],
        out_shape=[
            jax.ShapeDtypeStruct((rows, width), jnp.bfloat16),
            jax.ShapeDtypeStruct((keys, width), jnp.bfloat16),
            jax.ShapeDtypeStruct((keys, width), jnp.bfloat16),
        ],
        name="cross_bwd",
    )(q, k, v, ok, do)


HEADS = 16
HEAD_DIM = 64


EPSILON = 1e-05
NEG_BIG = -1e30


def norm_rows(value, gain, shift):
    center = value - jnp.mean(value, axis=-1, keepdims=True)
    spread = jnp.mean(center * center, axis=-1, keepdims=True)
    return center * lax.rsqrt(spread + EPSILON) * gain + shift


def project(rows, weight):
    return jnp.einsum("bsd,de->bse", rows, weight, preferred_element_type=jnp.float32)


def project_back(grads, weight):
    return jnp.einsum("bse,de->bsd", grads, weight, preferred_element_type=jnp.float32)


def weight_grad(rows, grads):
    return jnp.einsum("bsd,bse->de", rows, grads, preferred_element_type=jnp.float32)


def row_total(grads):
    return jnp.sum(grads.astype(jnp.float32), axis=(0, 1))


def split_heads(value):
    return value.reshape(value.shape[0], value.shape[1], HEADS, HEAD_DIM)


def join_heads(value):
    return value.reshape(value.shape[0], value.shape[1], HEADS * HEAD_DIM)


def scores_of(queries, keys_in, allowed):
    raw_scores = (
        jnp.einsum(
            "bqhd,bkhd->bhqk",
            split_heads(queries),
            split_heads(keys_in),
            preferred_element_type=jnp.float32,
        )
        * 0.125
    )
    return jnp.where(allowed, raw_scores, NEG_BIG)


def attend(queries, keys_in, values_in, allowed):
    scores = scores_of(queries, keys_in, allowed)
    row_max = jnp.max(scores, axis=-1, keepdims=True)
    exponent = jnp.exp(scores - row_max)
    total = jnp.sum(exponent, axis=-1, keepdims=True)
    attn_weights = exponent / total
    mixed_rows = jnp.einsum(
        "bhqk,bkhd->bqhd",
        attn_weights.astype(jnp.bfloat16),
        split_heads(values_in),
        preferred_element_type=jnp.float32,
    )
    return (join_heads(mixed_rows).astype(jnp.bfloat16), row_max + jnp.log(total))


def attend_back(queries, keys_in, values_in, allowed, log_total, grad_mixed):
    attn_weights = jnp.exp(scores_of(queries, keys_in, allowed) - log_total)
    grad_heads = split_heads(grad_mixed)
    grad_weights = jnp.einsum(
        "bqhd,bkhd->bhqk", grad_heads, split_heads(values_in), preferred_element_type=jnp.float32
    )
    grad_values = jnp.einsum(
        "bhqk,bqhd->bkhd",
        attn_weights.astype(jnp.bfloat16),
        grad_heads,
        preferred_element_type=jnp.float32,
    )
    inner_sum = jnp.sum(grad_weights * attn_weights, axis=-1, keepdims=True)
    grad_scores = (attn_weights * (grad_weights - inner_sum)).astype(jnp.bfloat16)
    grad_queries = (
        jnp.einsum(
            "bhqk,bkhd->bqhd", grad_scores, split_heads(keys_in), preferred_element_type=jnp.float32
        )
        * 0.125
    )
    grad_keys = (
        jnp.einsum(
            "bhqk,bqhd->bkhd", grad_scores, split_heads(queries), preferred_element_type=jnp.float32
        )
        * 0.125
    )
    return (join_heads(grad_queries), join_heads(grad_keys), join_heads(grad_values))


def per_device(
    images,
    encoder_states,
    image_row,
    image_seg,
    caption_seg,
    ln1_gain,
    ln1_bias,
    w_query,
    w_key,
    w_value,
    w_out,
    ln2_gain,
    ln2_bias,
    c_query,
    c_key,
    c_value,
    c_out,
    ln3_gain,
    ln3_bias,
    w_in,
    b_in,
    w_outer,
    b_outer,
    cotangent,
):
    mixing = (
        lax.all_gather(ln1_gain, ("dp", "seq"), axis=0, tiled=True),
        lax.all_gather(ln1_bias, ("dp", "seq"), axis=0, tiled=True),
        lax.all_gather(w_query, ("dp", "seq"), axis=0, tiled=True),
        lax.all_gather(w_key, ("dp", "seq"), axis=0, tiled=True),
        lax.all_gather(w_value, ("dp", "seq"), axis=0, tiled=True),
        lax.all_gather(w_out, ("dp", "seq"), axis=0, tiled=True),
        lax.all_gather(ln2_gain, ("dp", "seq"), axis=0, tiled=True),
        lax.all_gather(ln2_bias, ("dp", "seq"), axis=0, tiled=True),
        lax.all_gather(c_query, ("dp", "seq"), axis=0, tiled=True),
        lax.all_gather(c_key, ("dp", "seq"), axis=0, tiled=True),
        lax.all_gather(c_value, ("dp", "seq"), axis=0, tiled=True),
        lax.all_gather(c_out, ("dp", "seq"), axis=0, tiled=True),
    )
    (
        gain_a,
        bias_a,
        query_w,
        key_w,
        value_w,
        out_w,
        gain_b,
        bias_b,
        cross_qw,
        cross_kw,
        cross_vw,
        cross_ow,
    ) = mixing
    shard = images.shape[1]
    seq_index = lax.axis_index("seq")
    full_len = shard * lax.axis_size("seq")
    inputs_f = images.astype(jnp.float32)
    gain_a32, bias_a32 = (gain_a.astype(jnp.float32), bias_a.astype(jnp.float32))
    normed_a = norm_rows(inputs_f, gain_a32, bias_a32).astype(jnp.bfloat16)
    queries = project(normed_a, query_w).astype(jnp.bfloat16)
    keys_local = project(normed_a, key_w).astype(jnp.bfloat16)
    values_local = project(normed_a, value_w).astype(jnp.bfloat16)
    keys_all, values_all = (
        lax.all_gather(keys_local, "seq", axis=1, tiled=True),
        lax.all_gather(values_local, "seq", axis=1, tiled=True),
    )
    query_pos = seq_index * shard + jnp.arange(shard, dtype=jnp.int32)
    key_pos = jnp.arange(full_len, dtype=jnp.int32)
    causal = (key_pos[None, :] <= query_pos[:, None])[None, None]
    self_out, self_lse = attend(queries, keys_all, values_all, causal)
    after_self = inputs_f + project(self_out, out_w)
    gain_b32, bias_b32 = (gain_b.astype(jnp.float32), bias_b.astype(jnp.float32))
    normed_b = norm_rows(after_self, gain_b32, bias_b32).astype(jnp.bfloat16)
    cross_queries = project(normed_b, cross_qw).astype(jnp.bfloat16)
    encoder_all = lax.all_gather(encoder_states, "dp", axis=0, tiled=True)
    caption = jnp.take(encoder_all, image_row, axis=0)
    cross_keys = project(caption, cross_kw).astype(jnp.bfloat16)
    cross_values = project(caption, cross_vw).astype(jnp.bfloat16)
    caption_mask = (jnp.take(caption_seg, image_row, axis=0) == image_seg[:, None])[
        :, None, None, :
    ]
    cross_out, cross_lse = attend(cross_queries, cross_keys, cross_values, caption_mask)
    after_cross = after_self + project(cross_out, cross_ow)
    feed_weights = (
        lax.all_gather(ln3_gain, ("dp", "seq"), axis=0, tiled=True),
        lax.all_gather(ln3_bias, ("dp", "seq"), axis=0, tiled=True),
        lax.all_gather(w_in, ("dp", "seq"), axis=0, tiled=True),
        lax.all_gather(b_in, ("dp", "seq"), axis=0, tiled=True),
        lax.all_gather(w_outer, ("dp", "seq"), axis=0, tiled=True),
        lax.all_gather(b_outer, ("dp", "seq"), axis=0, tiled=True),
    )
    gain_c, bias_c, inner_w, inner_b, outer_w, outer_b = feed_weights
    gain_c32, bias_c32 = (gain_c.astype(jnp.float32), bias_c.astype(jnp.float32))
    normed_c = norm_rows(after_cross, gain_c32, bias_c32).astype(jnp.bfloat16)
    hidden_pre = project(normed_c, inner_w) + inner_b.astype(jnp.float32)
    activated = jax.nn.gelu(hidden_pre).astype(jnp.bfloat16)
    result = after_cross + project(activated, outer_w) + outer_b.astype(jnp.float32)
    block_out = result.astype(jnp.bfloat16)
    inner_wb, outer_wb = (feed_weights[2], feed_weights[4])
    grad_result = cotangent.astype(jnp.float32)
    grad_outer_w = weight_grad(activated, cotangent)
    grad_outer_b = row_total(cotangent)
    grad_act = project_back(cotangent, outer_wb)
    _, gelu_back = jax.vjp(jax.nn.gelu, hidden_pre)
    grad_hidden = gelu_back(grad_act)[0].astype(jnp.bfloat16)
    grad_inner_w = weight_grad(normed_c, grad_hidden)
    grad_inner_b = row_total(grad_hidden)
    grad_normed_c = project_back(grad_hidden, inner_wb)
    _, norm_c_back = jax.vjp(norm_rows, after_cross, gain_c32, bias_c32)
    grad_cross_part, grad_gain_c, grad_bias_c = norm_c_back(grad_normed_c)
    grad_after_cross = grad_result + grad_cross_part
    feed_sums = (
        lax.psum_scatter(grad_gain_c, ("dp", "seq"), scatter_dimension=0, tiled=True),
        lax.psum_scatter(grad_bias_c, ("dp", "seq"), scatter_dimension=0, tiled=True),
        lax.psum_scatter(grad_inner_w, ("dp", "seq"), scatter_dimension=0, tiled=True),
        lax.psum_scatter(grad_inner_b, ("dp", "seq"), scatter_dimension=0, tiled=True),
        lax.psum_scatter(grad_outer_w, ("dp", "seq"), scatter_dimension=0, tiled=True),
        lax.psum_scatter(grad_outer_b, ("dp", "seq"), scatter_dimension=0, tiled=True),
    )
    query_wb, key_wb, value_wb, out_wb = (mixing[2], mixing[3], mixing[4], mixing[5])
    cross_qwb, cross_kwb, cross_vwb, cross_owb = (mixing[8], mixing[9], mixing[10], mixing[11])
    grad_branch_b = grad_after_cross.astype(jnp.bfloat16)
    grad_cross_ow = weight_grad(cross_out, grad_branch_b)
    grad_cross_out = project_back(grad_branch_b, cross_owb).astype(jnp.bfloat16)
    grad_cq_raw, grad_ck_raw, grad_cv_raw = attend_back(
        cross_queries, cross_keys, cross_values, caption_mask, cross_lse, grad_cross_out
    )
    grad_cross_q = grad_cq_raw.astype(jnp.bfloat16)
    grad_ck_sum, grad_cv_sum = (
        lax.psum_scatter(
            grad_ck_raw.astype(jnp.bfloat16), "seq", scatter_dimension=1, tiled=True
        ).astype(jnp.float32),
        lax.psum_scatter(
            grad_cv_raw.astype(jnp.bfloat16), "seq", scatter_dimension=1, tiled=True
        ).astype(jnp.float32),
    )
    grad_ck_low = grad_ck_sum.astype(jnp.bfloat16)
    grad_cv_low = grad_cv_sum.astype(jnp.bfloat16)
    piece_len = grad_ck_sum.shape[1]
    caption_piece = lax.dynamic_slice_in_dim(caption, seq_index * piece_len, piece_len, 1)
    grad_cross_kw = weight_grad(caption_piece, grad_ck_low)
    grad_cross_vw = weight_grad(caption_piece, grad_cv_low)
    grad_caption = project_back(grad_ck_low, cross_kwb) + project_back(grad_cv_low, cross_vwb)
    row_count = encoder_all.shape[0]
    row_onehot = (image_row[:, None] == jnp.arange(row_count, dtype=jnp.int32)[None, :]).astype(
        jnp.float32
    )
    grad_rows = jnp.einsum("br,bsd->rsd", row_onehot, grad_caption, precision=lax.Precision.HIGHEST)
    caption_grad = lax.psum_scatter(
        grad_rows.astype(jnp.bfloat16), "dp", scatter_dimension=0, tiled=True
    ).astype(jnp.float32)
    grad_cross_qw = weight_grad(normed_b, grad_cross_q)
    grad_normed_b = project_back(grad_cross_q, cross_qwb)
    _, norm_b_back = jax.vjp(norm_rows, after_self, gain_b32, bias_b32)
    grad_self_part, grad_gain_b, grad_bias_b = norm_b_back(grad_normed_b)
    grad_after_self = grad_after_cross + grad_self_part
    grad_branch_a = grad_after_self.astype(jnp.bfloat16)
    grad_out_w = weight_grad(self_out, grad_branch_a)
    grad_self_out = project_back(grad_branch_a, out_wb).astype(jnp.bfloat16)
    keys_back, values_back = (keys_all, values_all)
    grad_q_raw, grad_k_raw, grad_v_raw = attend_back(
        queries, keys_back, values_back, causal, self_lse, grad_self_out
    )
    grad_k_sum, grad_v_sum = (
        lax.psum_scatter(
            grad_k_raw.astype(jnp.bfloat16), "seq", scatter_dimension=1, tiled=True
        ).astype(jnp.float32),
        lax.psum_scatter(
            grad_v_raw.astype(jnp.bfloat16), "seq", scatter_dimension=1, tiled=True
        ).astype(jnp.float32),
    )
    grad_q_low = grad_q_raw.astype(jnp.bfloat16)
    grad_k_low = grad_k_sum.astype(jnp.bfloat16)
    grad_v_low = grad_v_sum.astype(jnp.bfloat16)
    grad_query_w = weight_grad(normed_a, grad_q_low)
    grad_key_w = weight_grad(normed_a, grad_k_low)
    grad_value_w = weight_grad(normed_a, grad_v_low)
    grad_normed_a = (
        project_back(grad_q_low, query_wb)
        + project_back(grad_k_low, key_wb)
        + project_back(grad_v_low, value_wb)
    )
    _, norm_a_back = jax.vjp(norm_rows, inputs_f, gain_a32, bias_a32)
    grad_input_part, grad_gain_a, grad_bias_a = norm_a_back(grad_normed_a)
    image_grad = grad_after_self + grad_input_part
    mix_sums = (
        lax.psum_scatter(grad_gain_a, ("dp", "seq"), scatter_dimension=0, tiled=True),
        lax.psum_scatter(grad_bias_a, ("dp", "seq"), scatter_dimension=0, tiled=True),
        lax.psum_scatter(grad_query_w, ("dp", "seq"), scatter_dimension=0, tiled=True),
        lax.psum_scatter(grad_key_w, ("dp", "seq"), scatter_dimension=0, tiled=True),
        lax.psum_scatter(grad_value_w, ("dp", "seq"), scatter_dimension=0, tiled=True),
        lax.psum_scatter(grad_out_w, ("dp", "seq"), scatter_dimension=0, tiled=True),
        lax.psum_scatter(grad_gain_b, ("dp", "seq"), scatter_dimension=0, tiled=True),
        lax.psum_scatter(grad_bias_b, ("dp", "seq"), scatter_dimension=0, tiled=True),
        lax.psum_scatter(grad_cross_qw, ("dp", "seq"), scatter_dimension=0, tiled=True),
        lax.psum_scatter(grad_cross_kw, ("dp", "seq"), scatter_dimension=0, tiled=True),
        lax.psum_scatter(grad_cross_vw, ("dp", "seq"), scatter_dimension=0, tiled=True),
        lax.psum_scatter(grad_cross_ow, ("dp", "seq"), scatter_dimension=0, tiled=True),
    )
    return (
        block_out,
        image_grad,
        caption_grad,
        mix_sums[0],
        mix_sums[1],
        mix_sums[2],
        mix_sums[3],
        mix_sums[4],
        mix_sums[5],
        mix_sums[6],
        mix_sums[7],
        mix_sums[8],
        mix_sums[9],
        mix_sums[10],
        mix_sums[11],
        feed_sums[0],
        feed_sums[1],
        feed_sums[2],
        feed_sums[3],
        feed_sums[4],
        feed_sums[5],
    )


def rows2(rows, weight):
    return jnp.dot(rows, weight, preferred_element_type=jnp.float32)


def rows2_back(grads, weight):
    return lax.dot_general(grads, weight, NT, preferred_element_type=jnp.float32)


def grad2(rows, grads):
    return lax.dot_general(rows, grads, TN, preferred_element_type=jnp.float32).astype(jnp.bfloat16)


def unpack(table, sizes):
    wide, at = [], 0
    for size in sizes:
        wide.append(table[:, at : at + size].reshape(-1))
        at += size
    return wide


def block_device(
    images,
    encoder_states,
    image_row,
    image_seg,
    caption_seg,
    ln1_gain,
    ln1_bias,
    w_query,
    w_key,
    w_value,
    w_out,
    ln2_gain,
    ln2_bias,
    c_query,
    c_key,
    c_value,
    c_out,
    ln3_gain,
    ln3_bias,
    w_in,
    b_in,
    w_outer,
    b_outer,
    cotangent,
):
    core = lax.axis_index("seq")
    shard = images.shape[1]
    other = [(0, 1), (1, 0)]
    vectors = (ln1_gain, ln1_bias, ln2_gain, ln2_bias, ln3_gain, ln3_bias, b_outer, b_in)
    sizes = [v.shape[0] for v in vectors]
    packed = jnp.concatenate([v.astype(jnp.float32) for v in (*vectors, image_row)])
    packed = jnp.pad(packed, (0, 1024 - packed.shape[0])).reshape(8, 128)
    half = encoder_states.shape[1] // 2
    tokens = lax.dynamic_slice_in_dim(encoder_states[0], core * half, half, 0)
    (
        query_w,
        key_w,
        value_w,
        table,
        out_w,
        cross_qw,
        cross_kw,
        cross_vw,
        cross_ow,
        encoder_all,
        image_all,
    ) = gather_all(
        [
            w_query,
            w_key,
            w_value,
            packed,
            w_out,
            c_query,
            c_key,
            c_value,
            c_out,
            tokens,
        ],
        3,
        images[0],
        1,
    )
    table = table.reshape(32, 1024)
    gain_a, bias_a, gain_b, bias_b, gain_c, bias_c, outer_b, inner_b = unpack(table, sizes)
    rows_all = table[::2, sum(sizes)].astype(jnp.int32)
    inner_w = lax.all_gather(w_in, ("dp", "seq"), axis=0, tiled=True)
    outer_w = lax.all_gather(w_outer, ("dp", "seq"), axis=0, tiled=True)
    inputs_f = images[0].astype(jnp.float32)
    image_f = image_all.astype(jnp.float32)
    normed_a = norm_rows(image_f, gain_a, bias_a).astype(jnp.bfloat16)
    queries = rows2(normed_a, query_w).astype(jnp.bfloat16)
    keys = rows2(normed_a, key_w).astype(jnp.bfloat16)
    values = rows2(normed_a, value_w).astype(jnp.bfloat16)
    self_heads, self_lse, self_out = self_fwd(queries, keys, values, 3)
    after_self = inputs_f + rows2(self_out, out_w)
    normed_b = norm_rows(after_self, gain_b, bias_b).astype(jnp.bfloat16)
    cross_queries = rows2(normed_b, cross_qw).astype(jnp.bfloat16)
    encoder_all = encoder_all.reshape(-1, 2 * half, encoder_all.shape[1])
    caption = jnp.take(encoder_all, image_row, axis=0)[0]
    cross_keys = rows2(caption, cross_kw).astype(jnp.bfloat16)
    cross_values = rows2(caption, cross_vw).astype(jnp.bfloat16)
    allowed = (jnp.take(caption_seg, image_row, axis=0)[0] == image_seg).astype(jnp.float32)
    cross_out = cross_fwd(
        cross_queries, cross_keys, cross_values, jnp.broadcast_to(allowed[None, :], (8, 2 * half))
    )
    after_cross = after_self + rows2(cross_out, cross_ow)
    normed_c = norm_rows(after_cross, gain_c, bias_c).astype(jnp.bfloat16)
    hidden_pre = rows2(normed_c, inner_w) + inner_b
    activated = jax.nn.gelu(hidden_pre).astype(jnp.bfloat16)
    result = after_cross + rows2(activated, outer_w) + outer_b
    block_out = result.astype(jnp.bfloat16)
    grad_out = cotangent[0]
    grad_outer_w = grad2(activated, grad_out)
    grad_outer_b = jnp.sum(grad_out.astype(jnp.float32), axis=0)
    _, gelu_back = jax.vjp(jax.nn.gelu, hidden_pre)
    grad_hidden = gelu_back(rows2_back(grad_out, outer_w))[0].astype(jnp.bfloat16)
    grad_inner_w = grad2(normed_c, grad_hidden)
    grad_inner_b = jnp.sum(grad_hidden.astype(jnp.float32), axis=0)
    _, norm_c_back = jax.vjp(norm_rows, after_cross, gain_c, bias_c)
    grad_cross_part, grad_gain_c, grad_bias_c = norm_c_back(rows2_back(grad_hidden, inner_w))
    grad_after_cross = grad_out.astype(jnp.float32) + grad_cross_part
    grad_branch_b = grad_after_cross.astype(jnp.bfloat16)
    grad_cross_ow = grad2(cross_out, grad_branch_b)
    grad_cross_out = rows2_back(grad_branch_b, cross_ow).astype(jnp.bfloat16)
    grad_cross_q, grad_ck, grad_cv = cross_bwd(
        cross_queries,
        cross_keys,
        cross_values,
        jnp.broadcast_to(allowed[:, None], (2 * half, 128)),
        grad_cross_out,
    )
    grad_ck = lax.psum_scatter(grad_ck, "seq", scatter_dimension=0, tiled=True)
    grad_cv = lax.psum_scatter(grad_cv, "seq", scatter_dimension=0, tiled=True)
    caption_piece = lax.dynamic_slice_in_dim(caption, core * half, half, 0)
    grad_cross_kw = grad2(caption_piece, grad_ck)
    grad_cross_vw = grad2(caption_piece, grad_cv)
    grad_caption = rows2_back(grad_ck, cross_kw) + rows2_back(grad_cv, cross_vw)
    grads_all = lax.all_gather(grad_caption.astype(jnp.bfloat16), "dp", axis=0)
    mine = (rows_all == lax.axis_index("dp")).astype(jnp.bfloat16)
    caption_grad = jnp.einsum("b,bsd->sd", mine, grads_all, preferred_element_type=jnp.float32)
    grad_cross_qw = grad2(normed_b, grad_cross_q)
    _, norm_b_back = jax.vjp(norm_rows, after_self, gain_b, bias_b)
    grad_self_part, grad_gain_b, grad_bias_b = norm_b_back(rows2_back(grad_cross_q, cross_qw))
    grad_after_self = grad_after_cross + grad_self_part
    grad_branch_a = grad_after_self.astype(jnp.bfloat16)
    grad_out_w = grad2(self_out, grad_branch_a)
    grad_self_out = rows2_back(grad_branch_a, out_w).astype(jnp.bfloat16)
    grad_q, grad_k, grad_v = self_bwd(
        queries, keys, values, self_heads, self_lse, grad_self_out, 4
    )
    grad_query_w = grad2(normed_a, grad_q)
    grad_key_w = grad2(normed_a, grad_k)
    grad_value_w = grad2(normed_a, grad_v)

    def back_to_rows(core_of):
        at = core_of * shard
        cut = lambda g: lax.dynamic_slice_in_dim(g, at, shard, 0)
        return (
            rows2_back(cut(grad_q), query_w)
            + rows2_back(cut(grad_k), key_w)
            + rows2_back(cut(grad_v), value_w)
        )

    theirs = back_to_rows(1 - core).astype(jnp.bfloat16)
    grad_normed_a = back_to_rows(core) + lax.ppermute(theirs, "seq", other).astype(jnp.float32)
    _, norm_a_back = jax.vjp(norm_rows, inputs_f, gain_a, bias_a)
    grad_input_part, grad_gain_a, grad_bias_a = norm_a_back(grad_normed_a)
    image_grad = grad_after_self + grad_input_part
    sums = (
        grad_gain_a,
        grad_bias_a,
        grad_gain_b,
        grad_bias_b,
        grad_gain_c,
        grad_bias_c,
        grad_outer_b,
        grad_inner_b,
    )
    grid = jnp.concatenate([v.reshape(32, -1) for v in sums], axis=1)
    grid = jnp.pad(grid, ((0, 0), (0, 1024 - grid.shape[1]))).reshape(256, 128)
    big = scatter_all(
        [
            grad_query_w,
            grad_key_w,
            grad_value_w,
            grad_out_w,
            grad_cross_qw,
            grad_cross_kw,
            grad_cross_vw,
            grad_cross_ow,
            grad_inner_w,
            grad_outer_w,
            grid,
        ],
        3,
        2,
    )
    small = unpack(big[-1].reshape(1, 1024), sizes)
    return (
        block_out[None],
        image_grad[None],
        caption_grad[None],
        small[0],
        small[1],
        big[0],
        big[1],
        big[2],
        big[3],
        small[2],
        small[3],
        big[4],
        big[5],
        big[6],
        big[7],
        small[4],
        small[5],
        big[8],
        small[7],
        big[9],
        small[6],
    )


def solution(mesh):
    in_specs = (
        P("dp", "seq", None),
        P("dp", None, None),
        P("dp"),
        P("dp"),
        P(),
        P(("dp", "seq")),
        P(("dp", "seq")),
        P(("dp", "seq"), None),
        P(("dp", "seq"), None),
        P(("dp", "seq"), None),
        P(("dp", "seq"), None),
        P(("dp", "seq")),
        P(("dp", "seq")),
        P(("dp", "seq"), None),
        P(("dp", "seq"), None),
        P(("dp", "seq"), None),
        P(("dp", "seq"), None),
        P(("dp", "seq")),
        P(("dp", "seq")),
        P(("dp", "seq"), None),
        P(("dp", "seq")),
        P(("dp", "seq"), None),
        P(("dp", "seq")),
        P("dp", "seq", None),
    )
    out_specs = (
        P("dp", "seq", None),
        P("dp", "seq", None),
        P("dp", "seq", None),
        P(("dp", "seq")),
        P(("dp", "seq")),
        P(("dp", "seq"), None),
        P(("dp", "seq"), None),
        P(("dp", "seq"), None),
        P(("dp", "seq"), None),
        P(("dp", "seq")),
        P(("dp", "seq")),
        P(("dp", "seq"), None),
        P(("dp", "seq"), None),
        P(("dp", "seq"), None),
        P(("dp", "seq"), None),
        P(("dp", "seq")),
        P(("dp", "seq")),
        P(("dp", "seq"), None),
        P(("dp", "seq")),
        P(("dp", "seq"), None),
        P(("dp", "seq")),
    )
    kernels = mesh.shape["dp"] == 16 and mesh.shape["seq"] == 2
    return jax.shard_map(
        block_device if kernels else per_device,
        mesh=mesh,
        in_specs=in_specs,
        out_specs=out_specs,
        check_vma=False,
    )
```

```python
import functools

import jax
import jax.numpy as jnp
from jax import lax
from jax.experimental import pallas as pl
from jax.experimental.pallas import tpu as pltpu
from jax.sharding import PartitionSpec as P

MESH = pl.DeviceIdType.MESH
ANY = pl.BlockSpec(memory_space=pl.ANY)


def place():
    dp, c = lax.axis_index("dp"), lax.axis_index("seq")
    x, y, z = dp % 2, (dp // 2) % 2, dp // 4
    return z, y, x, c


def flip(bit, on):
    return bit + on * (1 - 2 * bit)


def zxor(z, k):
    if k == 0:
        return z
    if k == 1:
        return z + 1 - 2 * (z % 2)
    if k == 2:
        return z + 2 - 4 * (z // 2)
    return 3 - z


def chip(z, y, x):
    return z * 4 + y * 2 + x


def greet(partners):
    barrier = pltpu.get_barrier_semaphore()
    for partner in partners:
        pl.semaphore_signal(barrier, inc=1, device_id=partner, device_id_type=MESH)
    pl.semaphore_wait(barrier, len(partners))


class Gather:
    def __init__(self, split, own, full, send_sem, recv_sem, local_sem):
        self.split, self.own, self.full = split, own, full
        self.send_sem, self.recv_sem, self.local_sem = send_sem, recv_sem, local_sem
        z, y, x, c = place()
        self.z, self.y, self.x, self.c = z, y, x, c
        self.yx = {
            (0, 0): (y, x),
            (1, 0): (flip(y, 1 - c), flip(x, c)),
            (0, 1): (flip(y, c), flip(x, 1 - c)),
            (1, 1): (1 - y, 1 - x),
        }
        self.other = (chip(z, y, x), 1 - c)

    def partners(self):
        z, c = self.z, self.c
        return [(chip(zxor(z, k), self.y, self.x), c) for k in (1, 2, 3)] + [
            (chip(z, *self.yx[1, 0]), c),
            (chip(z, *self.yx[0, 1]), c),
            self.other,
        ]

    def block(self, g, k, way, core):
        rows = self.own[g].shape[0]
        r = chip(zxor(self.z, k), *self.yx[way])
        if g < self.split:
            return self.full[g].at[pl.ds(pl.multiple_of(2 * r * rows, rows), 2 * rows)]
        return self.full[g].at[pl.ds(pl.multiple_of((2 * r + core) * rows, rows), rows)]

    def remote(self, g, src, dst, to, idx):
        return pltpu.make_async_remote_copy(
            src_ref=src,
            dst_ref=dst,
            send_sem=self.send_sem.at[g, idx],
            recv_sem=self.recv_sem.at[g, idx],
            device_id=to,
            device_id_type=MESH,
        )

    def copy(self, g, src, k, way, core, to, idx):
        return self.remote(g, src, self.block(g, k, way, core), to, idx)

    def forward(self, g, k, way, src=None):
        z, c = self.z, self.c
        src = self.block(g, k, way, c) if src is None else src
        i1, i2 = way
        sends = []
        if i1 == 0 and i2 == 0:
            sends.append(((chip(z, *self.yx[1, 0]), c), 3 + k))
        if i2 == 0:
            sends.append(((chip(z, *self.yx[0, 1]), c), 7 + i1 * 4 + k))
        if g >= self.split:
            sends.append((self.other, 15 + i2 * 8 + i1 * 4 + k))
        for to, idx in sends:
            self.copy(g, src, k, way, c, to, idx).start()

    def half(self, g, core):
        rows, columns = self.own[g].shape
        columns //= 2
        at = pl.multiple_of((2 * chip(self.z, self.y, self.x) + self.c) * rows, rows)
        return (
            self.own[g].at[:, pl.ds(pl.multiple_of(core * columns, columns), columns)],
            self.full[g].at[pl.ds(at, rows)],
        )

    def keep(self, g):
        if g < self.split:
            src, dst = self.half(g, self.c)
        else:
            src, dst = self.own[g], self.block(g, 0, (0, 0), self.c)
        return pltpu.make_async_copy(src, dst, self.local_sem.at[g])

    def swap(self, g):
        src, dst = self.half(g, 1 - self.c)
        return self.remote(g, src, dst, self.other, 15)

    def start(self, g):
        self.keep(g).start()
        if g < self.split:
            self.swap(g).start()
        else:
            self.begin(g, self.own[g])

    def swapped(self, g):
        self.swap(g).wait_recv()
        self.keep(g).wait()
        self.begin(g, self.block(g, 0, (0, 0), self.c))

    def begin(self, g, src):
        for k in (1, 2, 3):
            to = (chip(zxor(self.z, k), self.y, self.x), self.c)
            self.copy(g, src, 0, (0, 0), self.c, to, k - 1).start()
        self.forward(g, 0, (0, 0), src)

    def arrive(self, g, k, way, core, idx):
        block = self.block(g, k, way, core)
        self.remote(g, block, block, self.other, idx).wait_recv()

    def along_z(self, g):
        for k in (1, 2, 3):
            self.arrive(g, k, (0, 0), self.c, k - 1)
            self.forward(g, k, (0, 0))

    def first(self, g):
        for k in range(4):
            self.arrive(g, k, (1, 0), self.c, 3 + k)
            self.forward(g, k, (1, 0))

    def second(self, g):
        for i1 in range(2):
            for k in range(4):
                self.arrive(g, k, (i1, 1), self.c, 7 + i1 * 4 + k)
                self.forward(g, k, (i1, 1))

    def ready(self, g):
        if g >= self.split:
            for i2 in range(2):
                for i1 in range(2):
                    for k in range(4):
                        self.arrive(g, k, (i2, i1), 1 - self.c, 15 + i2 * 8 + i1 * 4 + k)
            self.keep(g).wait()

    def sent(self, g):
        if g < self.split:
            self.swap(g).wait_send()
        block = self.block(g, 0, (0, 0), self.c)
        for idx in range(15 if g < self.split else 31):
            self.remote(g, block, block, self.other, idx).wait_send()


AHEAD = 4


NT = (((1,), (1,)), ((), ()))
TN = (((0,), (0,)), ((), ()))
NN = (((1,), (0,)), ((), ()))


def mul(a, b, dims=NN):
    return lax.dot_general(a, b, dims, preferred_element_type=jnp.float32)


def low_lanes(rows):
    return lax.broadcasted_iota(jnp.int32, (rows, 128), 1) < 64


def self_fwd_pair(q_ref, k_ref, v_ref, lse_ref, put):
    length, b = q_ref.shape[0], 256
    low = low_lanes(b)
    row = lax.broadcasted_iota(jnp.int32, (b, b), 0)
    col = lax.broadcasted_iota(jnp.int32, (b, b), 1)
    for n in range(b, length + 1, b):
        q = q_ref[n - b : n, :] * jnp.asarray(0.125, jnp.bfloat16)
        mixed, lses = [], []
        for mine in (low, ~low):
            s = mul(jnp.where(mine, q, jnp.zeros_like(q)), k_ref[0:n, :], NT)
            last = jnp.where(col <= row, s[:, n - b :], NEG_BIG)
            s = jnp.concatenate([s[:, : n - b], last], axis=1) if n > b else last
            top = jnp.max(s, axis=1, keepdims=True)
            e = jnp.exp(s - top)
            total = jnp.sum(e, axis=1, keepdims=True)
            mixed.append(mul(e.astype(jnp.bfloat16), v_ref[0:n, :]) / total)
            lses.append(jnp.broadcast_to(top + jnp.log(total), (b, 128)))
        put(n - b, jnp.where(low, mixed[0], mixed[1]).astype(jnp.bfloat16))
        turned = jnp.where(low, lses[0], lses[1]).T
        lse_ref[0, :, n - b : n] = jnp.concatenate([turned[0:1], turned[64:65]], axis=0)


def self_bwd_pair(q_ref, k_ref, v_ref, o_ref, do_ref, lse_ref, dq_ref, dk_ref, dv_ref, acc):
    length, b = q_ref.shape[0], 256
    low = low_lanes(b)
    row = lax.broadcasted_iota(jnp.int32, (b, b), 0)
    col = lax.broadcasted_iota(jnp.int32, (b, b), 1)
    prod = do_ref[...].astype(jnp.float32) * o_ref[...].astype(jnp.float32)
    lane = lax.broadcasted_iota(jnp.int32, (8, 128), 1)
    head = lax.broadcasted_iota(jnp.int32, (8, 128), 0)
    pick = jnp.where(lane // 64 == head, 1.0, 0.0)
    inner = lax.dot_general(
        pick, prod, NT, precision=lax.Precision.HIGHEST, preferred_element_type=jnp.float32
    )
    acc[...] = jnp.zeros_like(acc)
    for at in range(0, length, b):
        k, v = k_ref[at : at + b, :], v_ref[at : at + b, :]
        qs, dos = q_ref[at:length, :], do_ref[at:length, :]
        dks, dvs = [], []
        for h, mine in enumerate((low, ~low)):
            km = jnp.where(mine, k, jnp.zeros_like(k))
            vm = jnp.where(mine, v, jnp.zeros_like(v))
            s = mul(km * jnp.asarray(0.125, jnp.bfloat16), qs, NT)
            w = jnp.exp(s - lse_ref[0, h : h + 1, at:length])
            first = jnp.where(row <= col, w[:, :b], 0.0)
            w = jnp.concatenate([first, w[:, b:]], axis=1) if length - at > b else first
            ds = (w * (mul(vm, dos, NT) - inner[h : h + 1, at:length])).astype(jnp.bfloat16)
            dvs.append(mul(w.astype(jnp.bfloat16), dos))
            dks.append(mul(ds, qs))
            acc[at:length, :] += mul(ds, km, TN)
        dk_ref[at : at + b, :] = (jnp.where(low, dks[0], dks[1]) * 0.125).astype(jnp.bfloat16)
        dv_ref[at : at + b, :] = jnp.where(low, dvs[0], dvs[1]).astype(jnp.bfloat16)
    dq_ref[...] = (acc[...] * 0.125).astype(jnp.bfloat16)


def cross_fwd_body(q_ref, k_ref, v_ref, ok_ref, o_ref):
    low = low_lanes(q_ref.shape[0])
    q = q_ref[...] * jnp.asarray(0.125, jnp.bfloat16)
    mixed = []
    for mine in (low, ~low):
        s = mul(jnp.where(mine, q, jnp.zeros_like(q)), k_ref[...], NT)
        s = jnp.where(ok_ref[0:1, :] > 0, s, NEG_BIG)
        e = jnp.exp(s - jnp.max(s, axis=1, keepdims=True))
        total = jnp.sum(e, axis=1, keepdims=True)
        mixed.append(mul(e.astype(jnp.bfloat16), v_ref[...]) / total)
    o_ref[...] = jnp.where(low, mixed[0], mixed[1]).astype(jnp.bfloat16)


def cross_bwd_body(q_ref, k_ref, v_ref, ok_ref, do_ref, dq_ref, dk_ref, dv_ref):
    keys = k_ref.shape[0]
    low = low_lanes(keys)
    wide = low_lanes(q_ref.shape[0])
    q, do, k, v = q_ref[...], do_ref[...], k_ref[...], v_ref[...]
    dqs, dks, dvs = [], [], []
    for mine in (low, ~low):
        km = jnp.where(mine, k, jnp.zeros_like(k))
        vm = jnp.where(mine, v, jnp.zeros_like(v))
        s = mul(km * jnp.asarray(0.125, jnp.bfloat16), q, NT)
        s = jnp.where(ok_ref[:, 0:1] > 0, s, NEG_BIG)
        e = jnp.exp(s - jnp.max(s, axis=0, keepdims=True))
        w = e / jnp.sum(e, axis=0, keepdims=True)
        dw = mul(vm, do, NT)
        inner = jnp.sum(dw * w, axis=0, keepdims=True)
        ds = (w * (dw - inner)).astype(jnp.bfloat16)
        dvs.append(mul(w.astype(jnp.bfloat16), do))
        dks.append(mul(ds, q))
        dqs.append(mul(ds, km, TN))
    dq_ref[...] = (jnp.where(wide, dqs[0], dqs[1]) * 0.125).astype(jnp.bfloat16)
    dk_ref[...] = (jnp.where(low, dks[0], dks[1]) * 0.125).astype(jnp.bfloat16)
    dv_ref[...] = jnp.where(low, dvs[0], dvs[1]).astype(jnp.bfloat16)


class Scatter:
    def __init__(self, late, tile, got, part, from_late, out, sems, credit=None):
        self.late, self.tile, self.got = late, tile, got
        self.slots, self.count, self.free = credit or (None, None, None)
        self.part, self.from_late, self.out = part, from_late, out
        self.send_sem, self.recv_sem = sems
        z, y, x, c = place()
        self.z, self.y, self.x, self.c = z, y, x, c
        self.other = (chip(z, y, x), 1 - c)

    def ways(self, core):
        y, x = self.y, self.x
        return [
            flip(y, core * i1 + (1 - core) * i2) * 2 + flip(x, (1 - core) * i1 + core * i2)
            for i1 in range(2)
            for i2 in range(2)
        ]

    def partners(self):
        z, c = self.z, self.c
        way = self.ways(c)
        return [(zxor(z, k) * 4 + way[0], c) for k in (1, 2, 3)] + [
            (z * 4 + way[2], c),
            (z * 4 + way[1], c),
            self.other,
        ]

    def mine(self, u, j):
        way = self.ways(self.c)[j]
        return self.tile(u).at[:, way] if self.late(u) else self.tile(u).at[:, way, self.c]

    def remote(self, src, dst, u, idx, to):
        return pltpu.make_async_remote_copy(
            src_ref=src,
            dst_ref=dst,
            send_sem=self.send_sem.at[u, idx],
            recv_sem=self.recv_sem.at[u, idx],
            device_id=to,
            device_id_type=MESH,
        )

    def to_core(self, u, j):
        c = self.c
        src = self.tile(u).at[:, self.ways(1 - c)[j], 1 - c]
        return self.remote(src, self.got(u, 0).at[j], u, j, self.other)

    def to_first(self, u, i):
        to = (self.z * 4 + self.ways(self.c)[2], self.c)
        return self.remote(self.mine(u, 2 + i), self.got(u, 1).at[i], u, 4 + i, to)

    def to_second(self, u):
        to = (self.z * 4 + self.ways(self.c)[1], self.c)
        return self.remote(self.mine(u, 1), self.got(u, 2), u, 6, to)

    def to_z(self, u, k):
        zk = zxor(self.z, k)
        to = (zk * 4 + self.ways(self.c)[0], self.c)
        return self.remote(self.mine(u, 0).at[zk], self.got(u, 3).at[k - 1], u, 6 + k, to)

    def to_late(self, u):
        rows = self.part(u).shape[0] // 2
        theirs = pl.ds(pl.multiple_of((1 - self.c) * rows, rows), rows)
        return self.remote(self.part(u).at[theirs], self.from_late(u), u, 0, self.other)

    def add(self, u, j, term):
        mine = self.mine(u, j)

        @pl.loop(0, 4)
        def _(i):
            mine[i] = mine[i] + term[i]

    def step0(self, u):
        if self.slots and u >= self.slots:
            pl.semaphore_wait(self.free, 1)
        if not self.late(u):
            for j in (2, 3, 0, 1):
                self.to_core(u, j).start()

    def step1(self, u):
        for j in (2, 3, 0, 1):
            if not self.late(u):
                self.to_core(u, j).wait_recv()
                self.add(u, j, self.got(u, 0).at[j])
            if j > 1:
                self.to_first(u, j - 2).start()
        if self.slots and u < self.count - self.slots:
            pl.semaphore_signal(self.free, inc=1, device_id=self.other, device_id_type=MESH)

    def step2(self, u):
        for i in (1, 0):
            self.to_first(u, i).wait_recv()
            self.add(u, i, self.got(u, 1).at[i])
            if i == 1:
                self.to_second(u).start()

    def step3(self, u):
        self.to_second(u).wait_recv()
        self.add(u, 0, self.got(u, 2))
        for k in (2, 3, 1):
            self.to_z(u, k).start()

    def step4(self, u):
        got = self.got(u, 3)
        for k in (1, 2, 3):
            self.to_z(u, k).wait_recv()
        total = self.mine(u, 0)[self.z].astype(jnp.float32) + got[0].astype(jnp.float32)
        total = total + (got[1].astype(jnp.float32) + got[2].astype(jnp.float32))
        if self.late(u):
            self.part(u)[...] = total
            self.to_late(u).start()
        else:
            self.out(u, total, None)

    def step5(self, u):
        if self.late(u):
            rows = self.part(u).shape[0] // 2
            self.to_late(u).wait_recv()
            mine = self.part(u)[pl.ds(pl.multiple_of(self.c * rows, rows), rows)]
            self.out(u, mine, self.from_late(u)[...])

    def sent(self, u):
        if not self.late(u):
            for j in range(4):
                self.to_core(u, j).wait_send()
        for i in range(2):
            self.to_first(u, i).wait_send()
        self.to_second(u).wait_send()
        for k in (1, 2, 3):
            self.to_z(u, k).wait_send()

    def slot(self, t, units):
        for lag, step in (
            (1, self.step1),
            (2, self.step2),
            (3, self.step3),
            (4, self.step4),
            (5, self.step5),
        ):
            if 0 <= t - lag < units and not (lag == 1 and self.late(t - lag)):
                step(t - lag)


def turn(src, dst):
    @pl.loop(0, src.shape[1] // 128)
    def _(i):
        at = pl.multiple_of(i * 128, 128)
        dst[pl.ds(at, 128), :] = src[:, pl.ds(at, 128)].T


def product(rows, right, tile):
    @pl.loop(0, 2)
    def _(i):
        value = mul(rows(i), right[...]).astype(tile.dtype)
        tile[pl.ds(2 * i, 2)] = value.reshape((2, *tile.shape[1:]))


def middle_body(
    h3, du, act, gm, w_in, w_outer, c_out, c_query, w_out, y2, y1, cq, ck, cv, c_key, c_value, ok, vec, sums_in, *refs
):
    out_in, out_outer, sums_out, cap_out, block_out, db2_out, dcq_out, dck_out, dcv_out, da_out, dy1_out, do_out = refs[:12]
    (h3_v, du_v, act_v, gm_v, left, left_act, tiles, got0, got1, got2, got3) = refs[12:23]
    (w_v, acc, y_v, dy_v, db_v, da_v, dc_v, cq_v, dcq_v, kv_v, dkv_v, cap_v) = refs[23:35]
    send_sem, recv_sem, load_sem, w_sem, out_sem, free_sem = refs[35:]
    units, depth, slots = 8, tiles.shape[0], got0.shape[0]
    rows, width = gm_v.shape
    step = 128

    def out(u, total, _):
        if u < 4:
            out_in[:, u * 1024 : (u + 1) * 1024] = total
        else:
            out_outer[(u - 4) * 32 : (u - 3) * 32, :] = total

    got = (got0, got1, got2, got3)
    ring = Scatter(
        lambda u: False,
        lambda u: tiles.at[u % depth],
        lambda u, i: got[i].at[u % slots if i == 0 else u],
        None,
        None,
        out,
        (send_sem, recv_sem),
        (slots, units, free_sem),
    )
    pairs = {
        "h3": (h3, h3_v),
        "du": (du, du_v),
        "act": (act, act_v),
        "gm": (gm, gm_v),
        "y2": (y2, y_v),
        "cq": (cq, cq_v),
        "ck": (ck, kv_v.at[0]),
        "cv": (cv, kv_v.at[1]),
        "y1": (y1, y_v),
    }
    loads = {
        name: pltpu.make_async_copy(src, dst, load_sem.at[i])
        for i, (name, (src, dst)) in enumerate(pairs.items())
    }
    parts = [w_in.at[:, pl.ds(i * 1024, 1024)] for i in range(4)]
    parts += [c_out, c_query, c_key, c_value, w_out]
    parts += [w_outer.at[pl.ds(i * 1024, 1024)] for i in range(4)]
    weights = [
        pltpu.make_async_copy(part, w_v.at[n % 2], w_sem.at[n % 2]) for n, part in enumerate(parts)
    ]
    stores = [
        pltpu.make_async_copy(src, dst, out_sem.at[i])
        for i, (src, dst) in enumerate(
            (
                (db_v, db2_out),
                (dcq_v, dcq_out),
                (dkv_v.at[0], dck_out),
                (dkv_v.at[1], dcv_out),
                (da_v, da_out),
                (dy_v, dy1_out),
                (dc_v, do_out),
                (h3_v, block_out),
            )
        )
    ]

    def use(n, work):
        weights[n].wait()
        work(w_v.at[n % 2])
        if n + 2 < len(weights):
            weights[n + 2].start()

    def over_rows(work):
        @pl.loop(0, rows // step)
        def _(i):
            work(pl.ds(i * step, step))

    def make(u):
        if u >= depth:
            ring.sent(u - depth)
        tile = tiles.at[u % depth]
        if u < 4:
            right = du_v.at[:, u * 1024 : (u + 1) * 1024]
            product(lambda i: left[pl.ds(i * 512, 512), :], right, tile)
        else:
            product(
                lambda i, b=u - 4: left_act[pl.ds(i * 16, 16), b].reshape(512, 512), gm_v, tile
            )
        ring.step0(u)

    def turn_act(t):
        @pl.loop(t * 8, t * 8 + 8)
        def _(r):
            at = pl.multiple_of(r * 128, 128)
            left_act[r] = act_v[:, pl.ds(at, 128)].T.reshape(4, 32, 512)

    def add_dh3(j):
        def work(w):
            def body(at):
                term = mul(du_v[at, j * 1024 : (j + 1) * 1024], w[...], NT)
                acc[at, :] = term if j == 0 else acc[at, :] + term

            over_rows(body)

        use(j, work)

    def norm3():
        loads["y2"].wait()
        sums_out[...] = sums_in[...]

        def body(at):
            value = y_v[at, :]
            grads, dgain, dbias = norm_back(value, vec[4:5, :], acc[at, :])
            dy = gm_v[at, :].astype(jnp.float32) + grads
            dy_v[at, :] = dy
            db_v[at, :] = dy.astype(jnp.bfloat16)
            acc[at, :] = value + vec[6:7, :]
            sums_out[4:5, :] += dgain
            sums_out[5:6, :] += dbias

        over_rows(body)
        stores[0].start()
        loads["y1"].start()

    def back_out(w):
        def body(at):
            dc_v[at, :] = mul(db_v[at, :], w[...], NT).astype(jnp.bfloat16)

        over_rows(body)

    def cross(lo, hi):
        @pl.loop(lo, hi)
        def _(i):
            at = pl.ds(pl.multiple_of(i * 128, 128), 128)
            cross_bwd_body(
                cq_v.at[:, at],
                kv_v.at[0, :, at],
                kv_v.at[1, :, at],
                ok.at[1],
                dc_v.at[:, at],
                dcq_v.at[:, at],
                dkv_v.at[0, :, at],
                dkv_v.at[1, :, at],
            )

    def norm2(w):
        loads["y1"].wait()

        def body(at):
            dh = mul(dcq_v[at, :], w[...], NT)
            grads, dgain, dbias = norm_back(y_v[at, :], vec[2:3, :], dh)
            dy = dy_v[at, :] + grads
            dy_v[at, :] = dy
            da_v[at, :] = dy.astype(jnp.bfloat16)
            sums_out[2:3, :] += dgain
            sums_out[3:4, :] += dbias

        over_rows(body)
        stores[4].start()
        stores[5].start()

    def back_key(w):
        cap_v[...] = mul(dkv_v[0], w[...], NT)

    def back_value(w):
        cap_out[...] = (cap_v[...] + mul(dkv_v[1], w[...], NT)).astype(jnp.bfloat16)

    def back_self(w):
        def body(at):
            dc_v[at, :] = mul(da_v[at, :], w[...], NT).astype(jnp.bfloat16)

        over_rows(body)
        stores[6].start()

    def add_out(j):
        def work(w):
            def body(at):
                term = acc[at, :] + mul(act_v[at, j * 1024 : (j + 1) * 1024], w[...])
                if j < 3:
                    acc[at, :] = term
                else:
                    h3_v[at, :] = term.astype(jnp.bfloat16)

            over_rows(body)

        use(9 + j, work)

    for name in ("h3", "du", "gm", "act", "y2", "cq", "ck", "cv"):
        loads[name].start()
    weights[0].start()
    weights[1].start()
    greet(ring.partners())
    loads["h3"].wait()
    turn(h3_v, left)
    loads["du"].wait()
    make(0)
    make(1)
    add_dh3(0)
    ring.slot(1, 1)
    make(2)
    loads["act"].wait()
    turn_act(0)
    ring.slot(2, 2)
    add_dh3(1)
    add_dh3(2)
    make(3)
    ring.slot(3, 3)
    turn_act(1)
    add_dh3(3)
    loads["gm"].wait()
    norm3()
    ring.slot(4, 4)
    turn_act(2)
    turn_act(3)
    make(4)
    use(4, back_out)
    ring.slot(5, 5)
    make(5)
    for name in ("cq", "ck", "cv"):
        loads[name].wait()
    cross(0, 4)
    ring.slot(6, 6)
    make(6)
    cross(4, 8)
    for i in (1, 2, 3):
        stores[i].start()
    ring.slot(7, 7)
    make(7)
    use(5, norm2)
    ring.slot(8, 8)
    use(6, back_key)
    use(7, back_value)
    use(8, back_self)
    ring.slot(9, units)
    add_out(0)
    add_out(1)
    ring.slot(10, units)
    add_out(2)
    add_out(3)
    stores[7].start()
    ring.slot(11, units)
    ring.slot(12, units)
    for u in range(max(units - depth, 0), units):
        ring.sent(u)
    for store in stores:
        store.wait()


def middle(operands, collective_id):
    depth, bf, f32, vm = 5, jnp.bfloat16, jnp.float32, pltpu.VMEM
    shape = jax.ShapeDtypeStruct
    rows = (512, 1024)
    inside = pl.BlockSpec(memory_space=pltpu.VMEM)
    return pl.pallas_call(
        middle_body,
        out_shape=[
            shape((32, 4096), f32),
            shape((128, 1024), f32),
            shape((16, 1024), f32),
            shape((128, 1024), bf),
            shape(rows, bf),
            shape(rows, bf),
            shape(rows, bf),
            shape((128, 1024), bf),
            shape((128, 1024), bf),
            shape(rows, bf),
            shape(rows, f32),
            shape(rows, bf),
        ],
        in_specs=[ANY] * 16 + [inside] * 3,
        out_specs=[inside] * 4 + [ANY] * 8,
        scratch_shapes=[
            vm(rows, bf),
            vm((512, 4096), bf),
            vm((512, 4096), bf),
            vm(rows, bf),
            vm((1024, 512), bf),
            vm((32, 4, 32, 512), bf),
            vm((depth, 4, 4, 2, 32, 1024), bf),
            vm((4, 4, 4, 32, 1024), bf),
            vm((8, 2, 4, 32, 1024), bf),
            vm((8, 4, 32, 1024), bf),
            vm((8, 3, 32, 1024), bf),
            vm((2, 1024, 1024), bf),
            vm(rows, f32),
            vm(rows, f32),
            vm(rows, f32),
            vm(rows, bf),
            vm(rows, bf),
            vm(rows, bf),
            vm(rows, bf),
            vm(rows, bf),
            vm((2, 128, 1024), bf),
            vm((2, 128, 1024), bf),
            vm((128, 1024), f32),
            pltpu.SemaphoreType.DMA((8, 10)),
            pltpu.SemaphoreType.DMA((8, 10)),
            pltpu.SemaphoreType.DMA((9,)),
            pltpu.SemaphoreType.DMA((2,)),
            pltpu.SemaphoreType.DMA((8,)),
            pltpu.SemaphoreType.REGULAR,
        ],
        compiler_params=pltpu.CompilerParams(
            collective_id=collective_id,
            has_side_effects=True,
            vmem_limit_bytes=59 * 1024 * 1024,
        ),
        name="middle",
    )(*operands)


def tail_body(q, k, v, o, lse, grad, h1, attn, da, h2, dcq, cattn, db2, e, dck, dcv, wq, wk, wv, x, dy1, gain, sums, cap, row, image_out, *refs):
    outs, total_out, refs = refs[:9], refs[9], refs[10:]
    (q_v, k_v, v_v, o_v, lse_v, do_v, cap_v, a_v, r_v, e_v, dc_v, x_v, dx_v, gain_v, sum_v) = refs[:15]
    (acc, dq_v, dk_v, dv_v, left, left1, left_e, tiles, late_tiles) = refs[15:24]
    big, late = refs[24:28], refs[28:31]
    part, from_late, give_v, take_v, got_sum = refs[31:36]
    send_sem, recv_sem, load_sem, pair_send, pair_recv, keep_sem, row_sem, sum_send, sum_recv = refs[36:]
    normal, units, depth = 7, 10, tiles.shape[0]
    dp, c = lax.axis_index("dp"), lax.axis_index("seq")
    length, width = q_v.shape
    pairs, rows = width // 128, length // 2
    mine = pl.ds(pl.multiple_of(c * rows, rows), rows)
    theirs = pl.ds(pl.multiple_of((1 - c) * rows, rows), rows)

    def out(u, total, other):
        if u < 5:
            outs[u][...] = total
        elif u < normal:
            outs[5][(u - 5) * 32 : (u - 4) * 32, :] = total
        else:
            half = total.shape[1]
            outs[u - 1][:, pl.ds(pl.multiple_of(c * half, half), half)] = total
            outs[u - 1][:, pl.ds(pl.multiple_of((1 - c) * half, half), half)] = other

    ring = Scatter(
        lambda u: u >= normal,
        lambda u: tiles.at[u % depth] if u < normal else late_tiles.at[u - normal],
        lambda u, i: big[i].at[u] if u < normal else late[i - 1].at[u - normal],
        lambda u: part.at[u - normal],
        lambda u: from_late.at[u - normal],
        out,
        (send_sem, recv_sem),
    )

    def load(i, src, dst):
        return pltpu.make_async_copy(src, dst, load_sem.at[i])

    loads = {
        "a0": load(0, attn, a_v.at[0]),
        "r0": load(1, da, r_v.at[0]),
        "q": load(2, q, q_v),
        "k": load(3, k, k_v),
        "v": load(4, v, v_v),
        "o": load(5, o, o_v),
        "lse": load(6, lse, lse_v),
        "a1": load(7, h2, a_v.at[1]),
        "r1": load(8, dcq, r_v.at[1]),
        "a2": load(9, cattn, a_v.at[0]),
        "r2": load(10, db2, r_v.at[0]),
        "e": load(11, e, e_v),
        "ck": load(12, dck, dc_v.at[0]),
        "cv": load(13, dcv, dc_v.at[1]),
        "h0": load(14, h1.at[pl.ds(0, 512)], a_v.at[1]),
        "h1": load(22, h1.at[pl.ds(512, 512)], a_v.at[0]),
        "cap": load(23, cap, cap_v),
        "wq": load(15, wq, q_v),
        "wk": load(16, wk, k_v),
        "wv": load(17, wv, v_v),
        "x": load(18, x, x_v),
        "dy1": load(19, dy1, dx_v),
        "gain": load(20, gain.at[pl.ds(0, 8)], gain_v),
        "sums": load(21, sums, sum_v),
    }

    def lane(i, core):
        return pl.ds(pl.multiple_of(core * width + i * 128, 128), 128)

    def keep(i):
        return pltpu.make_async_copy(grad.at[:, lane(i, c)], do_v.at[i, mine], keep_sem.at[i])

    def give(i):
        return pltpu.make_async_remote_copy(
            src_ref=grad.at[:, lane(i, 1 - c)],
            dst_ref=do_v.at[i, mine],
            send_sem=pair_send.at[i],
            recv_sem=pair_recv.at[i],
            device_id=ring.other,
            device_id_type=MESH,
        )

    later = ("a2", "r2", "h0", "h1", "wq", "wk", "wv")
    for name in loads:
        if name not in later:
            loads[name].start()
    greet(ring.partners())
    for i in range(pairs):
        give(i).start()
        keep(i).start()

    def pair(i):
        keep(i).wait()
        give(i).wait()
        at = pl.ds(i * 128, 128)
        self_bwd_pair(
            q_v.at[:, at],
            k_v.at[:, at],
            v_v.at[:, at],
            o_v.at[:, at],
            do_v.at[i],
            lse_v.at[pl.ds(i, 1)],
            dq_v.at[:, at],
            dk_v.at[:, at],
            dv_v.at[:, at],
            acc,
        )

    def make(u):
        if u >= depth and u < normal:
            ring.sent(u - depth)
        if u < 3:
            loads[f"a{u}"].wait()
            loads[f"r{u}"].wait()
            turn(a_v.at[u % 2], left)
            product(lambda i: left[pl.ds(i * 512, 512), :], r_v.at[u % 2], tiles.at[u % depth])
            for name in (("a2", "r2"), ("h0",), ("h1",))[u]:
                loads[name].start()
        elif u in (5, 6):
            if u == 5:
                loads["cap"].wait()
            tile = tiles.at[u % depth]
            for core in range(2):
                at = core * 64 + (u - 5) * 32
                block = cap_v[at : at + 32, :]

                @pl.loop(0, 16)
                def _(i, core=core, block=block):
                    hit = row[0:1, :] == i.astype(jnp.float32)
                    tile[i // 4, i % 4, core] = jnp.where(hit, block, jnp.zeros_like(block))

        elif u < normal:
            if u == 3:
                loads["e"].wait()
                loads["ck"].wait()
                loads["cv"].wait()
                turn(e_v, left_e)
            product(lambda i: left_e[pl.ds(i * 512, 512), :], dc_v.at[u - 3], tiles.at[u % depth])
        else:
            if u == normal:
                loads["h0"].wait()
                turn(a_v.at[1], left1.at[:, pl.ds(0, 512)])
                loads["h1"].wait()
                turn(a_v.at[0], left1.at[:, pl.ds(512, 512)])
            right, tile = (dq_v, dk_v, dv_v)[u - normal], late_tiles.at[u - normal]
            product(lambda i: left1[pl.ds(i * 512, 512), :], right, tile)
            ring.step1(u)
            return
        ring.step0(u)

    swap = pltpu.make_async_remote_copy(
        src_ref=give_v,
        dst_ref=take_v,
        send_sem=row_sem.at[0],
        recv_sem=row_sem.at[1],
        device_id=ring.other,
        device_id_type=MESH,
    )

    def back(at):
        total = mul(dq_v[at, :], q_v[...], NT) + mul(dk_v[at, :], k_v[...], NT)
        return total + mul(dv_v[at, :], v_v[...], NT)

    def give_rows():
        for name in ("wq", "wk", "wv"):
            loads[name].wait()

        @pl.loop(0, rows // 128)
        def _(i):
            at = pl.ds(pl.multiple_of((1 - c) * rows + i * 128, 128), 128)
            give_v[pl.ds(i * 128, 128), :] = back(at).astype(jnp.bfloat16)

        swap.start()

    def take_rows():
        swap.wait_recv()
        for name in ("x", "dy1", "gain", "sums"):
            loads[name].wait()
        step = 128

        @pl.loop(0, rows // step)
        def _(i):
            at = pl.ds(i * step, step)
            whole = pl.ds(pl.multiple_of(c * rows + i * step, step), step)
            dh = back(whole) + take_v[at, :].astype(jnp.float32)
            grads, dgain, dbias = norm_back(x_v[at, :].astype(jnp.float32), gain_v[0:1, :], dh)
            dx_v[at, :] = dx_v[at, :] + grads
            sum_v[0:1, :] = sum_v[0:1, :] + dgain
            sum_v[1:2, :] = sum_v[1:2, :] + dbias

    write = pltpu.make_async_copy(dx_v, image_out, row_sem.at[2])

    way = ring.ways(c)
    peers = [
        [ring.other],
        [(ring.z * 4 + way[2], c)],
        [(ring.z * 4 + way[1], c)],
        [(zxor(ring.z, n) * 4 + way[0], c) for n in (1, 2, 3)],
    ]

    def sum_send_of(s, n):
        return pltpu.make_async_remote_copy(
            src_ref=sum_v if s == 0 else got_sum.at[5 + s],
            dst_ref=got_sum.at[s + n],
            send_sem=sum_send.at[s + n],
            recv_sem=sum_recv.at[s + n],
            device_id=peers[s][n],
            device_id_type=MESH,
        )

    def start_sum(s):
        for n in range(len(peers[s])):
            sum_send_of(s, n).start()

    def take_sum(s):
        total = sum_v[...] if s == 0 else got_sum[5 + s]
        for n in range(len(peers[s])):
            sum_send_of(s, n).wait_recv()
            total = total + got_sum[s + n]
        if s == 3:
            total_out[...] = total
        else:
            got_sum[6 + s] = total
            start_sum(s + 1)

    make(0)
    make(1)
    ring.step1(0)
    make(2)
    ring.step1(1)
    make(3)
    ring.step1(2)
    make(4)
    ring.step1(3)
    ring.step1(4)
    for name in ("q", "k", "v", "o", "lse"):
        loads[name].wait()
    pair(0)
    ring.step2(0)
    ring.step2(1)
    pair(1)
    ring.step3(0)
    ring.step2(2)
    pair(2)
    ring.step3(1)
    ring.step2(3)
    ring.step4(0)
    ring.step3(2)
    pair(3)
    for name in ("wq", "wk", "wv"):
        loads[name].start()
    ring.step2(4)
    for u in range(normal, units):
        make(u)
    give_rows()
    ring.step3(3)
    ring.step4(1)
    make(5)
    ring.step1(5)
    ring.step4(2)
    make(6)
    ring.step1(6)
    ring.step3(4)
    take_rows()
    write.start()
    start_sum(0)
    ring.step2(7)
    ring.step4(3)
    ring.step2(8)
    ring.step4(4)
    take_sum(0)
    ring.step3(7)
    ring.step2(9)
    ring.step2(5)
    ring.step2(6)
    take_sum(1)
    ring.step3(8)
    ring.step3(9)
    ring.step4(7)
    take_sum(2)
    ring.step3(5)
    ring.step3(6)
    ring.step4(8)
    ring.step4(9)
    ring.step5(7)
    take_sum(3)
    ring.step4(5)
    ring.step4(6)
    ring.step5(8)
    ring.step5(9)
    for u in range(normal - depth, units):
        ring.sent(u)
    for u in range(normal, units):
        ring.to_late(u).wait_send()
    swap.wait_send()
    write.wait()
    for s in range(4):
        for n in range(len(peers[s])):
            sum_send_of(s, n).wait_send()


def norm_back(value, gain, dh):
    center = value - jnp.mean(value, axis=1, keepdims=True)
    r = lax.rsqrt(jnp.mean(center * center, axis=1, keepdims=True) + EPSILON)
    hat = center * r
    dhg = dh * gain
    grads = r * (
        dhg
        - jnp.mean(dhg, axis=1, keepdims=True)
        - hat * jnp.mean(dhg * hat, axis=1, keepdims=True)
    )
    return grads, jnp.sum(dh * hat, axis=0, keepdims=True), jnp.sum(dh, axis=0, keepdims=True)


def scatter_tail(operands, collective_id):
    bf, f32, depth = jnp.bfloat16, jnp.float32, 5
    vm = pltpu.VMEM
    outs = [jax.ShapeDtypeStruct((512, 1024), f32)] + [
        jax.ShapeDtypeStruct((64 if i == 5 else 32, 1024), f32) for i in range(9)
    ]
    outs.append(jax.ShapeDtypeStruct((16, 1024), f32))
    return pl.pallas_call(
        tail_body,
        out_shape=outs,
        in_specs=[ANY] * (len(operands) - 1) + [pl.BlockSpec(memory_space=pltpu.VMEM)],
        out_specs=[ANY] + [pl.BlockSpec(memory_space=pltpu.VMEM)] * 10,
        scratch_shapes=[
            vm((1024, 512), bf),
            vm((1024, 512), bf),
            vm((1024, 512), bf),
            vm((1024, 512), bf),
            vm((4, 2, 1024), f32),
            vm((4, 1024, 128), bf),
            vm((128, 1024), bf),
            vm((2, 512, 1024), bf),
            vm((2, 512, 1024), bf),
            vm((128, 1024), bf),
            vm((2, 128, 1024), bf),
            vm((512, 1024), bf),
            vm((512, 1024), f32),
            vm((8, 1024), f32),
            vm((16, 1024), f32),
            vm((1024, 128), f32),
            vm((1024, 512), bf),
            vm((1024, 512), bf),
            vm((1024, 512), bf),
            vm((1024, 512), bf),
            vm((1024, 1024), bf),
            vm((1024, 128), bf),
            vm((depth, 4, 4, 2, 32, 1024), bf),
            vm((3, 4, 4, 64, 512), bf),
            vm((7, 4, 4, 32, 1024), bf),
            vm((7, 2, 4, 32, 1024), bf),
            vm((7, 4, 32, 1024), bf),
            vm((7, 3, 32, 1024), bf),
            vm((3, 2, 4, 64, 512), bf),
            vm((3, 4, 64, 512), bf),
            vm((3, 3, 64, 512), bf),
            vm((3, 64, 512), f32),
            vm((3, 32, 512), f32),
            vm((512, 1024), bf),
            vm((512, 1024), bf),
            vm((9, 16, 1024), f32),
            pltpu.SemaphoreType.DMA((10, 10)),
            pltpu.SemaphoreType.DMA((10, 10)),
            pltpu.SemaphoreType.DMA((24,)),
            pltpu.SemaphoreType.DMA((4,)),
            pltpu.SemaphoreType.DMA((4,)),
            pltpu.SemaphoreType.DMA((4,)),
            pltpu.SemaphoreType.DMA((3,)),
            pltpu.SemaphoreType.DMA((6,)),
            pltpu.SemaphoreType.DMA((6,)),
        ],
        compiler_params=pltpu.CompilerParams(
            collective_id=collective_id,
            has_side_effects=True,
            vmem_limit_bytes=59 * 1024 * 1024,
        ),
        name="scatter_tail",
    )(*operands)


def norm_fwd(value, gain, shift):
    center = value - jnp.mean(value, axis=1, keepdims=True)
    spread = jnp.mean(center * center, axis=1, keepdims=True)
    return center * lax.rsqrt(spread + EPSILON) * gain + shift


GELU_IN = 0.7978845608028654
GELU_CUBE = 0.044715


def gelu_both(u):
    square = u * u
    t = jnp.tanh(GELU_IN * (u + GELU_CUBE * (square * u)))
    half = 0.5 * (1.0 + t)
    slope = half + 0.5 * u * (1.0 - t * t) * (GELU_IN * (1.0 + 3.0 * GELU_CUBE * square))
    return u * half, slope


FRONT_IN = (
    "w_query",
    "w_key",
    "w_value",
    "packed",
    "w_out",
    "encoder",
    "c_query",
    "c_key",
    "c_value",
    "c_out",
    "w_outer",
    "w_in",
    "images",
    "gm",
    "caption_seg",
    "image_row",
    "image_seg",
)
FRONT_OUT = (
    "wq",
    "wk",
    "wv",
    "w_out_all",
    "c_query_all",
    "c_key_all",
    "c_value_all",
    "c_out_all",
    "w_outer_all",
    "w_in_all",
    "h1",
    "q",
    "k",
    "v",
    "heads",
    "attn",
    "y1",
    "h2",
    "cq",
    "ck",
    "cv",
    "caption",
    "cattn",
    "y2",
    "h3",
    "act",
    "du",
    "lse",
    "vec",
    "ok",
    "sums",
)
FRONT_VMEM = (
    "table",
    "enc",
    "both",
    "wqkv",
    "h1_v",
    "q_v",
    "k_v",
    "v_v",
    "obuf",
    "attn_v",
    "y1_v",
    "h2_v",
    "cq_v",
    "kv_v",
    "cap_v",
    "cattn_v",
    "y2_v",
    "h3_v",
    "gm_v",
    "dact",
    "act_v",
    "du_v",
    "w_v",
    "bin",
)


def front_body(*refs):
    names = FRONT_IN + FRONT_OUT + FRONT_VMEM
    r = dict(zip(names, refs))
    (send_sem, recv_sem, local_sem, pair_sem, give_send, give_recv, keep_sem, w_sem, out_sem, gm_sem) = refs[len(names) :]
    c = lax.axis_index("seq")
    rows, step = 512, 128
    own = [r["w_query"], r["w_key"], r["w_value"], r["packed"], r["w_out"]]
    own += [r["encoder"].at[:, pl.ds(pl.multiple_of(c * 64, 64), 64)]]
    own += [r["c_query"], r["c_key"], r["c_value"], r["c_out"], r["w_outer"]]
    own += [r["w_in"].at[:, i * 1024 : (i + 1) * 1024] for i in range(4)]
    full = [r["wqkv"].at[i] for i in range(3)] + [r["table"], r["w_out_all"], r["enc"]]
    full += [r["c_query_all"], r["c_key_all"], r["c_value_all"], r["c_out_all"], r["w_outer_all"]]
    full += [r["w_in_all"].at[:, i * 1024 : (i + 1) * 1024] for i in range(4)]
    n = len(own)
    ring = Gather(3, own, full, send_sem, recv_sem, local_sem)
    order = [3, 0, 1, 2, *range(4, n)]

    def slot(t):
        if t < n:
            ring.along_z(order[t])
        if 0 < t < n - AHEAD:
            ring.start(order[t + AHEAD])
        if 0 <= t - 1 < n:
            ring.first(order[t - 1])
        if 0 <= t - 2 < n:
            ring.second(order[t - 2])

    mine = r["both"].at[pl.ds(pl.multiple_of(c * rows, rows), rows)]
    keep_image = pltpu.make_async_copy(r["images"], mine, pair_sem.at[0])
    give_image = pltpu.make_async_remote_copy(
        src_ref=r["images"],
        dst_ref=mine,
        send_sem=pair_sem.at[1],
        recv_sem=pair_sem.at[2],
        device_id=ring.other,
        device_id_type=MESH,
    )
    load_gm = pltpu.make_async_copy(r["gm"], r["gm_v"], gm_sem)
    places = [
        ("wqkv", 0, "wq"),
        ("wqkv", 1, "wk"),
        ("wqkv", 2, "wv"),
        ("h1_v", None, "h1"),
        ("q_v", None, "q"),
        ("k_v", None, "k"),
        ("v_v", None, "v"),
        ("attn_v", None, "attn"),
        ("y1_v", None, "y1"),
        ("h2_v", None, "h2"),
        ("cq_v", None, "cq"),
        ("kv_v", 0, "ck"),
        ("kv_v", 1, "cv"),
        ("cap_v", None, "caption"),
        ("cattn_v", None, "cattn"),
        ("y2_v", None, "y2"),
        ("h3_v", None, "h3"),
        ("act_v", None, "act"),
        ("du_v", None, "du"),
    ]
    stores = {
        dst: pltpu.make_async_copy(r[src] if at is None else r[src].at[at], r[dst], out_sem.at[i])
        for i, (src, at, dst) in enumerate(places)
    }
    parts = [r["w_out_all"], r["c_query_all"], r["c_key_all"], r["c_value_all"], r["c_out_all"]]
    parts += [r["w_outer_all"].at[i * 1024 : (i + 1) * 1024] for i in range(4)] + full[11:]
    weights = [
        pltpu.make_async_copy(part, r["w_v"].at[i % 2], w_sem.at[i % 2])
        for i, part in enumerate(parts)
    ]

    def weight(i):
        weights[i].wait()
        return r["w_v"].at[i % 2]

    def over(count, work):
        @pl.loop(0, count // step)
        def _(i):
            work(pl.ds(i * step, step))

    vec, table = r["vec"], r["table"]

    def unpack():
        for i in range(8):
            lanes = slice(i * 128, (i + 1) * 128)
            at = 4 * i * 16
            vec[:, lanes] = (table[at : at + 16] + table[at + 16 : at + 32]) + (
                table[at + 32 : at + 48] + table[at + 48 : at + 64]
            )
            for j in range(4):
                at = (8 * j + i) * 16 + 7
                r["bin"][j : j + 1, lanes] = table[at : at + 1]

    def row(i):
        return vec[i : i + 1, :]

    def norm1(at):
        value = norm_fwd(r["both"][at, :].astype(jnp.float32), row(0), row(1))
        r["h1_v"][at, :] = value.astype(jnp.bfloat16)

    def project(i):
        def work(at):
            value = mul(r["h1_v"][at, :], r["wqkv"][i])
            r[("q_v", "k_v", "v_v")[i]][at, :] = value.astype(jnp.bfloat16)

        over(2 * rows, work)
        stores[("wq", "wk", "wv")[i]].start()
        stores[("q", "k", "v")[i]].start()

    def keep(i):
        at = pl.multiple_of(c * 512 + i * 128, 128)
        src = r["obuf"].at[i, pl.ds(pl.multiple_of(c * rows, rows), rows)]
        return pltpu.make_async_copy(src, r["attn_v"].at[:, pl.ds(at, 128)], keep_sem.at[i])

    def give(i):
        at = pl.multiple_of(c * 512 + i * 128, 128)
        return pltpu.make_async_remote_copy(
            src_ref=r["obuf"].at[i, pl.ds(pl.multiple_of((1 - c) * rows, rows), rows)],
            dst_ref=r["attn_v"].at[:, pl.ds(at, 128)],
            send_sem=give_send.at[i],
            recv_sem=give_recv.at[i],
            device_id=ring.other,
            device_id_type=MESH,
        )

    def pair(i):
        at = pl.ds(i * 128, 128)

        def put(start, value):
            r["obuf"][i, pl.ds(start, value.shape[0]), :] = value
            r["heads"][pl.ds(start, value.shape[0]), i * 128 : (i + 1) * 128] = value

        self_fwd_pair(
            r["q_v"].at[:, at], r["k_v"].at[:, at], r["v_v"].at[:, at], r["lse"].at[pl.ds(i, 1)], put
        )
        keep(i).start()
        give(i).start()

    def self_out(w):
        def work(at):
            image = r["images_f"](at)
            y1 = image + mul(r["attn_v"][at, :], w[...])
            r["y1_v"][at, :] = y1
            r["h2_v"][at, :] = norm_fwd(y1, row(2), row(3)).astype(jnp.bfloat16)

        over(rows, work)

    def own_image(at):
        start = pl.multiple_of(c * rows + at.start, step)
        return r["both"][pl.ds(start, step), :].astype(jnp.float32)

    r["images_f"] = own_image

    def cross_query(w):
        def work(at):
            r["cq_v"][at, :] = mul(r["h2_v"][at, :], w[...]).astype(jnp.bfloat16)

        over(rows, work)

    def pick_caption():
        line = r["image_row"][0]
        r["cap_v"][0:64, :] = r["enc"][2 * line]
        r["cap_v"][64:128, :] = r["enc"][2 * line + 1]
        chosen = lax.broadcasted_iota(jnp.int32, (16, 128), 0) == line
        seg = jnp.sum(jnp.where(chosen, r["caption_seg"][...], 0), axis=0, keepdims=True)
        allowed = jnp.where(seg == r["image_seg"][0], 1.0, 0.0)
        wide = jnp.broadcast_to(allowed, (128, 128))
        r["ok"][0] = wide
        r["ok"][1] = wide.T

    def cross_out(w):
        def work(at):
            y2 = r["y1_v"][at, :] + mul(r["cattn_v"][at, :], w[...])
            r["y2_v"][at, :] = y2
            r["h3_v"][at, :] = norm_fwd(y2, row(4), row(5)).astype(jnp.bfloat16)

        over(rows, work)

    def cross():
        @pl.loop(0, 8)
        def _(i):
            at = pl.ds(pl.multiple_of(i * 128, 128), 128)
            cross_fwd_body(
                r["cq_v"].at[:, at],
                r["kv_v"].at[0, :, at],
                r["kv_v"].at[1, :, at],
                r["ok"].at[0],
                r["cattn_v"].at[:, at],
            )

    def back_outer(j, w):
        def work(at):
            r["dact"][at, j * 1024 : (j + 1) * 1024] = mul(r["gm_v"][at, :], w[...], NT)

        over(rows, work)

    def hidden(j, w):
        lanes = slice(j * 1024, (j + 1) * 1024)

        def work(at):
            u = mul(r["h3_v"][at, :], w[...]) + r["bin"][j : j + 1, :]
            act, slope = gelu_both(u)
            r["act_v"][at, lanes] = act.astype(jnp.bfloat16)
            du = (r["dact"][at, lanes] * slope).astype(jnp.bfloat16)
            r["du_v"][at, lanes] = du
            r["sums"][7 + j : 8 + j, :] += jnp.sum(du.astype(jnp.float32), axis=0, keepdims=True)

        over(rows, work)

    greet(ring.partners())
    for g in (3, 0, 1, 2):
        ring.start(g)
    keep_image.start()
    give_image.start()
    for g in range(3):
        ring.swapped(g)
    ring.start(4)
    load_gm.start()
    r["sums"][...] = jnp.zeros_like(r["sums"])
    slot(0)
    slot(1)
    slot(2)
    ring.ready(3)
    unpack()
    keep_image.wait()
    give_image.wait_recv()
    over(2 * rows, norm1)
    stores["h1"].start()
    slot(3)
    project(0)
    slot(4)
    project(1)
    slot(5)
    project(2)
    pair(0)
    slot(6)
    pair(1)
    ring.ready(4)
    weights[0].start()
    pair(2)
    pair(3)
    slot(7)
    for i in range(4):
        keep(i).wait()
        give(i).wait_recv()
    stores["attn"].start()
    self_out(weight(0))
    stores["y1"].start()
    stores["h2"].start()
    ring.ready(5)
    pick_caption()
    stores["caption"].start()
    slot(8)
    ring.ready(6)
    weights[1].start()
    cross_query(weight(1))
    stores["cq"].start()
    slot(9)
    ring.ready(7)
    weights[2].start()
    r["kv_v"][0] = mul(r["cap_v"][...], weight(2)[...]).astype(jnp.bfloat16)
    stores["ck"].start()
    slot(10)
    ring.ready(8)
    weights[3].start()
    r["kv_v"][1] = mul(r["cap_v"][...], weight(3)[...]).astype(jnp.bfloat16)
    stores["cv"].start()
    cross()
    stores["cattn"].start()
    slot(11)
    ring.ready(9)
    weights[4].start()
    cross_out(weight(4))
    stores["y2"].start()
    stores["h3"].start()
    load_gm.wait()
    r["sums"][6:7, :] = jnp.sum(r["gm_v"][...].astype(jnp.float32), axis=0, keepdims=True)
    slot(12)
    ring.ready(10)
    weights[5].start()
    weights[6].start()
    back_outer(0, weight(5))
    weights[7].start()
    back_outer(1, weight(6))
    weights[8].start()
    slot(13)
    back_outer(2, weight(7))
    ring.ready(11)
    weights[9].start()
    back_outer(3, weight(8))
    for j in range(4):
        if j < 3:
            slot(14 + j)
        hidden(j, weight(9 + j))
        if j < 3:
            ring.ready(12 + j)
            weights[10 + j].start()
    stores["act"].start()
    stores["du"].start()
    for g in range(n):
        ring.sent(g)
    give_image.wait_send()
    for i in range(4):
        give(i).wait_send()
    for store in stores.values():
        store.wait()


def front(operands, collective_id):
    bf, f32, vm, shape = jnp.bfloat16, jnp.float32, pltpu.VMEM, jax.ShapeDtypeStruct
    square, rows, head = (1024, 1024), (512, 1024), (1024, 512)
    inside = pl.BlockSpec(memory_space=pltpu.VMEM)
    scalar = pl.BlockSpec(memory_space=pltpu.SMEM)
    outs = (
        [shape(head, bf)] * 3
        + [shape(square, bf)] * 5
        + [shape((4096, 1024), bf), shape((1024, 4096), bf), shape(square, bf)]
        + [shape(head, bf)] * 4
        + [shape(rows, bf), shape(rows, f32), shape(rows, bf), shape(rows, bf)]
        + [shape((128, 1024), bf)] * 3
        + [shape(rows, bf), shape(rows, f32), shape(rows, bf)]
        + [shape((512, 4096), bf)] * 2
        + [shape((4, 2, 1024), f32), shape((16, 1024), f32), shape((2, 128, 128), f32)]
        + [shape((16, 1024), f32)]
    )
    places = [ANY] * 14 + [inside] + [ANY] * 12 + [inside] * 4
    n = 15
    return pl.pallas_call(
        front_body,
        out_shape=outs,
        in_specs=[ANY] * 14 + [inside, scalar, scalar],
        out_specs=places,
        scratch_shapes=[
            vm((512, 128), f32),
            vm((32, 64, 1024), bf),
            vm(square, bf),
            vm((3, 1024, 512), bf),
            vm(square, bf),
            vm(head, bf),
            vm(head, bf),
            vm(head, bf),
            vm((4, 1024, 128), bf),
            vm(rows, bf),
            vm(rows, f32),
            vm(rows, bf),
            vm(rows, bf),
            vm((2, 128, 1024), bf),
            vm((128, 1024), bf),
            vm(rows, bf),
            vm(rows, f32),
            vm(rows, bf),
            vm(rows, bf),
            vm((512, 4096), f32),
            vm((512, 4096), bf),
            vm((512, 4096), bf),
            vm((2, 1024, 1024), bf),
            vm((4, 1024), f32),
            pltpu.SemaphoreType.DMA((n, 31)),
            pltpu.SemaphoreType.DMA((n, 31)),
            pltpu.SemaphoreType.DMA((n,)),
            pltpu.SemaphoreType.DMA((3,)),
            pltpu.SemaphoreType.DMA((4,)),
            pltpu.SemaphoreType.DMA((4,)),
            pltpu.SemaphoreType.DMA((4,)),
            pltpu.SemaphoreType.DMA((2,)),
            pltpu.SemaphoreType.DMA((19,)),
            pltpu.SemaphoreType.DMA,
        ],
        compiler_params=pltpu.CompilerParams(
            collective_id=collective_id,
            has_side_effects=True,
            vmem_limit_bytes=59 * 1024 * 1024,
        ),
        name="front",
    )(*operands)


HEADS = 16
HEAD_DIM = 64


EPSILON = 1e-05
NEG_BIG = -1e30


def norm_rows(value, gain, shift):
    center = value - jnp.mean(value, axis=-1, keepdims=True)
    spread = jnp.mean(center * center, axis=-1, keepdims=True)
    return center * lax.rsqrt(spread + EPSILON) * gain + shift


def project(rows, weight):
    return jnp.einsum("bsd,de->bse", rows, weight, preferred_element_type=jnp.float32)


def project_back(grads, weight):
    return jnp.einsum("bse,de->bsd", grads, weight, preferred_element_type=jnp.float32)


def weight_grad(rows, grads):
    return jnp.einsum("bsd,bse->de", rows, grads, preferred_element_type=jnp.float32)


def row_total(grads):
    return jnp.sum(grads.astype(jnp.float32), axis=(0, 1))


def split_heads(value):
    return value.reshape(value.shape[0], value.shape[1], HEADS, HEAD_DIM)


def join_heads(value):
    return value.reshape(value.shape[0], value.shape[1], HEADS * HEAD_DIM)


def scores_of(queries, keys_in, allowed):
    raw_scores = (
        jnp.einsum(
            "bqhd,bkhd->bhqk",
            split_heads(queries),
            split_heads(keys_in),
            preferred_element_type=jnp.float32,
        )
        * 0.125
    )
    return jnp.where(allowed, raw_scores, NEG_BIG)


def attend(queries, keys_in, values_in, allowed):
    scores = scores_of(queries, keys_in, allowed)
    row_max = jnp.max(scores, axis=-1, keepdims=True)
    exponent = jnp.exp(scores - row_max)
    total = jnp.sum(exponent, axis=-1, keepdims=True)
    attn_weights = exponent / total
    mixed_rows = jnp.einsum(
        "bhqk,bkhd->bqhd",
        attn_weights.astype(jnp.bfloat16),
        split_heads(values_in),
        preferred_element_type=jnp.float32,
    )
    return (join_heads(mixed_rows).astype(jnp.bfloat16), row_max + jnp.log(total))


def attend_back(queries, keys_in, values_in, allowed, log_total, grad_mixed):
    attn_weights = jnp.exp(scores_of(queries, keys_in, allowed) - log_total)
    grad_heads = split_heads(grad_mixed)
    grad_weights = jnp.einsum(
        "bqhd,bkhd->bhqk", grad_heads, split_heads(values_in), preferred_element_type=jnp.float32
    )
    grad_values = jnp.einsum(
        "bhqk,bqhd->bkhd",
        attn_weights.astype(jnp.bfloat16),
        grad_heads,
        preferred_element_type=jnp.float32,
    )
    inner_sum = jnp.sum(grad_weights * attn_weights, axis=-1, keepdims=True)
    grad_scores = (attn_weights * (grad_weights - inner_sum)).astype(jnp.bfloat16)
    grad_queries = (
        jnp.einsum(
            "bhqk,bkhd->bqhd", grad_scores, split_heads(keys_in), preferred_element_type=jnp.float32
        )
        * 0.125
    )
    grad_keys = (
        jnp.einsum(
            "bhqk,bqhd->bkhd", grad_scores, split_heads(queries), preferred_element_type=jnp.float32
        )
        * 0.125
    )
    return (join_heads(grad_queries), join_heads(grad_keys), join_heads(grad_values))


def per_device(
    images,
    encoder_states,
    image_row,
    image_seg,
    caption_seg,
    ln1_gain,
    ln1_bias,
    w_query,
    w_key,
    w_value,
    w_out,
    ln2_gain,
    ln2_bias,
    c_query,
    c_key,
    c_value,
    c_out,
    ln3_gain,
    ln3_bias,
    w_in,
    b_in,
    w_outer,
    b_outer,
    cotangent,
):
    mixing = (
        lax.all_gather(ln1_gain, ("dp", "seq"), axis=0, tiled=True),
        lax.all_gather(ln1_bias, ("dp", "seq"), axis=0, tiled=True),
        lax.all_gather(w_query, ("dp", "seq"), axis=0, tiled=True),
        lax.all_gather(w_key, ("dp", "seq"), axis=0, tiled=True),
        lax.all_gather(w_value, ("dp", "seq"), axis=0, tiled=True),
        lax.all_gather(w_out, ("dp", "seq"), axis=0, tiled=True),
        lax.all_gather(ln2_gain, ("dp", "seq"), axis=0, tiled=True),
        lax.all_gather(ln2_bias, ("dp", "seq"), axis=0, tiled=True),
        lax.all_gather(c_query, ("dp", "seq"), axis=0, tiled=True),
        lax.all_gather(c_key, ("dp", "seq"), axis=0, tiled=True),
        lax.all_gather(c_value, ("dp", "seq"), axis=0, tiled=True),
        lax.all_gather(c_out, ("dp", "seq"), axis=0, tiled=True),
    )
    (
        gain_a,
        bias_a,
        query_w,
        key_w,
        value_w,
        out_w,
        gain_b,
        bias_b,
        cross_qw,
        cross_kw,
        cross_vw,
        cross_ow,
    ) = mixing
    shard = images.shape[1]
    seq_index = lax.axis_index("seq")
    full_len = shard * lax.axis_size("seq")
    inputs_f = images.astype(jnp.float32)
    gain_a32, bias_a32 = (gain_a.astype(jnp.float32), bias_a.astype(jnp.float32))
    normed_a = norm_rows(inputs_f, gain_a32, bias_a32).astype(jnp.bfloat16)
    queries = project(normed_a, query_w).astype(jnp.bfloat16)
    keys_local = project(normed_a, key_w).astype(jnp.bfloat16)
    values_local = project(normed_a, value_w).astype(jnp.bfloat16)
    keys_all, values_all = (
        lax.all_gather(keys_local, "seq", axis=1, tiled=True),
        lax.all_gather(values_local, "seq", axis=1, tiled=True),
    )
    query_pos = seq_index * shard + jnp.arange(shard, dtype=jnp.int32)
    key_pos = jnp.arange(full_len, dtype=jnp.int32)
    causal = (key_pos[None, :] <= query_pos[:, None])[None, None]
    self_out, self_lse = attend(queries, keys_all, values_all, causal)
    after_self = inputs_f + project(self_out, out_w)
    gain_b32, bias_b32 = (gain_b.astype(jnp.float32), bias_b.astype(jnp.float32))
    normed_b = norm_rows(after_self, gain_b32, bias_b32).astype(jnp.bfloat16)
    cross_queries = project(normed_b, cross_qw).astype(jnp.bfloat16)
    encoder_all = lax.all_gather(encoder_states, "dp", axis=0, tiled=True)
    caption = jnp.take(encoder_all, image_row, axis=0)
    cross_keys = project(caption, cross_kw).astype(jnp.bfloat16)
    cross_values = project(caption, cross_vw).astype(jnp.bfloat16)
    caption_mask = (jnp.take(caption_seg, image_row, axis=0) == image_seg[:, None])[
        :, None, None, :
    ]
    cross_out, cross_lse = attend(cross_queries, cross_keys, cross_values, caption_mask)
    after_cross = after_self + project(cross_out, cross_ow)
    feed_weights = (
        lax.all_gather(ln3_gain, ("dp", "seq"), axis=0, tiled=True),
        lax.all_gather(ln3_bias, ("dp", "seq"), axis=0, tiled=True),
        lax.all_gather(w_in, ("dp", "seq"), axis=0, tiled=True),
        lax.all_gather(b_in, ("dp", "seq"), axis=0, tiled=True),
        lax.all_gather(w_outer, ("dp", "seq"), axis=0, tiled=True),
        lax.all_gather(b_outer, ("dp", "seq"), axis=0, tiled=True),
    )
    gain_c, bias_c, inner_w, inner_b, outer_w, outer_b = feed_weights
    gain_c32, bias_c32 = (gain_c.astype(jnp.float32), bias_c.astype(jnp.float32))
    normed_c = norm_rows(after_cross, gain_c32, bias_c32).astype(jnp.bfloat16)
    hidden_pre = project(normed_c, inner_w) + inner_b.astype(jnp.float32)
    activated = jax.nn.gelu(hidden_pre).astype(jnp.bfloat16)
    result = after_cross + project(activated, outer_w) + outer_b.astype(jnp.float32)
    block_out = result.astype(jnp.bfloat16)
    inner_wb, outer_wb = (feed_weights[2], feed_weights[4])
    grad_result = cotangent.astype(jnp.float32)
    grad_outer_w = weight_grad(activated, cotangent)
    grad_outer_b = row_total(cotangent)
    grad_act = project_back(cotangent, outer_wb)
    _, gelu_back = jax.vjp(jax.nn.gelu, hidden_pre)
    grad_hidden = gelu_back(grad_act)[0].astype(jnp.bfloat16)
    grad_inner_w = weight_grad(normed_c, grad_hidden)
    grad_inner_b = row_total(grad_hidden)
    grad_normed_c = project_back(grad_hidden, inner_wb)
    _, norm_c_back = jax.vjp(norm_rows, after_cross, gain_c32, bias_c32)
    grad_cross_part, grad_gain_c, grad_bias_c = norm_c_back(grad_normed_c)
    grad_after_cross = grad_result + grad_cross_part
    feed_sums = (
        lax.psum_scatter(grad_gain_c, ("dp", "seq"), scatter_dimension=0, tiled=True),
        lax.psum_scatter(grad_bias_c, ("dp", "seq"), scatter_dimension=0, tiled=True),
        lax.psum_scatter(grad_inner_w, ("dp", "seq"), scatter_dimension=0, tiled=True),
        lax.psum_scatter(grad_inner_b, ("dp", "seq"), scatter_dimension=0, tiled=True),
        lax.psum_scatter(grad_outer_w, ("dp", "seq"), scatter_dimension=0, tiled=True),
        lax.psum_scatter(grad_outer_b, ("dp", "seq"), scatter_dimension=0, tiled=True),
    )
    query_wb, key_wb, value_wb, out_wb = (mixing[2], mixing[3], mixing[4], mixing[5])
    cross_qwb, cross_kwb, cross_vwb, cross_owb = (mixing[8], mixing[9], mixing[10], mixing[11])
    grad_branch_b = grad_after_cross.astype(jnp.bfloat16)
    grad_cross_ow = weight_grad(cross_out, grad_branch_b)
    grad_cross_out = project_back(grad_branch_b, cross_owb).astype(jnp.bfloat16)
    grad_cq_raw, grad_ck_raw, grad_cv_raw = attend_back(
        cross_queries, cross_keys, cross_values, caption_mask, cross_lse, grad_cross_out
    )
    grad_cross_q = grad_cq_raw.astype(jnp.bfloat16)
    grad_ck_sum, grad_cv_sum = (
        lax.psum_scatter(
            grad_ck_raw.astype(jnp.bfloat16), "seq", scatter_dimension=1, tiled=True
        ).astype(jnp.float32),
        lax.psum_scatter(
            grad_cv_raw.astype(jnp.bfloat16), "seq", scatter_dimension=1, tiled=True
        ).astype(jnp.float32),
    )
    grad_ck_low = grad_ck_sum.astype(jnp.bfloat16)
    grad_cv_low = grad_cv_sum.astype(jnp.bfloat16)
    piece_len = grad_ck_sum.shape[1]
    caption_piece = lax.dynamic_slice_in_dim(caption, seq_index * piece_len, piece_len, 1)
    grad_cross_kw = weight_grad(caption_piece, grad_ck_low)
    grad_cross_vw = weight_grad(caption_piece, grad_cv_low)
    grad_caption = project_back(grad_ck_low, cross_kwb) + project_back(grad_cv_low, cross_vwb)
    row_count = encoder_all.shape[0]
    row_onehot = (image_row[:, None] == jnp.arange(row_count, dtype=jnp.int32)[None, :]).astype(
        jnp.float32
    )
    grad_rows = jnp.einsum("br,bsd->rsd", row_onehot, grad_caption, precision=lax.Precision.HIGHEST)
    caption_grad = lax.psum_scatter(
        grad_rows.astype(jnp.bfloat16), "dp", scatter_dimension=0, tiled=True
    ).astype(jnp.float32)
    grad_cross_qw = weight_grad(normed_b, grad_cross_q)
    grad_normed_b = project_back(grad_cross_q, cross_qwb)
    _, norm_b_back = jax.vjp(norm_rows, after_self, gain_b32, bias_b32)
    grad_self_part, grad_gain_b, grad_bias_b = norm_b_back(grad_normed_b)
    grad_after_self = grad_after_cross + grad_self_part
    grad_branch_a = grad_after_self.astype(jnp.bfloat16)
    grad_out_w = weight_grad(self_out, grad_branch_a)
    grad_self_out = project_back(grad_branch_a, out_wb).astype(jnp.bfloat16)
    keys_back, values_back = (keys_all, values_all)
    grad_q_raw, grad_k_raw, grad_v_raw = attend_back(
        queries, keys_back, values_back, causal, self_lse, grad_self_out
    )
    grad_k_sum, grad_v_sum = (
        lax.psum_scatter(
            grad_k_raw.astype(jnp.bfloat16), "seq", scatter_dimension=1, tiled=True
        ).astype(jnp.float32),
        lax.psum_scatter(
            grad_v_raw.astype(jnp.bfloat16), "seq", scatter_dimension=1, tiled=True
        ).astype(jnp.float32),
    )
    grad_q_low = grad_q_raw.astype(jnp.bfloat16)
    grad_k_low = grad_k_sum.astype(jnp.bfloat16)
    grad_v_low = grad_v_sum.astype(jnp.bfloat16)
    grad_query_w = weight_grad(normed_a, grad_q_low)
    grad_key_w = weight_grad(normed_a, grad_k_low)
    grad_value_w = weight_grad(normed_a, grad_v_low)
    grad_normed_a = (
        project_back(grad_q_low, query_wb)
        + project_back(grad_k_low, key_wb)
        + project_back(grad_v_low, value_wb)
    )
    _, norm_a_back = jax.vjp(norm_rows, inputs_f, gain_a32, bias_a32)
    grad_input_part, grad_gain_a, grad_bias_a = norm_a_back(grad_normed_a)
    image_grad = grad_after_self + grad_input_part
    mix_sums = (
        lax.psum_scatter(grad_gain_a, ("dp", "seq"), scatter_dimension=0, tiled=True),
        lax.psum_scatter(grad_bias_a, ("dp", "seq"), scatter_dimension=0, tiled=True),
        lax.psum_scatter(grad_query_w, ("dp", "seq"), scatter_dimension=0, tiled=True),
        lax.psum_scatter(grad_key_w, ("dp", "seq"), scatter_dimension=0, tiled=True),
        lax.psum_scatter(grad_value_w, ("dp", "seq"), scatter_dimension=0, tiled=True),
        lax.psum_scatter(grad_out_w, ("dp", "seq"), scatter_dimension=0, tiled=True),
        lax.psum_scatter(grad_gain_b, ("dp", "seq"), scatter_dimension=0, tiled=True),
        lax.psum_scatter(grad_bias_b, ("dp", "seq"), scatter_dimension=0, tiled=True),
        lax.psum_scatter(grad_cross_qw, ("dp", "seq"), scatter_dimension=0, tiled=True),
        lax.psum_scatter(grad_cross_kw, ("dp", "seq"), scatter_dimension=0, tiled=True),
        lax.psum_scatter(grad_cross_vw, ("dp", "seq"), scatter_dimension=0, tiled=True),
        lax.psum_scatter(grad_cross_ow, ("dp", "seq"), scatter_dimension=0, tiled=True),
    )
    return (
        block_out,
        image_grad,
        caption_grad,
        mix_sums[0],
        mix_sums[1],
        mix_sums[2],
        mix_sums[3],
        mix_sums[4],
        mix_sums[5],
        mix_sums[6],
        mix_sums[7],
        mix_sums[8],
        mix_sums[9],
        mix_sums[10],
        mix_sums[11],
        feed_sums[0],
        feed_sums[1],
        feed_sums[2],
        feed_sums[3],
        feed_sums[4],
        feed_sums[5],
    )


def block_device(
    images,
    encoder_states,
    image_row,
    image_seg,
    caption_seg,
    ln1_gain,
    ln1_bias,
    w_query,
    w_key,
    w_value,
    w_out,
    ln2_gain,
    ln2_bias,
    c_query,
    c_key,
    c_value,
    c_out,
    ln3_gain,
    ln3_bias,
    w_in,
    b_in,
    w_outer,
    b_outer,
    cotangent,
):
    core = lax.axis_index("seq")
    index = 2 * lax.axis_index("dp") + core
    width = images.shape[2]
    vectors = (ln1_gain, ln1_bias, ln2_gain, ln2_bias, ln3_gain, ln3_bias, b_outer)
    lanes, hidden_lanes = b_outer.shape[0], b_in.shape[0]
    stack = jnp.tile(jnp.stack(vectors).astype(jnp.float32), (1, 128 // lanes))
    place_of = jnp.arange(128, dtype=jnp.int32) // lanes == index % (128 // lanes)
    packed = jnp.concatenate(
        [
            jnp.where(place_of[None], stack, 0.0),
            b_in.astype(jnp.float32)[None],
            jnp.zeros((8, 128), jnp.float32),
        ]
    )
    o = dict(
        zip(
            FRONT_OUT,
            front(
                [
                    w_query,
                    w_key,
                    w_value,
                    packed,
                    w_out,
                    encoder_states,
                    c_query,
                    c_key,
                    c_value,
                    c_out,
                    w_outer,
                    w_in,
                    images[0],
                    cotangent[0],
                    caption_seg,
                    image_row,
                    image_seg,
                ],
                1,
            ),
        )
    )
    (
        grad_inner_w,
        grad_outer_w,
        sums,
        grad_caption,
        block_out,
        grad_branch_b,
        grad_cross_q,
        grad_ck,
        grad_cv,
        grad_branch_a,
        grad_after_self,
        grad_self_out,
    ) = middle(
        [o["h3"], o["du"], o["act"], cotangent[0], o["w_in_all"], o["w_outer_all"]]
        + [o["c_out_all"], o["c_query_all"], o["w_out_all"], o["y2"], o["y1"]]
        + [o["cq"], o["ck"], o["cv"], o["c_key_all"], o["c_value_all"]]
        + [o["ok"], o["vec"], o["sums"]],
        2,
    )
    image_grad, *big, total = scatter_tail(
        [o["q"], o["k"], o["v"], o["heads"], o["lse"], grad_self_out, o["h1"], o["attn"]]
        + [grad_branch_a, o["h2"], grad_cross_q, o["cattn"], grad_branch_b, o["caption"]]
        + [grad_ck, grad_cv, o["wq"], o["wk"], o["wv"], images[0], grad_after_self, o["vec"], sums]
        + [grad_caption, jnp.broadcast_to(image_row.astype(jnp.float32)[:, None], (8, width))],
        4,
    )
    cut = lax.dynamic_slice_in_dim(total, index * lanes, lanes, 1)
    per_row = width // hidden_lanes
    at = (7 + index // per_row, index % per_row * hidden_lanes)
    inner_cut = lax.dynamic_slice(total, at, (1, hidden_lanes))[0]
    return (
        block_out[None],
        image_grad[None],
        big[5][None],
        cut[0],
        cut[1],
        big[6],
        big[7],
        big[8],
        big[0],
        cut[2],
        cut[3],
        big[1],
        big[3],
        big[4],
        big[2],
        cut[4],
        cut[5],
        grad_inner_w,
        inner_cut,
        grad_outer_w,
        cut[6],
    )


def solution(mesh):
    in_specs = (
        P("dp", "seq", None),
        P("dp", None, None),
        P("dp"),
        P("dp"),
        P(),
        P(("dp", "seq")),
        P(("dp", "seq")),
        P(("dp", "seq"), None),
        P(("dp", "seq"), None),
        P(("dp", "seq"), None),
        P(("dp", "seq"), None),
        P(("dp", "seq")),
        P(("dp", "seq")),
        P(("dp", "seq"), None),
        P(("dp", "seq"), None),
        P(("dp", "seq"), None),
        P(("dp", "seq"), None),
        P(("dp", "seq")),
        P(("dp", "seq")),
        P(("dp", "seq"), None),
        P(("dp", "seq")),
        P(("dp", "seq"), None),
        P(("dp", "seq")),
        P("dp", "seq", None),
    )
    out_specs = (
        P("dp", "seq", None),
        P("dp", "seq", None),
        P("dp", "seq", None),
        P(("dp", "seq")),
        P(("dp", "seq")),
        P(("dp", "seq"), None),
        P(("dp", "seq"), None),
        P(("dp", "seq"), None),
        P(("dp", "seq"), None),
        P(("dp", "seq")),
        P(("dp", "seq")),
        P(("dp", "seq"), None),
        P(("dp", "seq"), None),
        P(("dp", "seq"), None),
        P(("dp", "seq"), None),
        P(("dp", "seq")),
        P(("dp", "seq")),
        P(("dp", "seq"), None),
        P(("dp", "seq")),
        P(("dp", "seq"), None),
        P(("dp", "seq")),
    )
    kernels = mesh.shape["dp"] == 16 and mesh.shape["seq"] == 2
    return jax.shard_map(
        block_device if kernels else per_device,
        mesh=mesh,
        in_specs=in_specs,
        out_specs=out_specs,
        check_vma=False,
    )
```

```python
import functools

import jax
import jax.numpy as jnp
from jax import lax
from jax.experimental import pallas as pl
from jax.experimental.pallas import tpu as pltpu
from jax.sharding import PartitionSpec as P

MESH = pl.DeviceIdType.MESH
ANY = pl.BlockSpec(memory_space=pl.ANY)


def place():
    dp, c = lax.axis_index("dp"), lax.axis_index("seq")
    x, y, z = dp % 2, (dp // 2) % 2, dp // 4
    return z, y, x, c


def flip(bit, on):
    return bit + on * (1 - 2 * bit)


def zxor(z, k):
    if k == 0:
        return z
    if k == 1:
        return z + 1 - 2 * (z % 2)
    if k == 2:
        return z + 2 - 4 * (z // 2)
    return 3 - z


def chip(z, y, x):
    return z * 4 + y * 2 + x


def greet(partners):
    barrier = pltpu.get_barrier_semaphore()
    for partner in partners:
        pl.semaphore_signal(barrier, inc=1, device_id=partner, device_id_type=MESH)
    pl.semaphore_wait(barrier, len(partners))


class Gather:
    def __init__(self, split, own, full, send_sem, recv_sem, local_sem):
        self.split, self.own, self.full = split, own, full
        self.send_sem, self.recv_sem, self.local_sem = send_sem, recv_sem, local_sem
        z, y, x, c = place()
        self.z, self.y, self.x, self.c = z, y, x, c
        self.yx = {
            (0, 0): (y, x),
            (1, 0): (flip(y, 1 - c), flip(x, c)),
            (0, 1): (flip(y, c), flip(x, 1 - c)),
            (1, 1): (1 - y, 1 - x),
        }
        self.other = (chip(z, y, x), 1 - c)

    def partners(self):
        z, c = self.z, self.c
        return [(chip(zxor(z, k), self.y, self.x), c) for k in (1, 2, 3)] + [
            (chip(z, *self.yx[1, 0]), c),
            (chip(z, *self.yx[0, 1]), c),
            self.other,
        ]

    def block(self, g, k, way, core):
        rows = self.own[g].shape[0]
        r = chip(zxor(self.z, k), *self.yx[way])
        if g < self.split:
            return self.full[g].at[pl.ds(pl.multiple_of(2 * r * rows, rows), 2 * rows)]
        return self.full[g].at[pl.ds(pl.multiple_of((2 * r + core) * rows, rows), rows)]

    def remote(self, g, src, dst, to, idx):
        return pltpu.make_async_remote_copy(
            src_ref=src,
            dst_ref=dst,
            send_sem=self.send_sem.at[g, idx],
            recv_sem=self.recv_sem.at[g, idx],
            device_id=to,
            device_id_type=MESH,
        )

    def copy(self, g, src, k, way, core, to, idx):
        return self.remote(g, src, self.block(g, k, way, core), to, idx)

    def forward(self, g, k, way, src=None):
        z, c = self.z, self.c
        src = self.block(g, k, way, c) if src is None else src
        i1, i2 = way
        sends = []
        if i1 == 0 and i2 == 0:
            sends.append(((chip(z, *self.yx[1, 0]), c), 3 + k))
        if i2 == 0:
            sends.append(((chip(z, *self.yx[0, 1]), c), 7 + i1 * 4 + k))
        if g >= self.split:
            sends.append((self.other, 15 + i2 * 8 + i1 * 4 + k))
        for to, idx in sends:
            self.copy(g, src, k, way, c, to, idx).start()

    def half(self, g, core):
        rows, columns = self.own[g].shape
        columns //= 2
        at = pl.multiple_of((2 * chip(self.z, self.y, self.x) + self.c) * rows, rows)
        return (
            self.own[g].at[:, pl.ds(pl.multiple_of(core * columns, columns), columns)],
            self.full[g].at[pl.ds(at, rows)],
        )

    def keep(self, g):
        if g < self.split:
            src, dst = self.half(g, self.c)
        else:
            src, dst = self.own[g], self.block(g, 0, (0, 0), self.c)
        return pltpu.make_async_copy(src, dst, self.local_sem.at[g])

    def swap(self, g):
        src, dst = self.half(g, 1 - self.c)
        return self.remote(g, src, dst, self.other, 15)

    def start(self, g):
        self.keep(g).start()
        if g < self.split:
            self.swap(g).start()
        else:
            self.begin(g, self.own[g])

    def swapped(self, g):
        self.swap(g).wait_recv()
        self.keep(g).wait()
        self.begin(g, self.block(g, 0, (0, 0), self.c))

    def begin(self, g, src):
        for k in (1, 2, 3):
            to = (chip(zxor(self.z, k), self.y, self.x), self.c)
            self.copy(g, src, 0, (0, 0), self.c, to, k - 1).start()
        self.forward(g, 0, (0, 0), src)

    def arrive(self, g, k, way, core, idx):
        block = self.block(g, k, way, core)
        self.remote(g, block, block, self.other, idx).wait_recv()

    def along_z(self, g):
        for k in (1, 2, 3):
            self.arrive(g, k, (0, 0), self.c, k - 1)
            self.forward(g, k, (0, 0))

    def first(self, g):
        for k in range(4):
            self.arrive(g, k, (1, 0), self.c, 3 + k)
            self.forward(g, k, (1, 0))

    def second(self, g):
        for i1 in range(2):
            for k in range(4):
                self.arrive(g, k, (i1, 1), self.c, 7 + i1 * 4 + k)
                self.forward(g, k, (i1, 1))

    def ready(self, g):
        if g >= self.split:
            for i2 in range(2):
                for i1 in range(2):
                    for k in range(4):
                        self.arrive(g, k, (i2, i1), 1 - self.c, 15 + i2 * 8 + i1 * 4 + k)
            self.keep(g).wait()

    def sent(self, g):
        if g < self.split:
            self.swap(g).wait_send()
        block = self.block(g, 0, (0, 0), self.c)
        for idx in range(15 if g < self.split else 31):
            self.remote(g, block, block, self.other, idx).wait_send()


AHEAD = 4


NT = (((1,), (1,)), ((), ()))
TN = (((0,), (0,)), ((), ()))
NN = (((1,), (0,)), ((), ()))


def mul(a, b, dims=NN):
    return lax.dot_general(a, b, dims, preferred_element_type=jnp.float32)


def low_lanes(rows):
    return lax.broadcasted_iota(jnp.int32, (rows, 128), 1) < 64


def self_fwd_pair(q_ref, k_ref, v_ref, lse_ref, put):
    length, b = q_ref.shape[0], 256
    low = low_lanes(b)
    row = lax.broadcasted_iota(jnp.int32, (b, b), 0)
    col = lax.broadcasted_iota(jnp.int32, (b, b), 1)
    for n in range(b, length + 1, b):
        q = q_ref[n - b : n, :] * jnp.asarray(0.125, jnp.bfloat16)
        mixed, lses = [], []
        for mine in (low, ~low):
            s = mul(jnp.where(mine, q, jnp.zeros_like(q)), k_ref[0:n, :], NT)
            last = jnp.where(col <= row, s[:, n - b :], NEG_BIG)
            s = jnp.concatenate([s[:, : n - b], last], axis=1) if n > b else last
            top = jnp.max(s, axis=1, keepdims=True)
            e = jnp.exp(s - top)
            total = jnp.sum(e, axis=1, keepdims=True)
            mixed.append(mul(e.astype(jnp.bfloat16), v_ref[0:n, :]) / total)
            lses.append(jnp.broadcast_to(top + jnp.log(total), (b, 128)))
        put(n - b, jnp.where(low, mixed[0], mixed[1]).astype(jnp.bfloat16))
        turned = jnp.where(low, lses[0], lses[1]).T
        lse_ref[0, :, n - b : n] = jnp.concatenate([turned[0:1], turned[64:65]], axis=0)


def self_bwd_pair(q_ref, k_ref, v_ref, o_ref, do_ref, lse_ref, dq_ref, dk_ref, dv_ref, acc):
    length, b = q_ref.shape[0], 256
    low = low_lanes(b)
    row = lax.broadcasted_iota(jnp.int32, (b, b), 0)
    col = lax.broadcasted_iota(jnp.int32, (b, b), 1)
    prod = do_ref[...].astype(jnp.float32) * o_ref[...].astype(jnp.float32)
    lane = lax.broadcasted_iota(jnp.int32, (8, 128), 1)
    head = lax.broadcasted_iota(jnp.int32, (8, 128), 0)
    pick = jnp.where(lane // 64 == head, 1.0, 0.0)
    inner = lax.dot_general(
        pick, prod, NT, precision=lax.Precision.HIGHEST, preferred_element_type=jnp.float32
    )
    acc[...] = jnp.zeros_like(acc)
    for at in range(0, length, b):
        k, v = k_ref[at : at + b, :], v_ref[at : at + b, :]
        qs, dos = q_ref[at:length, :], do_ref[at:length, :]
        dks, dvs = [], []
        for h, mine in enumerate((low, ~low)):
            km = jnp.where(mine, k, jnp.zeros_like(k))
            vm = jnp.where(mine, v, jnp.zeros_like(v))
            s = mul(km * jnp.asarray(0.125, jnp.bfloat16), qs, NT)
            w = jnp.exp(s - lse_ref[0, h : h + 1, at:length])
            first = jnp.where(row <= col, w[:, :b], 0.0)
            w = jnp.concatenate([first, w[:, b:]], axis=1) if length - at > b else first
            ds = (w * (mul(vm, dos, NT) - inner[h : h + 1, at:length])).astype(jnp.bfloat16)
            dvs.append(mul(w.astype(jnp.bfloat16), dos))
            dks.append(mul(ds, qs))
            acc[at:length, :] += mul(ds, km, TN)
        dk_ref[at : at + b, :] = (jnp.where(low, dks[0], dks[1]) * 0.125).astype(jnp.bfloat16)
        dv_ref[at : at + b, :] = jnp.where(low, dvs[0], dvs[1]).astype(jnp.bfloat16)
    dq_ref[...] = (acc[...] * 0.125).astype(jnp.bfloat16)


def cross_fwd_body(q_ref, k_ref, v_ref, ok_ref, o_ref):
    low = low_lanes(q_ref.shape[0])
    q = q_ref[...] * jnp.asarray(0.125, jnp.bfloat16)
    mixed = []
    for mine in (low, ~low):
        s = mul(jnp.where(mine, q, jnp.zeros_like(q)), k_ref[...], NT)
        s = jnp.where(ok_ref[0:1, :] > 0, s, NEG_BIG)
        e = jnp.exp(s - jnp.max(s, axis=1, keepdims=True))
        total = jnp.sum(e, axis=1, keepdims=True)
        mixed.append(mul(e.astype(jnp.bfloat16), v_ref[...]) / total)
    o_ref[...] = jnp.where(low, mixed[0], mixed[1]).astype(jnp.bfloat16)


def cross_bwd_body(q_ref, k_ref, v_ref, ok_ref, do_ref, dq_ref, dk_ref, dv_ref):
    keys = k_ref.shape[0]
    low = low_lanes(keys)
    wide = low_lanes(q_ref.shape[0])
    q, do, k, v = q_ref[...], do_ref[...], k_ref[...], v_ref[...]
    dqs, dks, dvs = [], [], []
    for mine in (low, ~low):
        km = jnp.where(mine, k, jnp.zeros_like(k))
        vm = jnp.where(mine, v, jnp.zeros_like(v))
        s = mul(km * jnp.asarray(0.125, jnp.bfloat16), q, NT)
        s = jnp.where(ok_ref[:, 0:1] > 0, s, NEG_BIG)
        e = jnp.exp(s - jnp.max(s, axis=0, keepdims=True))
        w = e / jnp.sum(e, axis=0, keepdims=True)
        dw = mul(vm, do, NT)
        inner = jnp.sum(dw * w, axis=0, keepdims=True)
        ds = (w * (dw - inner)).astype(jnp.bfloat16)
        dvs.append(mul(w.astype(jnp.bfloat16), do))
        dks.append(mul(ds, q))
        dqs.append(mul(ds, km, TN))
    dq_ref[...] = (jnp.where(wide, dqs[0], dqs[1]) * 0.125).astype(jnp.bfloat16)
    dk_ref[...] = (jnp.where(low, dks[0], dks[1]) * 0.125).astype(jnp.bfloat16)
    dv_ref[...] = jnp.where(low, dvs[0], dvs[1]).astype(jnp.bfloat16)


class Scatter:
    def __init__(self, late, tile, got, part, from_late, out, sems, credit):
        self.late, self.tile, self.got = late, tile, got
        self.slots, self.count, self.free = credit
        self.part, self.from_late, self.out = part, from_late, out
        self.send_sem, self.recv_sem = sems
        z, y, x, c = place()
        self.z, self.y, self.x, self.c = z, y, x, c
        self.other = (chip(z, y, x), 1 - c)

    def ways(self, core):
        y, x = self.y, self.x
        return [
            flip(y, core * i1 + (1 - core) * i2) * 2 + flip(x, (1 - core) * i1 + core * i2)
            for i1 in range(2)
            for i2 in range(2)
        ]

    def partners(self):
        z, c = self.z, self.c
        way = self.ways(c)
        return [(zxor(z, k) * 4 + way[0], c) for k in (1, 2, 3)] + [
            (z * 4 + way[2], c),
            (z * 4 + way[1], c),
            self.other,
        ]

    def mine(self, u, j):
        way = self.ways(self.c)[j]
        return self.tile(u).at[:, way] if self.late(u) else self.tile(u).at[:, way, self.c]

    def remote(self, src, dst, u, idx, to):
        return pltpu.make_async_remote_copy(
            src_ref=src,
            dst_ref=dst,
            send_sem=self.send_sem.at[u, idx],
            recv_sem=self.recv_sem.at[u, idx],
            device_id=to,
            device_id_type=MESH,
        )

    def to_core(self, u, j):
        c = self.c
        src = self.tile(u).at[:, self.ways(1 - c)[j], 1 - c]
        return self.remote(src, self.got(u, 0).at[j], u, j, self.other)

    def to_first(self, u, i):
        to = (self.z * 4 + self.ways(self.c)[2], self.c)
        return self.remote(self.mine(u, 2 + i), self.got(u, 1).at[i], u, 4 + i, to)

    def to_second(self, u):
        to = (self.z * 4 + self.ways(self.c)[1], self.c)
        return self.remote(self.mine(u, 1), self.got(u, 2), u, 6, to)

    def to_z(self, u, k):
        zk = zxor(self.z, k)
        to = (zk * 4 + self.ways(self.c)[0], self.c)
        return self.remote(self.mine(u, 0).at[zk], self.got(u, 3).at[k - 1], u, 6 + k, to)

    def to_late(self, u):
        rows = self.part(u).shape[0] // 2
        theirs = pl.ds(pl.multiple_of((1 - self.c) * rows, rows), rows)
        return self.remote(self.part(u).at[theirs], self.from_late(u), u, 0, self.other)

    def add(self, u, j, term):
        mine = self.mine(u, j)

        @pl.loop(0, 4)
        def _(i):
            mine[i] = mine[i] + term[i]

    def step0(self, u):
        if self.late(u):
            return
        if u >= self.slots:
            pl.semaphore_wait(self.free, 1)
        if not self.late(u):
            for j in (2, 3, 0, 1):
                self.to_core(u, j).start()

    def step1(self, u):
        for j in (2, 3, 0, 1):
            if not self.late(u):
                self.to_core(u, j).wait_recv()
                self.add(u, j, self.got(u, 0).at[j])
            if j > 1:
                self.to_first(u, j - 2).start()
        if not self.late(u) and u < self.count - self.slots:
            pl.semaphore_signal(self.free, inc=1, device_id=self.other, device_id_type=MESH)

    def step2(self, u):
        for i in (1, 0):
            self.to_first(u, i).wait_recv()
            self.add(u, i, self.got(u, 1).at[i])
            if i == 1:
                self.to_second(u).start()

    def step3(self, u):
        self.to_second(u).wait_recv()
        self.add(u, 0, self.got(u, 2))
        for k in (2, 3, 1):
            self.to_z(u, k).start()

    def step4(self, u):
        got = self.got(u, 3)
        for k in (1, 2, 3):
            self.to_z(u, k).wait_recv()
        total = self.mine(u, 0)[self.z].astype(jnp.float32) + got[0].astype(jnp.float32)
        total = total + (got[1].astype(jnp.float32) + got[2].astype(jnp.float32))
        if self.late(u):
            self.part(u)[...] = total
            self.to_late(u).start()
        else:
            self.out(u, total, None)

    def step5(self, u):
        if self.late(u):
            rows = self.part(u).shape[0] // 2
            self.to_late(u).wait_recv()
            mine = self.part(u)[pl.ds(pl.multiple_of(self.c * rows, rows), rows)]
            self.out(u, mine, self.from_late(u)[...])

    def sent(self, u):
        if not self.late(u):
            for j in range(4):
                self.to_core(u, j).wait_send()
        for i in range(2):
            self.to_first(u, i).wait_send()
        self.to_second(u).wait_send()
        for k in (1, 2, 3):
            self.to_z(u, k).wait_send()

    def slot(self, t, order):
        for lag, step in (
            (1, self.step1),
            (1 + LAG, self.step2),
            (1 + 2 * LAG, self.step3),
            (1 + 3 * LAG, self.step4),
            (2 + 3 * LAG, self.step5),
        ):
            if 0 <= t - lag < len(order):
                step(order[t - lag])


LAG = 2
DEPTH = 2 + 3 * LAG


def turn(src, dst):
    @pl.loop(0, src.shape[1] // 128)
    def _(i):
        at = pl.multiple_of(i * 128, 128)
        dst[pl.ds(at, 128), :] = src[:, pl.ds(at, 128)].T


def product(rows, right, tile):
    @pl.loop(0, 2)
    def _(i):
        value = mul(rows(i), right[...]).astype(tile.dtype)
        tile[pl.ds(2 * i, 2)] = value.reshape((2, *tile.shape[1:]))


def middle_body(
    h3, du, act, gm, w_in, w_outer, c_out, c_query, w_out, y2, y1, cq, ck, cv, c_key, c_value, ok, vec, sums_in, *refs
):
    out_in, out_outer, sums_out, cap_out, block_out, db2_out, dcq_out, dck_out, dcv_out, da_out, dy1_out, do_out = refs[:12]
    (h3_v, du_v, act_v, gm_v, left, left_act, tiles, got0, got1, got2, got3) = refs[12:23]
    (w_v, acc, y_v, dy_v, db_v, da_v, dc_v, cq_v, dcq_v, kv_v, dkv_v, cap_v) = refs[23:35]
    send_sem, recv_sem, load_sem, w_sem, out_sem, free_sem = refs[35:]
    units, depth, slots = 16, tiles.shape[0], got0.shape[0]
    rows, width = gm_v.shape
    step = 128

    def out(u, total, _):
        if u < 8:
            out_in[:, u * 512 : (u + 1) * 512] = total
        else:
            b, h = divmod(u - 8, 2)
            out_outer[b * 32 : (b + 1) * 32, h * 512 : (h + 1) * 512] = total

    got = (got0, got1, got2, got3)
    ring = Scatter(
        lambda u: False,
        lambda u: tiles.at[u % depth],
        lambda u, i: got[i].at[u % slots if i == 0 else u],
        None,
        None,
        out,
        (send_sem, recv_sem),
        (slots, units, free_sem),
    )
    pairs = {
        "h3": (h3, h3_v),
        "du": (du, du_v),
        "act": (act, act_v),
        "gm": (gm, gm_v),
        "y2": (y2, y_v),
        "cq": (cq, cq_v),
        "ck": (ck, kv_v.at[0]),
        "cv": (cv, kv_v.at[1]),
        "y1": (y1, y_v),
    }
    loads = {
        name: pltpu.make_async_copy(src, dst, load_sem.at[i])
        for i, (name, (src, dst)) in enumerate(pairs.items())
    }
    parts = [w_in.at[:, pl.ds(i * 1024, 1024)] for i in range(4)]
    parts += [c_out, c_query, c_key, c_value, w_out]
    parts += [w_outer.at[pl.ds(i * 1024, 1024)] for i in range(4)]
    weights = [
        pltpu.make_async_copy(part, w_v.at[n % 2], w_sem.at[n % 2]) for n, part in enumerate(parts)
    ]
    stores = [
        pltpu.make_async_copy(src, dst, out_sem.at[i])
        for i, (src, dst) in enumerate(
            (
                (db_v, db2_out),
                (dcq_v, dcq_out),
                (dkv_v.at[0], dck_out),
                (dkv_v.at[1], dcv_out),
                (da_v, da_out),
                (dy_v, dy1_out),
                (dc_v, do_out),
                (h3_v, block_out),
            )
        )
    ]

    def use(n, work):
        weights[n].wait()
        work(w_v.at[n % 2])
        if n + 2 < len(weights):
            weights[n + 2].start()

    def over_rows(work):
        @pl.loop(0, rows // step)
        def _(i):
            work(pl.ds(i * step, step))

    def make(u):
        if u >= depth:
            ring.sent(u - depth)
        tile = tiles.at[u % depth]
        if u < 8:
            right = du_v.at[:, u * 512 : (u + 1) * 512]
            product(lambda i: left[pl.ds(i * 512, 512), :], right, tile)
        else:
            b, h = divmod(u - 8, 2)
            right = gm_v.at[:, h * 512 : (h + 1) * 512]
            product(lambda i: left_act[pl.ds(i * 16, 16), b].reshape(512, 512), right, tile)
        ring.step0(u)

    def turn_act(t):
        @pl.loop(t * 8, t * 8 + 8)
        def _(r):
            at = pl.multiple_of(r * 128, 128)
            left_act[r] = act_v[:, pl.ds(at, 128)].T.reshape(4, 32, 512)

    def add_dh3(j):
        def work(w):
            def body(at):
                term = mul(du_v[at, j * 1024 : (j + 1) * 1024], w[...], NT)
                acc[at, :] = term if j == 0 else acc[at, :] + term

            over_rows(body)

        use(j, work)

    def norm3():
        loads["y2"].wait()
        sums_out[...] = sums_in[...]

        def body(at):
            value = y_v[at, :]
            grads, dgain, dbias = norm_back(value, vec[4:5, :], acc[at, :])
            dy = gm_v[at, :].astype(jnp.float32) + grads
            dy_v[at, :] = dy
            db_v[at, :] = dy.astype(jnp.bfloat16)
            acc[at, :] = value + vec[6:7, :]
            sums_out[4:5, :] += dgain
            sums_out[5:6, :] += dbias

        over_rows(body)
        stores[0].start()
        loads["y1"].start()

    def back_out(w):
        def body(at):
            dc_v[at, :] = mul(db_v[at, :], w[...], NT).astype(jnp.bfloat16)

        over_rows(body)

    def cross(lo, hi):
        @pl.loop(lo, hi)
        def _(i):
            at = pl.ds(pl.multiple_of(i * 128, 128), 128)
            cross_bwd_body(
                cq_v.at[:, at],
                kv_v.at[0, :, at],
                kv_v.at[1, :, at],
                ok.at[1],
                dc_v.at[:, at],
                dcq_v.at[:, at],
                dkv_v.at[0, :, at],
                dkv_v.at[1, :, at],
            )

    def norm2(w):
        loads["y1"].wait()

        def body(at):
            dh = mul(dcq_v[at, :], w[...], NT)
            grads, dgain, dbias = norm_back(y_v[at, :], vec[2:3, :], dh)
            dy = dy_v[at, :] + grads
            dy_v[at, :] = dy
            da_v[at, :] = dy.astype(jnp.bfloat16)
            sums_out[2:3, :] += dgain
            sums_out[3:4, :] += dbias

        over_rows(body)
        stores[4].start()
        stores[5].start()

    def back_key(w):
        cap_v[...] = mul(dkv_v[0], w[...], NT)

    def back_value(w):
        cap_out[...] = (cap_v[...] + mul(dkv_v[1], w[...], NT)).astype(jnp.bfloat16)

    def back_self(w):
        def body(at):
            dc_v[at, :] = mul(da_v[at, :], w[...], NT).astype(jnp.bfloat16)

        over_rows(body)
        stores[6].start()

    def add_out(j):
        def work(w):
            def body(at):
                term = acc[at, :] + mul(act_v[at, j * 1024 : (j + 1) * 1024], w[...])
                if j < 3:
                    acc[at, :] = term
                else:
                    h3_v[at, :] = term.astype(jnp.bfloat16)

            over_rows(body)

        use(9 + j, work)

    for name in ("h3", "du", "gm", "act", "y2", "cq", "ck", "cv"):
        loads[name].start()
    weights[0].start()
    weights[1].start()
    greet(ring.partners())
    loads["h3"].wait()
    turn(h3_v, left)
    loads["du"].wait()

    def need(*names):
        for name in names:
            loads[name].wait()

    def store(*which):
        for i in which:
            stores[i].start()

    tasks = {
        0: [lambda: add_dh3(0)],
        1: [lambda: add_dh3(1)],
        2: [lambda: add_dh3(2)],
        3: [lambda: add_dh3(3), lambda: need("act", "gm")],
        4: [norm3],
        5: [lambda: turn_act(0), lambda: turn_act(1)],
        6: [lambda: turn_act(2), lambda: turn_act(3)],
        7: [lambda: use(4, back_out), lambda: need("cq", "ck", "cv")],
        8: [lambda: cross(0, 3)],
        9: [lambda: cross(3, 6)],
        10: [lambda: cross(6, 8), lambda: store(1, 2, 3)],
        11: [lambda: use(5, norm2)],
        12: [lambda: use(6, back_key), lambda: use(7, back_value)],
        13: [lambda: use(8, back_self)],
        14: [lambda: add_out(0)],
        15: [lambda: add_out(1)],
        16: [lambda: add_out(2)],
        17: [lambda: add_out(3), lambda: store(7)],
    }
    for t in range(units + 2 + 3 * LAG):
        if t < units:
            make(t)
        ring.slot(t, range(units))
        for task in tasks.get(t, ()):
            task()
    for u in range(max(units - depth, 0), units):
        ring.sent(u)
    for store in stores:
        store.wait()


def middle(operands, collective_id):
    depth, bf, f32, vm = DEPTH, jnp.bfloat16, jnp.float32, pltpu.VMEM
    shape = jax.ShapeDtypeStruct
    rows = (512, 1024)
    inside = pl.BlockSpec(memory_space=pltpu.VMEM)
    return pl.pallas_call(
        middle_body,
        out_shape=[
            shape((32, 4096), f32),
            shape((128, 1024), f32),
            shape((16, 1024), f32),
            shape((128, 1024), bf),
            shape(rows, bf),
            shape(rows, bf),
            shape(rows, bf),
            shape((128, 1024), bf),
            shape((128, 1024), bf),
            shape(rows, bf),
            shape(rows, f32),
            shape(rows, bf),
        ],
        in_specs=[ANY] * 16 + [inside] * 3,
        out_specs=[inside] * 4 + [ANY] * 8,
        scratch_shapes=[
            vm(rows, bf),
            vm((512, 4096), bf),
            vm((512, 4096), bf),
            vm(rows, bf),
            vm((1024, 512), bf),
            vm((32, 4, 32, 512), bf),
            vm((depth, 4, 4, 2, 32, 512), bf),
            vm((6, 4, 4, 32, 512), bf),
            vm((16, 2, 4, 32, 512), bf),
            vm((16, 4, 32, 512), bf),
            vm((16, 3, 32, 512), bf),
            vm((2, 1024, 1024), bf),
            vm(rows, f32),
            vm(rows, f32),
            vm(rows, f32),
            vm(rows, bf),
            vm(rows, bf),
            vm(rows, bf),
            vm(rows, bf),
            vm(rows, bf),
            vm((2, 128, 1024), bf),
            vm((2, 128, 1024), bf),
            vm((128, 1024), f32),
            pltpu.SemaphoreType.DMA((16, 10)),
            pltpu.SemaphoreType.DMA((16, 10)),
            pltpu.SemaphoreType.DMA((9,)),
            pltpu.SemaphoreType.DMA((2,)),
            pltpu.SemaphoreType.DMA((8,)),
            pltpu.SemaphoreType.REGULAR,
        ],
        compiler_params=pltpu.CompilerParams(
            collective_id=collective_id,
            has_side_effects=True,
            vmem_limit_bytes=59 * 1024 * 1024,
        ),
        name="middle",
    )(*operands)


def tail_body(q, k, v, o, lse, grad, h1, attn, da, h2, dcq, cattn, db2, e, dck, dcv, wq, wk, wv, x, dy1, gain, sums, cap, row, image_out, *refs):
    outs, total_out, refs = refs[:9], refs[9], refs[10:]
    (q_v, k_v, v_v, o_v, lse_v, do_v, cap_v, a_v, r_v, e_v, dc_v, x_v, dx_v, gain_v, sum_v) = refs[:15]
    (acc, dq_v, dk_v, dv_v, left, left1, left_e, tiles, late_tiles) = refs[15:24]
    big, late = refs[24:28], refs[28:31]
    part, from_late, give_v, take_v, got_sum = refs[31:36]
    send_sem, recv_sem, load_sem, pair_send, pair_recv, keep_sem, row_sem, sum_send, sum_recv, free_sem = refs[36:]
    normal, units, depth, slots = 14, 20, tiles.shape[0], refs[24].shape[0]
    dp, c = lax.axis_index("dp"), lax.axis_index("seq")
    length, width = q_v.shape
    pairs, rows = width // 128, length // 2
    mine = pl.ds(pl.multiple_of(c * rows, rows), rows)
    theirs = pl.ds(pl.multiple_of((1 - c) * rows, rows), rows)

    def out(u, total, other):
        what, h = divmod(u, 2)
        lanes = slice(h * 512, (h + 1) * 512)
        if what < 5:
            outs[what][:, lanes] = total
        elif u < normal:
            outs[5][(what - 5) * 32 : (what - 4) * 32, lanes] = total
        else:
            at = pl.multiple_of(c * 512 + h * 256, 128)
            outs[what - 1][:, pl.ds(at, 256)] = total
            at = pl.multiple_of((1 - c) * 512 + h * 256, 128)
            outs[what - 1][:, pl.ds(at, 256)] = other

    ring = Scatter(
        lambda u: u >= normal,
        lambda u: tiles.at[u % depth] if u < normal else late_tiles.at[u - normal],
        lambda u, i: late[i - 1].at[u - normal]
        if u >= normal
        else big[i].at[u % slots if i == 0 else u],
        lambda u: part.at[u - normal],
        lambda u: from_late.at[u - normal],
        out,
        (send_sem, recv_sem),
        (slots, normal, free_sem),
    )

    def load(i, src, dst):
        return pltpu.make_async_copy(src, dst, load_sem.at[i])

    loads = {
        "a0": load(0, attn, a_v.at[0]),
        "r0": load(1, da, r_v.at[0]),
        "q": load(2, q, q_v),
        "k": load(3, k, k_v),
        "v": load(4, v, v_v),
        "o": load(5, o, o_v),
        "lse": load(6, lse, lse_v),
        "a1": load(7, h2, a_v.at[1]),
        "r1": load(8, dcq, r_v.at[1]),
        "a2": load(9, cattn, a_v.at[0]),
        "r2": load(10, db2, r_v.at[0]),
        "e": load(11, e, e_v),
        "ck": load(12, dck, dc_v.at[0]),
        "cv": load(13, dcv, dc_v.at[1]),
        "h0": load(14, h1.at[pl.ds(0, 512)], a_v.at[1]),
        "h1": load(22, h1.at[pl.ds(512, 512)], a_v.at[0]),
        "cap": load(23, cap, cap_v),
        "wq": load(15, wq, q_v),
        "wk": load(16, wk, k_v),
        "wv": load(17, wv, v_v),
        "x": load(18, x, x_v),
        "dy1": load(19, dy1, dx_v),
        "gain": load(20, gain.at[pl.ds(0, 8)], gain_v),
        "sums": load(21, sums, sum_v),
    }

    def lane(i, core):
        return pl.ds(pl.multiple_of(core * width + i * 128, 128), 128)

    def keep(i):
        return pltpu.make_async_copy(grad.at[:, lane(i, c)], do_v.at[i, mine], keep_sem.at[i])

    def give(i):
        return pltpu.make_async_remote_copy(
            src_ref=grad.at[:, lane(i, 1 - c)],
            dst_ref=do_v.at[i, mine],
            send_sem=pair_send.at[i],
            recv_sem=pair_recv.at[i],
            device_id=ring.other,
            device_id_type=MESH,
        )

    for name in ("a0", "r0", "a1", "r1"):
        loads[name].start()
    greet(ring.partners())
    for i in range(pairs):
        give(i).start()
        keep(i).start()
    for name in ("q", "k", "v", "o", "lse", "e", "ck", "cv", "cap", "x", "dy1", "gain", "sums"):
        loads[name].start()

    def pair(i):
        keep(i).wait()
        give(i).wait()
        at = pl.ds(i * 128, 128)
        self_bwd_pair(
            q_v.at[:, at],
            k_v.at[:, at],
            v_v.at[:, at],
            o_v.at[:, at],
            do_v.at[i],
            lse_v.at[pl.ds(i, 1)],
            dq_v.at[:, at],
            dk_v.at[:, at],
            dv_v.at[:, at],
            acc,
        )

    def turn_late():
        loads["h0"].wait()
        turn(a_v.at[1], left1.at[:, pl.ds(0, 512)])
        loads["h1"].wait()
        turn(a_v.at[0], left1.at[:, pl.ds(512, 512)])

    def make(u):
        if depth <= u < normal:
            ring.sent(u - depth)
        what, h = divmod(u, 2)
        lanes = slice(h * 512, (h + 1) * 512)
        if what < 3:
            slot = what % 2
            if h == 0:
                loads[f"a{what}"].wait()
                loads[f"r{what}"].wait()
                turn(a_v.at[slot], left)
            right = r_v.at[slot, :, lanes]
            product(lambda i: left[pl.ds(i * 512, 512), :], right, tiles.at[u % depth])
            if h == 1:
                for name in (("a2", "r2"), ("h0",), ("h1",))[what]:
                    loads[name].start()
        elif what < 5:
            if what == 3 and h == 0:
                loads["e"].wait()
                loads["ck"].wait()
                loads["cv"].wait()
                turn(e_v, left_e)
            right = dc_v.at[what - 3, :, lanes]
            product(lambda i: left_e[pl.ds(i * 512, 512), :], right, tiles.at[u % depth])
        elif u < normal:
            if what == 5 and h == 0:
                loads["cap"].wait()
            tile = tiles.at[u % depth]
            for core in range(2):
                at = core * 64 + (what - 5) * 32
                block = cap_v[at : at + 32, lanes]

                @pl.loop(0, 16)
                def _(i, core=core, block=block):
                    hit = row[0:1, 0:512] == i.astype(jnp.float32)
                    tile[i // 4, i % 4, core] = jnp.where(hit, block, jnp.zeros_like(block))

        else:
            right = (dq_v, dk_v, dv_v)[what - 7].at[:, h * 256 : (h + 1) * 256]
            product(lambda i: left1[pl.ds(i * 512, 512), :], right, late_tiles.at[u - normal])
        ring.step0(u)

    swap = pltpu.make_async_remote_copy(
        src_ref=give_v,
        dst_ref=take_v,
        send_sem=row_sem.at[0],
        recv_sem=row_sem.at[1],
        device_id=ring.other,
        device_id_type=MESH,
    )

    def back(at):
        total = mul(dq_v[at, :], q_v[...], NT) + mul(dk_v[at, :], k_v[...], NT)
        return total + mul(dv_v[at, :], v_v[...], NT)

    def give_rows():
        for name in ("wq", "wk", "wv"):
            loads[name].wait()

        @pl.loop(0, rows // 128)
        def _(i):
            at = pl.ds(pl.multiple_of((1 - c) * rows + i * 128, 128), 128)
            give_v[pl.ds(i * 128, 128), :] = back(at).astype(jnp.bfloat16)

        swap.start()

    def take_rows():
        swap.wait_recv()
        for name in ("x", "dy1", "gain", "sums"):
            loads[name].wait()
        step = 128

        @pl.loop(0, rows // step)
        def _(i):
            at = pl.ds(i * step, step)
            whole = pl.ds(pl.multiple_of(c * rows + i * step, step), step)
            dh = back(whole) + take_v[at, :].astype(jnp.float32)
            grads, dgain, dbias = norm_back(x_v[at, :].astype(jnp.float32), gain_v[0:1, :], dh)
            dx_v[at, :] = dx_v[at, :] + grads
            sum_v[0:1, :] = sum_v[0:1, :] + dgain
            sum_v[1:2, :] = sum_v[1:2, :] + dbias

    write = pltpu.make_async_copy(dx_v, image_out, row_sem.at[2])

    way = ring.ways(c)
    peers = [
        [ring.other],
        [(ring.z * 4 + way[2], c)],
        [(ring.z * 4 + way[1], c)],
        [(zxor(ring.z, n) * 4 + way[0], c) for n in (1, 2, 3)],
    ]

    def sum_send_of(s, n):
        return pltpu.make_async_remote_copy(
            src_ref=sum_v if s == 0 else got_sum.at[5 + s],
            dst_ref=got_sum.at[s + n],
            send_sem=sum_send.at[s + n],
            recv_sem=sum_recv.at[s + n],
            device_id=peers[s][n],
            device_id_type=MESH,
        )

    def start_sum(s):
        for n in range(len(peers[s])):
            sum_send_of(s, n).start()

    def take_sum(s):
        total = sum_v[...] if s == 0 else got_sum[5 + s]
        for n in range(len(peers[s])):
            sum_send_of(s, n).wait_recv()
            total = total + got_sum[s + n]
        if s == 3:
            total_out[...] = total
        else:
            got_sum[6 + s] = total
            start_sum(s + 1)

    def start_pairs():
        for name in ("q", "k", "v", "o", "lse"):
            loads[name].wait()
        pair(0)

    def end_pairs():
        pair(pairs - 1)
        for name in ("wq", "wk", "wv"):
            loads[name].start()

    def own_rows():
        take_rows()
        write.start()
        start_sum(0)

    order = [*range(12), *range(normal, units), *range(12, normal)]
    tasks = {
        1: [start_pairs],
        3: [lambda: pair(1)],
        5: [lambda: pair(2)],
        7: [end_pairs],
        9: [turn_late],
        10: [give_rows],
        12: [own_rows],
        14: [lambda: take_sum(0)],
        16: [lambda: take_sum(1)],
        18: [lambda: take_sum(2)],
        20: [lambda: take_sum(3)],
    }
    for t in range(units + 3 + 3 * LAG):
        if t < units:
            make(order[t])
        ring.slot(t, order)
        for task in tasks.get(t, ()):
            task()
    for u in range(normal - depth, units):
        ring.sent(u)
    for u in range(normal, units):
        ring.to_late(u).wait_send()
    swap.wait_send()
    write.wait()
    for s in range(4):
        for n in range(len(peers[s])):
            sum_send_of(s, n).wait_send()


def norm_back(value, gain, dh):
    center = value - jnp.mean(value, axis=1, keepdims=True)
    r = lax.rsqrt(jnp.mean(center * center, axis=1, keepdims=True) + EPSILON)
    hat = center * r
    dhg = dh * gain
    grads = r * (
        dhg
        - jnp.mean(dhg, axis=1, keepdims=True)
        - hat * jnp.mean(dhg * hat, axis=1, keepdims=True)
    )
    return grads, jnp.sum(dh * hat, axis=0, keepdims=True), jnp.sum(dh, axis=0, keepdims=True)


def scatter_tail(operands, collective_id):
    bf, f32, depth = jnp.bfloat16, jnp.float32, DEPTH
    vm = pltpu.VMEM
    outs = [jax.ShapeDtypeStruct((512, 1024), f32)] + [
        jax.ShapeDtypeStruct((64 if i == 5 else 32, 1024), f32) for i in range(9)
    ]
    outs.append(jax.ShapeDtypeStruct((16, 1024), f32))
    return pl.pallas_call(
        tail_body,
        out_shape=outs,
        in_specs=[ANY] * (len(operands) - 1) + [pl.BlockSpec(memory_space=pltpu.VMEM)],
        out_specs=[ANY] + [pl.BlockSpec(memory_space=pltpu.VMEM)] * 10,
        scratch_shapes=[
            vm((1024, 512), bf),
            vm((1024, 512), bf),
            vm((1024, 512), bf),
            vm((1024, 512), bf),
            vm((4, 2, 1024), f32),
            vm((4, 1024, 128), bf),
            vm((128, 1024), bf),
            vm((2, 512, 1024), bf),
            vm((2, 512, 1024), bf),
            vm((128, 1024), bf),
            vm((2, 128, 1024), bf),
            vm((512, 1024), bf),
            vm((512, 1024), f32),
            vm((8, 1024), f32),
            vm((16, 1024), f32),
            vm((1024, 128), f32),
            vm((1024, 512), bf),
            vm((1024, 512), bf),
            vm((1024, 512), bf),
            vm((1024, 512), bf),
            vm((1024, 1024), bf),
            vm((1024, 128), bf),
            vm((depth, 4, 4, 2, 32, 512), bf),
            vm((6, 4, 4, 64, 256), bf),
            vm((6, 4, 4, 32, 512), bf),
            vm((14, 2, 4, 32, 512), bf),
            vm((14, 4, 32, 512), bf),
            vm((14, 3, 32, 512), bf),
            vm((6, 2, 4, 64, 256), bf),
            vm((6, 4, 64, 256), bf),
            vm((6, 3, 64, 256), bf),
            vm((6, 64, 256), f32),
            vm((6, 32, 256), f32),
            vm((512, 1024), bf),
            vm((512, 1024), bf),
            vm((9, 16, 1024), f32),
            pltpu.SemaphoreType.DMA((20, 10)),
            pltpu.SemaphoreType.DMA((20, 10)),
            pltpu.SemaphoreType.DMA((24,)),
            pltpu.SemaphoreType.DMA((4,)),
            pltpu.SemaphoreType.DMA((4,)),
            pltpu.SemaphoreType.DMA((4,)),
            pltpu.SemaphoreType.DMA((3,)),
            pltpu.SemaphoreType.DMA((6,)),
            pltpu.SemaphoreType.DMA((6,)),
            pltpu.SemaphoreType.REGULAR,
        ],
        compiler_params=pltpu.CompilerParams(
            collective_id=collective_id,
            has_side_effects=True,
            vmem_limit_bytes=59 * 1024 * 1024,
        ),
        name="scatter_tail",
    )(*operands)


def norm_fwd(value, gain, shift):
    center = value - jnp.mean(value, axis=1, keepdims=True)
    spread = jnp.mean(center * center, axis=1, keepdims=True)
    return center * lax.rsqrt(spread + EPSILON) * gain + shift


GELU_IN = 0.7978845608028654
GELU_CUBE = 0.044715


def gelu_both(u):
    square = u * u
    t = jnp.tanh(GELU_IN * (u + GELU_CUBE * (square * u)))
    half = 0.5 * (1.0 + t)
    slope = half + 0.5 * u * (1.0 - t * t) * (GELU_IN * (1.0 + 3.0 * GELU_CUBE * square))
    return u * half, slope


FRONT_IN = (
    "w_query",
    "w_key",
    "w_value",
    "packed",
    "w_out",
    "encoder",
    "c_query",
    "c_key",
    "c_value",
    "c_out",
    "w_outer",
    "w_in",
    "images",
    "gm",
    "caption_seg",
    "image_row",
    "image_seg",
)
FRONT_OUT = (
    "wq",
    "wk",
    "wv",
    "w_out_all",
    "c_query_all",
    "c_key_all",
    "c_value_all",
    "c_out_all",
    "w_outer_all",
    "w_in_all",
    "h1",
    "q",
    "k",
    "v",
    "heads",
    "attn",
    "y1",
    "h2",
    "cq",
    "ck",
    "cv",
    "caption",
    "cattn",
    "y2",
    "h3",
    "act",
    "du",
    "lse",
    "vec",
    "ok",
    "sums",
)
FRONT_VMEM = (
    "table",
    "enc",
    "both",
    "wqkv",
    "h1_v",
    "q_v",
    "k_v",
    "v_v",
    "obuf",
    "attn_v",
    "y1_v",
    "h2_v",
    "cq_v",
    "kv_v",
    "cap_v",
    "cattn_v",
    "y2_v",
    "h3_v",
    "gm_v",
    "dact",
    "act_v",
    "du_v",
    "w_v",
    "bin",
)


def front_body(*refs):
    names = FRONT_IN + FRONT_OUT + FRONT_VMEM
    r = dict(zip(names, refs))
    (send_sem, recv_sem, local_sem, pair_sem, give_send, give_recv, keep_sem, w_sem, out_sem, gm_sem) = refs[len(names) :]
    c = lax.axis_index("seq")
    rows, step = 512, 128
    own = [r["w_query"], r["w_key"], r["w_value"], r["packed"], r["w_out"]]
    own += [r["encoder"].at[:, pl.ds(pl.multiple_of(c * 64, 64), 64)]]
    own += [r["c_query"], r["c_key"], r["c_value"], r["c_out"], r["w_outer"]]
    own += [r["w_in"].at[:, i * 1024 : (i + 1) * 1024] for i in range(4)]
    full = [r["wqkv"].at[i] for i in range(3)] + [r["table"], r["w_out_all"], r["enc"]]
    full += [r["c_query_all"], r["c_key_all"], r["c_value_all"], r["c_out_all"], r["w_outer_all"]]
    full += [r["w_in_all"].at[:, i * 1024 : (i + 1) * 1024] for i in range(4)]
    n = len(own)
    ring = Gather(3, own, full, send_sem, recv_sem, local_sem)
    order = [3, 0, 1, 2, *range(4, n)]

    def slot(t, ahead=2):
        for lead, todo in ((3 * ahead + 1, begin), (2 * ahead, along), (ahead, first), (0, second)):
            for i in range(t + lead + 1):
                todo(i)

    done = set()

    def once(step, name):
        def run(i):
            if i < n and (name, i) not in done:
                done.add((name, i))
                step(order[i])

        return run

    begin, along = once(ring.start, "start"), once(ring.along_z, "z")
    first, second = once(ring.first, "first"), once(ring.second, "second")

    mine = r["both"].at[pl.ds(pl.multiple_of(c * rows, rows), rows)]
    keep_image = pltpu.make_async_copy(r["images"], mine, pair_sem.at[0])
    give_image = pltpu.make_async_remote_copy(
        src_ref=r["images"],
        dst_ref=mine,
        send_sem=pair_sem.at[1],
        recv_sem=pair_sem.at[2],
        device_id=ring.other,
        device_id_type=MESH,
    )
    load_gm = pltpu.make_async_copy(r["gm"], r["gm_v"], gm_sem)
    places = [
        ("wqkv", 0, "wq"),
        ("wqkv", 1, "wk"),
        ("wqkv", 2, "wv"),
        ("h1_v", None, "h1"),
        ("q_v", None, "q"),
        ("k_v", None, "k"),
        ("v_v", None, "v"),
        ("attn_v", None, "attn"),
        ("y1_v", None, "y1"),
        ("h2_v", None, "h2"),
        ("cq_v", None, "cq"),
        ("kv_v", 0, "ck"),
        ("kv_v", 1, "cv"),
        ("cap_v", None, "caption"),
        ("cattn_v", None, "cattn"),
        ("y2_v", None, "y2"),
        ("h3_v", None, "h3"),
        ("act_v", None, "act"),
        ("du_v", None, "du"),
    ]
    stores = {
        dst: pltpu.make_async_copy(r[src] if at is None else r[src].at[at], r[dst], out_sem.at[i])
        for i, (src, at, dst) in enumerate(places)
    }
    parts = [r["w_out_all"], r["c_query_all"], r["c_key_all"], r["c_value_all"], r["c_out_all"]]
    parts += [r["w_outer_all"].at[i * 1024 : (i + 1) * 1024] for i in range(4)] + full[11:]
    weights = [
        pltpu.make_async_copy(part, r["w_v"].at[i % 2], w_sem.at[i % 2])
        for i, part in enumerate(parts)
    ]

    def weight(i):
        weights[i].wait()
        return r["w_v"].at[i % 2]

    def over(count, work):
        @pl.loop(0, count // step)
        def _(i):
            work(pl.ds(i * step, step))

    vec, table = r["vec"], r["table"]

    def unpack():
        for i in range(8):
            lanes = slice(i * 128, (i + 1) * 128)
            at = 4 * i * 16
            vec[:, lanes] = (table[at : at + 16] + table[at + 16 : at + 32]) + (
                table[at + 32 : at + 48] + table[at + 48 : at + 64]
            )
            for j in range(4):
                at = (8 * j + i) * 16 + 7
                r["bin"][j : j + 1, lanes] = table[at : at + 1]

    def row(i):
        return vec[i : i + 1, :]

    def norm1(at):
        value = norm_fwd(r["both"][at, :].astype(jnp.float32), row(0), row(1))
        r["h1_v"][at, :] = value.astype(jnp.bfloat16)

    def project(i):
        def work(at):
            value = mul(r["h1_v"][at, :], r["wqkv"][i])
            r[("q_v", "k_v", "v_v")[i]][at, :] = value.astype(jnp.bfloat16)

        over(2 * rows, work)
        stores[("wq", "wk", "wv")[i]].start()
        stores[("q", "k", "v")[i]].start()

    def keep(i):
        at = pl.multiple_of(c * 512 + i * 128, 128)
        src = r["obuf"].at[i, pl.ds(pl.multiple_of(c * rows, rows), rows)]
        return pltpu.make_async_copy(src, r["attn_v"].at[:, pl.ds(at, 128)], keep_sem.at[i])

    def give(i):
        at = pl.multiple_of(c * 512 + i * 128, 128)
        return pltpu.make_async_remote_copy(
            src_ref=r["obuf"].at[i, pl.ds(pl.multiple_of((1 - c) * rows, rows), rows)],
            dst_ref=r["attn_v"].at[:, pl.ds(at, 128)],
            send_sem=give_send.at[i],
            recv_sem=give_recv.at[i],
            device_id=ring.other,
            device_id_type=MESH,
        )

    def pair(i):
        at = pl.ds(i * 128, 128)

        def put(start, value):
            r["obuf"][i, pl.ds(start, value.shape[0]), :] = value
            r["heads"][pl.ds(start, value.shape[0]), i * 128 : (i + 1) * 128] = value

        self_fwd_pair(
            r["q_v"].at[:, at], r["k_v"].at[:, at], r["v_v"].at[:, at], r["lse"].at[pl.ds(i, 1)], put
        )
        keep(i).start()
        give(i).start()

    def self_out(w):
        def work(at):
            image = r["images_f"](at)
            y1 = image + mul(r["attn_v"][at, :], w[...])
            r["y1_v"][at, :] = y1
            r["h2_v"][at, :] = norm_fwd(y1, row(2), row(3)).astype(jnp.bfloat16)

        over(rows, work)

    def own_image(at):
        start = pl.multiple_of(c * rows + at.start, step)
        return r["both"][pl.ds(start, step), :].astype(jnp.float32)

    r["images_f"] = own_image

    def cross_query(w):
        def work(at):
            r["cq_v"][at, :] = mul(r["h2_v"][at, :], w[...]).astype(jnp.bfloat16)

        over(rows, work)

    def pick_caption():
        line = r["image_row"][0]
        r["cap_v"][0:64, :] = r["enc"][2 * line]
        r["cap_v"][64:128, :] = r["enc"][2 * line + 1]
        chosen = lax.broadcasted_iota(jnp.int32, (16, 128), 0) == line
        seg = jnp.sum(jnp.where(chosen, r["caption_seg"][...], 0), axis=0, keepdims=True)
        allowed = jnp.where(seg == r["image_seg"][0], 1.0, 0.0)
        wide = jnp.broadcast_to(allowed, (128, 128))
        r["ok"][0] = wide
        r["ok"][1] = wide.T

    def cross_out(w):
        def work(at):
            y2 = r["y1_v"][at, :] + mul(r["cattn_v"][at, :], w[...])
            r["y2_v"][at, :] = y2
            r["h3_v"][at, :] = norm_fwd(y2, row(4), row(5)).astype(jnp.bfloat16)

        over(rows, work)

    def cross(lo, hi):
        @pl.loop(lo, hi)
        def _(i):
            at = pl.ds(pl.multiple_of(i * 128, 128), 128)
            cross_fwd_body(
                r["cq_v"].at[:, at],
                r["kv_v"].at[0, :, at],
                r["kv_v"].at[1, :, at],
                r["ok"].at[0],
                r["cattn_v"].at[:, at],
            )

    def back_outer(j, w):
        def work(at):
            r["dact"][at, j * 1024 : (j + 1) * 1024] = mul(r["gm_v"][at, :], w[...], NT)

        over(rows, work)

    def hidden(j, w):
        lanes = slice(j * 1024, (j + 1) * 1024)

        def work(at):
            u = mul(r["h3_v"][at, :], w[...]) + r["bin"][j : j + 1, :]
            act, slope = gelu_both(u)
            r["act_v"][at, lanes] = act.astype(jnp.bfloat16)
            du = (r["dact"][at, lanes] * slope).astype(jnp.bfloat16)
            r["du_v"][at, lanes] = du
            r["sums"][7 + j : 8 + j, :] += jnp.sum(du.astype(jnp.float32), axis=0, keepdims=True)

        over(rows, work)

    greet(ring.partners())
    for i in range(4):
        begin(i)
    keep_image.start()
    give_image.start()
    for g in range(3):
        ring.swapped(g)
    begin(4)
    load_gm.start()
    r["sums"][...] = jnp.zeros_like(r["sums"])
    slot(0, 1)
    ring.ready(3)
    unpack()
    keep_image.wait()
    give_image.wait_recv()
    slot(1, 1)
    over(2 * rows, norm1)
    stores["h1"].start()
    project(0)
    slot(2, 1)
    project(1)
    slot(3, 1)
    project(2)
    slot(3)
    pair(0)
    slot(4)
    ring.ready(4)
    weights[0].start()
    pair(1)
    along(9)
    pair(2)
    first(7)
    pair(3)
    slot(5)
    for i in range(4):
        keep(i).wait()
        give(i).wait_recv()
    stores["attn"].start()
    self_out(weight(0))
    stores["y1"].start()
    stores["h2"].start()
    slot(6)
    ring.ready(5)
    pick_caption()
    stores["caption"].start()
    ring.ready(6)
    weights[1].start()
    cross_query(weight(1))
    stores["cq"].start()
    slot(7)
    ring.ready(7)
    weights[2].start()
    r["kv_v"][0] = mul(r["cap_v"][...], weight(2)[...]).astype(jnp.bfloat16)
    stores["ck"].start()
    slot(8)
    ring.ready(8)
    weights[3].start()
    r["kv_v"][1] = mul(r["cap_v"][...], weight(3)[...]).astype(jnp.bfloat16)
    stores["cv"].start()
    cross(0, 4)
    slot(9)
    cross(4, 8)
    stores["cattn"].start()
    ring.ready(9)
    weights[4].start()
    cross_out(weight(4))
    stores["y2"].start()
    stores["h3"].start()
    load_gm.wait()
    r["sums"][6:7, :] = jnp.sum(r["gm_v"][...].astype(jnp.float32), axis=0, keepdims=True)
    slot(10)
    ring.ready(10)
    weights[5].start()
    weights[6].start()
    back_outer(0, weight(5))
    weights[7].start()
    back_outer(1, weight(6))
    weights[8].start()
    slot(11)
    back_outer(2, weight(7))
    ring.ready(11)
    weights[9].start()
    back_outer(3, weight(8))
    for j in range(4):
        if j < 3:
            slot(12 + j)
            ring.ready(12 + j)
            weights[10 + j].start()
        hidden(j, weight(9 + j))
    stores["act"].start()
    stores["du"].start()
    for g in range(n):
        ring.sent(g)
    give_image.wait_send()
    for i in range(4):
        give(i).wait_send()
    for store in stores.values():
        store.wait()


def front(operands, collective_id):
    bf, f32, vm, shape = jnp.bfloat16, jnp.float32, pltpu.VMEM, jax.ShapeDtypeStruct
    square, rows, head = (1024, 1024), (512, 1024), (1024, 512)
    inside = pl.BlockSpec(memory_space=pltpu.VMEM)
    scalar = pl.BlockSpec(memory_space=pltpu.SMEM)
    outs = (
        [shape(head, bf)] * 3
        + [shape(square, bf)] * 5
        + [shape((4096, 1024), bf), shape((1024, 4096), bf), shape(square, bf)]
        + [shape(head, bf)] * 4
        + [shape(rows, bf), shape(rows, f32), shape(rows, bf), shape(rows, bf)]
        + [shape((128, 1024), bf)] * 3
        + [shape(rows, bf), shape(rows, f32), shape(rows, bf)]
        + [shape((512, 4096), bf)] * 2
        + [shape((4, 2, 1024), f32), shape((16, 1024), f32), shape((2, 128, 128), f32)]
        + [shape((16, 1024), f32)]
    )
    places = [ANY] * 14 + [inside] + [ANY] * 12 + [inside] * 4
    n = 15
    return pl.pallas_call(
        front_body,
        out_shape=outs,
        in_specs=[ANY] * 14 + [inside, scalar, scalar],
        out_specs=places,
        scratch_shapes=[
            vm((512, 128), f32),
            vm((32, 64, 1024), bf),
            vm(square, bf),
            vm((3, 1024, 512), bf),
            vm(square, bf),
            vm(head, bf),
            vm(head, bf),
            vm(head, bf),
            vm((4, 1024, 128), bf),
            vm(rows, bf),
            vm(rows, f32),
            vm(rows, bf),
            vm(rows, bf),
            vm((2, 128, 1024), bf),
            vm((128, 1024), bf),
            vm(rows, bf),
            vm(rows, f32),
            vm(rows, bf),
            vm(rows, bf),
            vm((512, 4096), f32),
            vm((512, 4096), bf),
            vm((512, 4096), bf),
            vm((2, 1024, 1024), bf),
            vm((4, 1024), f32),
            pltpu.SemaphoreType.DMA((n, 31)),
            pltpu.SemaphoreType.DMA((n, 31)),
            pltpu.SemaphoreType.DMA((n,)),
            pltpu.SemaphoreType.DMA((3,)),
            pltpu.SemaphoreType.DMA((4,)),
            pltpu.SemaphoreType.DMA((4,)),
            pltpu.SemaphoreType.DMA((4,)),
            pltpu.SemaphoreType.DMA((2,)),
            pltpu.SemaphoreType.DMA((19,)),
            pltpu.SemaphoreType.DMA,
        ],
        compiler_params=pltpu.CompilerParams(
            collective_id=collective_id,
            has_side_effects=True,
            vmem_limit_bytes=59 * 1024 * 1024,
        ),
        name="front",
    )(*operands)


def emit_body(*refs):
    n = (len(refs) - 4) // 3
    srcs, total, dsts = refs[:n], refs[n], refs[n + 1 : 2 * n + 1]
    cut, share = refs[2 * n + 1 : 2 * n + 3]
    held, sem = refs[2 * n + 3 : -1], refs[-1]
    loads = [pltpu.make_async_copy(srcs[i], held[i], sem.at[i]) for i in range(n)]
    copies = [pltpu.make_async_copy(held[i], dsts[i], sem.at[i]) for i in range(n)]
    for load in loads:
        load.start()
    index = 2 * lax.axis_index("dp") + lax.axis_index("seq")
    block = total[:, pl.ds(pl.multiple_of(index // 4 * 128, 128), 128)]
    moved = block
    for k in range(1, 4):
        moved = jnp.where(index % 4 == k, pltpu.roll(block, 128 - 32 * k, 1), moved)
    cut[...] = moved[0:8]
    block = total[:, pl.ds(pl.multiple_of(index % 8 * 128, 128), 128)]
    chosen = lax.broadcasted_iota(jnp.int32, block.shape, 0) == 7 + index // 8
    share[...] = jnp.broadcast_to(
        jnp.sum(jnp.where(chosen, block, 0.0), axis=0, keepdims=True), (8, 128)
    )
    for load, copy in zip(loads, copies):
        load.wait()
        copy.start()
    for copy in copies:
        copy.wait()


def emit(arrays, total):
    inside = pl.BlockSpec(memory_space=pltpu.VMEM)
    n = len(arrays)
    return pl.pallas_call(
        emit_body,
        out_shape=[jax.ShapeDtypeStruct(a.shape, a.dtype) for a in arrays]
        + [jax.ShapeDtypeStruct((8, 128), jnp.float32)] * 2,
        in_specs=[ANY] * n + [inside],
        out_specs=[ANY] * n + [inside] * 2,
        scratch_shapes=[pltpu.VMEM(a.shape, a.dtype) for a in arrays]
        + [pltpu.SemaphoreType.DMA((n,))],
        name="emit",
    )(*arrays, total)


HEADS = 16
HEAD_DIM = 64


EPSILON = 1e-05
NEG_BIG = -1e30


def norm_rows(value, gain, shift):
    center = value - jnp.mean(value, axis=-1, keepdims=True)
    spread = jnp.mean(center * center, axis=-1, keepdims=True)
    return center * lax.rsqrt(spread + EPSILON) * gain + shift


def project(rows, weight):
    return jnp.einsum("bsd,de->bse", rows, weight, preferred_element_type=jnp.float32)


def project_back(grads, weight):
    return jnp.einsum("bse,de->bsd", grads, weight, preferred_element_type=jnp.float32)


def weight_grad(rows, grads):
    return jnp.einsum("bsd,bse->de", rows, grads, preferred_element_type=jnp.float32)


def row_total(grads):
    return jnp.sum(grads.astype(jnp.float32), axis=(0, 1))


def split_heads(value):
    return value.reshape(value.shape[0], value.shape[1], HEADS, HEAD_DIM)


def join_heads(value):
    return value.reshape(value.shape[0], value.shape[1], HEADS * HEAD_DIM)


def scores_of(queries, keys_in, allowed):
    raw_scores = (
        jnp.einsum(
            "bqhd,bkhd->bhqk",
            split_heads(queries),
            split_heads(keys_in),
            preferred_element_type=jnp.float32,
        )
        * 0.125
    )
    return jnp.where(allowed, raw_scores, NEG_BIG)


def attend(queries, keys_in, values_in, allowed):
    scores = scores_of(queries, keys_in, allowed)
    row_max = jnp.max(scores, axis=-1, keepdims=True)
    exponent = jnp.exp(scores - row_max)
    total = jnp.sum(exponent, axis=-1, keepdims=True)
    attn_weights = exponent / total
    mixed_rows = jnp.einsum(
        "bhqk,bkhd->bqhd",
        attn_weights.astype(jnp.bfloat16),
        split_heads(values_in),
        preferred_element_type=jnp.float32,
    )
    return (join_heads(mixed_rows).astype(jnp.bfloat16), row_max + jnp.log(total))


def attend_back(queries, keys_in, values_in, allowed, log_total, grad_mixed):
    attn_weights = jnp.exp(scores_of(queries, keys_in, allowed) - log_total)
    grad_heads = split_heads(grad_mixed)
    grad_weights = jnp.einsum(
        "bqhd,bkhd->bhqk", grad_heads, split_heads(values_in), preferred_element_type=jnp.float32
    )
    grad_values = jnp.einsum(
        "bhqk,bqhd->bkhd",
        attn_weights.astype(jnp.bfloat16),
        grad_heads,
        preferred_element_type=jnp.float32,
    )
    inner_sum = jnp.sum(grad_weights * attn_weights, axis=-1, keepdims=True)
    grad_scores = (attn_weights * (grad_weights - inner_sum)).astype(jnp.bfloat16)
    grad_queries = (
        jnp.einsum(
            "bhqk,bkhd->bqhd", grad_scores, split_heads(keys_in), preferred_element_type=jnp.float32
        )
        * 0.125
    )
    grad_keys = (
        jnp.einsum(
            "bhqk,bqhd->bkhd", grad_scores, split_heads(queries), preferred_element_type=jnp.float32
        )
        * 0.125
    )
    return (join_heads(grad_queries), join_heads(grad_keys), join_heads(grad_values))


def per_device(
    images,
    encoder_states,
    image_row,
    image_seg,
    caption_seg,
    ln1_gain,
    ln1_bias,
    w_query,
    w_key,
    w_value,
    w_out,
    ln2_gain,
    ln2_bias,
    c_query,
    c_key,
    c_value,
    c_out,
    ln3_gain,
    ln3_bias,
    w_in,
    b_in,
    w_outer,
    b_outer,
    cotangent,
):
    mixing = (
        lax.all_gather(ln1_gain, ("dp", "seq"), axis=0, tiled=True),
        lax.all_gather(ln1_bias, ("dp", "seq"), axis=0, tiled=True),
        lax.all_gather(w_query, ("dp", "seq"), axis=0, tiled=True),
        lax.all_gather(w_key, ("dp", "seq"), axis=0, tiled=True),
        lax.all_gather(w_value, ("dp", "seq"), axis=0, tiled=True),
        lax.all_gather(w_out, ("dp", "seq"), axis=0, tiled=True),
        lax.all_gather(ln2_gain, ("dp", "seq"), axis=0, tiled=True),
        lax.all_gather(ln2_bias, ("dp", "seq"), axis=0, tiled=True),
        lax.all_gather(c_query, ("dp", "seq"), axis=0, tiled=True),
        lax.all_gather(c_key, ("dp", "seq"), axis=0, tiled=True),
        lax.all_gather(c_value, ("dp", "seq"), axis=0, tiled=True),
        lax.all_gather(c_out, ("dp", "seq"), axis=0, tiled=True),
    )
    (
        gain_a,
        bias_a,
        query_w,
        key_w,
        value_w,
        out_w,
        gain_b,
        bias_b,
        cross_qw,
        cross_kw,
        cross_vw,
        cross_ow,
    ) = mixing
    shard = images.shape[1]
    seq_index = lax.axis_index("seq")
    full_len = shard * lax.axis_size("seq")
    inputs_f = images.astype(jnp.float32)
    gain_a32, bias_a32 = (gain_a.astype(jnp.float32), bias_a.astype(jnp.float32))
    normed_a = norm_rows(inputs_f, gain_a32, bias_a32).astype(jnp.bfloat16)
    queries = project(normed_a, query_w).astype(jnp.bfloat16)
    keys_local = project(normed_a, key_w).astype(jnp.bfloat16)
    values_local = project(normed_a, value_w).astype(jnp.bfloat16)
    keys_all, values_all = (
        lax.all_gather(keys_local, "seq", axis=1, tiled=True),
        lax.all_gather(values_local, "seq", axis=1, tiled=True),
    )
    query_pos = seq_index * shard + jnp.arange(shard, dtype=jnp.int32)
    key_pos = jnp.arange(full_len, dtype=jnp.int32)
    causal = (key_pos[None, :] <= query_pos[:, None])[None, None]
    self_out, self_lse = attend(queries, keys_all, values_all, causal)
    after_self = inputs_f + project(self_out, out_w)
    gain_b32, bias_b32 = (gain_b.astype(jnp.float32), bias_b.astype(jnp.float32))
    normed_b = norm_rows(after_self, gain_b32, bias_b32).astype(jnp.bfloat16)
    cross_queries = project(normed_b, cross_qw).astype(jnp.bfloat16)
    encoder_all = lax.all_gather(encoder_states, "dp", axis=0, tiled=True)
    caption = jnp.take(encoder_all, image_row, axis=0)
    cross_keys = project(caption, cross_kw).astype(jnp.bfloat16)
    cross_values = project(caption, cross_vw).astype(jnp.bfloat16)
    caption_mask = (jnp.take(caption_seg, image_row, axis=0) == image_seg[:, None])[
        :, None, None, :
    ]
    cross_out, cross_lse = attend(cross_queries, cross_keys, cross_values, caption_mask)
    after_cross = after_self + project(cross_out, cross_ow)
    feed_weights = (
        lax.all_gather(ln3_gain, ("dp", "seq"), axis=0, tiled=True),
        lax.all_gather(ln3_bias, ("dp", "seq"), axis=0, tiled=True),
        lax.all_gather(w_in, ("dp", "seq"), axis=0, tiled=True),
        lax.all_gather(b_in, ("dp", "seq"), axis=0, tiled=True),
        lax.all_gather(w_outer, ("dp", "seq"), axis=0, tiled=True),
        lax.all_gather(b_outer, ("dp", "seq"), axis=0, tiled=True),
    )
    gain_c, bias_c, inner_w, inner_b, outer_w, outer_b = feed_weights
    gain_c32, bias_c32 = (gain_c.astype(jnp.float32), bias_c.astype(jnp.float32))
    normed_c = norm_rows(after_cross, gain_c32, bias_c32).astype(jnp.bfloat16)
    hidden_pre = project(normed_c, inner_w) + inner_b.astype(jnp.float32)
    activated = jax.nn.gelu(hidden_pre).astype(jnp.bfloat16)
    result = after_cross + project(activated, outer_w) + outer_b.astype(jnp.float32)
    block_out = result.astype(jnp.bfloat16)
    inner_wb, outer_wb = (feed_weights[2], feed_weights[4])
    grad_result = cotangent.astype(jnp.float32)
    grad_outer_w = weight_grad(activated, cotangent)
    grad_outer_b = row_total(cotangent)
    grad_act = project_back(cotangent, outer_wb)
    _, gelu_back = jax.vjp(jax.nn.gelu, hidden_pre)
    grad_hidden = gelu_back(grad_act)[0].astype(jnp.bfloat16)
    grad_inner_w = weight_grad(normed_c, grad_hidden)
    grad_inner_b = row_total(grad_hidden)
    grad_normed_c = project_back(grad_hidden, inner_wb)
    _, norm_c_back = jax.vjp(norm_rows, after_cross, gain_c32, bias_c32)
    grad_cross_part, grad_gain_c, grad_bias_c = norm_c_back(grad_normed_c)
    grad_after_cross = grad_result + grad_cross_part
    feed_sums = (
        lax.psum_scatter(grad_gain_c, ("dp", "seq"), scatter_dimension=0, tiled=True),
        lax.psum_scatter(grad_bias_c, ("dp", "seq"), scatter_dimension=0, tiled=True),
        lax.psum_scatter(grad_inner_w, ("dp", "seq"), scatter_dimension=0, tiled=True),
        lax.psum_scatter(grad_inner_b, ("dp", "seq"), scatter_dimension=0, tiled=True),
        lax.psum_scatter(grad_outer_w, ("dp", "seq"), scatter_dimension=0, tiled=True),
        lax.psum_scatter(grad_outer_b, ("dp", "seq"), scatter_dimension=0, tiled=True),
    )
    query_wb, key_wb, value_wb, out_wb = (mixing[2], mixing[3], mixing[4], mixing[5])
    cross_qwb, cross_kwb, cross_vwb, cross_owb = (mixing[8], mixing[9], mixing[10], mixing[11])
    grad_branch_b = grad_after_cross.astype(jnp.bfloat16)
    grad_cross_ow = weight_grad(cross_out, grad_branch_b)
    grad_cross_out = project_back(grad_branch_b, cross_owb).astype(jnp.bfloat16)
    grad_cq_raw, grad_ck_raw, grad_cv_raw = attend_back(
        cross_queries, cross_keys, cross_values, caption_mask, cross_lse, grad_cross_out
    )
    grad_cross_q = grad_cq_raw.astype(jnp.bfloat16)
    grad_ck_sum, grad_cv_sum = (
        lax.psum_scatter(
            grad_ck_raw.astype(jnp.bfloat16), "seq", scatter_dimension=1, tiled=True
        ).astype(jnp.float32),
        lax.psum_scatter(
            grad_cv_raw.astype(jnp.bfloat16), "seq", scatter_dimension=1, tiled=True
        ).astype(jnp.float32),
    )
    grad_ck_low = grad_ck_sum.astype(jnp.bfloat16)
    grad_cv_low = grad_cv_sum.astype(jnp.bfloat16)
    piece_len = grad_ck_sum.shape[1]
    caption_piece = lax.dynamic_slice_in_dim(caption, seq_index * piece_len, piece_len, 1)
    grad_cross_kw = weight_grad(caption_piece, grad_ck_low)
    grad_cross_vw = weight_grad(caption_piece, grad_cv_low)
    grad_caption = project_back(grad_ck_low, cross_kwb) + project_back(grad_cv_low, cross_vwb)
    row_count = encoder_all.shape[0]
    row_onehot = (image_row[:, None] == jnp.arange(row_count, dtype=jnp.int32)[None, :]).astype(
        jnp.float32
    )
    grad_rows = jnp.einsum("br,bsd->rsd", row_onehot, grad_caption, precision=lax.Precision.HIGHEST)
    caption_grad = lax.psum_scatter(
        grad_rows.astype(jnp.bfloat16), "dp", scatter_dimension=0, tiled=True
    ).astype(jnp.float32)
    grad_cross_qw = weight_grad(normed_b, grad_cross_q)
    grad_normed_b = project_back(grad_cross_q, cross_qwb)
    _, norm_b_back = jax.vjp(norm_rows, after_self, gain_b32, bias_b32)
    grad_self_part, grad_gain_b, grad_bias_b = norm_b_back(grad_normed_b)
    grad_after_self = grad_after_cross + grad_self_part
    grad_branch_a = grad_after_self.astype(jnp.bfloat16)
    grad_out_w = weight_grad(self_out, grad_branch_a)
    grad_self_out = project_back(grad_branch_a, out_wb).astype(jnp.bfloat16)
    keys_back, values_back = (keys_all, values_all)
    grad_q_raw, grad_k_raw, grad_v_raw = attend_back(
        queries, keys_back, values_back, causal, self_lse, grad_self_out
    )
    grad_k_sum, grad_v_sum = (
        lax.psum_scatter(
            grad_k_raw.astype(jnp.bfloat16), "seq", scatter_dimension=1, tiled=True
        ).astype(jnp.float32),
        lax.psum_scatter(
            grad_v_raw.astype(jnp.bfloat16), "seq", scatter_dimension=1, tiled=True
        ).astype(jnp.float32),
    )
    grad_q_low = grad_q_raw.astype(jnp.bfloat16)
    grad_k_low = grad_k_sum.astype(jnp.bfloat16)
    grad_v_low = grad_v_sum.astype(jnp.bfloat16)
    grad_query_w = weight_grad(normed_a, grad_q_low)
    grad_key_w = weight_grad(normed_a, grad_k_low)
    grad_value_w = weight_grad(normed_a, grad_v_low)
    grad_normed_a = (
        project_back(grad_q_low, query_wb)
        + project_back(grad_k_low, key_wb)
        + project_back(grad_v_low, value_wb)
    )
    _, norm_a_back = jax.vjp(norm_rows, inputs_f, gain_a32, bias_a32)
    grad_input_part, grad_gain_a, grad_bias_a = norm_a_back(grad_normed_a)
    image_grad = grad_after_self + grad_input_part
    mix_sums = (
        lax.psum_scatter(grad_gain_a, ("dp", "seq"), scatter_dimension=0, tiled=True),
        lax.psum_scatter(grad_bias_a, ("dp", "seq"), scatter_dimension=0, tiled=True),
        lax.psum_scatter(grad_query_w, ("dp", "seq"), scatter_dimension=0, tiled=True),
        lax.psum_scatter(grad_key_w, ("dp", "seq"), scatter_dimension=0, tiled=True),
        lax.psum_scatter(grad_value_w, ("dp", "seq"), scatter_dimension=0, tiled=True),
        lax.psum_scatter(grad_out_w, ("dp", "seq"), scatter_dimension=0, tiled=True),
        lax.psum_scatter(grad_gain_b, ("dp", "seq"), scatter_dimension=0, tiled=True),
        lax.psum_scatter(grad_bias_b, ("dp", "seq"), scatter_dimension=0, tiled=True),
        lax.psum_scatter(grad_cross_qw, ("dp", "seq"), scatter_dimension=0, tiled=True),
        lax.psum_scatter(grad_cross_kw, ("dp", "seq"), scatter_dimension=0, tiled=True),
        lax.psum_scatter(grad_cross_vw, ("dp", "seq"), scatter_dimension=0, tiled=True),
        lax.psum_scatter(grad_cross_ow, ("dp", "seq"), scatter_dimension=0, tiled=True),
    )
    return (
        block_out,
        image_grad,
        caption_grad,
        mix_sums[0],
        mix_sums[1],
        mix_sums[2],
        mix_sums[3],
        mix_sums[4],
        mix_sums[5],
        mix_sums[6],
        mix_sums[7],
        mix_sums[8],
        mix_sums[9],
        mix_sums[10],
        mix_sums[11],
        feed_sums[0],
        feed_sums[1],
        feed_sums[2],
        feed_sums[3],
        feed_sums[4],
        feed_sums[5],
    )


def block_device(
    images,
    encoder_states,
    image_row,
    image_seg,
    caption_seg,
    ln1_gain,
    ln1_bias,
    w_query,
    w_key,
    w_value,
    w_out,
    ln2_gain,
    ln2_bias,
    c_query,
    c_key,
    c_value,
    c_out,
    ln3_gain,
    ln3_bias,
    w_in,
    b_in,
    w_outer,
    b_outer,
    cotangent,
):
    core = lax.axis_index("seq")
    index = 2 * lax.axis_index("dp") + core
    width = images.shape[2]
    vectors = (ln1_gain, ln1_bias, ln2_gain, ln2_bias, ln3_gain, ln3_bias, b_outer)
    lanes = b_outer.shape[0]
    stack = jnp.tile(jnp.stack(vectors).astype(jnp.float32), (1, 128 // lanes))
    place_of = jnp.arange(128, dtype=jnp.int32) // lanes == index % (128 // lanes)
    packed = jnp.concatenate(
        [
            jnp.where(place_of[None], stack, 0.0),
            b_in.astype(jnp.float32)[None],
            jnp.zeros((8, 128), jnp.float32),
        ]
    )
    o = dict(
        zip(
            FRONT_OUT,
            front(
                [
                    w_query,
                    w_key,
                    w_value,
                    packed,
                    w_out,
                    encoder_states,
                    c_query,
                    c_key,
                    c_value,
                    c_out,
                    w_outer,
                    w_in,
                    images[0],
                    cotangent[0],
                    caption_seg,
                    image_row,
                    image_seg,
                ],
                1,
            ),
        )
    )
    (
        grad_inner_w,
        grad_outer_w,
        sums,
        grad_caption,
        block_out,
        grad_branch_b,
        grad_cross_q,
        grad_ck,
        grad_cv,
        grad_branch_a,
        grad_after_self,
        grad_self_out,
    ) = middle(
        [o["h3"], o["du"], o["act"], cotangent[0], o["w_in_all"], o["w_outer_all"]]
        + [o["c_out_all"], o["c_query_all"], o["w_out_all"], o["y2"], o["y1"]]
        + [o["cq"], o["ck"], o["cv"], o["c_key_all"], o["c_value_all"]]
        + [o["ok"], o["vec"], o["sums"]],
        2,
    )
    image_grad, *big, total = scatter_tail(
        [o["q"], o["k"], o["v"], o["heads"], o["lse"], grad_self_out, o["h1"], o["attn"]]
        + [grad_branch_a, o["h2"], grad_cross_q, o["cattn"], grad_branch_b, o["caption"]]
        + [grad_ck, grad_cv, o["wq"], o["wk"], o["wv"], images[0], grad_after_self, o["vec"], sums]
        + [grad_caption, jnp.broadcast_to(image_row.astype(jnp.float32)[:, None], (8, width))],
        4,
    )
    block_out, image_grad, grad_inner_w, grad_outer_w, *big, cut, share = emit(
        [block_out, image_grad, grad_inner_w, grad_outer_w, *big], total
    )
    small = [cut[i, :lanes] for i in range(7)]
    return (
        block_out[None],
        image_grad[None],
        big[5][None],
        small[0],
        small[1],
        big[6],
        big[7],
        big[8],
        big[0],
        small[2],
        small[3],
        big[1],
        big[3],
        big[4],
        big[2],
        small[4],
        small[5],
        grad_inner_w,
        share[0],
        grad_outer_w,
        small[6],
    )


def solution(mesh):
    in_specs = (
        P("dp", "seq", None),
        P("dp", None, None),
        P("dp"),
        P("dp"),
        P(),
        P(("dp", "seq")),
        P(("dp", "seq")),
        P(("dp", "seq"), None),
        P(("dp", "seq"), None),
        P(("dp", "seq"), None),
        P(("dp", "seq"), None),
        P(("dp", "seq")),
        P(("dp", "seq")),
        P(("dp", "seq"), None),
        P(("dp", "seq"), None),
        P(("dp", "seq"), None),
        P(("dp", "seq"), None),
        P(("dp", "seq")),
        P(("dp", "seq")),
        P(("dp", "seq"), None),
        P(("dp", "seq")),
        P(("dp", "seq"), None),
        P(("dp", "seq")),
        P("dp", "seq", None),
    )
    out_specs = (
        P("dp", "seq", None),
        P("dp", "seq", None),
        P("dp", "seq", None),
        P(("dp", "seq")),
        P(("dp", "seq")),
        P(("dp", "seq"), None),
        P(("dp", "seq"), None),
        P(("dp", "seq"), None),
        P(("dp", "seq"), None),
        P(("dp", "seq")),
        P(("dp", "seq")),
        P(("dp", "seq"), None),
        P(("dp", "seq"), None),
        P(("dp", "seq"), None),
        P(("dp", "seq"), None),
        P(("dp", "seq")),
        P(("dp", "seq")),
        P(("dp", "seq"), None),
        P(("dp", "seq")),
        P(("dp", "seq"), None),
        P(("dp", "seq")),
    )
    kernels = mesh.shape["dp"] == 16 and mesh.shape["seq"] == 2
    return jax.shard_map(
        block_device if kernels else per_device,
        mesh=mesh,
        in_specs=in_specs,
        out_specs=out_specs,
        check_vma=False,
    )
```

```python
import functools

import jax
import jax.numpy as jnp
from jax import lax
from jax.experimental import pallas as pl
from jax.experimental.pallas import tpu as pltpu
from jax.sharding import PartitionSpec as P

MESH = pl.DeviceIdType.MESH
ANY = pl.BlockSpec(memory_space=pl.ANY)


def place():
    dp, c = lax.axis_index("dp"), lax.axis_index("seq")
    x, y, z = dp % 2, (dp // 2) % 2, dp // 4
    return z, y, x, c


def flip(bit, on):
    return bit + on * (1 - 2 * bit)


def zxor(z, k):
    if k == 0:
        return z
    if k == 1:
        return z + 1 - 2 * (z % 2)
    if k == 2:
        return z + 2 - 4 * (z // 2)
    return 3 - z


def chip(z, y, x):
    return z * 4 + y * 2 + x


def greet(partners):
    barrier = pltpu.get_barrier_semaphore()
    for partner in partners:
        pl.semaphore_signal(barrier, inc=1, device_id=partner, device_id_type=MESH)
    pl.semaphore_wait(barrier, len(partners))


class Gather:
    def __init__(self, split, flat, own, full, send_sem, recv_sem, local_sem):
        self.split, self.flat, self.own, self.full = split, flat, own, full
        self.send_sem, self.recv_sem, self.local_sem = send_sem, recv_sem, local_sem
        z, y, x, c = place()
        self.z, self.y, self.x, self.c = z, y, x, c
        self.yx = {
            (0, 0): (y, x),
            (1, 0): (flip(y, 1 - c), flip(x, c)),
            (0, 1): (flip(y, c), flip(x, 1 - c)),
            (1, 1): (1 - y, 1 - x),
        }
        self.other = (chip(z, y, x), 1 - c)

    def partners(self):
        z, c = self.z, self.c
        return [(chip(zxor(z, k), self.y, self.x), c) for k in (1, 2, 3)] + [
            (chip(z, *self.yx[1, 0]), c),
            (chip(z, *self.yx[0, 1]), c),
            self.other,
        ]

    def block(self, g, k, way, core):
        rows = self.own[g].shape[0]
        r = chip(zxor(self.z, k), *self.yx[way])
        if g < self.split:
            return self.full[g].at[pl.ds(pl.multiple_of(2 * r * rows, rows), 2 * rows)]
        return self.full[g].at[pl.ds(pl.multiple_of((2 * r + core) * rows, rows), rows)]

    def remote(self, g, src, dst, to, idx):
        return pltpu.make_async_remote_copy(
            src_ref=src,
            dst_ref=dst,
            send_sem=self.send_sem.at[g, idx],
            recv_sem=self.recv_sem.at[g, idx],
            device_id=to,
            device_id_type=MESH,
        )

    def copy(self, g, src, k, way, core, to, idx):
        return self.remote(g, src, self.block(g, k, way, core), to, idx)

    def forward(self, g, k, way, src=None):
        z, c = self.z, self.c
        src = self.block(g, k, way, c) if src is None else src
        i1, i2 = way
        sends = []
        if i1 == 0 and i2 == 0:
            sends.append(((chip(z, *self.yx[1, 0]), c), 3 + k))
        if i2 == 0:
            sends.append(((chip(z, *self.yx[0, 1]), c), 7 + i1 * 4 + k))
        if g >= self.split:
            sends.append((self.other, 15 + i2 * 8 + i1 * 4 + k))
        for to, idx in sends:
            self.copy(g, src, k, way, c, to, idx).start()

    def half(self, g, core):
        rows, columns = self.own[g].shape
        columns //= 2
        at = pl.multiple_of((2 * chip(self.z, self.y, self.x) + self.c) * rows, rows)
        return (
            self.own[g].at[:, pl.ds(pl.multiple_of(core * columns, columns), columns)],
            self.full[g].at[pl.ds(at, rows)],
        )

    def keep(self, g):
        if g < self.split:
            src, dst = self.half(g, self.c)
        else:
            src, dst = self.own[g], self.block(g, 0, (0, 0), self.c)
        return pltpu.make_async_copy(src, dst, self.local_sem.at[g])

    def swap(self, g):
        src, dst = self.half(g, 1 - self.c)
        return self.remote(g, src, dst, self.other, 15)

    def start(self, g):
        self.keep(g).start()
        if g < self.split:
            self.swap(g).start()
        else:
            self.begin(g, self.own[g])

    def swapped(self, g):
        self.swap(g).wait_recv()
        self.keep(g).wait()
        self.begin(g, self.block(g, 0, (0, 0), self.c))

    def begin(self, g, src):
        for k in (1, 2, 3):
            to = (chip(zxor(self.z, k), self.y, self.x), self.c)
            self.copy(g, src, 0, (0, 0), self.c, to, k - 1).start()
        self.forward(g, 0, (0, 0), src)

    def spread(self, g, way):
        self.forward(g, 0, way)
        for k in (1, 2, 3):
            to = (chip(zxor(self.z, k), self.y, self.x), self.c)
            idx = 3 + k if way[1] == 0 else 7 + way[0] * 4 + k
            self.copy(g, self.block(g, 0, way, self.c), 0, way, self.c, to, idx).start()

    def pass_on(self, g, k, way, idx):
        self.arrive(g, k, way, self.c, idx)
        at = 15 + way[1] * 8 + way[0] * 4 + k
        self.copy(g, self.block(g, k, way, self.c), k, way, self.c, self.other, at).start()

    def arrive(self, g, k, way, core, idx):
        block = self.block(g, k, way, core)
        self.remote(g, block, block, self.other, idx).wait_recv()

    def along_z(self, g):
        if g in self.flat:
            self.arrive(g, 0, (1, 0), self.c, 3)
            self.spread(g, (1, 0))
            return
        for k in (1, 2, 3):
            self.arrive(g, k, (0, 0), self.c, k - 1)
            self.forward(g, k, (0, 0))

    def first(self, g):
        if g in self.flat:
            for i1 in range(2):
                self.arrive(g, 0, (i1, 1), self.c, 7 + i1 * 4)
                self.spread(g, (i1, 1))
            return
        for k in range(4):
            self.arrive(g, k, (1, 0), self.c, 3 + k)
            self.forward(g, k, (1, 0))

    def second(self, g):
        if g in self.flat:
            for k in (1, 2, 3):
                self.pass_on(g, k, (0, 0), k - 1)
                self.pass_on(g, k, (1, 0), 3 + k)
                self.pass_on(g, k, (0, 1), 7 + k)
                self.pass_on(g, k, (1, 1), 11 + k)
            return
        for i1 in range(2):
            for k in range(4):
                self.arrive(g, k, (i1, 1), self.c, 7 + i1 * 4 + k)
                self.forward(g, k, (i1, 1))

    def ready(self, g):
        if g >= self.split:
            for i2 in range(2):
                for i1 in range(2):
                    for k in range(4):
                        self.arrive(g, k, (i2, i1), 1 - self.c, 15 + i2 * 8 + i1 * 4 + k)
            self.keep(g).wait()

    def sent(self, g):
        if g < self.split:
            self.swap(g).wait_send()
        block = self.block(g, 0, (0, 0), self.c)
        for idx in range(15 if g < self.split else 31):
            self.remote(g, block, block, self.other, idx).wait_send()


AHEAD = 4


NT = (((1,), (1,)), ((), ()))
TN = (((0,), (0,)), ((), ()))
NN = (((1,), (0,)), ((), ()))


def mul(a, b, dims=NN):
    return lax.dot_general(a, b, dims, preferred_element_type=jnp.float32)


def low_lanes(rows):
    return lax.broadcasted_iota(jnp.int32, (rows, 128), 1) < 64


def self_fwd_pair(q_ref, k_ref, v_ref, lse_ref, put):
    length, b = q_ref.shape[0], 256
    low = low_lanes(b)
    row = lax.broadcasted_iota(jnp.int32, (b, b), 0)
    col = lax.broadcasted_iota(jnp.int32, (b, b), 1)
    for n in range(b, length + 1, b):
        q = q_ref[n - b : n, :] * jnp.asarray(0.125, jnp.bfloat16)

        def head(h, carry):
            mixed, lses = carry
            mine = low == (h == 0)
            s = mul(jnp.where(mine, q, jnp.zeros_like(q)), k_ref[0:n, :], NT)
            last = jnp.where(col <= row, s[:, n - b :], NEG_BIG)
            s = jnp.concatenate([s[:, : n - b], last], axis=1) if n > b else last
            top = jnp.max(s, axis=1, keepdims=True)
            e = jnp.exp(s - top)
            total = jnp.sum(e, axis=1, keepdims=True)
            value = mul(e.astype(jnp.bfloat16), v_ref[0:n, :]) / total
            lse = jnp.broadcast_to(top + jnp.log(total), (b, 128))
            return jnp.where(mine, value, mixed), jnp.where(mine, lse, lses)

        zero = jnp.zeros((b, 128), jnp.float32)
        mixed, lses = lax.fori_loop(0, 2, head, (zero, zero))
        put(n - b, mixed.astype(jnp.bfloat16))
        turned = lses.T
        lse_ref[0, :, n - b : n] = jnp.concatenate([turned[0:1], turned[64:65]], axis=0)


def self_bwd_pair(q_ref, k_ref, v_ref, o_ref, do_ref, lse_ref, dq_ref, dk_ref, dv_ref, acc):
    length, b = q_ref.shape[0], 256
    low = low_lanes(b)
    row = lax.broadcasted_iota(jnp.int32, (b, b), 0)
    col = lax.broadcasted_iota(jnp.int32, (b, b), 1)
    prod = do_ref[...].astype(jnp.float32) * o_ref[...].astype(jnp.float32)
    lane = lax.broadcasted_iota(jnp.int32, (8, 128), 1)
    head = lax.broadcasted_iota(jnp.int32, (8, 128), 0)
    pick = jnp.where(lane // 64 == head, 1.0, 0.0)
    inner = lax.dot_general(
        pick, prod, NT, precision=lax.Precision.HIGHEST, preferred_element_type=jnp.float32
    )
    acc[...] = jnp.zeros_like(acc)
    for at in range(0, length, b):
        k, v = k_ref[at : at + b, :], v_ref[at : at + b, :]
        qs, dos = q_ref[at:length, :], do_ref[at:length, :]
        dks, dvs = [], []
        for h, mine in enumerate((low, ~low)):
            km = jnp.where(mine, k, jnp.zeros_like(k))
            vm = jnp.where(mine, v, jnp.zeros_like(v))
            s = mul(km * jnp.asarray(0.125, jnp.bfloat16), qs, NT)
            w = jnp.exp(s - lse_ref[0, h : h + 1, at:length])
            first = jnp.where(row <= col, w[:, :b], 0.0)
            w = jnp.concatenate([first, w[:, b:]], axis=1) if length - at > b else first
            ds = (w * (mul(vm, dos, NT) - inner[h : h + 1, at:length])).astype(jnp.bfloat16)
            dvs.append(mul(w.astype(jnp.bfloat16), dos))
            dks.append(mul(ds, qs))
            acc[at:length, :] += mul(ds, km, TN)
        dk_ref[at : at + b, :] = (jnp.where(low, dks[0], dks[1]) * 0.125).astype(jnp.bfloat16)
        dv_ref[at : at + b, :] = jnp.where(low, dvs[0], dvs[1]).astype(jnp.bfloat16)
    dq_ref[...] = (acc[...] * 0.125).astype(jnp.bfloat16)


def cross_fwd_body(q_ref, k_ref, v_ref, ok_ref, o_ref):
    low = low_lanes(q_ref.shape[0])
    q = q_ref[...] * jnp.asarray(0.125, jnp.bfloat16)
    mixed = []
    for mine in (low, ~low):
        s = mul(jnp.where(mine, q, jnp.zeros_like(q)), k_ref[...], NT)
        s = jnp.where(ok_ref[0:1, :] > 0, s, NEG_BIG)
        e = jnp.exp(s - jnp.max(s, axis=1, keepdims=True))
        total = jnp.sum(e, axis=1, keepdims=True)
        mixed.append(mul(e.astype(jnp.bfloat16), v_ref[...]) / total)
    o_ref[...] = jnp.where(low, mixed[0], mixed[1]).astype(jnp.bfloat16)


def cross_bwd_body(q_ref, k_ref, v_ref, ok_ref, do_ref, dq_ref, dk_ref, dv_ref):
    keys = k_ref.shape[0]
    low = low_lanes(keys)
    wide = low_lanes(q_ref.shape[0])
    q, do, k, v = q_ref[...], do_ref[...], k_ref[...], v_ref[...]
    dqs, dks, dvs = [], [], []
    for mine in (low, ~low):
        km = jnp.where(mine, k, jnp.zeros_like(k))
        vm = jnp.where(mine, v, jnp.zeros_like(v))
        s = mul(km * jnp.asarray(0.125, jnp.bfloat16), q, NT)
        s = jnp.where(ok_ref[:, 0:1] > 0, s, NEG_BIG)
        e = jnp.exp(s - jnp.max(s, axis=0, keepdims=True))
        w = e / jnp.sum(e, axis=0, keepdims=True)
        dw = mul(vm, do, NT)
        inner = jnp.sum(dw * w, axis=0, keepdims=True)
        ds = (w * (dw - inner)).astype(jnp.bfloat16)
        dvs.append(mul(w.astype(jnp.bfloat16), do))
        dks.append(mul(ds, q))
        dqs.append(mul(ds, km, TN))
    dq_ref[...] = (jnp.where(wide, dqs[0], dqs[1]) * 0.125).astype(jnp.bfloat16)
    dk_ref[...] = (jnp.where(low, dks[0], dks[1]) * 0.125).astype(jnp.bfloat16)
    dv_ref[...] = jnp.where(low, dvs[0], dvs[1]).astype(jnp.bfloat16)


class Scatter:
    def __init__(self, late, tile, got, part, from_late, out, sems, credit):
        self.late, self.tile, self.got = late, tile, got
        self.slots, self.count, self.free = credit
        self.part, self.from_late, self.out = part, from_late, out
        self.send_sem, self.recv_sem = sems
        z, y, x, c = place()
        self.z, self.y, self.x, self.c = z, y, x, c
        self.other = (chip(z, y, x), 1 - c)

    def ways(self, core):
        y, x = self.y, self.x
        return [
            flip(y, core * i1 + (1 - core) * i2) * 2 + flip(x, (1 - core) * i1 + core * i2)
            for i1 in range(2)
            for i2 in range(2)
        ]

    def partners(self):
        z, c = self.z, self.c
        way = self.ways(c)
        return [(zxor(z, k) * 4 + way[0], c) for k in (1, 2, 3)] + [
            (z * 4 + way[2], c),
            (z * 4 + way[1], c),
            self.other,
        ]

    def mine(self, u, j):
        way = self.ways(self.c)[j]
        return self.tile(u).at[:, way] if self.late(u) else self.tile(u).at[:, way, self.c]

    def remote(self, src, dst, u, idx, to):
        return pltpu.make_async_remote_copy(
            src_ref=src,
            dst_ref=dst,
            send_sem=self.send_sem.at[u, idx],
            recv_sem=self.recv_sem.at[u, idx],
            device_id=to,
            device_id_type=MESH,
        )

    def to_core(self, u, j):
        c = self.c
        src = self.tile(u).at[:, self.ways(1 - c)[j], 1 - c]
        return self.remote(src, self.got(u, 0).at[j], u, j, self.other)

    def to_first(self, u, i):
        to = (self.z * 4 + self.ways(self.c)[2], self.c)
        return self.remote(self.mine(u, 2 + i), self.got(u, 1).at[i], u, 4 + i, to)

    def to_second(self, u):
        to = (self.z * 4 + self.ways(self.c)[1], self.c)
        return self.remote(self.mine(u, 1), self.got(u, 2), u, 6, to)

    def to_z(self, u, k):
        zk = zxor(self.z, k)
        to = (zk * 4 + self.ways(self.c)[0], self.c)
        return self.remote(self.mine(u, 0).at[zk], self.got(u, 3).at[k - 1], u, 6 + k, to)

    def to_late(self, u):
        rows = self.part(u).shape[0] // 2
        theirs = pl.ds(pl.multiple_of((1 - self.c) * rows, rows), rows)
        return self.remote(self.part(u).at[theirs], self.from_late(u), u, 0, self.other)

    def add(self, u, j, term):
        mine = self.mine(u, j)

        @pl.loop(0, 4)
        def _(i):
            mine[i] = mine[i] + term[i]

    def step0(self, u):
        if self.late(u):
            return
        if u >= self.slots:
            pl.semaphore_wait(self.free, 1)
        if not self.late(u):
            for j in (2, 3, 0, 1):
                self.to_core(u, j).start()

    def step1(self, u):
        for j in (2, 3, 0, 1):
            if not self.late(u):
                self.to_core(u, j).wait_recv()
                self.add(u, j, self.got(u, 0).at[j])
            if j > 1:
                self.to_first(u, j - 2).start()
        if not self.late(u) and u < self.count - self.slots:
            pl.semaphore_signal(self.free, inc=1, device_id=self.other, device_id_type=MESH)

    def step2(self, u):
        for i in (1, 0):
            self.to_first(u, i).wait_recv()
            self.add(u, i, self.got(u, 1).at[i])
            if i == 1:
                self.to_second(u).start()

    def step3(self, u):
        self.to_second(u).wait_recv()
        self.add(u, 0, self.got(u, 2))
        for k in (2, 3, 1):
            self.to_z(u, k).start()

    def step4(self, u):
        got = self.got(u, 3)
        for k in (1, 2, 3):
            self.to_z(u, k).wait_recv()
        total = self.mine(u, 0)[self.z].astype(jnp.float32) + got[0].astype(jnp.float32)
        total = total + (got[1].astype(jnp.float32) + got[2].astype(jnp.float32))
        if self.late(u):
            self.part(u)[...] = total
            self.to_late(u).start()
        else:
            self.out(u, total, None)

    def step5(self, u):
        if self.late(u):
            rows = self.part(u).shape[0] // 2
            self.to_late(u).wait_recv()
            mine = self.part(u)[pl.ds(pl.multiple_of(self.c * rows, rows), rows)]
            self.out(u, mine, self.from_late(u)[...])

    def sent(self, u):
        if not self.late(u):
            for j in range(4):
                self.to_core(u, j).wait_send()
        for i in range(2):
            self.to_first(u, i).wait_send()
        self.to_second(u).wait_send()
        for k in (1, 2, 3):
            self.to_z(u, k).wait_send()

    def slot(self, t, order, gap=2):
        for lag, step in (
            (1, self.step1),
            (1 + gap, self.step2),
            (1 + 2 * gap, self.step3),
            (1 + 3 * gap, self.step4),
            (2 + 3 * gap, self.step5),
        ):
            if 0 <= t - lag < len(order):
                step(order[t - lag])


LAG = 2
DEPTH = 2 + 3 * LAG


def turn(src, dst):
    @pl.loop(0, src.shape[1] // 128)
    def _(i):
        at = pl.multiple_of(i * 128, 128)
        dst[pl.ds(at, 128), :] = src[:, pl.ds(at, 128)].T


def product(rows, right, tile):
    @pl.loop(0, 2)
    def _(i):
        value = mul(rows(i), right[...]).astype(tile.dtype)
        tile[pl.ds(2 * i, 2)] = value.reshape((2, *tile.shape[1:]))


def middle_body(
    h3, du, act, gm, w_in, w_outer, c_out, c_query, w_out, y2, y1, cq, ck, cv, c_key, c_value, ok, vec, sums_in, *refs
):
    out_in, out_outer, sums_out, cap_out, block_out, db2_out, dcq_out, dck_out, dcv_out, da_out, dy1_out, do_out = refs[:12]
    (h3_v, du_v, act_v, gm_v, left, left_act, tiles, got0, got1, got2, got3) = refs[12:23]
    (w_v, acc, y_v, dy_v, db_v, da_v, dc_v, cq_v, dcq_v, kv_v, dkv_v, cap_v) = refs[23:35]
    send_sem, recv_sem, load_sem, w_sem, out_sem, free_sem = refs[35:]
    units, depth, slots = 8, tiles.shape[0], got0.shape[0]
    rows, width = gm_v.shape
    step = 128

    def out(u, total, _):
        if u < 4:
            out_in[:, u * 1024 : (u + 1) * 1024] = total
        else:
            out_outer[(u - 4) * 32 : (u - 3) * 32, :] = total

    got = (got0, got1, got2, got3)
    ring = Scatter(
        lambda u: False,
        lambda u: tiles.at[u % depth],
        lambda u, i: got[i].at[u % slots if i == 0 else u],
        None,
        None,
        out,
        (send_sem, recv_sem),
        (slots, units, free_sem),
    )
    pairs = {
        "h3": (h3, h3_v),
        "du": (du, du_v),
        "act": (act, act_v),
        "gm": (gm, gm_v),
        "y2": (y2, y_v),
        "cq": (cq, cq_v),
        "ck": (ck, kv_v.at[0]),
        "cv": (cv, kv_v.at[1]),
        "y1": (y1, y_v),
    }
    loads = {
        name: pltpu.make_async_copy(src, dst, load_sem.at[i])
        for i, (name, (src, dst)) in enumerate(pairs.items())
    }
    parts = [w_in.at[:, pl.ds(i * 1024, 1024)] for i in range(4)]
    parts += [c_out, c_query, c_key, c_value, w_out]
    parts += [w_outer.at[pl.ds(i * 1024, 1024)] for i in range(4)]
    weights = [
        pltpu.make_async_copy(part, w_v.at[n % 2], w_sem.at[n % 2]) for n, part in enumerate(parts)
    ]
    stores = [
        pltpu.make_async_copy(src, dst, out_sem.at[i])
        for i, (src, dst) in enumerate(
            (
                (db_v, db2_out),
                (dcq_v, dcq_out),
                (dkv_v.at[0], dck_out),
                (dkv_v.at[1], dcv_out),
                (da_v, da_out),
                (dy_v, dy1_out),
                (dc_v, do_out),
                (h3_v, block_out),
            )
        )
    ]

    def use(n, work):
        weights[n].wait()
        work(w_v.at[n % 2])
        if n + 2 < len(weights):
            weights[n + 2].start()

    def over_rows(work):
        @pl.loop(0, rows // step)
        def _(i):
            work(pl.ds(i * step, step))

    def make(u):
        if u >= depth:
            ring.sent(u - depth)
        tile = tiles.at[u % depth]
        if u < 4:
            right = du_v.at[:, u * 1024 : (u + 1) * 1024]
            product(lambda i: left[pl.ds(i * 512, 512), :], right, tile)
        else:
            product(
                lambda i, b=u - 4: left_act[pl.ds(i * 16, 16), b].reshape(512, 512), gm_v, tile
            )
        ring.step0(u)

    def turn_act(t):
        @pl.loop(t * 8, t * 8 + 8)
        def _(r):
            at = pl.multiple_of(r * 128, 128)
            left_act[r] = act_v[:, pl.ds(at, 128)].T.reshape(4, 32, 512)

    def add_dh3(j):
        def work(w):
            def body(at):
                term = mul(du_v[at, j * 1024 : (j + 1) * 1024], w[...], NT)
                acc[at, :] = term if j == 0 else acc[at, :] + term

            over_rows(body)

        use(j, work)

    def norm3():
        loads["y2"].wait()
        sums_out[...] = sums_in[...]

        def body(at):
            value = y_v[at, :]
            grads, dgain, dbias = norm_back(value, vec[4:5, :], acc[at, :])
            dy = gm_v[at, :].astype(jnp.float32) + grads
            dy_v[at, :] = dy
            db_v[at, :] = dy.astype(jnp.bfloat16)
            acc[at, :] = value + vec[6:7, :]
            sums_out[4:5, :] += dgain
            sums_out[5:6, :] += dbias

        over_rows(body)
        stores[0].start()
        loads["y1"].start()

    def back_out(w):
        def body(at):
            dc_v[at, :] = mul(db_v[at, :], w[...], NT).astype(jnp.bfloat16)

        over_rows(body)

    def cross(lo, hi):
        @pl.loop(lo, hi)
        def _(i):
            at = pl.ds(pl.multiple_of(i * 128, 128), 128)
            cross_bwd_body(
                cq_v.at[:, at],
                kv_v.at[0, :, at],
                kv_v.at[1, :, at],
                ok.at[1],
                dc_v.at[:, at],
                dcq_v.at[:, at],
                dkv_v.at[0, :, at],
                dkv_v.at[1, :, at],
            )

    def norm2(w):
        loads["y1"].wait()

        def body(at):
            dh = mul(dcq_v[at, :], w[...], NT)
            grads, dgain, dbias = norm_back(y_v[at, :], vec[2:3, :], dh)
            dy = dy_v[at, :] + grads
            dy_v[at, :] = dy
            da_v[at, :] = dy.astype(jnp.bfloat16)
            sums_out[2:3, :] += dgain
            sums_out[3:4, :] += dbias

        over_rows(body)
        stores[4].start()
        stores[5].start()

    def back_key(w):
        cap_v[...] = mul(dkv_v[0], w[...], NT)

    def back_value(w):
        cap_out[...] = (cap_v[...] + mul(dkv_v[1], w[...], NT)).astype(jnp.bfloat16)

    def back_self(w):
        def body(at):
            dc_v[at, :] = mul(da_v[at, :], w[...], NT).astype(jnp.bfloat16)

        over_rows(body)
        stores[6].start()

    def add_out(j):
        def work(w):
            def body(at):
                term = acc[at, :] + mul(act_v[at, j * 1024 : (j + 1) * 1024], w[...])
                if j < 3:
                    acc[at, :] = term
                else:
                    h3_v[at, :] = term.astype(jnp.bfloat16)

            over_rows(body)

        use(9 + j, work)

    for name in ("h3", "du", "gm", "act", "y2", "cq", "ck", "cv"):
        loads[name].start()
    weights[0].start()
    weights[1].start()
    greet(ring.partners())
    loads["h3"].wait()
    turn(h3_v, left)
    loads["du"].wait()
    make(0)
    make(1)
    add_dh3(0)
    ring.slot(1, range(1), 1)
    make(2)
    loads["act"].wait()
    turn_act(0)
    ring.slot(2, range(2), 1)
    add_dh3(1)
    add_dh3(2)
    make(3)
    ring.slot(3, range(3), 1)
    turn_act(1)
    add_dh3(3)
    loads["gm"].wait()
    norm3()
    ring.slot(4, range(4), 1)
    turn_act(2)
    turn_act(3)
    make(4)
    use(4, back_out)
    ring.slot(5, range(5), 1)
    make(5)
    for name in ("cq", "ck", "cv"):
        loads[name].wait()
    cross(0, 4)
    ring.slot(6, range(6), 1)
    make(6)
    cross(4, 8)
    for i in (1, 2, 3):
        stores[i].start()
    ring.slot(7, range(7), 1)
    make(7)
    use(5, norm2)
    ring.slot(8, range(8), 1)
    use(6, back_key)
    use(7, back_value)
    use(8, back_self)
    ring.slot(9, range(units), 1)
    add_out(0)
    add_out(1)
    ring.slot(10, range(units), 1)
    add_out(2)
    add_out(3)
    stores[7].start()
    ring.slot(11, range(units), 1)
    ring.slot(12, range(units), 1)
    for u in range(max(units - depth, 0), units):
        ring.sent(u)
    for store in stores:
        store.wait()


def middle(operands, collective_id):
    depth, bf, f32, vm = 5, jnp.bfloat16, jnp.float32, pltpu.VMEM
    shape = jax.ShapeDtypeStruct
    rows = (512, 1024)
    inside = pl.BlockSpec(memory_space=pltpu.VMEM)
    return pl.pallas_call(
        middle_body,
        out_shape=[
            shape((32, 4096), f32),
            shape((128, 1024), f32),
            shape((16, 1024), f32),
            shape((128, 1024), bf),
            shape(rows, bf),
            shape(rows, bf),
            shape(rows, bf),
            shape((128, 1024), bf),
            shape((128, 1024), bf),
            shape(rows, bf),
            shape(rows, f32),
            shape(rows, bf),
        ],
        in_specs=[ANY] * 16 + [inside] * 3,
        out_specs=[inside] * 4 + [ANY] * 8,
        scratch_shapes=[
            vm(rows, bf),
            vm((512, 4096), bf),
            vm((512, 4096), bf),
            vm(rows, bf),
            vm((1024, 512), bf),
            vm((32, 4, 32, 512), bf),
            vm((depth, 4, 4, 2, 32, 1024), bf),
            vm((4, 4, 4, 32, 1024), bf),
            vm((8, 2, 4, 32, 1024), bf),
            vm((8, 4, 32, 1024), bf),
            vm((8, 3, 32, 1024), bf),
            vm((2, 1024, 1024), bf),
            vm(rows, f32),
            vm(rows, f32),
            vm(rows, f32),
            vm(rows, bf),
            vm(rows, bf),
            vm(rows, bf),
            vm(rows, bf),
            vm(rows, bf),
            vm((2, 128, 1024), bf),
            vm((2, 128, 1024), bf),
            vm((128, 1024), f32),
            pltpu.SemaphoreType.DMA((8, 10)),
            pltpu.SemaphoreType.DMA((8, 10)),
            pltpu.SemaphoreType.DMA((9,)),
            pltpu.SemaphoreType.DMA((2,)),
            pltpu.SemaphoreType.DMA((8,)),
            pltpu.SemaphoreType.REGULAR,
        ],
        compiler_params=pltpu.CompilerParams(
            collective_id=collective_id,
            has_side_effects=True,
            vmem_limit_bytes=59 * 1024 * 1024,
        ),
        name="middle",
    )(*operands)


def tail_body(q, k, v, o, lse, grad, h1, attn, da, h2, dcq, cattn, db2, e, dck, dcv, wq, wk, wv, x, dy1, gain, sums, cap, row, image_out, *refs):
    outs, total_out, refs = refs[:9], refs[9], refs[10:]
    (q_v, k_v, v_v, o_v, lse_v, do_v, cap_v, a_v, r_v, e_v, dc_v, x_v, dx_v, gain_v, sum_v) = refs[:15]
    (acc, dq_v, dk_v, dv_v, left, left1, left_e, tiles, late_tiles) = refs[15:24]
    big, late = refs[24:28], refs[28:31]
    part, from_late, give_v, take_v, got_sum = refs[31:36]
    send_sem, recv_sem, load_sem, pair_send, pair_recv, keep_sem, row_sem, sum_send, sum_recv, free_sem = refs[36:]
    normal, units, depth, slots = 14, 20, tiles.shape[0], refs[24].shape[0]
    dp, c = lax.axis_index("dp"), lax.axis_index("seq")
    length, width = q_v.shape
    pairs, rows = width // 128, length // 2
    mine = pl.ds(pl.multiple_of(c * rows, rows), rows)
    theirs = pl.ds(pl.multiple_of((1 - c) * rows, rows), rows)

    def out(u, total, other):
        what, h = divmod(u, 2)
        lanes = slice(h * 512, (h + 1) * 512)
        if what < 5:
            outs[what][:, lanes] = total
        elif u < normal:
            outs[5][(what - 5) * 32 : (what - 4) * 32, lanes] = total
        else:
            at = pl.multiple_of(c * 512 + h * 256, 128)
            outs[what - 1][:, pl.ds(at, 256)] = total
            at = pl.multiple_of((1 - c) * 512 + h * 256, 128)
            outs[what - 1][:, pl.ds(at, 256)] = other

    ring = Scatter(
        lambda u: u >= normal,
        lambda u: tiles.at[u % depth] if u < normal else late_tiles.at[u - normal],
        lambda u, i: late[i - 1].at[u - normal]
        if u >= normal
        else big[i].at[u % slots if i == 0 else u],
        lambda u: part.at[u - normal],
        lambda u: from_late.at[u - normal],
        out,
        (send_sem, recv_sem),
        (slots, normal, free_sem),
    )

    def load(i, src, dst):
        return pltpu.make_async_copy(src, dst, load_sem.at[i])

    loads = {
        "a0": load(0, attn, a_v.at[0]),
        "r0": load(1, da, r_v.at[0]),
        "q": load(2, q, q_v),
        "k": load(3, k, k_v),
        "v": load(4, v, v_v),
        "o": load(5, o, o_v),
        "lse": load(6, lse, lse_v),
        "a1": load(7, h2, a_v.at[1]),
        "r1": load(8, dcq, r_v.at[1]),
        "a2": load(9, cattn, a_v.at[0]),
        "r2": load(10, db2, r_v.at[0]),
        "e": load(11, e, e_v),
        "ck": load(12, dck, dc_v.at[0]),
        "cv": load(13, dcv, dc_v.at[1]),
        "h0": load(14, h1.at[pl.ds(0, 512)], a_v.at[1]),
        "h1": load(22, h1.at[pl.ds(512, 512)], a_v.at[0]),
        "cap": load(23, cap, cap_v),
        "wq": load(15, wq, q_v),
        "wk": load(16, wk, k_v),
        "wv": load(17, wv, v_v),
        "x": load(18, x, x_v),
        "dy1": load(19, dy1, dx_v),
        "gain": load(20, gain.at[pl.ds(0, 8)], gain_v),
        "sums": load(21, sums, sum_v),
    }

    def lane(i, core):
        return pl.ds(pl.multiple_of(core * width + i * 128, 128), 128)

    def keep(i):
        return pltpu.make_async_copy(grad.at[:, lane(i, c)], do_v.at[i, mine], keep_sem.at[i])

    def give(i):
        return pltpu.make_async_remote_copy(
            src_ref=grad.at[:, lane(i, 1 - c)],
            dst_ref=do_v.at[i, mine],
            send_sem=pair_send.at[i],
            recv_sem=pair_recv.at[i],
            device_id=ring.other,
            device_id_type=MESH,
        )

    for name in ("a0", "r0", "a1", "r1"):
        loads[name].start()
    greet(ring.partners())
    for i in range(pairs):
        give(i).start()
        keep(i).start()
    for name in ("q", "k", "v", "o", "lse", "e", "ck", "cv", "cap", "x", "dy1", "gain", "sums"):
        loads[name].start()

    def pair(i):
        keep(i).wait()
        give(i).wait()
        at = pl.ds(i * 128, 128)
        self_bwd_pair(
            q_v.at[:, at],
            k_v.at[:, at],
            v_v.at[:, at],
            o_v.at[:, at],
            do_v.at[i],
            lse_v.at[pl.ds(i, 1)],
            dq_v.at[:, at],
            dk_v.at[:, at],
            dv_v.at[:, at],
            acc,
        )

    def turn_late():
        loads["h0"].wait()
        turn(a_v.at[1], left1.at[:, pl.ds(0, 512)])
        loads["h1"].wait()
        turn(a_v.at[0], left1.at[:, pl.ds(512, 512)])

    def make(u):
        if depth <= u < normal:
            ring.sent(u - depth)
        what, h = divmod(u, 2)
        lanes = slice(h * 512, (h + 1) * 512)
        if what < 3:
            slot = what % 2
            if h == 0:
                loads[f"a{what}"].wait()
                loads[f"r{what}"].wait()
                turn(a_v.at[slot], left)
            right = r_v.at[slot, :, lanes]
            product(lambda i: left[pl.ds(i * 512, 512), :], right, tiles.at[u % depth])
            if h == 1:
                for name in (("a2", "r2"), ("h0",), ("h1",))[what]:
                    loads[name].start()
        elif what < 5:
            if what == 3 and h == 0:
                loads["e"].wait()
                loads["ck"].wait()
                loads["cv"].wait()
                turn(e_v, left_e)
            right = dc_v.at[what - 3, :, lanes]
            product(lambda i: left_e[pl.ds(i * 512, 512), :], right, tiles.at[u % depth])
        elif u < normal:
            if what == 5 and h == 0:
                loads["cap"].wait()
            tile = tiles.at[u % depth]
            for core in range(2):
                at = core * 64 + (what - 5) * 32
                block = cap_v[at : at + 32, lanes]

                @pl.loop(0, 16)
                def _(i, core=core, block=block):
                    hit = row[0:1, 0:512] == i.astype(jnp.float32)
                    tile[i // 4, i % 4, core] = jnp.where(hit, block, jnp.zeros_like(block))

        else:
            right = (dq_v, dk_v, dv_v)[what - 7].at[:, h * 256 : (h + 1) * 256]
            product(lambda i: left1[pl.ds(i * 512, 512), :], right, late_tiles.at[u - normal])
        ring.step0(u)

    swap = pltpu.make_async_remote_copy(
        src_ref=give_v,
        dst_ref=take_v,
        send_sem=row_sem.at[0],
        recv_sem=row_sem.at[1],
        device_id=ring.other,
        device_id_type=MESH,
    )

    def back(at):
        total = mul(dq_v[at, :], q_v[...], NT) + mul(dk_v[at, :], k_v[...], NT)
        return total + mul(dv_v[at, :], v_v[...], NT)

    def give_rows():
        for name in ("wq", "wk", "wv"):
            loads[name].wait()

        @pl.loop(0, rows // 128)
        def _(i):
            at = pl.ds(pl.multiple_of((1 - c) * rows + i * 128, 128), 128)
            give_v[pl.ds(i * 128, 128), :] = back(at).astype(jnp.bfloat16)

        swap.start()

    def take_rows():
        swap.wait_recv()
        for name in ("x", "dy1", "gain", "sums"):
            loads[name].wait()
        step = 128

        @pl.loop(0, rows // step)
        def _(i):
            at = pl.ds(i * step, step)
            whole = pl.ds(pl.multiple_of(c * rows + i * step, step), step)
            dh = back(whole) + take_v[at, :].astype(jnp.float32)
            grads, dgain, dbias = norm_back(x_v[at, :].astype(jnp.float32), gain_v[0:1, :], dh)
            dx_v[at, :] = dx_v[at, :] + grads
            sum_v[0:1, :] = sum_v[0:1, :] + dgain
            sum_v[1:2, :] = sum_v[1:2, :] + dbias

    write = pltpu.make_async_copy(dx_v, image_out, row_sem.at[2])

    way = ring.ways(c)
    peers = [
        [ring.other],
        [(ring.z * 4 + way[2], c)],
        [(ring.z * 4 + way[1], c)],
        [(zxor(ring.z, n) * 4 + way[0], c) for n in (1, 2, 3)],
    ]

    def sum_send_of(s, n):
        return pltpu.make_async_remote_copy(
            src_ref=sum_v if s == 0 else got_sum.at[5 + s],
            dst_ref=got_sum.at[s + n],
            send_sem=sum_send.at[s + n],
            recv_sem=sum_recv.at[s + n],
            device_id=peers[s][n],
            device_id_type=MESH,
        )

    def start_sum(s):
        for n in range(len(peers[s])):
            sum_send_of(s, n).start()

    def take_sum(s):
        total = sum_v[...] if s == 0 else got_sum[5 + s]
        for n in range(len(peers[s])):
            sum_send_of(s, n).wait_recv()
            total = total + got_sum[s + n]
        if s == 3:
            total_out[...] = total
        else:
            got_sum[6 + s] = total
            start_sum(s + 1)

    def start_pairs():
        for name in ("q", "k", "v", "o", "lse"):
            loads[name].wait()
        pair(0)

    def end_pairs():
        pair(pairs - 1)
        for name in ("wq", "wk", "wv"):
            loads[name].start()

    def own_rows():
        take_rows()
        write.start()
        start_sum(0)

    order = [*range(12), *range(normal, units), *range(12, normal)]
    tasks = {
        1: [start_pairs],
        3: [lambda: pair(1)],
        5: [lambda: pair(2)],
        7: [end_pairs],
        9: [turn_late],
        10: [give_rows],
        12: [own_rows],
        14: [lambda: take_sum(0)],
        16: [lambda: take_sum(1)],
        18: [lambda: take_sum(2)],
        20: [lambda: take_sum(3)],
    }
    for t in range(units + 3 + 3 * LAG):
        if t < units:
            make(order[t])
        ring.slot(t, order)
        for task in tasks.get(t, ()):
            task()
    for u in range(normal - depth, units):
        ring.sent(u)
    for u in range(normal, units):
        ring.to_late(u).wait_send()
    swap.wait_send()
    write.wait()
    for s in range(4):
        for n in range(len(peers[s])):
            sum_send_of(s, n).wait_send()


def norm_back(value, gain, dh):
    center = value - jnp.mean(value, axis=1, keepdims=True)
    r = lax.rsqrt(jnp.mean(center * center, axis=1, keepdims=True) + EPSILON)
    hat = center * r
    dhg = dh * gain
    grads = r * (
        dhg
        - jnp.mean(dhg, axis=1, keepdims=True)
        - hat * jnp.mean(dhg * hat, axis=1, keepdims=True)
    )
    return grads, jnp.sum(dh * hat, axis=0, keepdims=True), jnp.sum(dh, axis=0, keepdims=True)


def scatter_tail(operands, collective_id):
    bf, f32, depth = jnp.bfloat16, jnp.float32, DEPTH
    vm = pltpu.VMEM
    outs = [jax.ShapeDtypeStruct((512, 1024), f32)] + [
        jax.ShapeDtypeStruct((64 if i == 5 else 32, 1024), f32) for i in range(9)
    ]
    outs.append(jax.ShapeDtypeStruct((16, 1024), f32))
    return pl.pallas_call(
        tail_body,
        out_shape=outs,
        in_specs=[ANY] * (len(operands) - 1) + [pl.BlockSpec(memory_space=pltpu.VMEM)],
        out_specs=[ANY] + [pl.BlockSpec(memory_space=pltpu.VMEM)] * 10,
        scratch_shapes=[
            vm((1024, 512), bf),
            vm((1024, 512), bf),
            vm((1024, 512), bf),
            vm((1024, 512), bf),
            vm((4, 2, 1024), f32),
            vm((4, 1024, 128), bf),
            vm((128, 1024), bf),
            vm((2, 512, 1024), bf),
            vm((2, 512, 1024), bf),
            vm((128, 1024), bf),
            vm((2, 128, 1024), bf),
            vm((512, 1024), bf),
            vm((512, 1024), f32),
            vm((8, 1024), f32),
            vm((16, 1024), f32),
            vm((1024, 128), f32),
            vm((1024, 512), bf),
            vm((1024, 512), bf),
            vm((1024, 512), bf),
            vm((1024, 512), bf),
            vm((1024, 1024), bf),
            vm((1024, 128), bf),
            vm((depth, 4, 4, 2, 32, 512), bf),
            vm((6, 4, 4, 64, 256), bf),
            vm((6, 4, 4, 32, 512), bf),
            vm((14, 2, 4, 32, 512), bf),
            vm((14, 4, 32, 512), bf),
            vm((14, 3, 32, 512), bf),
            vm((6, 2, 4, 64, 256), bf),
            vm((6, 4, 64, 256), bf),
            vm((6, 3, 64, 256), bf),
            vm((6, 64, 256), f32),
            vm((6, 32, 256), f32),
            vm((512, 1024), bf),
            vm((512, 1024), bf),
            vm((9, 16, 1024), f32),
            pltpu.SemaphoreType.DMA((20, 10)),
            pltpu.SemaphoreType.DMA((20, 10)),
            pltpu.SemaphoreType.DMA((24,)),
            pltpu.SemaphoreType.DMA((4,)),
            pltpu.SemaphoreType.DMA((4,)),
            pltpu.SemaphoreType.DMA((4,)),
            pltpu.SemaphoreType.DMA((3,)),
            pltpu.SemaphoreType.DMA((6,)),
            pltpu.SemaphoreType.DMA((6,)),
            pltpu.SemaphoreType.REGULAR,
        ],
        compiler_params=pltpu.CompilerParams(
            collective_id=collective_id,
            has_side_effects=True,
            vmem_limit_bytes=59 * 1024 * 1024,
        ),
        name="scatter_tail",
    )(*operands)


def norm_fwd(value, gain, shift):
    center = value - jnp.mean(value, axis=1, keepdims=True)
    spread = jnp.mean(center * center, axis=1, keepdims=True)
    return center * lax.rsqrt(spread + EPSILON) * gain + shift


GELU_IN = 0.7978845608028654
GELU_CUBE = 0.044715


def gelu_both(u):
    square = u * u
    t = jnp.tanh(GELU_IN * (u + GELU_CUBE * (square * u)))
    half = 0.5 * (1.0 + t)
    slope = half + 0.5 * u * (1.0 - t * t) * (GELU_IN * (1.0 + 3.0 * GELU_CUBE * square))
    return u * half, slope


FRONT_IN = (
    "w_query",
    "w_key",
    "w_value",
    "packed",
    "w_out",
    "encoder",
    "c_query",
    "c_key",
    "c_value",
    "c_out",
    "w_outer",
    "w_in",
    "images",
    "gm",
    "caption_seg",
    "image_row",
    "image_seg",
)
FRONT_OUT = (
    "wq",
    "wk",
    "wv",
    "w_out_all",
    "c_query_all",
    "c_key_all",
    "c_value_all",
    "c_out_all",
    "w_outer_all",
    "w_in_all",
    "h1",
    "q",
    "k",
    "v",
    "heads",
    "attn",
    "y1",
    "h2",
    "cq",
    "ck",
    "cv",
    "caption",
    "cattn",
    "y2",
    "h3",
    "act",
    "du",
    "lse",
    "vec",
    "ok",
    "sums",
)
FRONT_VMEM = (
    "table",
    "enc",
    "both",
    "wqkv",
    "h1_v",
    "q_v",
    "k_v",
    "v_v",
    "obuf",
    "attn_v",
    "y1_v",
    "h2_v",
    "cq_v",
    "kv_v",
    "cap_v",
    "cattn_v",
    "y2_v",
    "h3_v",
    "gm_v",
    "dact",
    "act_v",
    "du_v",
    "w_v",
    "bin",
)


def front_body(*refs):
    names = FRONT_IN + FRONT_OUT + FRONT_VMEM
    r = dict(zip(names, refs))
    (send_sem, recv_sem, local_sem, pair_sem, give_send, give_recv, keep_sem, w_sem, out_sem, gm_sem) = refs[len(names) :]
    c = lax.axis_index("seq")
    rows, step = 512, 128
    own = [r["w_query"], r["w_key"], r["w_value"], r["packed"], r["w_out"]]
    own += [r["encoder"].at[:, pl.ds(pl.multiple_of(c * 64, 64), 64)]]
    own += [r["c_query"], r["c_key"], r["c_value"], r["c_out"], r["w_outer"]]
    own += [r["w_in"].at[:, i * 1024 : (i + 1) * 1024] for i in range(4)]
    full = [r["wqkv"].at[i] for i in range(3)] + [r["table"], r["w_out_all"], r["enc"]]
    full += [r["c_query_all"], r["c_key_all"], r["c_value_all"], r["c_out_all"], r["w_outer_all"]]
    full += [r["w_in_all"].at[:, i * 1024 : (i + 1) * 1024] for i in range(4)]
    n = len(own)
    ring = Gather(3, (), own, full, send_sem, recv_sem, local_sem)
    order = [3, 0, 1, 2, *range(4, n)]

    def slot(t, ahead=2):
        for lead, todo in ((3 * ahead + 1, begin), (2 * ahead, along), (ahead, first), (0, second)):
            for i in range(t + lead + 1):
                todo(i)

    done = set()

    def once(step, name):
        def run(i):
            if i < n and (name, i) not in done:
                done.add((name, i))
                step(order[i])

        return run

    begin, along = once(ring.start, "start"), once(ring.along_z, "z")
    first, second = once(ring.first, "first"), once(ring.second, "second")

    mine = r["both"].at[pl.ds(pl.multiple_of(c * rows, rows), rows)]
    keep_image = pltpu.make_async_copy(r["images"], mine, pair_sem.at[0])
    give_image = pltpu.make_async_remote_copy(
        src_ref=r["images"],
        dst_ref=mine,
        send_sem=pair_sem.at[1],
        recv_sem=pair_sem.at[2],
        device_id=ring.other,
        device_id_type=MESH,
    )
    load_gm = pltpu.make_async_copy(r["gm"], r["gm_v"], gm_sem)
    places = [
        ("wqkv", 0, "wq"),
        ("wqkv", 1, "wk"),
        ("wqkv", 2, "wv"),
        ("h1_v", None, "h1"),
        ("q_v", None, "q"),
        ("k_v", None, "k"),
        ("v_v", None, "v"),
        ("attn_v", None, "attn"),
        ("y1_v", None, "y1"),
        ("h2_v", None, "h2"),
        ("cq_v", None, "cq"),
        ("kv_v", 0, "ck"),
        ("kv_v", 1, "cv"),
        ("cap_v", None, "caption"),
        ("cattn_v", None, "cattn"),
        ("y2_v", None, "y2"),
        ("h3_v", None, "h3"),
    ]
    stores = {
        dst: pltpu.make_async_copy(r[src] if at is None else r[src].at[at], r[dst], out_sem.at[i])
        for i, (src, at, dst) in enumerate(places)
    }
    for j in range(4):
        lanes = slice(j * 1024, (j + 1) * 1024)
        for i, (src, dst) in enumerate((("act_v", "act"), ("du_v", "du"))):
            stores[dst, j] = pltpu.make_async_copy(
                r[src].at[:, lanes], r[dst].at[:, lanes], out_sem.at[len(places) + 2 * j + i]
            )
    parts = [r["w_out_all"], r["c_query_all"], r["c_key_all"], r["c_value_all"], r["c_out_all"]]
    parts += [r["w_outer_all"].at[i * 1024 : (i + 1) * 1024] for i in range(4)] + full[11:]
    weights = [
        pltpu.make_async_copy(part, r["w_v"].at[i % 2], w_sem.at[i % 2])
        for i, part in enumerate(parts)
    ]

    def weight(i):
        weights[i].wait()
        return r["w_v"].at[i % 2]

    def over(count, work):
        @pl.loop(0, count // step)
        def _(i):
            work(pl.ds(i * step, step))

    vec, table = r["vec"], r["table"]

    def unpack():
        for i in range(8):
            lanes = slice(i * 128, (i + 1) * 128)
            at = 4 * i * 16
            vec[:, lanes] = (table[at : at + 16] + table[at + 16 : at + 32]) + (
                table[at + 32 : at + 48] + table[at + 48 : at + 64]
            )
            for j in range(4):
                at = (8 * j + i) * 16 + 7
                r["bin"][j : j + 1, lanes] = table[at : at + 1]

    def row(i):
        return vec[i : i + 1, :]

    def norm1(at):
        value = norm_fwd(r["both"][at, :].astype(jnp.float32), row(0), row(1))
        r["h1_v"][at, :] = value.astype(jnp.bfloat16)

    def project(i):
        def work(at):
            value = mul(r["h1_v"][at, :], r["wqkv"][i])
            r[("q_v", "k_v", "v_v")[i]][at, :] = value.astype(jnp.bfloat16)

        over(2 * rows, work)
        stores[("wq", "wk", "wv")[i]].start()
        stores[("q", "k", "v")[i]].start()

    def keep(i):
        at = pl.multiple_of(c * 512 + i * 128, 128)
        src = r["obuf"].at[i, pl.ds(pl.multiple_of(c * rows, rows), rows)]
        return pltpu.make_async_copy(src, r["attn_v"].at[:, pl.ds(at, 128)], keep_sem.at[i])

    def give(i):
        at = pl.multiple_of(c * 512 + i * 128, 128)
        return pltpu.make_async_remote_copy(
            src_ref=r["obuf"].at[i, pl.ds(pl.multiple_of((1 - c) * rows, rows), rows)],
            dst_ref=r["attn_v"].at[:, pl.ds(at, 128)],
            send_sem=give_send.at[i],
            recv_sem=give_recv.at[i],
            device_id=ring.other,
            device_id_type=MESH,
        )

    def pair(i):
        at = pl.ds(i * 128, 128)

        def put(start, value):
            r["obuf"][i, pl.ds(start, value.shape[0]), :] = value
            r["heads"][pl.ds(start, value.shape[0]), i * 128 : (i + 1) * 128] = value

        self_fwd_pair(
            r["q_v"].at[:, at], r["k_v"].at[:, at], r["v_v"].at[:, at], r["lse"].at[pl.ds(i, 1)], put
        )
        keep(i).start()
        give(i).start()

    def self_out(w):
        def work(at):
            image = r["images_f"](at)
            y1 = image + mul(r["attn_v"][at, :], w[...])
            r["y1_v"][at, :] = y1
            r["h2_v"][at, :] = norm_fwd(y1, row(2), row(3)).astype(jnp.bfloat16)

        over(rows, work)

    def own_image(at):
        start = pl.multiple_of(c * rows + at.start, step)
        return r["both"][pl.ds(start, step), :].astype(jnp.float32)

    r["images_f"] = own_image

    def cross_query(w):
        def work(at):
            r["cq_v"][at, :] = mul(r["h2_v"][at, :], w[...]).astype(jnp.bfloat16)

        over(rows, work)

    def pick_caption():
        line = r["image_row"][0]
        r["cap_v"][0:64, :] = r["enc"][2 * line]
        r["cap_v"][64:128, :] = r["enc"][2 * line + 1]
        chosen = lax.broadcasted_iota(jnp.int32, (16, 128), 0) == line
        seg = jnp.sum(jnp.where(chosen, r["caption_seg"][...], 0), axis=0, keepdims=True)
        allowed = jnp.where(seg == r["image_seg"][0], 1.0, 0.0)
        wide = jnp.broadcast_to(allowed, (128, 128))
        r["ok"][0] = wide
        r["ok"][1] = wide.T

    def cross_out(w):
        def work(at):
            y2 = r["y1_v"][at, :] + mul(r["cattn_v"][at, :], w[...])
            r["y2_v"][at, :] = y2
            r["h3_v"][at, :] = norm_fwd(y2, row(4), row(5)).astype(jnp.bfloat16)

        over(rows, work)

    def cross(lo, hi):
        @pl.loop(lo, hi)
        def _(i):
            at = pl.ds(pl.multiple_of(i * 128, 128), 128)
            cross_fwd_body(
                r["cq_v"].at[:, at],
                r["kv_v"].at[0, :, at],
                r["kv_v"].at[1, :, at],
                r["ok"].at[0],
                r["cattn_v"].at[:, at],
            )

    def back_outer(j, w):
        def work(at):
            r["dact"][at, j * 1024 : (j + 1) * 1024] = mul(r["gm_v"][at, :], w[...], NT)

        over(rows, work)

    def hidden(j, w):
        lanes = slice(j * 1024, (j + 1) * 1024)

        def work(at):
            u = mul(r["h3_v"][at, :], w[...]) + r["bin"][j : j + 1, :]
            act, slope = gelu_both(u)
            r["act_v"][at, lanes] = act.astype(jnp.bfloat16)
            du = (r["dact"][at, lanes] * slope).astype(jnp.bfloat16)
            r["du_v"][at, lanes] = du
            r["sums"][7 + j : 8 + j, :] += jnp.sum(du.astype(jnp.float32), axis=0, keepdims=True)

        over(rows, work)

    greet(ring.partners())
    for i in range(4):
        begin(i)
    keep_image.start()
    give_image.start()
    for g in range(3):
        ring.swapped(g)
    begin(4)
    load_gm.start()
    r["sums"][...] = jnp.zeros_like(r["sums"])
    slot(0, 1)
    ring.ready(3)
    unpack()
    keep_image.wait()
    give_image.wait_recv()
    slot(1, 1)
    over(2 * rows, norm1)
    stores["h1"].start()
    project(0)
    slot(2, 1)
    project(1)
    slot(3, 1)
    project(2)
    slot(3)
    pair(0)
    slot(4)
    ring.ready(4)
    weights[0].start()
    pair(1)
    along(9)
    pair(2)
    first(7)
    pair(3)
    slot(5)
    for i in range(4):
        keep(i).wait()
        give(i).wait_recv()
    stores["attn"].start()
    self_out(weight(0))
    stores["y1"].start()
    stores["h2"].start()
    slot(6)
    ring.ready(5)
    pick_caption()
    stores["caption"].start()
    ring.ready(6)
    weights[1].start()
    cross_query(weight(1))
    stores["cq"].start()
    slot(7)
    ring.ready(7)
    weights[2].start()
    r["kv_v"][0] = mul(r["cap_v"][...], weight(2)[...]).astype(jnp.bfloat16)
    stores["ck"].start()
    slot(8)
    ring.ready(8)
    weights[3].start()
    r["kv_v"][1] = mul(r["cap_v"][...], weight(3)[...]).astype(jnp.bfloat16)
    stores["cv"].start()
    cross(0, 4)
    slot(9)
    cross(4, 8)
    stores["cattn"].start()
    ring.ready(9)
    weights[4].start()
    cross_out(weight(4))
    stores["y2"].start()
    stores["h3"].start()
    load_gm.wait()
    r["sums"][6:7, :] = jnp.sum(r["gm_v"][...].astype(jnp.float32), axis=0, keepdims=True)
    slot(10)
    ring.ready(10)
    weights[5].start()
    weights[6].start()
    back_outer(0, weight(5))
    weights[7].start()
    back_outer(1, weight(6))
    weights[8].start()
    slot(11)
    back_outer(2, weight(7))
    ring.ready(11)
    weights[9].start()
    back_outer(3, weight(8))
    for j in range(4):
        if j < 3:
            slot(12 + j)
            ring.ready(12 + j)
            weights[10 + j].start()
        hidden(j, weight(9 + j))
        stores["act", j].start()
        stores["du", j].start()
    for g in range(n):
        ring.sent(g)
    give_image.wait_send()
    for i in range(4):
        give(i).wait_send()
    for store in stores.values():
        store.wait()


def front(operands, collective_id):
    bf, f32, vm, shape = jnp.bfloat16, jnp.float32, pltpu.VMEM, jax.ShapeDtypeStruct
    square, rows, head = (1024, 1024), (512, 1024), (1024, 512)
    inside = pl.BlockSpec(memory_space=pltpu.VMEM)
    scalar = pl.BlockSpec(memory_space=pltpu.SMEM)
    outs = (
        [shape(head, bf)] * 3
        + [shape(square, bf)] * 5
        + [shape((4096, 1024), bf), shape((1024, 4096), bf), shape(square, bf)]
        + [shape(head, bf)] * 4
        + [shape(rows, bf), shape(rows, f32), shape(rows, bf), shape(rows, bf)]
        + [shape((128, 1024), bf)] * 3
        + [shape(rows, bf), shape(rows, f32), shape(rows, bf)]
        + [shape((512, 4096), bf)] * 2
        + [shape((4, 2, 1024), f32), shape((16, 1024), f32), shape((2, 128, 128), f32)]
        + [shape((16, 1024), f32)]
    )
    places = [ANY] * 14 + [inside] + [ANY] * 12 + [inside] * 4
    n = 15
    return pl.pallas_call(
        front_body,
        out_shape=outs,
        in_specs=[ANY] * 14 + [inside, scalar, scalar],
        out_specs=places,
        scratch_shapes=[
            vm((512, 128), f32),
            vm((32, 64, 1024), bf),
            vm(square, bf),
            vm((3, 1024, 512), bf),
            vm(square, bf),
            vm(head, bf),
            vm(head, bf),
            vm(head, bf),
            vm((4, 1024, 128), bf),
            vm(rows, bf),
            vm(rows, f32),
            vm(rows, bf),
            vm(rows, bf),
            vm((2, 128, 1024), bf),
            vm((128, 1024), bf),
            vm(rows, bf),
            vm(rows, f32),
            vm(rows, bf),
            vm(rows, bf),
            vm((512, 4096), f32),
            vm((512, 4096), bf),
            vm((512, 4096), bf),
            vm((2, 1024, 1024), bf),
            vm((4, 1024), f32),
            pltpu.SemaphoreType.DMA((n, 31)),
            pltpu.SemaphoreType.DMA((n, 31)),
            pltpu.SemaphoreType.DMA((n,)),
            pltpu.SemaphoreType.DMA((3,)),
            pltpu.SemaphoreType.DMA((4,)),
            pltpu.SemaphoreType.DMA((4,)),
            pltpu.SemaphoreType.DMA((4,)),
            pltpu.SemaphoreType.DMA((2,)),
            pltpu.SemaphoreType.DMA((25,)),
            pltpu.SemaphoreType.DMA,
        ],
        compiler_params=pltpu.CompilerParams(
            collective_id=collective_id,
            has_side_effects=True,
            vmem_limit_bytes=59 * 1024 * 1024,
        ),
        name="front",
    )(*operands)


def emit_body(*refs):
    n = (len(refs) - 10) // 3
    srcs, total, dsts = refs[:n], refs[n], refs[n + 1 : 2 * n + 1]
    cuts, share = refs[2 * n + 1 : 2 * n + 8], refs[2 * n + 8]
    held, sem = refs[2 * n + 9 : -1], refs[-1]
    loads = [pltpu.make_async_copy(srcs[i], held[i], sem.at[i]) for i in range(n)]
    copies = [pltpu.make_async_copy(held[i], dsts[i], sem.at[i]) for i in range(n)]
    for load in loads:
        load.start()
    index = 2 * lax.axis_index("dp") + lax.axis_index("seq")
    block = total[:, pl.ds(pl.multiple_of(index // 4 * 128, 128), 128)]
    moved = block
    for k in range(1, 4):
        moved = jnp.where(index % 4 == k, pltpu.roll(block, 128 - 32 * k, 1), moved)
    for i, cut in enumerate(cuts):
        cut[...] = moved[i, 0:32]
    block = total[:, pl.ds(pl.multiple_of(index % 8 * 128, 128), 128)]
    chosen = lax.broadcasted_iota(jnp.int32, block.shape, 0) == 7 + index // 8
    share[...] = jnp.sum(jnp.where(chosen, block, 0.0), axis=0)
    for load, copy in zip(loads, copies):
        load.wait()
        copy.start()
    for copy in copies:
        copy.wait()


def emit(arrays, total):
    inside = pl.BlockSpec(memory_space=pltpu.VMEM)
    n = len(arrays)
    return pl.pallas_call(
        emit_body,
        out_shape=[jax.ShapeDtypeStruct(a.shape, a.dtype) for a in arrays]
        + [jax.ShapeDtypeStruct((32,), jnp.float32)] * 7
        + [jax.ShapeDtypeStruct((128,), jnp.float32)],
        in_specs=[ANY] * n + [inside],
        out_specs=[ANY] * n + [inside] * 8,
        scratch_shapes=[pltpu.VMEM(a.shape, a.dtype) for a in arrays]
        + [pltpu.SemaphoreType.DMA((n,))],
        name="emit",
    )(*arrays, total)


HEADS = 16
HEAD_DIM = 64


EPSILON = 1e-05
NEG_BIG = -1e30


def norm_rows(value, gain, shift):
    center = value - jnp.mean(value, axis=-1, keepdims=True)
    spread = jnp.mean(center * center, axis=-1, keepdims=True)
    return center * lax.rsqrt(spread + EPSILON) * gain + shift


def project(rows, weight):
    return jnp.einsum("bsd,de->bse", rows, weight, preferred_element_type=jnp.float32)


def project_back(grads, weight):
    return jnp.einsum("bse,de->bsd", grads, weight, preferred_element_type=jnp.float32)


def weight_grad(rows, grads):
    return jnp.einsum("bsd,bse->de", rows, grads, preferred_element_type=jnp.float32)


def row_total(grads):
    return jnp.sum(grads.astype(jnp.float32), axis=(0, 1))


def split_heads(value):
    return value.reshape(value.shape[0], value.shape[1], HEADS, HEAD_DIM)


def join_heads(value):
    return value.reshape(value.shape[0], value.shape[1], HEADS * HEAD_DIM)


def scores_of(queries, keys_in, allowed):
    raw_scores = (
        jnp.einsum(
            "bqhd,bkhd->bhqk",
            split_heads(queries),
            split_heads(keys_in),
            preferred_element_type=jnp.float32,
        )
        * 0.125
    )
    return jnp.where(allowed, raw_scores, NEG_BIG)


def attend(queries, keys_in, values_in, allowed):
    scores = scores_of(queries, keys_in, allowed)
    row_max = jnp.max(scores, axis=-1, keepdims=True)
    exponent = jnp.exp(scores - row_max)
    total = jnp.sum(exponent, axis=-1, keepdims=True)
    attn_weights = exponent / total
    mixed_rows = jnp.einsum(
        "bhqk,bkhd->bqhd",
        attn_weights.astype(jnp.bfloat16),
        split_heads(values_in),
        preferred_element_type=jnp.float32,
    )
    return (join_heads(mixed_rows).astype(jnp.bfloat16), row_max + jnp.log(total))


def attend_back(queries, keys_in, values_in, allowed, log_total, grad_mixed):
    attn_weights = jnp.exp(scores_of(queries, keys_in, allowed) - log_total)
    grad_heads = split_heads(grad_mixed)
    grad_weights = jnp.einsum(
        "bqhd,bkhd->bhqk", grad_heads, split_heads(values_in), preferred_element_type=jnp.float32
    )
    grad_values = jnp.einsum(
        "bhqk,bqhd->bkhd",
        attn_weights.astype(jnp.bfloat16),
        grad_heads,
        preferred_element_type=jnp.float32,
    )
    inner_sum = jnp.sum(grad_weights * attn_weights, axis=-1, keepdims=True)
    grad_scores = (attn_weights * (grad_weights - inner_sum)).astype(jnp.bfloat16)
    grad_queries = (
        jnp.einsum(
            "bhqk,bkhd->bqhd", grad_scores, split_heads(keys_in), preferred_element_type=jnp.float32
        )
        * 0.125
    )
    grad_keys = (
        jnp.einsum(
            "bhqk,bqhd->bkhd", grad_scores, split_heads(queries), preferred_element_type=jnp.float32
        )
        * 0.125
    )
    return (join_heads(grad_queries), join_heads(grad_keys), join_heads(grad_values))


def per_device(
    images,
    encoder_states,
    image_row,
    image_seg,
    caption_seg,
    ln1_gain,
    ln1_bias,
    w_query,
    w_key,
    w_value,
    w_out,
    ln2_gain,
    ln2_bias,
    c_query,
    c_key,
    c_value,
    c_out,
    ln3_gain,
    ln3_bias,
    w_in,
    b_in,
    w_outer,
    b_outer,
    cotangent,
):
    mixing = (
        lax.all_gather(ln1_gain, ("dp", "seq"), axis=0, tiled=True),
        lax.all_gather(ln1_bias, ("dp", "seq"), axis=0, tiled=True),
        lax.all_gather(w_query, ("dp", "seq"), axis=0, tiled=True),
        lax.all_gather(w_key, ("dp", "seq"), axis=0, tiled=True),
        lax.all_gather(w_value, ("dp", "seq"), axis=0, tiled=True),
        lax.all_gather(w_out, ("dp", "seq"), axis=0, tiled=True),
        lax.all_gather(ln2_gain, ("dp", "seq"), axis=0, tiled=True),
        lax.all_gather(ln2_bias, ("dp", "seq"), axis=0, tiled=True),
        lax.all_gather(c_query, ("dp", "seq"), axis=0, tiled=True),
        lax.all_gather(c_key, ("dp", "seq"), axis=0, tiled=True),
        lax.all_gather(c_value, ("dp", "seq"), axis=0, tiled=True),
        lax.all_gather(c_out, ("dp", "seq"), axis=0, tiled=True),
    )
    (
        gain_a,
        bias_a,
        query_w,
        key_w,
        value_w,
        out_w,
        gain_b,
        bias_b,
        cross_qw,
        cross_kw,
        cross_vw,
        cross_ow,
    ) = mixing
    shard = images.shape[1]
    seq_index = lax.axis_index("seq")
    full_len = shard * lax.axis_size("seq")
    inputs_f = images.astype(jnp.float32)
    gain_a32, bias_a32 = (gain_a.astype(jnp.float32), bias_a.astype(jnp.float32))
    normed_a = norm_rows(inputs_f, gain_a32, bias_a32).astype(jnp.bfloat16)
    queries = project(normed_a, query_w).astype(jnp.bfloat16)
    keys_local = project(normed_a, key_w).astype(jnp.bfloat16)
    values_local = project(normed_a, value_w).astype(jnp.bfloat16)
    keys_all, values_all = (
        lax.all_gather(keys_local, "seq", axis=1, tiled=True),
        lax.all_gather(values_local, "seq", axis=1, tiled=True),
    )
    query_pos = seq_index * shard + jnp.arange(shard, dtype=jnp.int32)
    key_pos = jnp.arange(full_len, dtype=jnp.int32)
    causal = (key_pos[None, :] <= query_pos[:, None])[None, None]
    self_out, self_lse = attend(queries, keys_all, values_all, causal)
    after_self = inputs_f + project(self_out, out_w)
    gain_b32, bias_b32 = (gain_b.astype(jnp.float32), bias_b.astype(jnp.float32))
    normed_b = norm_rows(after_self, gain_b32, bias_b32).astype(jnp.bfloat16)
    cross_queries = project(normed_b, cross_qw).astype(jnp.bfloat16)
    encoder_all = lax.all_gather(encoder_states, "dp", axis=0, tiled=True)
    caption = jnp.take(encoder_all, image_row, axis=0)
    cross_keys = project(caption, cross_kw).astype(jnp.bfloat16)
    cross_values = project(caption, cross_vw).astype(jnp.bfloat16)
    caption_mask = (jnp.take(caption_seg, image_row, axis=0) == image_seg[:, None])[
        :, None, None, :
    ]
    cross_out, cross_lse = attend(cross_queries, cross_keys, cross_values, caption_mask)
    after_cross = after_self + project(cross_out, cross_ow)
    feed_weights = (
        lax.all_gather(ln3_gain, ("dp", "seq"), axis=0, tiled=True),
        lax.all_gather(ln3_bias, ("dp", "seq"), axis=0, tiled=True),
        lax.all_gather(w_in, ("dp", "seq"), axis=0, tiled=True),
        lax.all_gather(b_in, ("dp", "seq"), axis=0, tiled=True),
        lax.all_gather(w_outer, ("dp", "seq"), axis=0, tiled=True),
        lax.all_gather(b_outer, ("dp", "seq"), axis=0, tiled=True),
    )
    gain_c, bias_c, inner_w, inner_b, outer_w, outer_b = feed_weights
    gain_c32, bias_c32 = (gain_c.astype(jnp.float32), bias_c.astype(jnp.float32))
    normed_c = norm_rows(after_cross, gain_c32, bias_c32).astype(jnp.bfloat16)
    hidden_pre = project(normed_c, inner_w) + inner_b.astype(jnp.float32)
    activated = jax.nn.gelu(hidden_pre).astype(jnp.bfloat16)
    result = after_cross + project(activated, outer_w) + outer_b.astype(jnp.float32)
    block_out = result.astype(jnp.bfloat16)
    inner_wb, outer_wb = (feed_weights[2], feed_weights[4])
    grad_result = cotangent.astype(jnp.float32)
    grad_outer_w = weight_grad(activated, cotangent)
    grad_outer_b = row_total(cotangent)
    grad_act = project_back(cotangent, outer_wb)
    _, gelu_back = jax.vjp(jax.nn.gelu, hidden_pre)
    grad_hidden = gelu_back(grad_act)[0].astype(jnp.bfloat16)
    grad_inner_w = weight_grad(normed_c, grad_hidden)
    grad_inner_b = row_total(grad_hidden)
    grad_normed_c = project_back(grad_hidden, inner_wb)
    _, norm_c_back = jax.vjp(norm_rows, after_cross, gain_c32, bias_c32)
    grad_cross_part, grad_gain_c, grad_bias_c = norm_c_back(grad_normed_c)
    grad_after_cross = grad_result + grad_cross_part
    feed_sums = (
        lax.psum_scatter(grad_gain_c, ("dp", "seq"), scatter_dimension=0, tiled=True),
        lax.psum_scatter(grad_bias_c, ("dp", "seq"), scatter_dimension=0, tiled=True),
        lax.psum_scatter(grad_inner_w, ("dp", "seq"), scatter_dimension=0, tiled=True),
        lax.psum_scatter(grad_inner_b, ("dp", "seq"), scatter_dimension=0, tiled=True),
        lax.psum_scatter(grad_outer_w, ("dp", "seq"), scatter_dimension=0, tiled=True),
        lax.psum_scatter(grad_outer_b, ("dp", "seq"), scatter_dimension=0, tiled=True),
    )
    query_wb, key_wb, value_wb, out_wb = (mixing[2], mixing[3], mixing[4], mixing[5])
    cross_qwb, cross_kwb, cross_vwb, cross_owb = (mixing[8], mixing[9], mixing[10], mixing[11])
    grad_branch_b = grad_after_cross.astype(jnp.bfloat16)
    grad_cross_ow = weight_grad(cross_out, grad_branch_b)
    grad_cross_out = project_back(grad_branch_b, cross_owb).astype(jnp.bfloat16)
    grad_cq_raw, grad_ck_raw, grad_cv_raw = attend_back(
        cross_queries, cross_keys, cross_values, caption_mask, cross_lse, grad_cross_out
    )
    grad_cross_q = grad_cq_raw.astype(jnp.bfloat16)
    grad_ck_sum, grad_cv_sum = (
        lax.psum_scatter(
            grad_ck_raw.astype(jnp.bfloat16), "seq", scatter_dimension=1, tiled=True
        ).astype(jnp.float32),
        lax.psum_scatter(
            grad_cv_raw.astype(jnp.bfloat16), "seq", scatter_dimension=1, tiled=True
        ).astype(jnp.float32),
    )
    grad_ck_low = grad_ck_sum.astype(jnp.bfloat16)
    grad_cv_low = grad_cv_sum.astype(jnp.bfloat16)
    piece_len = grad_ck_sum.shape[1]
    caption_piece = lax.dynamic_slice_in_dim(caption, seq_index * piece_len, piece_len, 1)
    grad_cross_kw = weight_grad(caption_piece, grad_ck_low)
    grad_cross_vw = weight_grad(caption_piece, grad_cv_low)
    grad_caption = project_back(grad_ck_low, cross_kwb) + project_back(grad_cv_low, cross_vwb)
    row_count = encoder_all.shape[0]
    row_onehot = (image_row[:, None] == jnp.arange(row_count, dtype=jnp.int32)[None, :]).astype(
        jnp.float32
    )
    grad_rows = jnp.einsum("br,bsd->rsd", row_onehot, grad_caption, precision=lax.Precision.HIGHEST)
    caption_grad = lax.psum_scatter(
        grad_rows.astype(jnp.bfloat16), "dp", scatter_dimension=0, tiled=True
    ).astype(jnp.float32)
    grad_cross_qw = weight_grad(normed_b, grad_cross_q)
    grad_normed_b = project_back(grad_cross_q, cross_qwb)
    _, norm_b_back = jax.vjp(norm_rows, after_self, gain_b32, bias_b32)
    grad_self_part, grad_gain_b, grad_bias_b = norm_b_back(grad_normed_b)
    grad_after_self = grad_after_cross + grad_self_part
    grad_branch_a = grad_after_self.astype(jnp.bfloat16)
    grad_out_w = weight_grad(self_out, grad_branch_a)
    grad_self_out = project_back(grad_branch_a, out_wb).astype(jnp.bfloat16)
    keys_back, values_back = (keys_all, values_all)
    grad_q_raw, grad_k_raw, grad_v_raw = attend_back(
        queries, keys_back, values_back, causal, self_lse, grad_self_out
    )
    grad_k_sum, grad_v_sum = (
        lax.psum_scatter(
            grad_k_raw.astype(jnp.bfloat16), "seq", scatter_dimension=1, tiled=True
        ).astype(jnp.float32),
        lax.psum_scatter(
            grad_v_raw.astype(jnp.bfloat16), "seq", scatter_dimension=1, tiled=True
        ).astype(jnp.float32),
    )
    grad_q_low = grad_q_raw.astype(jnp.bfloat16)
    grad_k_low = grad_k_sum.astype(jnp.bfloat16)
    grad_v_low = grad_v_sum.astype(jnp.bfloat16)
    grad_query_w = weight_grad(normed_a, grad_q_low)
    grad_key_w = weight_grad(normed_a, grad_k_low)
    grad_value_w = weight_grad(normed_a, grad_v_low)
    grad_normed_a = (
        project_back(grad_q_low, query_wb)
        + project_back(grad_k_low, key_wb)
        + project_back(grad_v_low, value_wb)
    )
    _, norm_a_back = jax.vjp(norm_rows, inputs_f, gain_a32, bias_a32)
    grad_input_part, grad_gain_a, grad_bias_a = norm_a_back(grad_normed_a)
    image_grad = grad_after_self + grad_input_part
    mix_sums = (
        lax.psum_scatter(grad_gain_a, ("dp", "seq"), scatter_dimension=0, tiled=True),
        lax.psum_scatter(grad_bias_a, ("dp", "seq"), scatter_dimension=0, tiled=True),
        lax.psum_scatter(grad_query_w, ("dp", "seq"), scatter_dimension=0, tiled=True),
        lax.psum_scatter(grad_key_w, ("dp", "seq"), scatter_dimension=0, tiled=True),
        lax.psum_scatter(grad_value_w, ("dp", "seq"), scatter_dimension=0, tiled=True),
        lax.psum_scatter(grad_out_w, ("dp", "seq"), scatter_dimension=0, tiled=True),
        lax.psum_scatter(grad_gain_b, ("dp", "seq"), scatter_dimension=0, tiled=True),
        lax.psum_scatter(grad_bias_b, ("dp", "seq"), scatter_dimension=0, tiled=True),
        lax.psum_scatter(grad_cross_qw, ("dp", "seq"), scatter_dimension=0, tiled=True),
        lax.psum_scatter(grad_cross_kw, ("dp", "seq"), scatter_dimension=0, tiled=True),
        lax.psum_scatter(grad_cross_vw, ("dp", "seq"), scatter_dimension=0, tiled=True),
        lax.psum_scatter(grad_cross_ow, ("dp", "seq"), scatter_dimension=0, tiled=True),
    )
    return (
        block_out,
        image_grad,
        caption_grad,
        mix_sums[0],
        mix_sums[1],
        mix_sums[2],
        mix_sums[3],
        mix_sums[4],
        mix_sums[5],
        mix_sums[6],
        mix_sums[7],
        mix_sums[8],
        mix_sums[9],
        mix_sums[10],
        mix_sums[11],
        feed_sums[0],
        feed_sums[1],
        feed_sums[2],
        feed_sums[3],
        feed_sums[4],
        feed_sums[5],
    )


def block_device(
    images,
    encoder_states,
    image_row,
    image_seg,
    caption_seg,
    ln1_gain,
    ln1_bias,
    w_query,
    w_key,
    w_value,
    w_out,
    ln2_gain,
    ln2_bias,
    c_query,
    c_key,
    c_value,
    c_out,
    ln3_gain,
    ln3_bias,
    w_in,
    b_in,
    w_outer,
    b_outer,
    cotangent,
):
    core = lax.axis_index("seq")
    index = 2 * lax.axis_index("dp") + core
    width = images.shape[2]
    vectors = (ln1_gain, ln1_bias, ln2_gain, ln2_bias, ln3_gain, ln3_bias, b_outer)
    lanes = b_outer.shape[0]
    stack = jnp.tile(jnp.stack(vectors).astype(jnp.float32), (1, 128 // lanes))
    place_of = jnp.arange(128, dtype=jnp.int32) // lanes == index % (128 // lanes)
    packed = jnp.concatenate(
        [
            jnp.where(place_of[None], stack, 0.0),
            b_in.astype(jnp.float32)[None],
            jnp.zeros((8, 128), jnp.float32),
        ]
    )
    o = dict(
        zip(
            FRONT_OUT,
            front(
                [
                    w_query,
                    w_key,
                    w_value,
                    packed,
                    w_out,
                    encoder_states,
                    c_query,
                    c_key,
                    c_value,
                    c_out,
                    w_outer,
                    w_in,
                    images[0],
                    cotangent[0],
                    caption_seg,
                    image_row,
                    image_seg,
                ],
                1,
            ),
        )
    )
    (
        grad_inner_w,
        grad_outer_w,
        sums,
        grad_caption,
        block_out,
        grad_branch_b,
        grad_cross_q,
        grad_ck,
        grad_cv,
        grad_branch_a,
        grad_after_self,
        grad_self_out,
    ) = middle(
        [o["h3"], o["du"], o["act"], cotangent[0], o["w_in_all"], o["w_outer_all"]]
        + [o["c_out_all"], o["c_query_all"], o["w_out_all"], o["y2"], o["y1"]]
        + [o["cq"], o["ck"], o["cv"], o["c_key_all"], o["c_value_all"]]
        + [o["ok"], o["vec"], o["sums"]],
        2,
    )
    image_grad, *big, total = scatter_tail(
        [o["q"], o["k"], o["v"], o["heads"], o["lse"], grad_self_out, o["h1"], o["attn"]]
        + [grad_branch_a, o["h2"], grad_cross_q, o["cattn"], grad_branch_b, o["caption"]]
        + [grad_ck, grad_cv, o["wq"], o["wk"], o["wv"], images[0], grad_after_self, o["vec"], sums]
        + [grad_caption, jnp.broadcast_to(image_row.astype(jnp.float32)[:, None], (8, width))],
        4,
    )
    arrays = emit([block_out, image_grad, grad_inner_w, grad_outer_w, *big], total)
    block_out, image_grad, grad_inner_w, grad_outer_w, *big = arrays[:-8]
    small, share = arrays[-8:-1], arrays[-1]
    return (
        block_out[None],
        image_grad[None],
        big[5][None],
        small[0],
        small[1],
        big[6],
        big[7],
        big[8],
        big[0],
        small[2],
        small[3],
        big[1],
        big[3],
        big[4],
        big[2],
        small[4],
        small[5],
        grad_inner_w,
        share,
        grad_outer_w,
        small[6],
    )


def solution(mesh):
    in_specs = (
        P("dp", "seq", None),
        P("dp", None, None),
        P("dp"),
        P("dp"),
        P(),
        P(("dp", "seq")),
        P(("dp", "seq")),
        P(("dp", "seq"), None),
        P(("dp", "seq"), None),
        P(("dp", "seq"), None),
        P(("dp", "seq"), None),
        P(("dp", "seq")),
        P(("dp", "seq")),
        P(("dp", "seq"), None),
        P(("dp", "seq"), None),
        P(("dp", "seq"), None),
        P(("dp", "seq"), None),
        P(("dp", "seq")),
        P(("dp", "seq")),
        P(("dp", "seq"), None),
        P(("dp", "seq")),
        P(("dp", "seq"), None),
        P(("dp", "seq")),
        P("dp", "seq", None),
    )
    out_specs = (
        P("dp", "seq", None),
        P("dp", "seq", None),
        P("dp", "seq", None),
        P(("dp", "seq")),
        P(("dp", "seq")),
        P(("dp", "seq"), None),
        P(("dp", "seq"), None),
        P(("dp", "seq"), None),
        P(("dp", "seq"), None),
        P(("dp", "seq")),
        P(("dp", "seq")),
        P(("dp", "seq"), None),
        P(("dp", "seq"), None),
        P(("dp", "seq"), None),
        P(("dp", "seq"), None),
        P(("dp", "seq")),
        P(("dp", "seq")),
        P(("dp", "seq"), None),
        P(("dp", "seq")),
        P(("dp", "seq"), None),
        P(("dp", "seq")),
    )
    kernels = mesh.shape["dp"] == 16 and mesh.shape["seq"] == 2
    return jax.shard_map(
        block_device if kernels else per_device,
        mesh=mesh,
        in_specs=in_specs,
        out_specs=out_specs,
        check_vma=False,
    )
```

```python
import functools

import jax
import jax.numpy as jnp
from jax import lax
from jax.experimental import pallas as pl
from jax.experimental.pallas import tpu as pltpu
from jax.sharding import PartitionSpec as P

MESH = pl.DeviceIdType.MESH
ANY = pl.BlockSpec(memory_space=pl.ANY)


def place():
    dp, c = lax.axis_index("dp"), lax.axis_index("seq")
    x, y, z = dp % 2, (dp // 2) % 2, dp // 4
    return z, y, x, c


def flip(bit, on):
    return bit + on * (1 - 2 * bit)


def zxor(z, k):
    if k == 0:
        return z
    if k == 1:
        return z + 1 - 2 * (z % 2)
    if k == 2:
        return z + 2 - 4 * (z // 2)
    return 3 - z


def chip(z, y, x):
    return z * 4 + y * 2 + x


def greet(partners):
    barrier = pltpu.get_barrier_semaphore()
    for partner in partners:
        pl.semaphore_signal(barrier, inc=1, device_id=partner, device_id_type=MESH)
    pl.semaphore_wait(barrier, len(partners))


class Gather:
    def __init__(self, split, flat, own, full, send_sem, recv_sem, local_sem):
        self.split, self.flat, self.own, self.full = split, flat, own, full
        self.send_sem, self.recv_sem, self.local_sem = send_sem, recv_sem, local_sem
        z, y, x, c = place()
        self.z, self.y, self.x, self.c = z, y, x, c
        self.yx = {
            (0, 0): (y, x),
            (1, 0): (flip(y, 1 - c), flip(x, c)),
            (0, 1): (flip(y, c), flip(x, 1 - c)),
            (1, 1): (1 - y, 1 - x),
        }
        self.other = (chip(z, y, x), 1 - c)

    def partners(self):
        z, c = self.z, self.c
        return [(chip(zxor(z, k), self.y, self.x), c) for k in (1, 2, 3)] + [
            (chip(z, *self.yx[1, 0]), c),
            (chip(z, *self.yx[0, 1]), c),
            self.other,
        ]

    def block(self, g, k, way, core):
        rows = self.own[g].shape[0]
        r = chip(zxor(self.z, k), *self.yx[way])
        if g < self.split:
            return self.full[g].at[pl.ds(pl.multiple_of(2 * r * rows, rows), 2 * rows)]
        return self.full[g].at[pl.ds(pl.multiple_of((2 * r + core) * rows, rows), rows)]

    def remote(self, g, src, dst, to, idx):
        return pltpu.make_async_remote_copy(
            src_ref=src,
            dst_ref=dst,
            send_sem=self.send_sem.at[g, idx],
            recv_sem=self.recv_sem.at[g, idx],
            device_id=to,
            device_id_type=MESH,
        )

    def copy(self, g, src, k, way, core, to, idx):
        return self.remote(g, src, self.block(g, k, way, core), to, idx)

    def forward(self, g, k, way, src=None):
        z, c = self.z, self.c
        src = self.block(g, k, way, c) if src is None else src
        i1, i2 = way
        sends = []
        if i1 == 0 and i2 == 0:
            sends.append(((chip(z, *self.yx[1, 0]), c), 3 + k))
        if i2 == 0:
            sends.append(((chip(z, *self.yx[0, 1]), c), 7 + i1 * 4 + k))
        if g >= self.split:
            sends.append((self.other, 15 + i2 * 8 + i1 * 4 + k))
        for to, idx in sends:
            self.copy(g, src, k, way, c, to, idx).start()

    def half(self, g, core):
        rows, columns = self.own[g].shape
        columns //= 2
        at = pl.multiple_of((2 * chip(self.z, self.y, self.x) + self.c) * rows, rows)
        return (
            self.own[g].at[:, pl.ds(pl.multiple_of(core * columns, columns), columns)],
            self.full[g].at[pl.ds(at, rows)],
        )

    def keep(self, g):
        if g < self.split:
            src, dst = self.half(g, self.c)
        else:
            src, dst = self.own[g], self.block(g, 0, (0, 0), self.c)
        return pltpu.make_async_copy(src, dst, self.local_sem.at[g])

    def swap(self, g):
        src, dst = self.half(g, 1 - self.c)
        return self.remote(g, src, dst, self.other, 15)

    def start(self, g):
        self.keep(g).start()
        if g < self.split:
            self.swap(g).start()
        else:
            self.begin(g, self.own[g])

    def swapped(self, g):
        self.swap(g).wait_recv()
        self.keep(g).wait()
        self.begin(g, self.block(g, 0, (0, 0), self.c))

    def begin(self, g, src):
        for k in (1, 2, 3):
            to = (chip(zxor(self.z, k), self.y, self.x), self.c)
            self.copy(g, src, 0, (0, 0), self.c, to, k - 1).start()
        self.forward(g, 0, (0, 0), src)

    def spread(self, g, way):
        self.forward(g, 0, way)
        for k in (1, 2, 3):
            to = (chip(zxor(self.z, k), self.y, self.x), self.c)
            idx = 3 + k if way[1] == 0 else 7 + way[0] * 4 + k
            self.copy(g, self.block(g, 0, way, self.c), 0, way, self.c, to, idx).start()

    def pass_on(self, g, k, way, idx):
        self.arrive(g, k, way, self.c, idx)
        at = 15 + way[1] * 8 + way[0] * 4 + k
        self.copy(g, self.block(g, k, way, self.c), k, way, self.c, self.other, at).start()

    def arrive(self, g, k, way, core, idx):
        block = self.block(g, k, way, core)
        self.remote(g, block, block, self.other, idx).wait_recv()

    def along_z(self, g):
        if g in self.flat:
            self.arrive(g, 0, (1, 0), self.c, 3)
            self.spread(g, (1, 0))
            return
        for k in (1, 2, 3):
            self.arrive(g, k, (0, 0), self.c, k - 1)
            self.forward(g, k, (0, 0))

    def first(self, g):
        if g in self.flat:
            for i1 in range(2):
                self.arrive(g, 0, (i1, 1), self.c, 7 + i1 * 4)
                self.spread(g, (i1, 1))
            return
        for k in range(4):
            self.arrive(g, k, (1, 0), self.c, 3 + k)
            self.forward(g, k, (1, 0))

    def second(self, g):
        if g in self.flat:
            for k in (1, 2, 3):
                self.pass_on(g, k, (0, 0), k - 1)
                self.pass_on(g, k, (1, 0), 3 + k)
                self.pass_on(g, k, (0, 1), 7 + k)
                self.pass_on(g, k, (1, 1), 11 + k)
            return
        for i1 in range(2):
            for k in range(4):
                self.arrive(g, k, (i1, 1), self.c, 7 + i1 * 4 + k)
                self.forward(g, k, (i1, 1))

    def ready(self, g):
        if g >= self.split:
            for i2 in range(2):
                for i1 in range(2):
                    for k in range(4):
                        self.arrive(g, k, (i2, i1), 1 - self.c, 15 + i2 * 8 + i1 * 4 + k)
            self.keep(g).wait()

    def sent(self, g):
        if g < self.split:
            self.swap(g).wait_send()
        block = self.block(g, 0, (0, 0), self.c)
        for idx in range(15 if g < self.split else 31):
            self.remote(g, block, block, self.other, idx).wait_send()


AHEAD = 4


NT = (((1,), (1,)), ((), ()))
TN = (((0,), (0,)), ((), ()))
NN = (((1,), (0,)), ((), ()))


def mul(a, b, dims=NN):
    return lax.dot_general(a, b, dims, preferred_element_type=jnp.float32)


def low_lanes(rows):
    return lax.broadcasted_iota(jnp.int32, (rows, 128), 1) < 64


def self_fwd_pair(q_ref, k_ref, v_ref, lse_ref, put):
    length, b = q_ref.shape[0], 256
    low = low_lanes(b)
    row = lax.broadcasted_iota(jnp.int32, (b, b), 0)
    col = lax.broadcasted_iota(jnp.int32, (b, b), 1)
    for n in range(b, length + 1, b):
        q = q_ref[n - b : n, :] * jnp.asarray(0.125, jnp.bfloat16)

        def head(h, carry):
            mixed, lses = carry
            mine = low == (h == 0)
            s = mul(jnp.where(mine, q, jnp.zeros_like(q)), k_ref[0:n, :], NT)
            last = jnp.where(col <= row, s[:, n - b :], NEG_BIG)
            s = jnp.concatenate([s[:, : n - b], last], axis=1) if n > b else last
            top = jnp.max(s, axis=1, keepdims=True)
            e = jnp.exp(s - top)
            total = jnp.sum(e, axis=1, keepdims=True)
            value = mul(e.astype(jnp.bfloat16), v_ref[0:n, :]) / total
            lse = jnp.broadcast_to(top + jnp.log(total), (b, 128))
            return jnp.where(mine, value, mixed), jnp.where(mine, lse, lses)

        zero = jnp.zeros((b, 128), jnp.float32)
        mixed, lses = lax.fori_loop(0, 2, head, (zero, zero))
        put(n - b, mixed.astype(jnp.bfloat16))
        turned = lses.T
        lse_ref[0, :, n - b : n] = jnp.concatenate([turned[0:1], turned[64:65]], axis=0)


def self_bwd_pair(q_ref, k_ref, v_ref, o_ref, do_ref, lse_ref, dq_ref, dk_ref, dv_ref, acc):
    length, b = q_ref.shape[0], 256
    low = low_lanes(b)
    row = lax.broadcasted_iota(jnp.int32, (b, b), 0)
    col = lax.broadcasted_iota(jnp.int32, (b, b), 1)
    prod = do_ref[...].astype(jnp.float32) * o_ref[...].astype(jnp.float32)
    lane = lax.broadcasted_iota(jnp.int32, (8, 128), 1)
    head = lax.broadcasted_iota(jnp.int32, (8, 128), 0)
    pick = jnp.where(lane // 64 == head, 1.0, 0.0)
    inner = lax.dot_general(
        pick, prod, NT, precision=lax.Precision.HIGHEST, preferred_element_type=jnp.float32
    )
    acc[...] = jnp.zeros_like(acc)
    for at in range(0, length, b):
        k, v = k_ref[at : at + b, :], v_ref[at : at + b, :]
        qs, dos = q_ref[at:length, :], do_ref[at:length, :]
        dks, dvs = [], []
        for h, mine in enumerate((low, ~low)):
            km = jnp.where(mine, k, jnp.zeros_like(k))
            vm = jnp.where(mine, v, jnp.zeros_like(v))
            s = mul(km * jnp.asarray(0.125, jnp.bfloat16), qs, NT)
            w = jnp.exp(s - lse_ref[0, h : h + 1, at:length])
            first = jnp.where(row <= col, w[:, :b], 0.0)
            w = jnp.concatenate([first, w[:, b:]], axis=1) if length - at > b else first
            ds = (w * (mul(vm, dos, NT) - inner[h : h + 1, at:length])).astype(jnp.bfloat16)
            dvs.append(mul(w.astype(jnp.bfloat16), dos))
            dks.append(mul(ds, qs))
            acc[at:length, :] += mul(ds, km, TN)
        dk_ref[at : at + b, :] = (jnp.where(low, dks[0], dks[1]) * 0.125).astype(jnp.bfloat16)
        dv_ref[at : at + b, :] = jnp.where(low, dvs[0], dvs[1]).astype(jnp.bfloat16)
    dq_ref[...] = (acc[...] * 0.125).astype(jnp.bfloat16)


def cross_fwd_body(q_ref, k_ref, v_ref, ok_ref, o_ref):
    low = low_lanes(q_ref.shape[0])
    q = q_ref[...] * jnp.asarray(0.125, jnp.bfloat16)
    mixed = []
    for mine in (low, ~low):
        s = mul(jnp.where(mine, q, jnp.zeros_like(q)), k_ref[...], NT)
        s = jnp.where(ok_ref[0:1, :] > 0, s, NEG_BIG)
        e = jnp.exp(s - jnp.max(s, axis=1, keepdims=True))
        total = jnp.sum(e, axis=1, keepdims=True)
        mixed.append(mul(e.astype(jnp.bfloat16), v_ref[...]) / total)
    o_ref[...] = jnp.where(low, mixed[0], mixed[1]).astype(jnp.bfloat16)


def cross_bwd_body(q_ref, k_ref, v_ref, ok_ref, do_ref, dq_ref, dk_ref, dv_ref):
    keys = k_ref.shape[0]
    low = low_lanes(keys)
    wide = low_lanes(q_ref.shape[0])
    q, do, k, v = q_ref[...], do_ref[...], k_ref[...], v_ref[...]
    dqs, dks, dvs = [], [], []
    for mine in (low, ~low):
        km = jnp.where(mine, k, jnp.zeros_like(k))
        vm = jnp.where(mine, v, jnp.zeros_like(v))
        s = mul(km * jnp.asarray(0.125, jnp.bfloat16), q, NT)
        s = jnp.where(ok_ref[:, 0:1] > 0, s, NEG_BIG)
        e = jnp.exp(s - jnp.max(s, axis=0, keepdims=True))
        w = e / jnp.sum(e, axis=0, keepdims=True)
        dw = mul(vm, do, NT)
        inner = jnp.sum(dw * w, axis=0, keepdims=True)
        ds = (w * (dw - inner)).astype(jnp.bfloat16)
        dvs.append(mul(w.astype(jnp.bfloat16), do))
        dks.append(mul(ds, q))
        dqs.append(mul(ds, km, TN))
    dq_ref[...] = (jnp.where(wide, dqs[0], dqs[1]) * 0.125).astype(jnp.bfloat16)
    dk_ref[...] = (jnp.where(low, dks[0], dks[1]) * 0.125).astype(jnp.bfloat16)
    dv_ref[...] = jnp.where(low, dvs[0], dvs[1]).astype(jnp.bfloat16)


class Scatter:
    def __init__(self, late, tile, got, part, from_late, out, sems, credit):
        self.late, self.tile, self.got = late, tile, got
        self.slots, self.count, self.free = credit
        self.part, self.from_late, self.out = part, from_late, out
        self.send_sem, self.recv_sem = sems
        z, y, x, c = place()
        self.z, self.y, self.x, self.c = z, y, x, c
        self.other = (chip(z, y, x), 1 - c)

    def ways(self, core):
        y, x = self.y, self.x
        return [
            flip(y, core * i1 + (1 - core) * i2) * 2 + flip(x, (1 - core) * i1 + core * i2)
            for i1 in range(2)
            for i2 in range(2)
        ]

    def partners(self):
        z, c = self.z, self.c
        way = self.ways(c)
        return [(zxor(z, k) * 4 + way[0], c) for k in (1, 2, 3)] + [
            (z * 4 + way[2], c),
            (z * 4 + way[1], c),
            self.other,
        ]

    def mine(self, u, j):
        way = self.ways(self.c)[j]
        return self.tile(u).at[:, way] if self.late(u) else self.tile(u).at[:, way, self.c]

    def remote(self, src, dst, u, idx, to):
        return pltpu.make_async_remote_copy(
            src_ref=src,
            dst_ref=dst,
            send_sem=self.send_sem.at[u, idx],
            recv_sem=self.recv_sem.at[u, idx],
            device_id=to,
            device_id_type=MESH,
        )

    def to_core(self, u, j):
        c = self.c
        src = self.tile(u).at[:, self.ways(1 - c)[j], 1 - c]
        return self.remote(src, self.got(u, 0).at[j], u, j, self.other)

    def to_first(self, u, i):
        to = (self.z * 4 + self.ways(self.c)[2], self.c)
        return self.remote(self.mine(u, 2 + i), self.got(u, 1).at[i], u, 4 + i, to)

    def to_second(self, u):
        to = (self.z * 4 + self.ways(self.c)[1], self.c)
        return self.remote(self.mine(u, 1), self.got(u, 2), u, 6, to)

    def to_z(self, u, k):
        zk = zxor(self.z, k)
        to = (zk * 4 + self.ways(self.c)[0], self.c)
        return self.remote(self.mine(u, 0).at[zk], self.got(u, 3).at[k - 1], u, 6 + k, to)

    def to_late(self, u):
        rows = self.part(u).shape[0] // 2
        theirs = pl.ds(pl.multiple_of((1 - self.c) * rows, rows), rows)
        return self.remote(self.part(u).at[theirs], self.from_late(u), u, 0, self.other)

    def add(self, u, j, term):
        mine = self.mine(u, j)

        @pl.loop(0, 4)
        def _(i):
            mine[i] = mine[i] + term[i]

    def step0(self, u):
        if self.late(u):
            return
        if u >= self.slots:
            pl.semaphore_wait(self.free, 1)
        if not self.late(u):
            for j in (2, 3, 0, 1):
                self.to_core(u, j).start()

    def step1(self, u):
        for j in (2, 3, 0, 1):
            if not self.late(u):
                self.to_core(u, j).wait_recv()
                self.add(u, j, self.got(u, 0).at[j])
            if j > 1:
                self.to_first(u, j - 2).start()
        if not self.late(u) and u < self.count - self.slots:
            pl.semaphore_signal(self.free, inc=1, device_id=self.other, device_id_type=MESH)

    def step2(self, u):
        for i in (1, 0):
            self.to_first(u, i).wait_recv()
            self.add(u, i, self.got(u, 1).at[i])
            if i == 1:
                self.to_second(u).start()

    def step3(self, u):
        self.to_second(u).wait_recv()
        self.add(u, 0, self.got(u, 2))
        for k in (2, 3, 1):
            self.to_z(u, k).start()

    def step4(self, u):
        got = self.got(u, 3)
        for k in (1, 2, 3):
            self.to_z(u, k).wait_recv()
        total = self.mine(u, 0)[self.z].astype(jnp.float32) + got[0].astype(jnp.float32)
        total = total + (got[1].astype(jnp.float32) + got[2].astype(jnp.float32))
        if self.late(u):
            self.part(u)[...] = total
            self.to_late(u).start()
        else:
            self.out(u, total, None)

    def step5(self, u):
        if self.late(u):
            rows = self.part(u).shape[0] // 2
            self.to_late(u).wait_recv()
            mine = self.part(u)[pl.ds(pl.multiple_of(self.c * rows, rows), rows)]
            self.out(u, mine, self.from_late(u)[...])

    def sent(self, u):
        if not self.late(u):
            for j in range(4):
                self.to_core(u, j).wait_send()
        for i in range(2):
            self.to_first(u, i).wait_send()
        self.to_second(u).wait_send()
        for k in (1, 2, 3):
            self.to_z(u, k).wait_send()

    def slot(self, t, order, gap=2):
        for lag, step in (
            (1, self.step1),
            (1 + gap, self.step2),
            (1 + 2 * gap, self.step3),
            (1 + 3 * gap, self.step4),
            (2 + 3 * gap, self.step5),
        ):
            if 0 <= t - lag < len(order):
                step(order[t - lag])


LAG = 2
DEPTH = 2 + 3 * LAG


def turn(src, dst):
    @pl.loop(0, src.shape[1] // 128)
    def _(i):
        at = pl.multiple_of(i * 128, 128)
        dst[pl.ds(at, 128), :] = src[:, pl.ds(at, 128)].T


def product(rows, right, tile):
    @pl.loop(0, 2)
    def _(i):
        value = mul(rows(i), right[...]).astype(tile.dtype)
        tile[pl.ds(2 * i, 2)] = value.reshape((2, *tile.shape[1:]))


def middle_body(
    h3, du, act, gm, w_in, w_outer, c_out, c_query, w_out, y2, y1, cq, ck, cv, c_key, c_value, ok, vec, sums_in, *refs
):
    out_in, out_outer, sums_out, cap_out, block_out, db2_out, dcq_out, dck_out, dcv_out, da_out, dy1_out, do_out = refs[:12]
    (h3_v, du_v, act_v, gm_v, left, left_act, tiles, got0, got1, got2, got3) = refs[12:23]
    (w_v, acc, y_v, dy_v, db_v, da_v, dc_v, cq_v, dcq_v, kv_v, dkv_v, cap_v) = refs[23:35]
    send_sem, recv_sem, load_sem, w_sem, out_sem, free_sem = refs[35:]
    units, depth, slots = 8, tiles.shape[0], got0.shape[0]
    rows, width = gm_v.shape
    step = 128

    def out(u, total, _):
        if u < 4:
            out_in[:, u * 1024 : (u + 1) * 1024] = total
        else:
            out_outer[(u - 4) * 32 : (u - 3) * 32, :] = total

    got = (got0, got1, got2, got3)
    ring = Scatter(
        lambda u: False,
        lambda u: tiles.at[u % depth],
        lambda u, i: got[i].at[u % slots if i == 0 else u],
        None,
        None,
        out,
        (send_sem, recv_sem),
        (slots, units, free_sem),
    )
    pairs = {
        "h3": (h3, h3_v),
        "du": (du, du_v),
        "act": (act, act_v),
        "gm": (gm, gm_v),
        "y2": (y2, y_v),
        "cq": (cq, cq_v),
        "ck": (ck, kv_v.at[0]),
        "cv": (cv, kv_v.at[1]),
        "y1": (y1, y_v),
    }
    loads = {
        name: pltpu.make_async_copy(src, dst, load_sem.at[i])
        for i, (name, (src, dst)) in enumerate(pairs.items())
    }
    parts = [w_in.at[:, pl.ds(i * 1024, 1024)] for i in range(4)]
    parts += [c_out, c_query, c_key, c_value, w_out]
    parts += [w_outer.at[pl.ds(i * 1024, 1024)] for i in range(4)]
    weights = [
        pltpu.make_async_copy(part, w_v.at[n % 2], w_sem.at[n % 2]) for n, part in enumerate(parts)
    ]
    stores = [
        pltpu.make_async_copy(src, dst, out_sem.at[i])
        for i, (src, dst) in enumerate(
            (
                (db_v, db2_out),
                (dcq_v, dcq_out),
                (dkv_v.at[0], dck_out),
                (dkv_v.at[1], dcv_out),
                (da_v, da_out),
                (dy_v, dy1_out),
                (dc_v, do_out),
                (h3_v, block_out),
            )
        )
    ]

    def use(n, work):
        weights[n].wait()
        work(w_v.at[n % 2])
        if n + 2 < len(weights):
            weights[n + 2].start()

    def over_rows(work):
        @pl.loop(0, rows // step)
        def _(i):
            work(pl.ds(i * step, step))

    def make(u):
        if u >= depth:
            ring.sent(u - depth)
        tile = tiles.at[u % depth]
        if u < 4:
            right = du_v.at[:, u * 1024 : (u + 1) * 1024]
            product(lambda i: left[pl.ds(i * 512, 512), :], right, tile)
        else:
            product(
                lambda i, b=u - 4: left_act[pl.ds(i * 16, 16), b].reshape(512, 512), gm_v, tile
            )
        ring.step0(u)

    def turn_act(t):
        @pl.loop(t * 8, t * 8 + 8)
        def _(r):
            at = pl.multiple_of(r * 128, 128)
            left_act[r] = act_v[:, pl.ds(at, 128)].T.reshape(4, 32, 512)

    def add_dh3(j):
        def work(w):
            def body(at):
                term = mul(du_v[at, j * 1024 : (j + 1) * 1024], w[...], NT)
                acc[at, :] = term if j == 0 else acc[at, :] + term

            over_rows(body)

        use(j, work)

    def norm3():
        loads["y2"].wait()
        sums_out[...] = sums_in[...]

        def body(at):
            value = y_v[at, :]
            grads, dgain, dbias = norm_back(value, vec[4:5, :], acc[at, :])
            dy = gm_v[at, :].astype(jnp.float32) + grads
            dy_v[at, :] = dy
            db_v[at, :] = dy.astype(jnp.bfloat16)
            acc[at, :] = value + vec[6:7, :]
            sums_out[4:5, :] += dgain
            sums_out[5:6, :] += dbias

        over_rows(body)
        stores[0].start()
        loads["y1"].start()

    def back_out(w):
        def body(at):
            dc_v[at, :] = mul(db_v[at, :], w[...], NT).astype(jnp.bfloat16)

        over_rows(body)

    def cross(lo, hi):
        @pl.loop(lo, hi)
        def _(i):
            at = pl.ds(pl.multiple_of(i * 128, 128), 128)
            cross_bwd_body(
                cq_v.at[:, at],
                kv_v.at[0, :, at],
                kv_v.at[1, :, at],
                ok.at[1],
                dc_v.at[:, at],
                dcq_v.at[:, at],
                dkv_v.at[0, :, at],
                dkv_v.at[1, :, at],
            )

    def norm2(w):
        loads["y1"].wait()

        def body(at):
            dh = mul(dcq_v[at, :], w[...], NT)
            grads, dgain, dbias = norm_back(y_v[at, :], vec[2:3, :], dh)
            dy = dy_v[at, :] + grads
            dy_v[at, :] = dy
            da_v[at, :] = dy.astype(jnp.bfloat16)
            sums_out[2:3, :] += dgain
            sums_out[3:4, :] += dbias

        over_rows(body)
        stores[4].start()
        stores[5].start()

    def back_key(w):
        cap_v[...] = mul(dkv_v[0], w[...], NT)

    def back_value(w):
        cap_out[...] = (cap_v[...] + mul(dkv_v[1], w[...], NT)).astype(jnp.bfloat16)

    def back_self(w):
        def body(at):
            dc_v[at, :] = mul(da_v[at, :], w[...], NT).astype(jnp.bfloat16)

        over_rows(body)
        stores[6].start()

    def add_out(j):
        def work(w):
            def body(at):
                term = acc[at, :] + mul(act_v[at, j * 1024 : (j + 1) * 1024], w[...])
                if j < 3:
                    acc[at, :] = term
                else:
                    h3_v[at, :] = term.astype(jnp.bfloat16)

            over_rows(body)

        use(9 + j, work)

    for name in ("h3", "du"):
        loads[name].start()
    weights[0].start()
    weights[1].start()
    greet(ring.partners())
    loads["h3"].wait()
    turn(h3_v, left)
    loads["du"].wait()
    for name in ("act", "gm", "y2", "cq", "ck", "cv"):
        loads[name].start()
    make(0)
    make(1)
    add_dh3(0)
    ring.slot(1, range(1), 1)
    make(2)
    loads["act"].wait()
    turn_act(0)
    ring.slot(2, range(2), 1)
    add_dh3(1)
    add_dh3(2)
    make(3)
    ring.slot(3, range(3), 1)
    turn_act(1)
    add_dh3(3)
    loads["gm"].wait()
    norm3()
    ring.slot(4, range(4), 1)
    turn_act(2)
    turn_act(3)
    make(4)
    use(4, back_out)
    ring.slot(5, range(5), 1)
    make(5)
    for name in ("cq", "ck", "cv"):
        loads[name].wait()
    cross(0, 4)
    ring.slot(6, range(6), 1)
    make(6)
    cross(4, 8)
    for i in (1, 2, 3):
        stores[i].start()
    ring.slot(7, range(7), 1)
    make(7)
    use(5, norm2)
    ring.slot(8, range(8), 1)
    use(6, back_key)
    use(7, back_value)
    use(8, back_self)
    ring.slot(9, range(units), 1)
    add_out(0)
    add_out(1)
    ring.slot(10, range(units), 1)
    add_out(2)
    add_out(3)
    stores[7].start()
    ring.slot(11, range(units), 1)
    ring.slot(12, range(units), 1)
    for u in range(max(units - depth, 0), units):
        ring.sent(u)
    for store in stores:
        store.wait()


def middle(operands, collective_id):
    depth, bf, f32, vm = 5, jnp.bfloat16, jnp.float32, pltpu.VMEM
    shape = jax.ShapeDtypeStruct
    rows = (512, 1024)
    inside = pl.BlockSpec(memory_space=pltpu.VMEM)
    return pl.pallas_call(
        middle_body,
        out_shape=[
            shape((32, 4096), f32),
            shape((128, 1024), f32),
            shape((16, 1024), f32),
            shape((128, 1024), bf),
            shape(rows, bf),
            shape(rows, bf),
            shape(rows, bf),
            shape((128, 1024), bf),
            shape((128, 1024), bf),
            shape(rows, bf),
            shape(rows, f32),
            shape(rows, bf),
        ],
        in_specs=[ANY] * 16 + [inside] * 3,
        out_specs=[inside] * 4 + [ANY] * 8,
        scratch_shapes=[
            vm(rows, bf),
            vm((512, 4096), bf),
            vm((512, 4096), bf),
            vm(rows, bf),
            vm((1024, 512), bf),
            vm((32, 4, 32, 512), bf),
            vm((depth, 4, 4, 2, 32, 1024), bf),
            vm((4, 4, 4, 32, 1024), bf),
            vm((8, 2, 4, 32, 1024), bf),
            vm((8, 4, 32, 1024), bf),
            vm((8, 3, 32, 1024), bf),
            vm((2, 1024, 1024), bf),
            vm(rows, f32),
            vm(rows, f32),
            vm(rows, f32),
            vm(rows, bf),
            vm(rows, bf),
            vm(rows, bf),
            vm(rows, bf),
            vm(rows, bf),
            vm((2, 128, 1024), bf),
            vm((2, 128, 1024), bf),
            vm((128, 1024), f32),
            pltpu.SemaphoreType.DMA((8, 10)),
            pltpu.SemaphoreType.DMA((8, 10)),
            pltpu.SemaphoreType.DMA((9,)),
            pltpu.SemaphoreType.DMA((2,)),
            pltpu.SemaphoreType.DMA((8,)),
            pltpu.SemaphoreType.REGULAR,
        ],
        compiler_params=pltpu.CompilerParams(
            collective_id=collective_id,
            has_side_effects=True,
            vmem_limit_bytes=59 * 1024 * 1024,
        ),
        name="middle",
    )(*operands)


def tail_body(q, k, v, o, lse, grad, h1, attn, da, h2, dcq, cattn, db2, e, dck, dcv, wq, wk, wv, x, dy1, gain, sums, cap, row, image_out, *refs):
    outs, total_out, refs = refs[:9], refs[9], refs[10:]
    (q_v, k_v, v_v, o_v, lse_v, do_v, cap_v, a_v, r_v, e_v, dc_v, x_v, dx_v, gain_v, sum_v) = refs[:15]
    (acc, dq_v, dk_v, dv_v, left, left1, left_e, tiles, late_tiles) = refs[15:24]
    big, late = refs[24:28], refs[28:31]
    part, from_late, give_v, take_v, got_sum = refs[31:36]
    send_sem, recv_sem, load_sem, pair_send, pair_recv, keep_sem, row_sem, sum_send, sum_recv, free_sem = refs[36:]
    normal, units, depth, slots = 14, 20, tiles.shape[0], refs[24].shape[0]
    dp, c = lax.axis_index("dp"), lax.axis_index("seq")
    length, width = q_v.shape
    pairs, rows = width // 128, length // 2
    mine = pl.ds(pl.multiple_of(c * rows, rows), rows)
    theirs = pl.ds(pl.multiple_of((1 - c) * rows, rows), rows)

    def out(u, total, other):
        what, h = divmod(u, 2)
        lanes = slice(h * 512, (h + 1) * 512)
        if what < 5:
            outs[what][:, lanes] = total
        elif u < normal:
            outs[5][(what - 5) * 32 : (what - 4) * 32, lanes] = total
        else:
            at = pl.multiple_of(c * 512 + h * 256, 128)
            outs[what - 1][:, pl.ds(at, 256)] = total
            at = pl.multiple_of((1 - c) * 512 + h * 256, 128)
            outs[what - 1][:, pl.ds(at, 256)] = other

    ring = Scatter(
        lambda u: u >= normal,
        lambda u: tiles.at[u % depth] if u < normal else late_tiles.at[u - normal],
        lambda u, i: late[i - 1].at[u - normal]
        if u >= normal
        else big[i].at[u % slots if i == 0 else u],
        lambda u: part.at[u - normal],
        lambda u: from_late.at[u - normal],
        out,
        (send_sem, recv_sem),
        (slots, normal, free_sem),
    )

    def load(i, src, dst):
        return pltpu.make_async_copy(src, dst, load_sem.at[i])

    loads = {
        "a0": load(0, attn, a_v.at[0]),
        "r0": load(1, da, r_v.at[0]),
        "q": load(2, q, q_v),
        "k": load(3, k, k_v),
        "v": load(4, v, v_v),
        "o": load(5, o, o_v),
        "lse": load(6, lse, lse_v),
        "a1": load(7, h2, a_v.at[1]),
        "r1": load(8, dcq, r_v.at[1]),
        "a2": load(9, cattn, a_v.at[0]),
        "r2": load(10, db2, r_v.at[0]),
        "e": load(11, e, e_v),
        "ck": load(12, dck, dc_v.at[0]),
        "cv": load(13, dcv, dc_v.at[1]),
        "h0": load(14, h1.at[pl.ds(0, 512)], a_v.at[1]),
        "h1": load(22, h1.at[pl.ds(512, 512)], a_v.at[0]),
        "cap": load(23, cap, cap_v),
        "wq": load(15, wq, q_v),
        "wk": load(16, wk, k_v),
        "wv": load(17, wv, v_v),
        "x": load(18, x, x_v),
        "dy1": load(19, dy1, dx_v),
        "gain": load(20, gain.at[pl.ds(0, 8)], gain_v),
        "sums": load(21, sums, sum_v),
    }

    def lane(i, core):
        return pl.ds(pl.multiple_of(core * width + i * 128, 128), 128)

    def keep(i):
        return pltpu.make_async_copy(grad.at[:, lane(i, c)], do_v.at[i, mine], keep_sem.at[i])

    def give(i):
        return pltpu.make_async_remote_copy(
            src_ref=grad.at[:, lane(i, 1 - c)],
            dst_ref=do_v.at[i, mine],
            send_sem=pair_send.at[i],
            recv_sem=pair_recv.at[i],
            device_id=ring.other,
            device_id_type=MESH,
        )

    for name in ("a0", "r0", "a1", "r1"):
        loads[name].start()
    greet(ring.partners())
    for i in range(pairs):
        give(i).start()
        keep(i).start()
    for name in ("q", "k", "v", "o", "lse", "e", "ck", "cv", "cap", "x", "dy1", "gain", "sums"):
        loads[name].start()

    def pair(i):
        keep(i).wait()
        give(i).wait()
        at = pl.ds(i * 128, 128)
        self_bwd_pair(
            q_v.at[:, at],
            k_v.at[:, at],
            v_v.at[:, at],
            o_v.at[:, at],
            do_v.at[i],
            lse_v.at[pl.ds(i, 1)],
            dq_v.at[:, at],
            dk_v.at[:, at],
            dv_v.at[:, at],
            acc,
        )

    def turn_late():
        loads["h0"].wait()
        turn(a_v.at[1], left1.at[:, pl.ds(0, 512)])
        loads["h1"].wait()
        turn(a_v.at[0], left1.at[:, pl.ds(512, 512)])

    def make(u):
        if depth <= u < normal:
            ring.sent(u - depth)
        what, h = divmod(u, 2)
        lanes = slice(h * 512, (h + 1) * 512)
        if what < 3:
            slot = what % 2
            if h == 0:
                loads[f"a{what}"].wait()
                loads[f"r{what}"].wait()
                turn(a_v.at[slot], left)
            right = r_v.at[slot, :, lanes]
            product(lambda i: left[pl.ds(i * 512, 512), :], right, tiles.at[u % depth])
            if h == 1:
                for name in (("a2", "r2"), ("h0",), ("h1",))[what]:
                    loads[name].start()
        elif what < 5:
            if what == 3 and h == 0:
                loads["e"].wait()
                loads["ck"].wait()
                loads["cv"].wait()
                turn(e_v, left_e)
            right = dc_v.at[what - 3, :, lanes]
            product(lambda i: left_e[pl.ds(i * 512, 512), :], right, tiles.at[u % depth])
        elif u < normal:
            if what == 5 and h == 0:
                loads["cap"].wait()
            tile = tiles.at[u % depth]
            for core in range(2):
                at = core * 64 + (what - 5) * 32
                block = cap_v[at : at + 32, lanes]

                @pl.loop(0, 16)
                def _(i, core=core, block=block):
                    hit = row[0:1, 0:512] == i.astype(jnp.float32)
                    tile[i // 4, i % 4, core] = jnp.where(hit, block, jnp.zeros_like(block))

        else:
            right = (dq_v, dk_v, dv_v)[what - 7].at[:, h * 256 : (h + 1) * 256]
            product(lambda i: left1[pl.ds(i * 512, 512), :], right, late_tiles.at[u - normal])
        ring.step0(u)

    swap = pltpu.make_async_remote_copy(
        src_ref=give_v,
        dst_ref=take_v,
        send_sem=row_sem.at[0],
        recv_sem=row_sem.at[1],
        device_id=ring.other,
        device_id_type=MESH,
    )

    def back(at):
        total = mul(dq_v[at, :], q_v[...], NT) + mul(dk_v[at, :], k_v[...], NT)
        return total + mul(dv_v[at, :], v_v[...], NT)

    def give_rows():
        for name in ("wq", "wk", "wv"):
            loads[name].wait()

        @pl.loop(0, rows // 128)
        def _(i):
            at = pl.ds(pl.multiple_of((1 - c) * rows + i * 128, 128), 128)
            give_v[pl.ds(i * 128, 128), :] = back(at).astype(jnp.bfloat16)

        swap.start()

    def take_rows():
        swap.wait_recv()
        for name in ("x", "dy1", "gain", "sums"):
            loads[name].wait()
        step = 128

        @pl.loop(0, rows // step)
        def _(i):
            at = pl.ds(i * step, step)
            whole = pl.ds(pl.multiple_of(c * rows + i * step, step), step)
            dh = back(whole) + take_v[at, :].astype(jnp.float32)
            grads, dgain, dbias = norm_back(x_v[at, :].astype(jnp.float32), gain_v[0:1, :], dh)
            dx_v[at, :] = dx_v[at, :] + grads
            sum_v[0:1, :] = sum_v[0:1, :] + dgain
            sum_v[1:2, :] = sum_v[1:2, :] + dbias

    write = pltpu.make_async_copy(dx_v, image_out, row_sem.at[2])

    way = ring.ways(c)
    peers = [
        [ring.other],
        [(ring.z * 4 + way[2], c)],
        [(ring.z * 4 + way[1], c)],
        [(zxor(ring.z, n) * 4 + way[0], c) for n in (1, 2, 3)],
    ]

    def sum_send_of(s, n):
        return pltpu.make_async_remote_copy(
            src_ref=sum_v if s == 0 else got_sum.at[5 + s],
            dst_ref=got_sum.at[s + n],
            send_sem=sum_send.at[s + n],
            recv_sem=sum_recv.at[s + n],
            device_id=peers[s][n],
            device_id_type=MESH,
        )

    def start_sum(s):
        for n in range(len(peers[s])):
            sum_send_of(s, n).start()

    def take_sum(s):
        total = sum_v[...] if s == 0 else got_sum[5 + s]
        for n in range(len(peers[s])):
            sum_send_of(s, n).wait_recv()
            total = total + got_sum[s + n]
        if s == 3:
            total_out[...] = total
        else:
            got_sum[6 + s] = total
            start_sum(s + 1)

    def start_pairs():
        for name in ("q", "k", "v", "o", "lse"):
            loads[name].wait()
        pair(0)

    def end_pairs():
        pair(pairs - 1)
        for name in ("wq", "wk", "wv"):
            loads[name].start()

    def own_rows():
        take_rows()
        write.start()
        start_sum(0)

    order = [*range(12), *range(normal, units), *range(12, normal)]
    tasks = {
        1: [start_pairs],
        3: [lambda: pair(1)],
        5: [lambda: pair(2)],
        7: [end_pairs],
        9: [turn_late],
        10: [give_rows],
        12: [own_rows],
        14: [lambda: take_sum(0)],
        16: [lambda: take_sum(1)],
        18: [lambda: take_sum(2)],
        20: [lambda: take_sum(3)],
    }
    for t in range(units + 3 + 3 * LAG):
        if t < units:
            make(order[t])
        ring.slot(t, order)
        for task in tasks.get(t, ()):
            task()
    for u in range(normal - depth, units):
        ring.sent(u)
    for u in range(normal, units):
        ring.to_late(u).wait_send()
    swap.wait_send()
    write.wait()
    for s in range(4):
        for n in range(len(peers[s])):
            sum_send_of(s, n).wait_send()


def norm_back(value, gain, dh):
    center = value - jnp.mean(value, axis=1, keepdims=True)
    r = lax.rsqrt(jnp.mean(center * center, axis=1, keepdims=True) + EPSILON)
    hat = center * r
    dhg = dh * gain
    grads = r * (
        dhg
        - jnp.mean(dhg, axis=1, keepdims=True)
        - hat * jnp.mean(dhg * hat, axis=1, keepdims=True)
    )
    return grads, jnp.sum(dh * hat, axis=0, keepdims=True), jnp.sum(dh, axis=0, keepdims=True)


def scatter_tail(operands, collective_id):
    bf, f32, depth = jnp.bfloat16, jnp.float32, DEPTH
    vm = pltpu.VMEM
    outs = [jax.ShapeDtypeStruct((512, 1024), f32)] + [
        jax.ShapeDtypeStruct((64 if i == 5 else 32, 1024), f32) for i in range(9)
    ]
    outs.append(jax.ShapeDtypeStruct((16, 1024), f32))
    return pl.pallas_call(
        tail_body,
        out_shape=outs,
        in_specs=[ANY] * (len(operands) - 1) + [pl.BlockSpec(memory_space=pltpu.VMEM)],
        out_specs=[ANY] + [pl.BlockSpec(memory_space=pltpu.VMEM)] * 10,
        scratch_shapes=[
            vm((1024, 512), bf),
            vm((1024, 512), bf),
            vm((1024, 512), bf),
            vm((1024, 512), bf),
            vm((4, 2, 1024), f32),
            vm((4, 1024, 128), bf),
            vm((128, 1024), bf),
            vm((2, 512, 1024), bf),
            vm((2, 512, 1024), bf),
            vm((128, 1024), bf),
            vm((2, 128, 1024), bf),
            vm((512, 1024), bf),
            vm((512, 1024), f32),
            vm((8, 1024), f32),
            vm((16, 1024), f32),
            vm((1024, 128), f32),
            vm((1024, 512), bf),
            vm((1024, 512), bf),
            vm((1024, 512), bf),
            vm((1024, 512), bf),
            vm((1024, 1024), bf),
            vm((1024, 128), bf),
            vm((depth, 4, 4, 2, 32, 512), bf),
            vm((6, 4, 4, 64, 256), bf),
            vm((6, 4, 4, 32, 512), bf),
            vm((14, 2, 4, 32, 512), bf),
            vm((14, 4, 32, 512), bf),
            vm((14, 3, 32, 512), bf),
            vm((6, 2, 4, 64, 256), bf),
            vm((6, 4, 64, 256), bf),
            vm((6, 3, 64, 256), bf),
            vm((6, 64, 256), f32),
            vm((6, 32, 256), f32),
            vm((512, 1024), bf),
            vm((512, 1024), bf),
            vm((9, 16, 1024), f32),
            pltpu.SemaphoreType.DMA((20, 10)),
            pltpu.SemaphoreType.DMA((20, 10)),
            pltpu.SemaphoreType.DMA((24,)),
            pltpu.SemaphoreType.DMA((4,)),
            pltpu.SemaphoreType.DMA((4,)),
            pltpu.SemaphoreType.DMA((4,)),
            pltpu.SemaphoreType.DMA((3,)),
            pltpu.SemaphoreType.DMA((6,)),
            pltpu.SemaphoreType.DMA((6,)),
            pltpu.SemaphoreType.REGULAR,
        ],
        compiler_params=pltpu.CompilerParams(
            collective_id=collective_id,
            has_side_effects=True,
            vmem_limit_bytes=59 * 1024 * 1024,
        ),
        name="scatter_tail",
    )(*operands)


def norm_fwd(value, gain, shift):
    center = value - jnp.mean(value, axis=1, keepdims=True)
    spread = jnp.mean(center * center, axis=1, keepdims=True)
    return center * lax.rsqrt(spread + EPSILON) * gain + shift


GELU_IN = 0.7978845608028654
GELU_CUBE = 0.044715


def gelu_both(u):
    square = u * u
    t = jnp.tanh(GELU_IN * (u + GELU_CUBE * (square * u)))
    half = 0.5 * (1.0 + t)
    slope = half + 0.5 * u * (1.0 - t * t) * (GELU_IN * (1.0 + 3.0 * GELU_CUBE * square))
    return u * half, slope


FRONT_IN = (
    "w_query",
    "w_key",
    "w_value",
    "packed",
    "w_out",
    "encoder",
    "c_query",
    "c_key",
    "c_value",
    "c_out",
    "w_outer",
    "w_in",
    "images",
    "gm",
    "caption_seg",
    "image_row",
    "image_seg",
)
FRONT_OUT = (
    "wq",
    "wk",
    "wv",
    "w_out_all",
    "c_query_all",
    "c_key_all",
    "c_value_all",
    "c_out_all",
    "w_outer_all",
    "w_in_all",
    "h1",
    "q",
    "k",
    "v",
    "heads",
    "attn",
    "y1",
    "h2",
    "cq",
    "ck",
    "cv",
    "caption",
    "cattn",
    "y2",
    "h3",
    "act",
    "du",
    "lse",
    "vec",
    "ok",
    "sums",
)
FRONT_VMEM = (
    "table",
    "enc",
    "both",
    "wqkv",
    "h1_v",
    "q_v",
    "k_v",
    "v_v",
    "obuf",
    "attn_v",
    "y1_v",
    "h2_v",
    "cq_v",
    "kv_v",
    "cap_v",
    "cattn_v",
    "y2_v",
    "h3_v",
    "gm_v",
    "dact",
    "act_v",
    "du_v",
    "w_v",
    "bin",
)


def front_body(*refs):
    names = FRONT_IN + FRONT_OUT + FRONT_VMEM
    r = dict(zip(names, refs))
    (send_sem, recv_sem, local_sem, pair_sem, give_send, give_recv, keep_sem, w_sem, out_sem, gm_sem) = refs[len(names) :]
    c = lax.axis_index("seq")
    rows, step = 512, 128
    own = [r["w_query"], r["w_key"], r["w_value"], r["packed"], r["w_out"]]
    own += [r["encoder"].at[:, pl.ds(pl.multiple_of(c * 64, 64), 64)]]
    own += [r["c_query"], r["c_key"], r["c_value"], r["c_out"], r["w_outer"]]
    own += [r["w_in"].at[:, i * 1024 : (i + 1) * 1024] for i in range(4)]
    full = [r["wqkv"].at[i] for i in range(3)] + [r["table"], r["w_out_all"], r["enc"]]
    full += [r["c_query_all"], r["c_key_all"], r["c_value_all"], r["c_out_all"], r["w_outer_all"]]
    full += [r["w_in_all"].at[:, i * 1024 : (i + 1) * 1024] for i in range(4)]
    n = len(own)
    ring = Gather(3, (), own, full, send_sem, recv_sem, local_sem)
    order = [3, 0, 1, 2, *range(4, n)]

    def slot(t, ahead=2):
        for lead, todo in ((3 * ahead + 1, begin), (2 * ahead, along), (ahead, first), (0, second)):
            for i in range(t + lead + 1):
                todo(i)

    done = set()

    def once(step, name):
        def run(i):
            if i < n and (name, i) not in done:
                done.add((name, i))
                step(order[i])

        return run

    begin, along = once(ring.start, "start"), once(ring.along_z, "z")
    first, second = once(ring.first, "first"), once(ring.second, "second")

    mine = r["both"].at[pl.ds(pl.multiple_of(c * rows, rows), rows)]
    keep_image = pltpu.make_async_copy(r["images"], mine, pair_sem.at[0])
    give_image = pltpu.make_async_remote_copy(
        src_ref=r["images"],
        dst_ref=mine,
        send_sem=pair_sem.at[1],
        recv_sem=pair_sem.at[2],
        device_id=ring.other,
        device_id_type=MESH,
    )
    load_gm = pltpu.make_async_copy(r["gm"], r["gm_v"], gm_sem)
    places = [
        ("wqkv", 0, "wq"),
        ("wqkv", 1, "wk"),
        ("wqkv", 2, "wv"),
        ("h1_v", None, "h1"),
        ("q_v", None, "q"),
        ("k_v", None, "k"),
        ("v_v", None, "v"),
        ("attn_v", None, "attn"),
        ("y1_v", None, "y1"),
        ("h2_v", None, "h2"),
        ("cq_v", None, "cq"),
        ("kv_v", 0, "ck"),
        ("kv_v", 1, "cv"),
        ("cap_v", None, "caption"),
        ("cattn_v", None, "cattn"),
        ("y2_v", None, "y2"),
        ("h3_v", None, "h3"),
    ]
    stores = {
        dst: pltpu.make_async_copy(r[src] if at is None else r[src].at[at], r[dst], out_sem.at[i])
        for i, (src, at, dst) in enumerate(places)
    }
    for j in range(4):
        lanes = slice(j * 1024, (j + 1) * 1024)
        for i, (src, dst) in enumerate((("act_v", "act"), ("du_v", "du"))):
            stores[dst, j] = pltpu.make_async_copy(
                r[src].at[:, lanes], r[dst].at[:, lanes], out_sem.at[len(places) + 2 * j + i]
            )
    parts = [r["w_out_all"], r["c_query_all"], r["c_key_all"], r["c_value_all"], r["c_out_all"]]
    parts += [r["w_outer_all"].at[i * 1024 : (i + 1) * 1024] for i in range(4)] + full[11:]
    weights = [
        pltpu.make_async_copy(part, r["w_v"].at[i % 2], w_sem.at[i % 2])
        for i, part in enumerate(parts)
    ]

    def weight(i):
        weights[i].wait()
        return r["w_v"].at[i % 2]

    def over(count, work):
        @pl.loop(0, count // step)
        def _(i):
            work(pl.ds(i * step, step))

    vec, table = r["vec"], r["table"]

    def unpack():
        for i in range(8):
            lanes = slice(i * 128, (i + 1) * 128)
            at = 4 * i * 16
            vec[:, lanes] = (table[at : at + 16] + table[at + 16 : at + 32]) + (
                table[at + 32 : at + 48] + table[at + 48 : at + 64]
            )
            for j in range(4):
                at = (8 * j + i) * 16 + 7
                r["bin"][j : j + 1, lanes] = table[at : at + 1]

    def row(i):
        return vec[i : i + 1, :]

    def norm1(at):
        value = norm_fwd(r["both"][at, :].astype(jnp.float32), row(0), row(1))
        r["h1_v"][at, :] = value.astype(jnp.bfloat16)

    def project(i):
        def work(at):
            value = mul(r["h1_v"][at, :], r["wqkv"][i])
            r[("q_v", "k_v", "v_v")[i]][at, :] = value.astype(jnp.bfloat16)

        over(2 * rows, work)
        stores[("wq", "wk", "wv")[i]].start()
        stores[("q", "k", "v")[i]].start()

    def keep(i):
        at = pl.multiple_of(c * 512 + i * 128, 128)
        src = r["obuf"].at[i, pl.ds(pl.multiple_of(c * rows, rows), rows)]
        return pltpu.make_async_copy(src, r["attn_v"].at[:, pl.ds(at, 128)], keep_sem.at[i])

    def give(i):
        at = pl.multiple_of(c * 512 + i * 128, 128)
        return pltpu.make_async_remote_copy(
            src_ref=r["obuf"].at[i, pl.ds(pl.multiple_of((1 - c) * rows, rows), rows)],
            dst_ref=r["attn_v"].at[:, pl.ds(at, 128)],
            send_sem=give_send.at[i],
            recv_sem=give_recv.at[i],
            device_id=ring.other,
            device_id_type=MESH,
        )

    def pair(i):
        at = pl.ds(i * 128, 128)

        def put(start, value):
            r["obuf"][i, pl.ds(start, value.shape[0]), :] = value
            r["heads"][pl.ds(start, value.shape[0]), i * 128 : (i + 1) * 128] = value

        self_fwd_pair(
            r["q_v"].at[:, at], r["k_v"].at[:, at], r["v_v"].at[:, at], r["lse"].at[pl.ds(i, 1)], put
        )
        keep(i).start()
        give(i).start()

    def self_out(w):
        def work(at):
            image = r["images_f"](at)
            y1 = image + mul(r["attn_v"][at, :], w[...])
            r["y1_v"][at, :] = y1
            r["h2_v"][at, :] = norm_fwd(y1, row(2), row(3)).astype(jnp.bfloat16)

        over(rows, work)

    def own_image(at):
        start = pl.multiple_of(c * rows + at.start, step)
        return r["both"][pl.ds(start, step), :].astype(jnp.float32)

    r["images_f"] = own_image

    def cross_query(w):
        def work(at):
            r["cq_v"][at, :] = mul(r["h2_v"][at, :], w[...]).astype(jnp.bfloat16)

        over(rows, work)

    def pick_caption():
        line = r["image_row"][0]
        r["cap_v"][0:64, :] = r["enc"][2 * line]
        r["cap_v"][64:128, :] = r["enc"][2 * line + 1]
        chosen = lax.broadcasted_iota(jnp.int32, (16, 128), 0) == line
        seg = jnp.sum(jnp.where(chosen, r["caption_seg"][...], 0), axis=0, keepdims=True)
        allowed = jnp.where(seg == r["image_seg"][0], 1.0, 0.0)
        wide = jnp.broadcast_to(allowed, (128, 128))
        r["ok"][0] = wide
        r["ok"][1] = wide.T

    def cross_out(w):
        def work(at):
            y2 = r["y1_v"][at, :] + mul(r["cattn_v"][at, :], w[...])
            r["y2_v"][at, :] = y2
            r["h3_v"][at, :] = norm_fwd(y2, row(4), row(5)).astype(jnp.bfloat16)

        over(rows, work)

    def cross(lo, hi):
        @pl.loop(lo, hi)
        def _(i):
            at = pl.ds(pl.multiple_of(i * 128, 128), 128)
            cross_fwd_body(
                r["cq_v"].at[:, at],
                r["kv_v"].at[0, :, at],
                r["kv_v"].at[1, :, at],
                r["ok"].at[0],
                r["cattn_v"].at[:, at],
            )

    def back_outer(j, w):
        def work(at):
            r["dact"][at, j * 1024 : (j + 1) * 1024] = mul(r["gm_v"][at, :], w[...], NT)

        over(rows, work)

    def hidden(j, w):
        lanes = slice(j * 1024, (j + 1) * 1024)

        def work(at):
            u = mul(r["h3_v"][at, :], w[...]) + r["bin"][j : j + 1, :]
            act, slope = gelu_both(u)
            r["act_v"][at, lanes] = act.astype(jnp.bfloat16)
            du = (r["dact"][at, lanes] * slope).astype(jnp.bfloat16)
            r["du_v"][at, lanes] = du
            r["sums"][7 + j : 8 + j, :] += jnp.sum(du.astype(jnp.float32), axis=0, keepdims=True)

        over(rows, work)

    greet(ring.partners())
    for i in range(4):
        begin(i)
    keep_image.start()
    give_image.start()
    for g in range(3):
        ring.swapped(g)
    begin(4)
    load_gm.start()
    r["sums"][...] = jnp.zeros_like(r["sums"])
    slot(0, 1)
    ring.ready(3)
    unpack()
    keep_image.wait()
    give_image.wait_recv()
    slot(1, 1)
    over(2 * rows, norm1)
    stores["h1"].start()
    project(0)
    slot(2, 1)
    project(1)
    slot(3, 1)
    project(2)
    slot(3)
    pair(0)
    slot(4)
    ring.ready(4)
    weights[0].start()
    pair(1)
    along(9)
    pair(2)
    first(7)
    pair(3)
    slot(5)
    for i in range(4):
        keep(i).wait()
        give(i).wait_recv()
    stores["attn"].start()
    self_out(weight(0))
    stores["y1"].start()
    stores["h2"].start()
    slot(6)
    ring.ready(5)
    pick_caption()
    stores["caption"].start()
    ring.ready(6)
    weights[1].start()
    cross_query(weight(1))
    stores["cq"].start()
    slot(7)
    ring.ready(7)
    weights[2].start()
    r["kv_v"][0] = mul(r["cap_v"][...], weight(2)[...]).astype(jnp.bfloat16)
    stores["ck"].start()
    slot(8)
    ring.ready(8)
    weights[3].start()
    r["kv_v"][1] = mul(r["cap_v"][...], weight(3)[...]).astype(jnp.bfloat16)
    stores["cv"].start()
    cross(0, 4)
    slot(9)
    cross(4, 8)
    stores["cattn"].start()
    ring.ready(9)
    weights[4].start()
    cross_out(weight(4))
    stores["y2"].start()
    stores["h3"].start()
    load_gm.wait()
    r["sums"][6:7, :] = jnp.sum(r["gm_v"][...].astype(jnp.float32), axis=0, keepdims=True)
    slot(10)
    ring.ready(10)
    weights[5].start()
    weights[6].start()
    back_outer(0, weight(5))
    weights[7].start()
    back_outer(1, weight(6))
    weights[8].start()
    slot(11)
    back_outer(2, weight(7))
    ring.ready(11)
    weights[9].start()
    back_outer(3, weight(8))
    for j in range(4):
        if j < 3:
            slot(12 + j)
            ring.ready(12 + j)
            weights[10 + j].start()
        hidden(j, weight(9 + j))
        stores["act", j].start()
        stores["du", j].start()
    for g in range(n):
        ring.sent(g)
    give_image.wait_send()
    for i in range(4):
        give(i).wait_send()
    for store in stores.values():
        store.wait()


def front(operands, collective_id):
    bf, f32, vm, shape = jnp.bfloat16, jnp.float32, pltpu.VMEM, jax.ShapeDtypeStruct
    square, rows, head = (1024, 1024), (512, 1024), (1024, 512)
    inside = pl.BlockSpec(memory_space=pltpu.VMEM)
    scalar = pl.BlockSpec(memory_space=pltpu.SMEM)
    outs = (
        [shape(head, bf)] * 3
        + [shape(square, bf)] * 5
        + [shape((4096, 1024), bf), shape((1024, 4096), bf), shape(square, bf)]
        + [shape(head, bf)] * 4
        + [shape(rows, bf), shape(rows, f32), shape(rows, bf), shape(rows, bf)]
        + [shape((128, 1024), bf)] * 3
        + [shape(rows, bf), shape(rows, f32), shape(rows, bf)]
        + [shape((512, 4096), bf)] * 2
        + [shape((4, 2, 1024), f32), shape((16, 1024), f32), shape((2, 128, 128), f32)]
        + [shape((16, 1024), f32)]
    )
    places = [ANY] * 14 + [inside] + [ANY] * 12 + [inside] * 4
    n = 15
    return pl.pallas_call(
        front_body,
        out_shape=outs,
        in_specs=[ANY] * 14 + [inside, scalar, scalar],
        out_specs=places,
        scratch_shapes=[
            vm((512, 128), f32),
            vm((32, 64, 1024), bf),
            vm(square, bf),
            vm((3, 1024, 512), bf),
            vm(square, bf),
            vm(head, bf),
            vm(head, bf),
            vm(head, bf),
            vm((4, 1024, 128), bf),
            vm(rows, bf),
            vm(rows, f32),
            vm(rows, bf),
            vm(rows, bf),
            vm((2, 128, 1024), bf),
            vm((128, 1024), bf),
            vm(rows, bf),
            vm(rows, f32),
            vm(rows, bf),
            vm(rows, bf),
            vm((512, 4096), f32),
            vm((512, 4096), bf),
            vm((512, 4096), bf),
            vm((2, 1024, 1024), bf),
            vm((4, 1024), f32),
            pltpu.SemaphoreType.DMA((n, 31)),
            pltpu.SemaphoreType.DMA((n, 31)),
            pltpu.SemaphoreType.DMA((n,)),
            pltpu.SemaphoreType.DMA((3,)),
            pltpu.SemaphoreType.DMA((4,)),
            pltpu.SemaphoreType.DMA((4,)),
            pltpu.SemaphoreType.DMA((4,)),
            pltpu.SemaphoreType.DMA((2,)),
            pltpu.SemaphoreType.DMA((25,)),
            pltpu.SemaphoreType.DMA,
        ],
        compiler_params=pltpu.CompilerParams(
            collective_id=collective_id,
            has_side_effects=True,
            vmem_limit_bytes=59 * 1024 * 1024,
        ),
        name="front",
    )(*operands)


def emit_body(*refs):
    n = (len(refs) - 10) // 3
    srcs, total, dsts = refs[:n], refs[n], refs[n + 1 : 2 * n + 1]
    cuts, share = refs[2 * n + 1 : 2 * n + 8], refs[2 * n + 8]
    held, sem = refs[2 * n + 9 : -1], refs[-1]
    loads = [pltpu.make_async_copy(srcs[i], held[i], sem.at[i]) for i in range(n)]
    copies = [pltpu.make_async_copy(held[i], dsts[i], sem.at[i]) for i in range(n)]
    for load in loads:
        load.start()
    index = 2 * lax.axis_index("dp") + lax.axis_index("seq")
    block = total[:, pl.ds(pl.multiple_of(index // 4 * 128, 128), 128)]
    moved = block
    for k in range(1, 4):
        moved = jnp.where(index % 4 == k, pltpu.roll(block, 128 - 32 * k, 1), moved)
    for i, cut in enumerate(cuts):
        cut[...] = moved[i, 0:32]
    block = total[:, pl.ds(pl.multiple_of(index % 8 * 128, 128), 128)]
    chosen = lax.broadcasted_iota(jnp.int32, block.shape, 0) == 7 + index // 8
    share[...] = jnp.sum(jnp.where(chosen, block, 0.0), axis=0)
    for load, copy in zip(loads, copies):
        load.wait()
        copy.start()
    for copy in copies:
        copy.wait()


def emit(arrays, total):
    inside = pl.BlockSpec(memory_space=pltpu.VMEM)
    n = len(arrays)
    return pl.pallas_call(
        emit_body,
        out_shape=[jax.ShapeDtypeStruct(a.shape, a.dtype) for a in arrays]
        + [jax.ShapeDtypeStruct((32,), jnp.float32)] * 7
        + [jax.ShapeDtypeStruct((128,), jnp.float32)],
        in_specs=[ANY] * n + [inside],
        out_specs=[ANY] * n + [inside] * 8,
        scratch_shapes=[pltpu.VMEM(a.shape, a.dtype) for a in arrays]
        + [pltpu.SemaphoreType.DMA((n,))],
        name="emit",
    )(*arrays, total)


HEADS = 16
HEAD_DIM = 64


EPSILON = 1e-05
NEG_BIG = -1e30


def norm_rows(value, gain, shift):
    center = value - jnp.mean(value, axis=-1, keepdims=True)
    spread = jnp.mean(center * center, axis=-1, keepdims=True)
    return center * lax.rsqrt(spread + EPSILON) * gain + shift


def project(rows, weight):
    return jnp.einsum("bsd,de->bse", rows, weight, preferred_element_type=jnp.float32)


def project_back(grads, weight):
    return jnp.einsum("bse,de->bsd", grads, weight, preferred_element_type=jnp.float32)


def weight_grad(rows, grads):
    return jnp.einsum("bsd,bse->de", rows, grads, preferred_element_type=jnp.float32)


def row_total(grads):
    return jnp.sum(grads.astype(jnp.float32), axis=(0, 1))


def split_heads(value):
    return value.reshape(value.shape[0], value.shape[1], HEADS, HEAD_DIM)


def join_heads(value):
    return value.reshape(value.shape[0], value.shape[1], HEADS * HEAD_DIM)


def scores_of(queries, keys_in, allowed):
    raw_scores = (
        jnp.einsum(
            "bqhd,bkhd->bhqk",
            split_heads(queries),
            split_heads(keys_in),
            preferred_element_type=jnp.float32,
        )
        * 0.125
    )
    return jnp.where(allowed, raw_scores, NEG_BIG)


def attend(queries, keys_in, values_in, allowed):
    scores = scores_of(queries, keys_in, allowed)
    row_max = jnp.max(scores, axis=-1, keepdims=True)
    exponent = jnp.exp(scores - row_max)
    total = jnp.sum(exponent, axis=-1, keepdims=True)
    attn_weights = exponent / total
    mixed_rows = jnp.einsum(
        "bhqk,bkhd->bqhd",
        attn_weights.astype(jnp.bfloat16),
        split_heads(values_in),
        preferred_element_type=jnp.float32,
    )
    return (join_heads(mixed_rows).astype(jnp.bfloat16), row_max + jnp.log(total))


def attend_back(queries, keys_in, values_in, allowed, log_total, grad_mixed):
    attn_weights = jnp.exp(scores_of(queries, keys_in, allowed) - log_total)
    grad_heads = split_heads(grad_mixed)
    grad_weights = jnp.einsum(
        "bqhd,bkhd->bhqk", grad_heads, split_heads(values_in), preferred_element_type=jnp.float32
    )
    grad_values = jnp.einsum(
        "bhqk,bqhd->bkhd",
        attn_weights.astype(jnp.bfloat16),
        grad_heads,
        preferred_element_type=jnp.float32,
    )
    inner_sum = jnp.sum(grad_weights * attn_weights, axis=-1, keepdims=True)
    grad_scores = (attn_weights * (grad_weights - inner_sum)).astype(jnp.bfloat16)
    grad_queries = (
        jnp.einsum(
            "bhqk,bkhd->bqhd", grad_scores, split_heads(keys_in), preferred_element_type=jnp.float32
        )
        * 0.125
    )
    grad_keys = (
        jnp.einsum(
            "bhqk,bqhd->bkhd", grad_scores, split_heads(queries), preferred_element_type=jnp.float32
        )
        * 0.125
    )
    return (join_heads(grad_queries), join_heads(grad_keys), join_heads(grad_values))


def per_device(
    images,
    encoder_states,
    image_row,
    image_seg,
    caption_seg,
    ln1_gain,
    ln1_bias,
    w_query,
    w_key,
    w_value,
    w_out,
    ln2_gain,
    ln2_bias,
    c_query,
    c_key,
    c_value,
    c_out,
    ln3_gain,
    ln3_bias,
    w_in,
    b_in,
    w_outer,
    b_outer,
    cotangent,
):
    mixing = (
        lax.all_gather(ln1_gain, ("dp", "seq"), axis=0, tiled=True),
        lax.all_gather(ln1_bias, ("dp", "seq"), axis=0, tiled=True),
        lax.all_gather(w_query, ("dp", "seq"), axis=0, tiled=True),
        lax.all_gather(w_key, ("dp", "seq"), axis=0, tiled=True),
        lax.all_gather(w_value, ("dp", "seq"), axis=0, tiled=True),
        lax.all_gather(w_out, ("dp", "seq"), axis=0, tiled=True),
        lax.all_gather(ln2_gain, ("dp", "seq"), axis=0, tiled=True),
        lax.all_gather(ln2_bias, ("dp", "seq"), axis=0, tiled=True),
        lax.all_gather(c_query, ("dp", "seq"), axis=0, tiled=True),
        lax.all_gather(c_key, ("dp", "seq"), axis=0, tiled=True),
        lax.all_gather(c_value, ("dp", "seq"), axis=0, tiled=True),
        lax.all_gather(c_out, ("dp", "seq"), axis=0, tiled=True),
    )
    (
        gain_a,
        bias_a,
        query_w,
        key_w,
        value_w,
        out_w,
        gain_b,
        bias_b,
        cross_qw,
        cross_kw,
        cross_vw,
        cross_ow,
    ) = mixing
    shard = images.shape[1]
    seq_index = lax.axis_index("seq")
    full_len = shard * lax.axis_size("seq")
    inputs_f = images.astype(jnp.float32)
    gain_a32, bias_a32 = (gain_a.astype(jnp.float32), bias_a.astype(jnp.float32))
    normed_a = norm_rows(inputs_f, gain_a32, bias_a32).astype(jnp.bfloat16)
    queries = project(normed_a, query_w).astype(jnp.bfloat16)
    keys_local = project(normed_a, key_w).astype(jnp.bfloat16)
    values_local = project(normed_a, value_w).astype(jnp.bfloat16)
    keys_all, values_all = (
        lax.all_gather(keys_local, "seq", axis=1, tiled=True),
        lax.all_gather(values_local, "seq", axis=1, tiled=True),
    )
    query_pos = seq_index * shard + jnp.arange(shard, dtype=jnp.int32)
    key_pos = jnp.arange(full_len, dtype=jnp.int32)
    causal = (key_pos[None, :] <= query_pos[:, None])[None, None]
    self_out, self_lse = attend(queries, keys_all, values_all, causal)
    after_self = inputs_f + project(self_out, out_w)
    gain_b32, bias_b32 = (gain_b.astype(jnp.float32), bias_b.astype(jnp.float32))
    normed_b = norm_rows(after_self, gain_b32, bias_b32).astype(jnp.bfloat16)
    cross_queries = project(normed_b, cross_qw).astype(jnp.bfloat16)
    encoder_all = lax.all_gather(encoder_states, "dp", axis=0, tiled=True)
    caption = jnp.take(encoder_all, image_row, axis=0)
    cross_keys = project(caption, cross_kw).astype(jnp.bfloat16)
    cross_values = project(caption, cross_vw).astype(jnp.bfloat16)
    caption_mask = (jnp.take(caption_seg, image_row, axis=0) == image_seg[:, None])[
        :, None, None, :
    ]
    cross_out, cross_lse = attend(cross_queries, cross_keys, cross_values, caption_mask)
    after_cross = after_self + project(cross_out, cross_ow)
    feed_weights = (
        lax.all_gather(ln3_gain, ("dp", "seq"), axis=0, tiled=True),
        lax.all_gather(ln3_bias, ("dp", "seq"), axis=0, tiled=True),
        lax.all_gather(w_in, ("dp", "seq"), axis=0, tiled=True),
        lax.all_gather(b_in, ("dp", "seq"), axis=0, tiled=True),
        lax.all_gather(w_outer, ("dp", "seq"), axis=0, tiled=True),
        lax.all_gather(b_outer, ("dp", "seq"), axis=0, tiled=True),
    )
    gain_c, bias_c, inner_w, inner_b, outer_w, outer_b = feed_weights
    gain_c32, bias_c32 = (gain_c.astype(jnp.float32), bias_c.astype(jnp.float32))
    normed_c = norm_rows(after_cross, gain_c32, bias_c32).astype(jnp.bfloat16)
    hidden_pre = project(normed_c, inner_w) + inner_b.astype(jnp.float32)
    activated = jax.nn.gelu(hidden_pre).astype(jnp.bfloat16)
    result = after_cross + project(activated, outer_w) + outer_b.astype(jnp.float32)
    block_out = result.astype(jnp.bfloat16)
    inner_wb, outer_wb = (feed_weights[2], feed_weights[4])
    grad_result = cotangent.astype(jnp.float32)
    grad_outer_w = weight_grad(activated, cotangent)
    grad_outer_b = row_total(cotangent)
    grad_act = project_back(cotangent, outer_wb)
    _, gelu_back = jax.vjp(jax.nn.gelu, hidden_pre)
    grad_hidden = gelu_back(grad_act)[0].astype(jnp.bfloat16)
    grad_inner_w = weight_grad(normed_c, grad_hidden)
    grad_inner_b = row_total(grad_hidden)
    grad_normed_c = project_back(grad_hidden, inner_wb)
    _, norm_c_back = jax.vjp(norm_rows, after_cross, gain_c32, bias_c32)
    grad_cross_part, grad_gain_c, grad_bias_c = norm_c_back(grad_normed_c)
    grad_after_cross = grad_result + grad_cross_part
    feed_sums = (
        lax.psum_scatter(grad_gain_c, ("dp", "seq"), scatter_dimension=0, tiled=True),
        lax.psum_scatter(grad_bias_c, ("dp", "seq"), scatter_dimension=0, tiled=True),
        lax.psum_scatter(grad_inner_w, ("dp", "seq"), scatter_dimension=0, tiled=True),
        lax.psum_scatter(grad_inner_b, ("dp", "seq"), scatter_dimension=0, tiled=True),
        lax.psum_scatter(grad_outer_w, ("dp", "seq"), scatter_dimension=0, tiled=True),
        lax.psum_scatter(grad_outer_b, ("dp", "seq"), scatter_dimension=0, tiled=True),
    )
    query_wb, key_wb, value_wb, out_wb = (mixing[2], mixing[3], mixing[4], mixing[5])
    cross_qwb, cross_kwb, cross_vwb, cross_owb = (mixing[8], mixing[9], mixing[10], mixing[11])
    grad_branch_b = grad_after_cross.astype(jnp.bfloat16)
    grad_cross_ow = weight_grad(cross_out, grad_branch_b)
    grad_cross_out = project_back(grad_branch_b, cross_owb).astype(jnp.bfloat16)
    grad_cq_raw, grad_ck_raw, grad_cv_raw = attend_back(
        cross_queries, cross_keys, cross_values, caption_mask, cross_lse, grad_cross_out
    )
    grad_cross_q = grad_cq_raw.astype(jnp.bfloat16)
    grad_ck_sum, grad_cv_sum = (
        lax.psum_scatter(
            grad_ck_raw.astype(jnp.bfloat16), "seq", scatter_dimension=1, tiled=True
        ).astype(jnp.float32),
        lax.psum_scatter(
            grad_cv_raw.astype(jnp.bfloat16), "seq", scatter_dimension=1, tiled=True
        ).astype(jnp.float32),
    )
    grad_ck_low = grad_ck_sum.astype(jnp.bfloat16)
    grad_cv_low = grad_cv_sum.astype(jnp.bfloat16)
    piece_len = grad_ck_sum.shape[1]
    caption_piece = lax.dynamic_slice_in_dim(caption, seq_index * piece_len, piece_len, 1)
    grad_cross_kw = weight_grad(caption_piece, grad_ck_low)
    grad_cross_vw = weight_grad(caption_piece, grad_cv_low)
    grad_caption = project_back(grad_ck_low, cross_kwb) + project_back(grad_cv_low, cross_vwb)
    row_count = encoder_all.shape[0]
    row_onehot = (image_row[:, None] == jnp.arange(row_count, dtype=jnp.int32)[None, :]).astype(
        jnp.float32
    )
    grad_rows = jnp.einsum("br,bsd->rsd", row_onehot, grad_caption, precision=lax.Precision.HIGHEST)
    caption_grad = lax.psum_scatter(
        grad_rows.astype(jnp.bfloat16), "dp", scatter_dimension=0, tiled=True
    ).astype(jnp.float32)
    grad_cross_qw = weight_grad(normed_b, grad_cross_q)
    grad_normed_b = project_back(grad_cross_q, cross_qwb)
    _, norm_b_back = jax.vjp(norm_rows, after_self, gain_b32, bias_b32)
    grad_self_part, grad_gain_b, grad_bias_b = norm_b_back(grad_normed_b)
    grad_after_self = grad_after_cross + grad_self_part
    grad_branch_a = grad_after_self.astype(jnp.bfloat16)
    grad_out_w = weight_grad(self_out, grad_branch_a)
    grad_self_out = project_back(grad_branch_a, out_wb).astype(jnp.bfloat16)
    keys_back, values_back = (keys_all, values_all)
    grad_q_raw, grad_k_raw, grad_v_raw = attend_back(
        queries, keys_back, values_back, causal, self_lse, grad_self_out
    )
    grad_k_sum, grad_v_sum = (
        lax.psum_scatter(
            grad_k_raw.astype(jnp.bfloat16), "seq", scatter_dimension=1, tiled=True
        ).astype(jnp.float32),
        lax.psum_scatter(
            grad_v_raw.astype(jnp.bfloat16), "seq", scatter_dimension=1, tiled=True
        ).astype(jnp.float32),
    )
    grad_q_low = grad_q_raw.astype(jnp.bfloat16)
    grad_k_low = grad_k_sum.astype(jnp.bfloat16)
    grad_v_low = grad_v_sum.astype(jnp.bfloat16)
    grad_query_w = weight_grad(normed_a, grad_q_low)
    grad_key_w = weight_grad(normed_a, grad_k_low)
    grad_value_w = weight_grad(normed_a, grad_v_low)
    grad_normed_a = (
        project_back(grad_q_low, query_wb)
        + project_back(grad_k_low, key_wb)
        + project_back(grad_v_low, value_wb)
    )
    _, norm_a_back = jax.vjp(norm_rows, inputs_f, gain_a32, bias_a32)
    grad_input_part, grad_gain_a, grad_bias_a = norm_a_back(grad_normed_a)
    image_grad = grad_after_self + grad_input_part
    mix_sums = (
        lax.psum_scatter(grad_gain_a, ("dp", "seq"), scatter_dimension=0, tiled=True),
        lax.psum_scatter(grad_bias_a, ("dp", "seq"), scatter_dimension=0, tiled=True),
        lax.psum_scatter(grad_query_w, ("dp", "seq"), scatter_dimension=0, tiled=True),
        lax.psum_scatter(grad_key_w, ("dp", "seq"), scatter_dimension=0, tiled=True),
        lax.psum_scatter(grad_value_w, ("dp", "seq"), scatter_dimension=0, tiled=True),
        lax.psum_scatter(grad_out_w, ("dp", "seq"), scatter_dimension=0, tiled=True),
        lax.psum_scatter(grad_gain_b, ("dp", "seq"), scatter_dimension=0, tiled=True),
        lax.psum_scatter(grad_bias_b, ("dp", "seq"), scatter_dimension=0, tiled=True),
        lax.psum_scatter(grad_cross_qw, ("dp", "seq"), scatter_dimension=0, tiled=True),
        lax.psum_scatter(grad_cross_kw, ("dp", "seq"), scatter_dimension=0, tiled=True),
        lax.psum_scatter(grad_cross_vw, ("dp", "seq"), scatter_dimension=0, tiled=True),
        lax.psum_scatter(grad_cross_ow, ("dp", "seq"), scatter_dimension=0, tiled=True),
    )
    return (
        block_out,
        image_grad,
        caption_grad,
        mix_sums[0],
        mix_sums[1],
        mix_sums[2],
        mix_sums[3],
        mix_sums[4],
        mix_sums[5],
        mix_sums[6],
        mix_sums[7],
        mix_sums[8],
        mix_sums[9],
        mix_sums[10],
        mix_sums[11],
        feed_sums[0],
        feed_sums[1],
        feed_sums[2],
        feed_sums[3],
        feed_sums[4],
        feed_sums[5],
    )


def block_device(
    images,
    encoder_states,
    image_row,
    image_seg,
    caption_seg,
    ln1_gain,
    ln1_bias,
    w_query,
    w_key,
    w_value,
    w_out,
    ln2_gain,
    ln2_bias,
    c_query,
    c_key,
    c_value,
    c_out,
    ln3_gain,
    ln3_bias,
    w_in,
    b_in,
    w_outer,
    b_outer,
    cotangent,
):
    core = lax.axis_index("seq")
    index = 2 * lax.axis_index("dp") + core
    width = images.shape[2]
    vectors = (ln1_gain, ln1_bias, ln2_gain, ln2_bias, ln3_gain, ln3_bias, b_outer)
    lanes = b_outer.shape[0]
    stack = jnp.tile(jnp.stack(vectors).astype(jnp.float32), (1, 128 // lanes))
    place_of = jnp.arange(128, dtype=jnp.int32) // lanes == index % (128 // lanes)
    packed = jnp.concatenate(
        [
            jnp.where(place_of[None], stack, 0.0),
            b_in.astype(jnp.float32)[None],
            jnp.zeros((8, 128), jnp.float32),
        ]
    )
    o = dict(
        zip(
            FRONT_OUT,
            front(
                [
                    w_query,
                    w_key,
                    w_value,
                    packed,
                    w_out,
                    encoder_states,
                    c_query,
                    c_key,
                    c_value,
                    c_out,
                    w_outer,
                    w_in,
                    images[0],
                    cotangent[0],
                    caption_seg,
                    image_row,
                    image_seg,
                ],
                1,
            ),
        )
    )
    (
        grad_inner_w,
        grad_outer_w,
        sums,
        grad_caption,
        block_out,
        grad_branch_b,
        grad_cross_q,
        grad_ck,
        grad_cv,
        grad_branch_a,
        grad_after_self,
        grad_self_out,
    ) = middle(
        [o["h3"], o["du"], o["act"], cotangent[0], o["w_in_all"], o["w_outer_all"]]
        + [o["c_out_all"], o["c_query_all"], o["w_out_all"], o["y2"], o["y1"]]
        + [o["cq"], o["ck"], o["cv"], o["c_key_all"], o["c_value_all"]]
        + [o["ok"], o["vec"], o["sums"]],
        2,
    )
    image_grad, *big, total = scatter_tail(
        [o["q"], o["k"], o["v"], o["heads"], o["lse"], grad_self_out, o["h1"], o["attn"]]
        + [grad_branch_a, o["h2"], grad_cross_q, o["cattn"], grad_branch_b, o["caption"]]
        + [grad_ck, grad_cv, o["wq"], o["wk"], o["wv"], images[0], grad_after_self, o["vec"], sums]
        + [grad_caption, jnp.broadcast_to(image_row.astype(jnp.float32)[:, None], (8, width))],
        4,
    )
    arrays = emit([block_out, image_grad, grad_inner_w, grad_outer_w, *big], total)
    block_out, image_grad, grad_inner_w, grad_outer_w, *big = arrays[:-8]
    small, share = arrays[-8:-1], arrays[-1]
    return (
        block_out[None],
        image_grad[None],
        big[5][None],
        small[0],
        small[1],
        big[6],
        big[7],
        big[8],
        big[0],
        small[2],
        small[3],
        big[1],
        big[3],
        big[4],
        big[2],
        small[4],
        small[5],
        grad_inner_w,
        share,
        grad_outer_w,
        small[6],
    )


def solution(mesh):
    in_specs = (
        P("dp", "seq", None),
        P("dp", None, None),
        P("dp"),
        P("dp"),
        P(),
        P(("dp", "seq")),
        P(("dp", "seq")),
        P(("dp", "seq"), None),
        P(("dp", "seq"), None),
        P(("dp", "seq"), None),
        P(("dp", "seq"), None),
        P(("dp", "seq")),
        P(("dp", "seq")),
        P(("dp", "seq"), None),
        P(("dp", "seq"), None),
        P(("dp", "seq"), None),
        P(("dp", "seq"), None),
        P(("dp", "seq")),
        P(("dp", "seq")),
        P(("dp", "seq"), None),
        P(("dp", "seq")),
        P(("dp", "seq"), None),
        P(("dp", "seq")),
        P("dp", "seq", None),
    )
    out_specs = (
        P("dp", "seq", None),
        P("dp", "seq", None),
        P("dp", "seq", None),
        P(("dp", "seq")),
        P(("dp", "seq")),
        P(("dp", "seq"), None),
        P(("dp", "seq"), None),
        P(("dp", "seq"), None),
        P(("dp", "seq"), None),
        P(("dp", "seq")),
        P(("dp", "seq")),
        P(("dp", "seq"), None),
        P(("dp", "seq"), None),
        P(("dp", "seq"), None),
        P(("dp", "seq"), None),
        P(("dp", "seq")),
        P(("dp", "seq")),
        P(("dp", "seq"), None),
        P(("dp", "seq")),
        P(("dp", "seq"), None),
        P(("dp", "seq")),
    )
    kernels = mesh.shape["dp"] == 16 and mesh.shape["seq"] == 2
    return jax.shard_map(
        block_device if kernels else per_device,
        mesh=mesh,
        in_specs=in_specs,
        out_specs=out_specs,
        check_vma=False,
    )
```
